32 devices in a mesh: batch: 2 (over core), tm: 16 (over z, y, x).
Axes of the slice: x: 2, y: 2, z: 4, core: 2. Of those that a mesh axis runs over, the one named last changes fastest.
Arguments:
- series_in: bfloat16 [28, 1536, 512], P('batch', 'tm'), may hold values from -6 to 6
- out_cotangent: bfloat16 [28, 1536, 512], P('batch', 'tm'), may hold values from -6 to 6
- out_mask: int32 [28, 1536], P('batch', 'tm'), may hold values 0 or 1
- down_twelve: bfloat16 [12, 512, 512], replicated, may hold values from -0.078125 to 0.078125
- down_sixteen: bfloat16 [16, 512, 512], replicated, may hold values from -0.0625 to 0.0625
- iso_twelve: bfloat16 [128, 2, 512, 512], P('tm', None, 'batch'), may hold values from -0.1875 to 0.1875
- iso_sixteen: bfloat16 [96, 2, 512, 512], P('tm', None, 'batch'), may hold values from -0.1875 to 0.1875
- up_twelve: bfloat16 [512, 12, 512], replicated, may hold values from -0.25 to 0.25
- up_sixteen: bfloat16 [512, 16, 512], replicated, may hold values from -0.25 to 0.25
- branch_bias: bfloat16 [6, 512], replicated, may hold values from -3 to 3
- merge_weight: bfloat16 [2, 512, 512], replicated, may hold values from -0.1875 to 0.1875
- hidden_weight: bfloat16 [512, 2048], replicated, may hold values from -0.25 to 0.25
- hidden_bias: bfloat16 [2048], replicated, may hold values from -3 to 3
- output_weight: bfloat16 [2048, 512], replicated, may hold values from -0.125 to 0.125
- head_bias: bfloat16 [2, 512], replicated, may hold values from -3 to 3
- norm_gain: bfloat16 [3, 512], replicated, may hold values from 0.5 to 1.5
- norm_shift: bfloat16 [3, 512], replicated, may hold values from -2 to 2
Outputs:
- result: bfloat16 [28, 1536, 512], P('batch', 'tm')
- grad_series: bfloat16 [28, 1536, 512], P('batch', 'tm')
- grad_down_twelve: float32 [12, 512, 512], P(None, 'batch', 'tm')
- grad_down_sixteen: float32 [16, 512, 512], P(None, 'batch', 'tm')
- grad_iso_twelve: float32 [128, 2, 512, 512], P('tm', None, 'batch')
- grad_iso_sixteen: float32 [96, 2, 512, 512], P('tm', None, 'batch')
- grad_up_twelve: float32 [512, 12, 512], P('batch', None, 'tm')
- grad_up_sixteen: float32 [512, 16, 512], P('batch', None, 'tm')
- grad_branch_bias: float32 [6, 512], P(None, 'tm')
- grad_merge_weight: float32 [2, 512, 512], P(None, 'batch', 'tm')
- grad_hidden_weight: float32 [512, 2048], P('batch', 'tm')
- grad_hidden_bias: float32 [2048], P('tm')
- grad_output_weight: float32 [2048, 512], P('batch', 'tm')
- grad_head_bias: float32 [2, 512], P(None, 'tm')
- grad_norm_gain: float32 [3, 512], P(None, 'tm')
- grad_norm_shift: float32 [3, 512], P(None, 'tm')
The draws below stay inside these ranges and needn't reach their ends.
All inputs are finite; a program needn't handle non-finite values. No bound on the sum of `out_mask` on one device may be relied on, other than what follows from the above.
Results may differ from the reference program's by a relative error of at most 0.015.
Values may be sent and summed in bfloat16 or wider, within the bound.
A program may use at most 320 MiB of HBM per device.

```python
import math
import jax
import jax.numpy as jnp
from jax import lax

D = 512
FF = 2048
SCALE_ONE = 12
SCALE_TWO = 16
LENGTH = 1536
SERIES = 28
BINS_ONE = 128
BINS_TWO = 96


def touch_ends(values, key, smallest, high):
    place = [jax.random.randint(jax.random.fold_in(key, axis), (), 0, length) for axis, length in enumerate(values.shape)]
    main_axis = values.shape.index(max(values.shape))
    beside = place[:main_axis] + [(place[main_axis] + 1) % values.shape[main_axis]] + place[main_axis + 1:]
    return values.at[tuple(place)].set(smallest).at[tuple(beside)].set(high)


def shard_levels(key, shape, cuts, low, largest):
    def one(dim, shards_of):
        draws = jax.random.uniform(jax.random.fold_in(jax.random.fold_in(key, 6), dim), (shards_of,), jnp.float32, low / len(cuts), largest / len(cuts))
        return jnp.repeat(jnp.exp(draws), shape[dim] // shards_of).reshape((-1,) + (1,) * (len(shape) - dim - 1))

    level = one(*cuts[0])
    for cut in cuts[1:]:
        level = level * one(*cut)
    return level


def gaussian(stream_key, extent, width, limit, cuts=(), held_as=jnp.bfloat16):
    drawn = jax.random.normal(stream_key, extent, jnp.float32) * width
    if len(cuts) > 0:
        drawn = shard_levels(stream_key, extent, cuts, -0.22, 0.18) * drawn
    return jnp.clip(drawn, min=-limit, max=limit).astype(held_as)


def setup_inputs(seed: int = 0) -> dict:
    key_list = jax.random.split(jax.random.key(seed), 18)
    series_in = gaussian(key_list[0], (SERIES, LENGTH, D), 1.0, 6.0, ((0, 2), (1, 16)))
    out_cotangent = gaussian(key_list[1], (SERIES, LENGTH, D), 1.0, 6.0, ((0, 2), (1, 16)))
    out_mask = touch_ends((jax.random.randint(key_list[2], (SERIES, LENGTH), 0, 4) < 3).astype(jnp.int32), jax.random.fold_in(key_list[2], 1), 0, 1)
    down_twelve = gaussian(key_list[3], (SCALE_ONE, D, D), (SCALE_ONE * D) ** -0.5, 0.078125)
    down_sixteen = gaussian(key_list[4], (SCALE_TWO, D, D), (SCALE_TWO * D) ** -0.5, 0.0625)
    iso_twelve = gaussian(key_list[5], (BINS_ONE, 2, D, D), (2 * D) ** -0.5, 0.1875, ((0, 16), (2, 2)))
    iso_sixteen = gaussian(key_list[6], (BINS_TWO, 2, D, D), (2 * D) ** -0.5, 0.1875, ((0, 16), (2, 2)))
    up_twelve = gaussian(key_list[7], (D, SCALE_ONE, D), D ** -0.5, 0.25)
    up_sixteen = gaussian(key_list[8], (D, SCALE_TWO, D), D ** -0.5, 0.25)
    branch_bias = gaussian(key_list[9], (6, D), 0.5, 3.0)
    merge_weight = gaussian(key_list[10], (2, D, D), (2 * D) ** -0.5, 0.1875)
    hidden_weight = gaussian(key_list[11], (D, FF), D ** -0.5, 0.25)
    hidden_bias = gaussian(key_list[12], (FF,), 0.5, 3.0)
    output_weight = gaussian(key_list[13], (FF, D), FF ** -0.5, 0.125)
    head_bias = gaussian(key_list[14], (2, D), 0.5, 3.0)
    norm_gain = jnp.clip(1.0 + 0.1 * jax.random.normal(key_list[15], (3, D), jnp.float32), 0.5, 1.5).astype(jnp.bfloat16)
    norm_shift = gaussian(key_list[16], (3, D), 0.3, 2.0)
    return dict(series_in=series_in, out_cotangent=out_cotangent, out_mask=out_mask, down_twelve=down_twelve, down_sixteen=down_sixteen, iso_twelve=iso_twelve, iso_sixteen=iso_sixteen, up_twelve=up_twelve, up_sixteen=up_sixteen, branch_bias=branch_bias, merge_weight=merge_weight, hidden_weight=hidden_weight, hidden_bias=hidden_bias, output_weight=output_weight, head_bias=head_bias, norm_gain=norm_gain, norm_shift=norm_shift)


HIGHEST = lax.Precision.HIGHEST
EPSILON = 1e-05

@jax.custom_vjp
def low(v):
    return lax.optimization_barrier(v.astype(jnp.bfloat16)).astype(jnp.float32)

@jax.custom_vjp
def low_back(v):
    return v

def low_keep(v):
    return (low(v), None)

def low_pass(kept, grad):
    return (grad,)

def back_keep(v):
    return (v, None)

def back_low(kept, grad):
    return (low(grad),)
low.defvjp(low_keep, low_pass)
low_back.defvjp(back_keep, back_low)

def matmul(left_side, right_side):
    return jnp.dot(left_side, right_side, precision=HIGHEST, preferred_element_type=jnp.float32)

def layer_norm(values, gain_row, bias_row):
    center = values - lax.optimization_barrier(jnp.mean(values, axis=-1, keepdims=True))
    spread = lax.optimization_barrier(jnp.mean(center * center, axis=-1, keepdims=True))
    return center * lax.rsqrt(spread + EPSILON) * gain_row + bias_row

def dft_tables(length):
    position = jnp.arange(length, dtype=jnp.int32)
    product = position[:, None] * position[None, :] % length
    angle_value = product.astype(jnp.float32) * (2.0 * math.pi / length)
    factor = 1.0 / math.sqrt(length)
    return (jnp.cos(angle_value) * factor, jnp.sin(angle_value) * factor)

def decompose(series_value, half_window):
    length = series_value.shape[0]
    padded = jnp.concatenate([jnp.repeat(series_value[:1], half_window, axis=0), series_value, jnp.repeat(series_value[-1:], half_window, axis=0)], axis=0)
    running = padded[0:length]
    for offset in range(1, 2 * half_window + 1):
        running = running + padded[offset:offset + length]
    return series_value - running / (2 * half_window + 1)

def branch(seasonal, down_weight, iso_weight, up_weight, bias_down, bias_iso, bias_up, gain_row, bias_row):
    length, channels = seasonal.shape
    kernel = down_weight.shape[0]
    pieces = length // kernel
    blocks = seasonal.reshape(pieces, kernel * channels)
    down_pre = low_back(matmul(blocks, down_weight.reshape(kernel * channels, channels)) + bias_down)
    down_value = low(jnp.tanh(down_pre))
    cosine, sine = dft_tables(pieces)
    spectrum_real = low_back(low(matmul(cosine, down_value)))
    spectrum_imag = low_back(low(-matmul(sine, down_value)))
    real_weight = iso_weight[:, 0]
    imag_weight = iso_weight[:, 1]
    mixed_real = jnp.einsum('fd,fde->fe', spectrum_real, real_weight, precision=HIGHEST) - jnp.einsum('fd,fde->fe', spectrum_imag, imag_weight, precision=HIGHEST)
    mixed_imag = jnp.einsum('fd,fde->fe', spectrum_real, imag_weight, precision=HIGHEST) + jnp.einsum('fd,fde->fe', spectrum_imag, real_weight, precision=HIGHEST)
    mixed_real = low_back(low(mixed_real))
    mixed_imag = low_back(low(mixed_imag))
    iso_out = low_back(matmul(cosine, mixed_real) - matmul(sine, mixed_imag))
    inner = low(layer_norm(jnp.tanh(iso_out + bias_iso) + down_value, gain_row, bias_row))
    up_pre = low_back(matmul(inner, up_weight.reshape(channels, kernel * channels)).reshape(length, channels) + bias_up)
    return layer_norm(jnp.tanh(up_pre) + seasonal, gain_row, bias_row)

def layer(series_value, params, mask_value):
    down_a, down_b, iso_a, iso_b, up_a, up_b, branch_bias, merge_weight, hidden_weight, hidden_bias, output_weight, head_bias, norm_gain, norm_shift = params
    seasonal_a = low(decompose(series_value, down_a.shape[0] // 2))
    seasonal_b = low(decompose(series_value, down_b.shape[0] // 2))
    branch_a = low(branch(seasonal_a, down_a, iso_a, up_a, branch_bias[0], branch_bias[2], branch_bias[4], norm_gain[0], norm_shift[0]))
    branch_b = low(branch(seasonal_b, down_b, iso_b, up_b, branch_bias[1], branch_bias[3], branch_bias[5], norm_gain[0], norm_shift[0]))
    merged = low_back(matmul(branch_a, merge_weight[0]) + matmul(branch_b, merge_weight[1]) + head_bias[0])
    first_norm = low(layer_norm(merged, norm_gain[1], norm_shift[1]))
    hidden = low(jax.nn.gelu(low_back(matmul(first_norm, hidden_weight) + hidden_bias)))
    feed_out = low_back(matmul(hidden, output_weight) + head_bias[1])
    return layer_norm(merged + feed_out, norm_gain[2], norm_shift[2]) * mask_value[:, None]

def reference(series_in, out_cotangent, out_mask, down_twelve, down_sixteen, iso_twelve, iso_sixteen, up_twelve, up_sixteen, branch_bias, merge_weight, hidden_weight, hidden_bias, output_weight, head_bias, norm_gain, norm_shift):
    weights = tuple((member.astype(jnp.float32) for member in (down_twelve, down_sixteen, iso_twelve, iso_sixteen, up_twelve, up_sixteen, branch_bias, merge_weight, hidden_weight, hidden_bias, output_weight, head_bias, norm_gain, norm_shift)))

    def one_series(carried, inputs):
        series_row, cotangent_row, mask_row = inputs
        mask_value = mask_row.astype(jnp.float32)

        def forward(series_value, *params):
            return layer(series_value, params, mask_value)
        outputs, pullback = jax.vjp(forward, series_row.astype(jnp.float32), *weights)
        grads = pullback(cotangent_row.astype(jnp.float32))
        summed = tuple((running + grad_term for running, grad_term in zip(carried, grads[1:])))
        return (summed, (outputs.astype(jnp.bfloat16), grads[0].astype(jnp.bfloat16)))
    initial = tuple((jnp.zeros_like(member) for member in weights))
    totals, (result, grad_series) = lax.scan(one_series, initial, (series_in, out_cotangent, out_mask))
    return (result, grad_series, totals[0], totals[1], totals[2], totals[3], totals[4], totals[5], totals[6], totals[7], totals[8], totals[9], totals[10], totals[11], totals[12], totals[13])
```

```python
import math

import jax
import jax.numpy as jnp
import numpy as np
from jax import lax
from jax.sharding import PartitionSpec as P

FLOAT = jnp.float32
HALF_FLOAT = jnp.bfloat16
HIGHEST = lax.Precision.HIGHEST
EPSILON = 1e-05


def extended_2(block, sides, width):
    for axis, dim in sides:
        count = lax.axis_size(axis)
        forward = [(i, i + 1) for i in range(count - 1)]
        backward = [(target, source) for source, target in forward]
        low = lax.ppermute(
            lax.slice_in_dim(block, block.shape[dim] - width, None, axis=dim), axis, forward
        )
        high = lax.ppermute(lax.slice_in_dim(block, 0, width, axis=dim), axis, backward)
        block = jnp.concatenate([low, block, high], axis=dim)
    return block


def layer_norm(values, gain_row, bias_row):
    center = values - jnp.mean(values, axis=-1, keepdims=True)
    spread = jnp.mean(center * center, axis=-1, keepdims=True)
    return center * lax.rsqrt(spread + EPSILON) * gain_row + bias_row


def mix_table(devices, bins):
    length = devices * bins
    index = np.arange(length)
    angle = (2.0 * math.pi / length) * (np.outer(index, index) % length)
    factor = 1.0 / math.sqrt(length)
    table = np.stack([np.cos(angle) * factor, -np.sin(angle) * factor])
    table = table.reshape(2, devices, bins, length).transpose(1, 0, 2, 3)
    table = table.reshape(2 * length, length).astype(np.float32)
    high = table.astype(HALF_FLOAT)
    low = (table - high.astype(np.float32)).astype(HALF_FLOAT)
    return jnp.asarray(high), jnp.asarray(low)


def swap(values):
    return lax.all_to_all(values, "tm", split_axis=0, concat_axis=0, tiled=True)


def pad_series(values, devices):
    count = values.shape[0]
    extra = -count % devices
    return jnp.pad(values, ((0, extra),) + ((0, 0),) * (values.ndim - 1))


def to_spectrum(values):
    devices = lax.axis_size("tm")
    count, pieces, channels = values.shape
    gathered = swap(pad_series(values, devices))
    slots = gathered.shape[0] // devices
    gathered = gathered.reshape(devices, slots, pieces, channels)
    high, low = mix_table(devices, pieces)
    outs = []
    for slot in range(slots):
        data = gathered[:, slot].reshape(devices * pieces, channels)
        total = jnp.dot(high, data, preferred_element_type=FLOAT) + jnp.dot(
            low, data, preferred_element_type=FLOAT
        )
        outs.append(total.astype(HALF_FLOAT).reshape(devices, 2, pieces, channels))
    spread = swap(jnp.stack(outs, axis=1).reshape(devices * slots, 2, pieces, channels))
    return jnp.transpose(spread[:count], (2, 1, 0, 3))


def to_signal(spectrum):
    devices = lax.axis_size("tm")
    bins, _, count, channels = spectrum.shape
    gathered = swap(pad_series(jnp.transpose(spectrum, (2, 1, 0, 3)), devices))
    slots = gathered.shape[0] // devices
    gathered = gathered.reshape(devices, slots, 2 * bins, channels)
    high, low = mix_table(devices, bins)
    outs = []
    for slot in range(slots):
        data = gathered[:, slot].reshape(devices * 2 * bins, channels)
        total = jnp.einsum("kp,kd->pd", high, data, preferred_element_type=FLOAT) + jnp.einsum(
            "kp,kd->pd", low, data, preferred_element_type=FLOAT
        )
        outs.append(total.reshape(devices, bins, channels))
    spread = swap(jnp.stack(outs, axis=1).reshape(devices * slots, bins, channels))
    return spread[:count]


def spectral_mix(spectrum, weight):
    real_side = spectrum[:, 0]
    imaginary_side = spectrum[:, 1]
    real_weight = weight[:, 0]
    imaginary_weight = weight[:, 1]
    real_out = jnp.einsum(
        "fbd,fde->fbe", real_side, real_weight, preferred_element_type=FLOAT
    ) - jnp.einsum("fbd,fde->fbe", imaginary_side, imaginary_weight, preferred_element_type=FLOAT)
    imaginary_out = jnp.einsum(
        "fbd,fde->fbe", real_side, imaginary_weight, preferred_element_type=FLOAT
    ) + jnp.einsum("fbd,fde->fbe", imaginary_side, real_weight, preferred_element_type=FLOAT)
    return jnp.stack([real_out, imaginary_out], axis=1)


def spectral_back(grad_mixed, weight):
    grad_real = grad_mixed[:, 0]
    grad_imaginary = grad_mixed[:, 1]
    real_weight = weight[:, 0]
    imaginary_weight = weight[:, 1]
    back_real = jnp.einsum(
        "fbe,fde->fbd", grad_real, real_weight, preferred_element_type=FLOAT
    ) + jnp.einsum("fbe,fde->fbd", grad_imaginary, imaginary_weight, preferred_element_type=FLOAT)
    back_imaginary = jnp.einsum(
        "fbe,fde->fbd", grad_imaginary, real_weight, preferred_element_type=FLOAT
    ) - jnp.einsum("fbe,fde->fbd", grad_real, imaginary_weight, preferred_element_type=FLOAT)
    return jnp.stack([back_real, back_imaginary], axis=1)


def spectral_weight_grad(spectrum, grad_mixed):
    real_side = spectrum[:, 0]
    imaginary_side = spectrum[:, 1]
    grad_real = grad_mixed[:, 0]
    grad_imaginary = grad_mixed[:, 1]
    weight_real = jnp.einsum(
        "fbd,fbe->fde", real_side, grad_real, preferred_element_type=FLOAT
    ) + jnp.einsum("fbd,fbe->fde", imaginary_side, grad_imaginary, preferred_element_type=FLOAT)
    weight_imaginary = jnp.einsum(
        "fbd,fbe->fde", real_side, grad_imaginary, preferred_element_type=FLOAT
    ) - jnp.einsum("fbd,fbe->fde", imaginary_side, grad_real, preferred_element_type=FLOAT)
    return jnp.stack([weight_real, weight_imaginary], axis=1)


def extend_series(series_in, rim_width):
    padded = extended_2(series_in, (("tm", 1),), rim_width)
    position = lax.axis_index("tm")
    final_index = lax.axis_size("tm") - 1
    step_count = series_in.shape[1]
    left_rim = jnp.where(
        position == 0,
        jnp.broadcast_to(series_in[:, :1], padded[:, :rim_width].shape),
        padded[:, :rim_width],
    )
    right_rim = jnp.where(
        position == final_index,
        jnp.broadcast_to(series_in[:, -1:], padded[:, rim_width + step_count :].shape),
        padded[:, rim_width + step_count :],
    )
    return jnp.concatenate([left_rim, series_in, right_rim], axis=1)


def band(step_count, rim_width, half_window):
    row = np.arange(step_count)[:, None] + rim_width
    column = np.arange(step_count + 2 * rim_width)[None, :]
    return (np.abs(row - column) <= half_window).astype(HALF_FLOAT)


def seasonal_part(extended, series_in, half_window, rim_width):
    step_count = series_in.shape[1]
    matrix = jnp.asarray(band(step_count, rim_width, half_window))
    running = jnp.einsum("qr,brd->bqd", matrix, extended, preferred_element_type=FLOAT)
    return (series_in.astype(FLOAT) - running / (2 * half_window + 1)).astype(HALF_FLOAT)


def mean_back(grad, half_window, rim_width, is_first, is_final):
    step_count = grad.shape[1]
    matrix = jnp.asarray(band(step_count, rim_width, half_window))
    high = grad.astype(HALF_FLOAT)
    low = (grad - high.astype(FLOAT)).astype(HALF_FLOAT)
    wide = jnp.einsum("qr,bqd->brd", matrix, high, preferred_element_type=FLOAT) + jnp.einsum(
        "qr,bqd->brd", matrix, low, preferred_element_type=FLOAT
    )
    return wide / (2 * half_window + 1)


def batch_split(values, split, join):
    return lax.all_to_all(values, "batch", split_axis=split, concat_axis=join, tiled=True)


def time_sum(values, dim):
    return lax.psum_scatter(
        values.astype(HALF_FLOAT), "tm", scatter_dimension=dim, tiled=True
    ).astype(FLOAT)


def branch_forward(seasonal_low, down_weight, iso_weight, up_weight, bias_rows, gain_row, bias_row):
    series_count, step_count, channels = seasonal_low.shape
    kernel = down_weight.shape[0]
    pieces = step_count // kernel
    blocks = seasonal_low.reshape(series_count * pieces, kernel * channels)
    down_act = jnp.tanh(
        jnp.dot(
            blocks, down_weight.reshape(kernel * channels, channels), preferred_element_type=FLOAT
        )
        + bias_rows[0]
    )
    down_low = down_act.astype(HALF_FLOAT).reshape(series_count, pieces, channels)
    spectrum_low = to_spectrum(down_low)
    mixed_low = spectral_mix(spectrum_low, iso_weight).astype(HALF_FLOAT)
    iso_act = jnp.tanh(to_signal(mixed_low) + bias_rows[1])
    inner_in = iso_act + down_low.astype(FLOAT)
    inner_low = layer_norm(inner_in, gain_row, bias_row).astype(HALF_FLOAT)
    up_pre = jnp.dot(
        inner_low.reshape(series_count * pieces, channels),
        up_weight.reshape(channels, kernel * channels),
        preferred_element_type=FLOAT,
    )
    up_act = jnp.tanh(up_pre.reshape(series_count, step_count, channels) + bias_rows[2])
    outer_in = up_act + seasonal_low.astype(FLOAT)
    branch_out = layer_norm(outer_in, gain_row, bias_row)
    return (
        branch_out,
        (blocks, down_act, spectrum_low, iso_act, inner_in, inner_low, up_act, outer_in),
    )


def branch_backward(
    grad_out, seasonal_low, down_weight, iso_weight, up_weight, gain_row, bias_row, kept
):
    blocks, down_act, spectrum_low, iso_act, inner_in, inner_low, up_act, outer_in = kept
    series_count, step_count, channels = seasonal_low.shape
    kernel = down_weight.shape[0]
    pieces = step_count // kernel
    normed_out, outer_pull = jax.vjp(layer_norm, outer_in, gain_row, bias_row)
    grad_outer, gain_outer, shift_outer = outer_pull(grad_out)
    grad_up = (grad_outer * (1.0 - up_act * up_act)).astype(HALF_FLOAT)
    up_rows = grad_up.reshape(series_count * pieces, kernel * channels)
    inner_rows = inner_low.reshape(series_count * pieces, channels)
    up_flat = up_weight.reshape(channels, kernel * channels)
    grad_up_weight = jnp.einsum(
        "nd,nk->dk",
        batch_split(inner_rows, 1, 0),
        lax.all_gather(up_rows, "batch", axis=0, tiled=True),
        preferred_element_type=FLOAT,
    ).reshape(-1, kernel, channels)
    grad_up_bias = jnp.sum(grad_up.astype(FLOAT), axis=(0, 1))
    grad_inner = jnp.einsum("nk,dk->nd", up_rows, up_flat, preferred_element_type=FLOAT).reshape(
        series_count, pieces, channels
    )
    normed_inner, inner_pull = jax.vjp(layer_norm, inner_in, gain_row, bias_row)
    grad_inner_in, gain_inner, shift_inner = inner_pull(grad_inner)
    grad_iso = grad_inner_in * (1.0 - iso_act * iso_act)
    grad_iso_bias = jnp.sum(grad_iso, axis=(0, 1))
    grad_mixed = to_spectrum(grad_iso.astype(HALF_FLOAT))
    grad_spectrum = spectral_back(grad_mixed, iso_weight).astype(HALF_FLOAT)
    grad_iso_weight = spectral_weight_grad(
        batch_split(spectrum_low, 3, 2), lax.all_gather(grad_mixed, "batch", axis=2, tiled=True)
    )
    grad_down = to_signal(grad_spectrum) + grad_inner_in
    down_shaped = down_act.reshape(series_count, pieces, channels)
    grad_down_pre = (grad_down * (1.0 - down_shaped * down_shaped)).astype(HALF_FLOAT)
    down_rows = grad_down_pre.reshape(series_count * pieces, channels)
    down_flat = down_weight.reshape(kernel * channels, channels)
    batch_blocks = batch_split(seasonal_low.reshape(-1, kernel, channels), 2, 0)
    grad_down_weight = jnp.einsum(
        "nkc,nd->kcd",
        batch_blocks,
        lax.all_gather(down_rows, "batch", axis=0, tiled=True),
        preferred_element_type=FLOAT,
    )
    grad_down_bias = jnp.sum(grad_down_pre.astype(FLOAT), axis=(0, 1))
    grad_seasonal = (
        jnp.einsum("nd,kd->nk", down_rows, down_flat, preferred_element_type=FLOAT).reshape(
            series_count, step_count, channels
        )
        + grad_outer
    )
    return (
        grad_seasonal,
        (
            grad_down_weight,
            grad_up_weight,
            grad_iso_weight,
            grad_down_bias,
            grad_iso_bias,
            grad_up_bias,
            gain_outer + gain_inner,
            shift_outer + shift_inner,
        ),
    )


def per_device(
    series_in,
    out_cotangent,
    out_mask,
    down_twelve,
    down_sixteen,
    iso_twelve,
    iso_sixteen,
    up_twelve,
    up_sixteen,
    branch_bias,
    merge_weight,
    hidden_weight,
    hidden_bias,
    output_weight,
    head_bias,
    norm_gain,
    norm_shift,
):
    series_dev, step_count, channels = series_in.shape
    row_count = series_dev * step_count
    half_one = down_twelve.shape[0] // 2
    half_two = down_sixteen.shape[0] // 2
    rim_width = max(half_one, half_two)
    iso_whole_one, iso_whole_two = (
        lax.all_gather(iso_twelve, "batch", axis=2, tiled=True),
        lax.all_gather(iso_sixteen, "batch", axis=2, tiled=True),
    )
    biases = branch_bias.astype(FLOAT)
    gains = norm_gain.astype(FLOAT)
    shifts = norm_shift.astype(FLOAT)
    heads = head_bias.astype(FLOAT)
    extended = extend_series(series_in, rim_width)
    seasonal_one = seasonal_part(extended, series_in, half_one, rim_width)
    seasonal_two = seasonal_part(extended, series_in, half_two, rim_width)
    out_one, kept_one = branch_forward(
        seasonal_one,
        down_twelve,
        iso_whole_one,
        up_twelve,
        (biases[0], biases[2], biases[4]),
        gains[0],
        shifts[0],
    )
    out_two, kept_two = branch_forward(
        seasonal_two,
        down_sixteen,
        iso_whole_two,
        up_sixteen,
        (biases[1], biases[3], biases[5]),
        gains[0],
        shifts[0],
    )
    branch_low = jnp.concatenate(
        [out_one.astype(HALF_FLOAT), out_two.astype(HALF_FLOAT)], axis=2
    ).reshape(row_count, 2 * channels)
    merge_flat = merge_weight.reshape(2 * channels, channels)
    merged = jnp.dot(branch_low, merge_flat, preferred_element_type=FLOAT) + heads[0]
    first_low = layer_norm(merged, gains[1], shifts[1]).astype(HALF_FLOAT)
    hidden_pre = jnp.dot(
        first_low, hidden_weight, preferred_element_type=FLOAT
    ) + hidden_bias.astype(FLOAT)
    hidden_low = jax.nn.gelu(hidden_pre).astype(HALF_FLOAT)
    final_in = merged + (
        jnp.dot(hidden_low, output_weight, preferred_element_type=FLOAT) + heads[1]
    )
    mask_rows = out_mask.astype(FLOAT).reshape(row_count, 1)
    result = (
        (layer_norm(final_in, gains[2], shifts[2]) * mask_rows)
        .astype(HALF_FLOAT)
        .reshape(series_dev, step_count, channels)
    )
    grad_result = out_cotangent.astype(FLOAT).reshape(row_count, channels) * mask_rows
    normed_final, final_pull = jax.vjp(layer_norm, final_in, gains[2], shifts[2])
    grad_final, gain_final, shift_final = final_pull(grad_result)
    grad_feed = grad_final.astype(HALF_FLOAT)
    grad_output_weight = jnp.einsum(
        "nf,nd->fd", hidden_low, grad_feed, preferred_element_type=FLOAT
    )
    grad_output_bias = jnp.sum(grad_feed.astype(FLOAT), axis=0)
    grad_hidden_low = jnp.einsum(
        "nd,fd->nf", grad_feed, output_weight, preferred_element_type=FLOAT
    )
    gelu_value, gelu_pull = jax.vjp(jax.nn.gelu, hidden_pre)
    grad_hidden_pre = gelu_pull(grad_hidden_low)[0].astype(HALF_FLOAT)
    grad_hidden_weight = jnp.einsum(
        "nd,nf->df", first_low, grad_hidden_pre, preferred_element_type=FLOAT
    )
    grad_hidden_bias = jnp.sum(grad_hidden_pre.astype(FLOAT), axis=0)
    grad_first = jnp.einsum(
        "nf,df->nd", grad_hidden_pre, hidden_weight, preferred_element_type=FLOAT
    )
    normed_first, first_pull = jax.vjp(layer_norm, merged, gains[1], shifts[1])
    grad_merged_norm, gain_first, shift_first = first_pull(grad_first)
    grad_merged = (grad_final + grad_merged_norm).astype(HALF_FLOAT)
    grad_merge_bias = jnp.sum(grad_merged.astype(FLOAT), axis=0)
    grad_merge_weight = jnp.einsum(
        "nk,nd->kd", branch_low, grad_merged, preferred_element_type=FLOAT
    ).reshape(2, channels, channels)
    grad_branch = jnp.einsum("nd,kd->nk", grad_merged, merge_flat, preferred_element_type=FLOAT)
    grad_out_one = grad_branch[:, :channels].reshape(series_dev, step_count, channels)
    grad_out_two = grad_branch[:, channels:].reshape(series_dev, step_count, channels)
    grad_seasonal_one, terms_one = branch_backward(
        grad_out_one,
        seasonal_one,
        down_twelve,
        iso_whole_one,
        up_twelve,
        gains[0],
        shifts[0],
        kept_one,
    )
    grad_seasonal_two, terms_two = branch_backward(
        grad_out_two,
        seasonal_two,
        down_sixteen,
        iso_whole_two,
        up_sixteen,
        gains[0],
        shifts[0],
        kept_two,
    )
    position = lax.axis_index("tm")
    final_index = lax.axis_size("tm") - 1
    wide = mean_back(grad_seasonal_one, half_one, rim_width, None, None) + mean_back(
        grad_seasonal_two, half_two, rim_width, None, None
    )
    low_rim = wide[:, :rim_width]
    high_rim = wide[:, rim_width + step_count :]
    forward = [(i, i + 1) for i in range(final_index)]
    from_low = lax.ppermute(high_rim, "tm", forward)
    from_high = lax.ppermute(low_rim, "tm", [(j, i) for i, j in forward])
    edge_low = jnp.where(
        position == 0,
        jnp.pad(jnp.sum(low_rim, axis=1, keepdims=True), ((0, 0), (0, rim_width - 1), (0, 0))),
        from_low,
    )
    edge_high = jnp.where(
        position == final_index,
        jnp.pad(jnp.sum(high_rim, axis=1, keepdims=True), ((0, 0), (rim_width - 1, 0), (0, 0))),
        from_high,
    )
    mean_total = wide[:, rim_width : rim_width + step_count] + jnp.concatenate(
        [
            edge_low,
            jnp.zeros((series_dev, step_count - 2 * rim_width, channels), FLOAT),
            edge_high,
        ],
        axis=1,
    )
    grad_series = (grad_seasonal_one + grad_seasonal_two - mean_total).astype(HALF_FLOAT)
    grad_branch_bias = jnp.stack(
        [terms_one[3], terms_two[3], terms_one[4], terms_two[4], terms_one[5], terms_two[5]]
    )
    vectors = jnp.concatenate(
        [
            grad_branch_bias,
            terms_one[6][None] + terms_two[6][None],
            gain_first[None],
            gain_final[None],
            terms_one[7][None] + terms_two[7][None],
            shift_first[None],
            shift_final[None],
            grad_merge_bias[None],
            grad_output_bias[None],
        ]
    )
    devices = lax.axis_size("tm")
    vector_count = vectors.shape[0]
    packed = jnp.concatenate(
        [
            vectors.reshape(vector_count, devices, -1).transpose(1, 0, 2).reshape(devices, -1),
            grad_hidden_bias.reshape(devices, -1),
        ],
        axis=1,
    )
    packed = lax.psum(lax.psum_scatter(packed, "tm", scatter_dimension=0, tiled=True), "batch")[0]
    width = channels // devices
    rows = packed[: vector_count * width].reshape(vector_count, width)
    vector_parts = (
        rows[:6],
        packed[vector_count * width :],
        rows[12:14],
        rows[6:9],
        rows[9:12],
    )
    merge_half = lax.psum_scatter(grad_merge_weight, "batch", scatter_dimension=1, tiled=True)
    hidden_half = lax.psum_scatter(grad_hidden_weight, "batch", scatter_dimension=0, tiled=True)
    output_half = lax.psum_scatter(grad_output_weight, "batch", scatter_dimension=0, tiled=True)
    matrix_parts = (
        time_sum(terms_one[0], 2),
        time_sum(terms_two[0], 2),
        time_sum(terms_one[1], 2),
        time_sum(terms_two[1], 2),
        time_sum(merge_half, 2),
        time_sum(hidden_half, 1),
        time_sum(output_half, 1),
    )
    iso_parts = (terms_one[2], terms_two[2])
    return (
        result,
        grad_series,
        matrix_parts[0],
        matrix_parts[1],
        iso_parts[0],
        iso_parts[1],
        matrix_parts[2],
        matrix_parts[3],
        vector_parts[0],
        matrix_parts[4],
        matrix_parts[5],
        vector_parts[1],
        matrix_parts[6],
        vector_parts[2],
        vector_parts[3],
        vector_parts[4],
    )


def solution(mesh):
    placed = (
        P("batch", "tm", None),
        P("batch", "tm", None),
        P("batch", "tm"),
        P(),
        P(),
        P("tm", None, "batch", None),
        P("tm", None, "batch", None),
        P(),
        P(),
        P(),
        P(),
        P(),
        P(),
        P(),
        P(),
        P(),
        P(),
    )
    return jax.shard_map(
        per_device,
        mesh=mesh,
        in_specs=placed,
        out_specs=(
            P("batch", "tm", None),
            P("batch", "tm", None),
            P(None, "batch", "tm"),
            P(None, "batch", "tm"),
            P("tm", None, "batch", None),
            P("tm", None, "batch", None),
            P("batch", None, "tm"),
            P("batch", None, "tm"),
            P(None, "tm"),
            P(None, "batch", "tm"),
            P("batch", "tm"),
            P("tm"),
            P("batch", "tm"),
            P(None, "tm"),
            P(None, "tm"),
            P(None, "tm"),
        ),
        check_vma=False,
    )
```

```python
import functools
import math

import jax
import jax.numpy as jnp
import numpy as np
from jax import lax
from jax.experimental import pallas as pl
from jax.experimental.pallas import tpu as pltpu
from jax.sharding import PartitionSpec as P

FLOAT = jnp.float32
HALF_FLOAT = jnp.bfloat16
HIGHEST = lax.Precision.HIGHEST
EPSILON = 1e-05
MESH = pl.DeviceIdType.MESH


def extended_2(block, sides, width):
    for axis, dim in sides:
        count = lax.axis_size(axis)
        forward = [(i, i + 1) for i in range(count - 1)]
        backward = [(target, source) for source, target in forward]
        low = lax.ppermute(
            lax.slice_in_dim(block, block.shape[dim] - width, None, axis=dim), axis, forward
        )
        high = lax.ppermute(lax.slice_in_dim(block, 0, width, axis=dim), axis, backward)
        block = jnp.concatenate([low, block, high], axis=dim)
    return block


def layer_norm(values, gain_row, bias_row):
    center = values - jnp.mean(values, axis=-1, keepdims=True)
    spread = jnp.mean(center * center, axis=-1, keepdims=True)
    return center * lax.rsqrt(spread + EPSILON) * gain_row + bias_row


def round_up(value, multiple):
    return -(-value // multiple) * multiple


def spectral_constants(devices, pieces_list):
    padded = [round_up(pieces, 8) for pieces in pieces_list]
    per_time, per_bin = sum(padded), 2 * sum(padded)
    table = np.zeros((devices, per_bin, devices, per_time), np.float64)
    offset = 0
    for pieces, wide in zip(pieces_list, padded):
        length = devices * pieces
        index = np.arange(length)
        angle = (2.0 * math.pi / length) * (np.outer(index, index) % length)
        factor = 1.0 / math.sqrt(length)
        for part, values in enumerate((np.cos(angle) * factor, -np.sin(angle) * factor)):
            row = 2 * offset + part * wide
            table[:, row : row + pieces, :, offset : offset + pieces] = values.reshape(
                devices, pieces, devices, pieces
            )
        offset += wide
    table = table.reshape(devices * per_bin, devices * per_time).astype(np.float32)
    high = table.astype(HALF_FLOAT)
    low = (table - high.astype(np.float32)).astype(HALF_FLOAT)
    order = []
    offset = 0
    for wide in padded:
        for one_bin in range(wide):
            for part in range(2):
                for series in range(devices):
                    order.append(series * per_bin + 2 * offset + part * wide + one_bin)
        offset += wide
    move = np.zeros((devices * per_bin, devices * per_bin), np.float32)
    move[np.arange(len(order)), order] = 1.0
    move = move.astype(HALF_FLOAT)
    return (
        jnp.asarray(np.stack([high, low])),
        jnp.asarray(np.stack([high.T, low.T])),
        jnp.asarray(move),
        jnp.asarray(np.ascontiguousarray(move.T)),
    )


def dot_nn(left, right):
    return jnp.dot(left, right, preferred_element_type=FLOAT)


def dot_nt(left, right):
    return lax.dot_general(left, right, (((1,), (1,)), ((), ())), preferred_element_type=FLOAT)


def spectral_kernel(sizes, back, *refs):
    devices, batches, count, pieces_list = sizes
    (x_ref, w1_ref, w2_ref, table_ref, inverse_ref, move_ref, unmove_ref) = refs[:7]
    spec_ref, signal_ref = refs[7:9]
    (one, two, three, mixed, spread, bins_out, four, w1, w2) = refs[9:18]
    (s1, r1, s2, r2, s3, r3, s4, r4, ws, wr, own) = refs[18:]
    me = lax.axis_index("tm")
    mine = lax.axis_index("batch")
    wide = [round_up(pieces, 8) for pieces in pieces_list]
    per_time, per_bin = sum(wide), 2 * sum(wide)
    weights = ((w1_ref, w1), (w2_ref, w2))

    barrier = pltpu.get_barrier_semaphore()

    @pl.loop(1, devices)
    def _(step):
        pl.semaphore_signal(
            barrier, inc=1, device_id=(mine, lax.rem(me + step, devices)), device_id_type=MESH
        )

    for step in range(1, batches):
        pl.semaphore_signal(
            barrier, inc=1, device_id=(lax.rem(mine + step, batches), me), device_id_type=MESH
        )
    pl.semaphore_wait(barrier, devices - 1 + batches - 1)

    def exchange(source, target, send_sem, recv_sem, limit_out, limit_in, rows, start):
        def remote(there, here):
            return pltpu.make_async_remote_copy(
                src_ref=source.at[pl.ds(pl.multiple_of(there * rows, rows), rows)],
                dst_ref=target.at[pl.ds(pl.multiple_of(here * rows, rows), rows)],
                send_sem=send_sem.at[there],
                recv_sem=recv_sem.at[here],
                device_id=(mine, there),
                device_id_type=MESH,
            )

        if start:

            @pl.loop(1, devices)
            def _(step):
                there = lax.rem(me + step, devices)

                @pl.when(there < limit_out)
                def _():
                    remote(there, me).start()

        else:

            @pl.loop(1, devices)
            def _(step):
                there = lax.rem(me + step, devices)

                @pl.when(there < limit_in)
                def _():
                    pltpu.make_async_remote_copy(
                        src_ref=source.at[pl.ds(0, rows)],
                        dst_ref=target.at[pl.ds(pl.multiple_of(there * rows, rows), rows)],
                        send_sem=send_sem.at[there],
                        recv_sem=recv_sem.at[there],
                        device_id=(mine, there),
                        device_id_type=MESH,
                    ).wait_recv()

    def drain(source, target, send_sem, recv_sem, limit_out, rows):
        @pl.loop(1, devices)
        def _(step):
            there = lax.rem(me + step, devices)

            @pl.when(there < limit_out)
            def _():
                pltpu.make_async_remote_copy(
                    src_ref=source.at[pl.ds(0, rows)],
                    dst_ref=target.at[pl.ds(0, rows)],
                    send_sem=send_sem.at[there],
                    recv_sem=recv_sem.at[there],
                    device_id=(mine, there),
                    device_id_type=MESH,
                ).wait_send()

    owner = me < count
    exchange(x_ref, one, s1, r1, count, None, per_time, True)

    def weight_copies(index):
        source, target = weights[index]
        rows = source.shape[2]
        place = target.at[:, :, pl.ds(pl.multiple_of(mine * rows, rows), rows)]
        local = pltpu.make_async_copy(source, place, own.at[index])
        remote = []
        for step in range(1, batches):
            there = lax.rem(mine + step, batches)
            back_there = lax.rem(mine + batches - step, batches)
            other = target.at[:, :, pl.ds(pl.multiple_of(back_there * rows, rows), rows)]
            remote.append(
                [
                    pltpu.make_async_remote_copy(
                        src_ref=source,
                        dst_ref=where,
                        send_sem=ws.at[index, step],
                        recv_sem=wr.at[index, step],
                        device_id=(there, me),
                        device_id_type=MESH,
                    )
                    for where in (place, other)
                ]
            )
        return local, remote

    for index in range(2):
        local, remote = weight_copies(index)
        local.start()
        for copy, _unused in remote:
            copy.start()

    here = pltpu.make_async_copy(
        x_ref.at[pl.ds(pl.multiple_of(jnp.minimum(me, count - 1) * per_time, per_time), per_time)],
        one.at[pl.ds(pl.multiple_of(me * per_time, per_time), per_time)],
        own.at[2],
    )
    here.start()
    if count < devices:
        two[pl.ds(count * per_bin, (devices - count) * per_bin)] = jnp.zeros(
            ((devices - count) * per_bin, two.shape[1]), two.dtype
        )
    here.wait()

    @pl.when(owner)
    def _():
        exchange(x_ref, one, s1, r1, None, devices, per_time, False)
        data = one[...]
        total = dot_nn(table_ref[0], data) + dot_nn(table_ref[1], data)
        bins_out[...] = total.astype(HALF_FLOAT)
        exchange(bins_out, two, s2, r2, devices, None, per_bin, True)
        place = pl.ds(pl.multiple_of(me * per_bin, per_bin), per_bin)
        two[place] = bins_out[place]

    exchange(bins_out, two, s2, r2, None, count, per_bin, False)
    spec_ref[...] = dot_nn(move_ref[...], two[...]).astype(HALF_FLOAT)
    base = 0
    for index in range(2):
        local, remote = weight_copies(index)
        local.wait()
        for copy, arrived in remote:
            copy.wait_send()
            arrived.wait_recv()
        target = weights[index][1]

        @pl.loop(0, pieces_list[index])
        def _(one_bin, base=base, target=target):
            place = pl.ds(
                pl.multiple_of(base + one_bin * 2 * devices, 2 * devices), 2 * devices
            )
            rows = spec_ref[place]
            if back:
                real = dot_nt(rows, target[one_bin, 0])
                imag = dot_nt(rows, target[one_bin, 1])
                out = jnp.concatenate(
                    [real[:devices] + imag[devices:], real[devices:] - imag[:devices]]
                )
            else:
                real = dot_nn(rows, target[one_bin, 0])
                imag = dot_nn(rows, target[one_bin, 1])
                out = jnp.concatenate(
                    [real[:devices] - imag[devices:], imag[:devices] + real[devices:]]
                )
            mixed[place] = out.astype(HALF_FLOAT)

        extra = wide[index] - pieces_list[index]
        if extra:
            mixed[
                pl.ds(base + pieces_list[index] * 2 * devices, extra * 2 * devices)
            ] = jnp.zeros((extra * 2 * devices, mixed.shape[1]), mixed.dtype)
        base += wide[index] * 2 * devices

    spread[...] = dot_nn(unmove_ref[...], mixed[...]).astype(HALF_FLOAT)
    exchange(spread, three, s3, r3, count, None, per_bin, True)

    @pl.when(owner)
    def _():
        place = pl.ds(pl.multiple_of(me * per_bin, per_bin), per_bin)
        three[place] = spread[place]
        exchange(spread, three, s3, r3, None, devices, per_bin, False)
        data = three[...]
        total = dot_nn(inverse_ref[0], data) + dot_nn(inverse_ref[1], data)
        four[...] = total
        exchange(four, signal_ref, s4, r4, devices, None, per_time, True)
        place = pl.ds(pl.multiple_of(me * per_time, per_time), per_time)
        signal_ref[place] = four[place]

    exchange(four, signal_ref, s4, r4, None, count, per_time, False)
    drain(x_ref, one, s1, r1, count, per_time)
    drain(spread, three, s3, r3, count, per_bin)

    @pl.when(owner)
    def _():
        drain(bins_out, two, s2, r2, devices, per_bin)
        drain(four, signal_ref, s4, r4, devices, per_time)


def spectral(values, weights, back):
    devices, batches = lax.axis_size("tm"), lax.axis_size("batch")
    pieces_list = tuple(value.shape[1] for value in values)
    count, _, channels = values[0].shape
    wide = [round_up(pieces, 8) for pieces in pieces_list]
    per_time, per_bin = sum(wide), 2 * sum(wide)
    assert count <= devices and per_time % 16 == 0
    packed = jnp.concatenate(
        [
            jnp.pad(value, ((0, 0), (0, room - value.shape[1]), (0, 0)))
            for value, room in zip(values, wide)
        ],
        axis=1,
    ).reshape(count * per_time, channels)
    constants = spectral_constants(devices, pieces_list)
    vmem = pl.BlockSpec(memory_space=pltpu.VMEM)
    hbm = pl.BlockSpec(memory_space=pl.ANY)
    rows_time, rows_bin = devices * per_time, devices * per_bin
    dma = pltpu.SemaphoreType.DMA
    spec, signal = pl.pallas_call(
        functools.partial(spectral_kernel, (devices, batches, count, pieces_list), back),
        out_shape=(
            jax.ShapeDtypeStruct((rows_bin, channels), HALF_FLOAT),
            jax.ShapeDtypeStruct((count * per_time, channels), FLOAT),
        ),
        in_specs=[hbm, hbm, hbm] + [vmem] * 4,
        out_specs=(vmem, vmem),
        scratch_shapes=[
            pltpu.VMEM((rows_time, channels), HALF_FLOAT),
            pltpu.VMEM((rows_bin, channels), HALF_FLOAT),
            pltpu.VMEM((rows_bin, channels), HALF_FLOAT),
            pltpu.VMEM((rows_bin, channels), HALF_FLOAT),
            pltpu.VMEM((rows_bin, channels), HALF_FLOAT),
            pltpu.VMEM((rows_bin, channels), HALF_FLOAT),
            pltpu.VMEM((rows_time, channels), FLOAT),
        ]
        + [
            pltpu.VMEM(
                (weight.shape[0], 2, weight.shape[2] * batches, channels), HALF_FLOAT
            )
            for weight in weights
        ]
        + [dma((devices,))] * 8
        + [dma((2, batches)), dma((2, batches)), dma((3,))],
        compiler_params=pltpu.CompilerParams(
            collective_id=1 if back else 0,
            has_side_effects=True,
            vmem_limit_bytes=60 * 1024 * 1024,
        ),
        cost_estimate=pl.CostEstimate(
            flops=2 * rows_bin * channels * channels * 4,
            bytes_accessed=4 * channels * channels * sum(pieces_list),
            transcendentals=0,
        ),
        name="spectral_back" if back else "spectral_forward",
    )(packed, *weights, *constants)
    signal = signal.reshape(count, per_time, channels)
    specs, signals, offset = [], [], 0
    for pieces, room in zip(pieces_list, wide):
        part = spec[2 * devices * offset : 2 * devices * (offset + pieces)]
        specs.append(part.reshape(pieces, 2, devices, channels)[:, :, :count])
        signals.append(signal[:, offset : offset + pieces])
        offset += room
    return specs, signals


def spectral_weight_grad(spectrum, grad_mixed):
    real_side = spectrum[:, 0]
    imaginary_side = spectrum[:, 1]
    grad_real = grad_mixed[:, 0]
    grad_imaginary = grad_mixed[:, 1]
    weight_real = jnp.einsum(
        "fbd,fbe->fde", real_side, grad_real, preferred_element_type=FLOAT
    ) + jnp.einsum("fbd,fbe->fde", imaginary_side, grad_imaginary, preferred_element_type=FLOAT)
    weight_imaginary = jnp.einsum(
        "fbd,fbe->fde", real_side, grad_imaginary, preferred_element_type=FLOAT
    ) - jnp.einsum("fbd,fbe->fde", imaginary_side, grad_real, preferred_element_type=FLOAT)
    return jnp.stack([weight_real, weight_imaginary], axis=1)


def extend_series(series_in, rim_width):
    padded = extended_2(series_in, (("tm", 1),), rim_width)
    position = lax.axis_index("tm")
    final_index = lax.axis_size("tm") - 1
    step_count = series_in.shape[1]
    left_rim = jnp.where(
        position == 0,
        jnp.broadcast_to(series_in[:, :1], padded[:, :rim_width].shape),
        padded[:, :rim_width],
    )
    right_rim = jnp.where(
        position == final_index,
        jnp.broadcast_to(series_in[:, -1:], padded[:, rim_width + step_count :].shape),
        padded[:, rim_width + step_count :],
    )
    return jnp.concatenate([left_rim, series_in, right_rim], axis=1)


def band(step_count, rim_width, half_window):
    row = np.arange(step_count)[:, None] + rim_width
    column = np.arange(step_count + 2 * rim_width)[None, :]
    return (np.abs(row - column) <= half_window).astype(HALF_FLOAT)


def seasonal_part(extended, series_in, half_window, rim_width):
    step_count = series_in.shape[1]
    matrix = jnp.asarray(band(step_count, rim_width, half_window))
    running = jnp.einsum("qr,brd->bqd", matrix, extended, preferred_element_type=FLOAT)
    return (series_in.astype(FLOAT) - running / (2 * half_window + 1)).astype(HALF_FLOAT)


def mean_back(grad, half_window, rim_width, is_first, is_final):
    step_count = grad.shape[1]
    matrix = jnp.asarray(band(step_count, rim_width, half_window))
    high = grad.astype(HALF_FLOAT)
    low = (grad - high.astype(FLOAT)).astype(HALF_FLOAT)
    wide = jnp.einsum("qr,bqd->brd", matrix, high, preferred_element_type=FLOAT) + jnp.einsum(
        "qr,bqd->brd", matrix, low, preferred_element_type=FLOAT
    )
    return wide / (2 * half_window + 1)


def batch_split(values, split, join):
    return lax.all_to_all(values, "batch", split_axis=split, concat_axis=join, tiled=True)


def time_sum(values, dim):
    return lax.psum_scatter(
        values.astype(HALF_FLOAT), "tm", scatter_dimension=dim, tiled=True
    ).astype(FLOAT)


def branch_down(seasonal_low, down_weight, bias_row):
    series_count, step_count, channels = seasonal_low.shape
    kernel = down_weight.shape[0]
    pieces = step_count // kernel
    blocks = seasonal_low.reshape(series_count * pieces, kernel * channels)
    down_act = jnp.tanh(
        jnp.dot(
            blocks, down_weight.reshape(kernel * channels, channels), preferred_element_type=FLOAT
        )
        + bias_row
    )
    return down_act.reshape(series_count, pieces, channels)


def branch_up(seasonal_low, down_act, iso_out, up_weight, bias_rows, gain_row, bias_row):
    series_count, step_count, channels = seasonal_low.shape
    kernel = up_weight.shape[1]
    pieces = step_count // kernel
    iso_act = jnp.tanh(iso_out + bias_rows[0])
    inner_in = iso_act + down_act.astype(HALF_FLOAT).astype(FLOAT)
    inner_low = layer_norm(inner_in, gain_row, bias_row).astype(HALF_FLOAT)
    up_pre = jnp.dot(
        inner_low.reshape(series_count * pieces, channels),
        up_weight.reshape(channels, kernel * channels),
        preferred_element_type=FLOAT,
    )
    up_act = jnp.tanh(up_pre.reshape(series_count, step_count, channels) + bias_rows[1])
    outer_in = up_act + seasonal_low.astype(FLOAT)
    branch_out = layer_norm(outer_in, gain_row, bias_row)
    return branch_out, (iso_act, inner_in, inner_low, up_act, outer_in)


def branch_up_back(grad_out, up_weight, gain_row, bias_row, kept):
    iso_act, inner_in, inner_low, up_act, outer_in = kept
    series_count, step_count, channels = grad_out.shape
    kernel = up_weight.shape[1]
    pieces = step_count // kernel
    normed_out, outer_pull = jax.vjp(layer_norm, outer_in, gain_row, bias_row)
    grad_outer, gain_outer, shift_outer = outer_pull(grad_out)
    grad_up = (grad_outer * (1.0 - up_act * up_act)).astype(HALF_FLOAT)
    up_rows = grad_up.reshape(series_count * pieces, kernel * channels)
    inner_rows = inner_low.reshape(series_count * pieces, channels)
    up_flat = up_weight.reshape(channels, kernel * channels)
    grad_up_weight = jnp.einsum(
        "nd,nk->dk",
        batch_split(inner_rows, 1, 0),
        lax.all_gather(up_rows, "batch", axis=0, tiled=True),
        preferred_element_type=FLOAT,
    ).reshape(-1, kernel, channels)
    grad_up_bias = jnp.sum(grad_up.astype(FLOAT), axis=(0, 1))
    grad_inner = jnp.einsum("nk,dk->nd", up_rows, up_flat, preferred_element_type=FLOAT).reshape(
        series_count, pieces, channels
    )
    normed_inner, inner_pull = jax.vjp(layer_norm, inner_in, gain_row, bias_row)
    grad_inner_in, gain_inner, shift_inner = inner_pull(grad_inner)
    grad_iso = grad_inner_in * (1.0 - iso_act * iso_act)
    grad_iso_bias = jnp.sum(grad_iso, axis=(0, 1))
    return (
        grad_iso.astype(HALF_FLOAT),
        grad_inner_in,
        grad_outer,
        (
            grad_up_weight,
            grad_iso_bias,
            grad_up_bias,
            gain_outer + gain_inner,
            shift_outer + shift_inner,
        ),
    )


def branch_down_back(grad_signal, grad_inner_in, grad_outer, seasonal_low, down_act, down_weight):
    series_count, step_count, channels = seasonal_low.shape
    kernel = down_weight.shape[0]
    pieces = step_count // kernel
    grad_down = grad_signal + grad_inner_in
    grad_down_pre = (grad_down * (1.0 - down_act * down_act)).astype(HALF_FLOAT)
    down_rows = grad_down_pre.reshape(series_count * pieces, channels)
    down_flat = down_weight.reshape(kernel * channels, channels)
    batch_blocks = batch_split(seasonal_low.reshape(-1, kernel, channels), 2, 0)
    grad_down_weight = jnp.einsum(
        "nkc,nd->kcd",
        batch_blocks,
        lax.all_gather(down_rows, "batch", axis=0, tiled=True),
        preferred_element_type=FLOAT,
    )
    grad_down_bias = jnp.sum(grad_down_pre.astype(FLOAT), axis=(0, 1))
    grad_seasonal = (
        jnp.einsum("nd,kd->nk", down_rows, down_flat, preferred_element_type=FLOAT).reshape(
            series_count, step_count, channels
        )
        + grad_outer
    )
    return grad_seasonal, grad_down_weight, grad_down_bias


def batch_split(values, split, join):
    return lax.all_to_all(values, "batch", split_axis=split, concat_axis=join, tiled=True)


def iso_weight_grad(spectrum, grad_mixed):
    return spectral_weight_grad(
        batch_split(spectrum, 3, 2), lax.all_gather(grad_mixed, "batch", axis=2, tiled=True)
    )


def time_sum(values, dim):
    return lax.psum_scatter(
        values.astype(HALF_FLOAT), "tm", scatter_dimension=dim, tiled=True
    ).astype(FLOAT)


def per_device(
    series_in,
    out_cotangent,
    out_mask,
    down_twelve,
    down_sixteen,
    iso_twelve,
    iso_sixteen,
    up_twelve,
    up_sixteen,
    branch_bias,
    merge_weight,
    hidden_weight,
    hidden_bias,
    output_weight,
    head_bias,
    norm_gain,
    norm_shift,
):
    series_dev, step_count, channels = series_in.shape
    row_count = series_dev * step_count
    half_one = down_twelve.shape[0] // 2
    half_two = down_sixteen.shape[0] // 2
    rim_width = max(half_one, half_two)
    biases = branch_bias.astype(FLOAT)
    gains = norm_gain.astype(FLOAT)
    shifts = norm_shift.astype(FLOAT)
    heads = head_bias.astype(FLOAT)
    extended = extend_series(series_in, rim_width)
    seasonal_one = seasonal_part(extended, series_in, half_one, rim_width)
    seasonal_two = seasonal_part(extended, series_in, half_two, rim_width)
    down_one = branch_down(seasonal_one, down_twelve, biases[0])
    down_two = branch_down(seasonal_two, down_sixteen, biases[1])
    iso_weights = (iso_twelve, iso_sixteen)
    spectra, iso_outs = spectral(
        (down_one.astype(HALF_FLOAT), down_two.astype(HALF_FLOAT)), iso_weights, False
    )
    out_one, kept_one = branch_up(
        seasonal_one,
        down_one,
        iso_outs[0],
        up_twelve,
        (biases[2], biases[4]),
        gains[0],
        shifts[0],
    )
    out_two, kept_two = branch_up(
        seasonal_two,
        down_two,
        iso_outs[1],
        up_sixteen,
        (biases[3], biases[5]),
        gains[0],
        shifts[0],
    )
    branch_low = jnp.concatenate(
        [out_one.astype(HALF_FLOAT), out_two.astype(HALF_FLOAT)], axis=2
    ).reshape(row_count, 2 * channels)
    merge_flat = merge_weight.reshape(2 * channels, channels)
    merged = jnp.dot(branch_low, merge_flat, preferred_element_type=FLOAT) + heads[0]
    first_low = layer_norm(merged, gains[1], shifts[1]).astype(HALF_FLOAT)
    hidden_pre = jnp.dot(
        first_low, hidden_weight, preferred_element_type=FLOAT
    ) + hidden_bias.astype(FLOAT)
    hidden_low = jax.nn.gelu(hidden_pre).astype(HALF_FLOAT)
    final_in = merged + (
        jnp.dot(hidden_low, output_weight, preferred_element_type=FLOAT) + heads[1]
    )
    mask_rows = out_mask.astype(FLOAT).reshape(row_count, 1)
    result = (
        (layer_norm(final_in, gains[2], shifts[2]) * mask_rows)
        .astype(HALF_FLOAT)
        .reshape(series_dev, step_count, channels)
    )
    grad_result = out_cotangent.astype(FLOAT).reshape(row_count, channels) * mask_rows
    normed_final, final_pull = jax.vjp(layer_norm, final_in, gains[2], shifts[2])
    grad_final, gain_final, shift_final = final_pull(grad_result)
    grad_feed = grad_final.astype(HALF_FLOAT)
    grad_output_weight = jnp.einsum(
        "nf,nd->fd", hidden_low, grad_feed, preferred_element_type=FLOAT
    )
    grad_output_bias = jnp.sum(grad_feed.astype(FLOAT), axis=0)
    grad_hidden_low = jnp.einsum(
        "nd,fd->nf", grad_feed, output_weight, preferred_element_type=FLOAT
    )
    gelu_value, gelu_pull = jax.vjp(jax.nn.gelu, hidden_pre)
    grad_hidden_pre = gelu_pull(grad_hidden_low)[0].astype(HALF_FLOAT)
    grad_hidden_weight = jnp.einsum(
        "nd,nf->df", first_low, grad_hidden_pre, preferred_element_type=FLOAT
    )
    grad_hidden_bias = jnp.sum(grad_hidden_pre.astype(FLOAT), axis=0)
    grad_first = jnp.einsum(
        "nf,df->nd", grad_hidden_pre, hidden_weight, preferred_element_type=FLOAT
    )
    normed_first, first_pull = jax.vjp(layer_norm, merged, gains[1], shifts[1])
    grad_merged_norm, gain_first, shift_first = first_pull(grad_first)
    grad_merged = (grad_final + grad_merged_norm).astype(HALF_FLOAT)
    grad_merge_bias = jnp.sum(grad_merged.astype(FLOAT), axis=0)
    grad_merge_weight = jnp.einsum(
        "nk,nd->kd", branch_low, grad_merged, preferred_element_type=FLOAT
    ).reshape(2, channels, channels)
    grad_branch = jnp.einsum("nd,kd->nk", grad_merged, merge_flat, preferred_element_type=FLOAT)
    grad_out_one = grad_branch[:, :channels].reshape(series_dev, step_count, channels)
    grad_out_two = grad_branch[:, channels:].reshape(series_dev, step_count, channels)
    iso_one, inner_one, outer_one, terms_one = branch_up_back(
        grad_out_one, up_twelve, gains[0], shifts[0], kept_one
    )
    iso_two, inner_two, outer_two, terms_two = branch_up_back(
        grad_out_two, up_sixteen, gains[0], shifts[0], kept_two
    )
    grads_mixed, grad_signals = spectral((iso_one, iso_two), iso_weights, True)
    grad_iso_one = iso_weight_grad(spectra[0], grads_mixed[0])
    grad_iso_two = iso_weight_grad(spectra[1], grads_mixed[1])
    grad_seasonal_one, grad_down_one, down_bias_one = branch_down_back(
        grad_signals[0], inner_one, outer_one, seasonal_one, down_one, down_twelve
    )
    grad_seasonal_two, grad_down_two, down_bias_two = branch_down_back(
        grad_signals[1], inner_two, outer_two, seasonal_two, down_two, down_sixteen
    )
    position = lax.axis_index("tm")
    final_index = lax.axis_size("tm") - 1
    wide = mean_back(grad_seasonal_one, half_one, rim_width, None, None) + mean_back(
        grad_seasonal_two, half_two, rim_width, None, None
    )
    low_rim = wide[:, :rim_width]
    high_rim = wide[:, rim_width + step_count :]
    forward = [(i, i + 1) for i in range(final_index)]
    from_low = lax.ppermute(high_rim, "tm", forward)
    from_high = lax.ppermute(low_rim, "tm", [(j, i) for i, j in forward])
    edge_low = jnp.where(
        position == 0,
        jnp.pad(jnp.sum(low_rim, axis=1, keepdims=True), ((0, 0), (0, rim_width - 1), (0, 0))),
        from_low,
    )
    edge_high = jnp.where(
        position == final_index,
        jnp.pad(jnp.sum(high_rim, axis=1, keepdims=True), ((0, 0), (rim_width - 1, 0), (0, 0))),
        from_high,
    )
    mean_total = wide[:, rim_width : rim_width + step_count] + jnp.concatenate(
        [
            edge_low,
            jnp.zeros((series_dev, step_count - 2 * rim_width, channels), FLOAT),
            edge_high,
        ],
        axis=1,
    )
    grad_series = (grad_seasonal_one + grad_seasonal_two - mean_total).astype(HALF_FLOAT)
    vectors = jnp.stack(
        [
            down_bias_one,
            down_bias_two,
            terms_one[1],
            terms_two[1],
            terms_one[2],
            terms_two[2],
            terms_one[3] + terms_two[3],
            gain_first,
            gain_final,
            terms_one[4] + terms_two[4],
            shift_first,
            shift_final,
            grad_merge_bias,
            grad_output_bias,
        ]
    )
    devices = lax.axis_size("tm")
    vector_count = vectors.shape[0]
    packed = jnp.concatenate(
        [
            vectors.reshape(vector_count, devices, -1).transpose(1, 0, 2).reshape(devices, -1),
            grad_hidden_bias.reshape(devices, -1),
        ],
        axis=1,
    )
    packed = lax.psum(lax.psum_scatter(packed, "tm", scatter_dimension=0, tiled=True), "batch")[0]
    width = channels // devices
    rows = packed[: vector_count * width].reshape(vector_count, width)
    vector_parts = (
        rows[:6],
        packed[vector_count * width :],
        rows[12:14],
        rows[6:9],
        rows[9:12],
    )
    merge_half = lax.psum_scatter(grad_merge_weight, "batch", scatter_dimension=1, tiled=True)
    hidden_half = lax.psum_scatter(grad_hidden_weight, "batch", scatter_dimension=0, tiled=True)
    output_half = lax.psum_scatter(grad_output_weight, "batch", scatter_dimension=0, tiled=True)
    matrix_parts = (
        time_sum(grad_down_one, 2),
        time_sum(grad_down_two, 2),
        time_sum(terms_one[0], 2),
        time_sum(terms_two[0], 2),
        time_sum(merge_half, 2),
        time_sum(hidden_half, 1),
        time_sum(output_half, 1),
    )
    iso_parts = (grad_iso_one, grad_iso_two)
    return (
        result,
        grad_series,
        matrix_parts[0],
        matrix_parts[1],
        iso_parts[0],
        iso_parts[1],
        matrix_parts[2],
        matrix_parts[3],
        vector_parts[0],
        matrix_parts[4],
        matrix_parts[5],
        vector_parts[1],
        matrix_parts[6],
        vector_parts[2],
        vector_parts[3],
        vector_parts[4],
    )


def solution(mesh):
    placed = (
        P("batch", "tm", None),
        P("batch", "tm", None),
        P("batch", "tm"),
        P(),
        P(),
        P("tm", None, "batch", None),
        P("tm", None, "batch", None),
        P(),
        P(),
        P(),
        P(),
        P(),
        P(),
        P(),
        P(),
        P(),
        P(),
    )
    return jax.shard_map(
        per_device,
        mesh=mesh,
        in_specs=placed,
        out_specs=(
            P("batch", "tm", None),
            P("batch", "tm", None),
            P(None, "batch", "tm"),
            P(None, "batch", "tm"),
            P("tm", None, "batch", None),
            P("tm", None, "batch", None),
            P("batch", None, "tm"),
            P("batch", None, "tm"),
            P(None, "tm"),
            P(None, "batch", "tm"),
            P("batch", "tm"),
            P("tm"),
            P("batch", "tm"),
            P(None, "tm"),
            P(None, "tm"),
            P(None, "tm"),
        ),
        check_vma=False,
    )
```

```python
import functools
import math

import jax
import jax.numpy as jnp
import numpy as np
from jax import lax
from jax.experimental import pallas as pl
from jax.experimental.pallas import tpu as pltpu
from jax.sharding import PartitionSpec as P

FLOAT = jnp.float32
HALF_FLOAT = jnp.bfloat16
HIGHEST = lax.Precision.HIGHEST
EPSILON = 1e-05
MESH = pl.DeviceIdType.MESH


def extended_2(block, sides, width):
    for axis, dim in sides:
        count = lax.axis_size(axis)
        forward = [(i, i + 1) for i in range(count - 1)]
        backward = [(target, source) for source, target in forward]
        low = lax.ppermute(
            lax.slice_in_dim(block, block.shape[dim] - width, None, axis=dim), axis, forward
        )
        high = lax.ppermute(lax.slice_in_dim(block, 0, width, axis=dim), axis, backward)
        block = jnp.concatenate([low, block, high], axis=dim)
    return block


def layer_norm(values, gain_row, bias_row):
    center = values - jnp.mean(values, axis=-1, keepdims=True)
    spread = jnp.mean(center * center, axis=-1, keepdims=True)
    return center * lax.rsqrt(spread + EPSILON) * gain_row + bias_row


def round_up(value, multiple):
    return -(-value // multiple) * multiple


def spectral_constants(devices, pieces_list):
    padded = [round_up(pieces, 8) for pieces in pieces_list]
    per_time, per_bin = sum(padded), 2 * sum(padded)
    table = np.zeros((devices, per_bin, devices, per_time), np.float64)
    offset = 0
    for pieces, wide in zip(pieces_list, padded):
        length = devices * pieces
        index = np.arange(length)
        angle = (2.0 * math.pi / length) * (np.outer(index, index) % length)
        factor = 1.0 / math.sqrt(length)
        for part, values in enumerate((np.cos(angle) * factor, -np.sin(angle) * factor)):
            row = 2 * offset + part * wide
            table[:, row : row + pieces, :, offset : offset + pieces] = values.reshape(
                devices, pieces, devices, pieces
            )
        offset += wide
    table = table.reshape(devices * per_bin, devices * per_time).astype(np.float32)
    high = table.astype(HALF_FLOAT)
    low = (table - high.astype(np.float32)).astype(HALF_FLOAT)
    order = []
    offset = 0
    for wide in padded:
        for one_bin in range(wide):
            for part in range(2):
                for series in range(devices):
                    order.append(series * per_bin + 2 * offset + part * wide + one_bin)
        offset += wide
    move = np.zeros((devices * per_bin, devices * per_bin), np.float32)
    move[np.arange(len(order)), order] = 1.0
    move = move.astype(HALF_FLOAT)
    return (
        jnp.asarray(np.stack([high, low])),
        jnp.asarray(np.stack([high.T, low.T])),
        jnp.asarray(move),
        jnp.asarray(np.ascontiguousarray(move.T)),
    )


def dot_nn(left, right):
    return jnp.dot(left, right, preferred_element_type=FLOAT)


def dot_nt(left, right):
    return lax.dot_general(left, right, (((1,), (1,)), ((), ())), preferred_element_type=FLOAT)


def spectral_kernel(sizes, back, *refs):
    devices, batches, count, pieces_list = sizes
    (x_ref, w1_ref, w2_ref, table_ref, inverse_ref, move_ref, unmove_ref) = refs[:7]
    spec_ref, signal_ref = refs[7:9]
    (one, two, three, mixed, spread, bins_out, four, w1, w2) = refs[9:18]
    (s1, r1, s2, r2, s3, r3, s4, r4, ws, wr, own) = refs[18:]
    me = lax.axis_index("tm")
    mine = lax.axis_index("batch")
    wide = [round_up(pieces, 8) for pieces in pieces_list]
    per_time, per_bin = sum(wide), 2 * sum(wide)
    weights = ((w1_ref, w1), (w2_ref, w2))

    barrier = pltpu.get_barrier_semaphore()

    @pl.loop(1, devices)
    def _(step):
        pl.semaphore_signal(
            barrier, inc=1, device_id=(mine, lax.rem(me + step, devices)), device_id_type=MESH
        )

    for step in range(1, batches):
        pl.semaphore_signal(
            barrier, inc=1, device_id=(lax.rem(mine + step, batches), me), device_id_type=MESH
        )
    pl.semaphore_wait(barrier, devices - 1 + batches - 1)

    def exchange(source, target, send_sem, recv_sem, limit_out, limit_in, rows, start):
        def remote(there, here):
            return pltpu.make_async_remote_copy(
                src_ref=source.at[pl.ds(pl.multiple_of(there * rows, rows), rows)],
                dst_ref=target.at[pl.ds(pl.multiple_of(here * rows, rows), rows)],
                send_sem=send_sem.at[there],
                recv_sem=recv_sem.at[here],
                device_id=(mine, there),
                device_id_type=MESH,
            )

        if start:

            @pl.loop(1, devices)
            def _(step):
                there = lax.rem(me + step, devices)

                @pl.when(there < limit_out)
                def _():
                    remote(there, me).start()

        else:

            @pl.loop(1, devices)
            def _(step):
                there = lax.rem(me + step, devices)

                @pl.when(there < limit_in)
                def _():
                    pltpu.make_async_remote_copy(
                        src_ref=source.at[pl.ds(0, rows)],
                        dst_ref=target.at[pl.ds(pl.multiple_of(there * rows, rows), rows)],
                        send_sem=send_sem.at[there],
                        recv_sem=recv_sem.at[there],
                        device_id=(mine, there),
                        device_id_type=MESH,
                    ).wait_recv()

    def drain(source, target, send_sem, recv_sem, limit_out, rows):
        @pl.loop(1, devices)
        def _(step):
            there = lax.rem(me + step, devices)

            @pl.when(there < limit_out)
            def _():
                pltpu.make_async_remote_copy(
                    src_ref=source.at[pl.ds(0, rows)],
                    dst_ref=target.at[pl.ds(0, rows)],
                    send_sem=send_sem.at[there],
                    recv_sem=recv_sem.at[there],
                    device_id=(mine, there),
                    device_id_type=MESH,
                ).wait_send()

    owner = me < count
    exchange(x_ref, one, s1, r1, count, None, per_time, True)

    def weight_copies(index):
        source, target = weights[index]
        rows = source.shape[2]
        place = target.at[:, :, pl.ds(pl.multiple_of(mine * rows, rows), rows)]
        local = pltpu.make_async_copy(source, place, own.at[index])
        remote = []
        for step in range(1, batches):
            there = lax.rem(mine + step, batches)
            back_there = lax.rem(mine + batches - step, batches)
            other = target.at[:, :, pl.ds(pl.multiple_of(back_there * rows, rows), rows)]
            remote.append(
                [
                    pltpu.make_async_remote_copy(
                        src_ref=source,
                        dst_ref=where,
                        send_sem=ws.at[index, step],
                        recv_sem=wr.at[index, step],
                        device_id=(there, me),
                        device_id_type=MESH,
                    )
                    for where in (place, other)
                ]
            )
        return local, remote

    for index in range(2):
        local, remote = weight_copies(index)
        local.start()
        for copy, _unused in remote:
            copy.start()

    here = pltpu.make_async_copy(
        x_ref.at[pl.ds(pl.multiple_of(jnp.minimum(me, count - 1) * per_time, per_time), per_time)],
        one.at[pl.ds(pl.multiple_of(me * per_time, per_time), per_time)],
        own.at[2],
    )
    here.start()
    if count < devices:
        two[pl.ds(count * per_bin, (devices - count) * per_bin)] = jnp.zeros(
            ((devices - count) * per_bin, two.shape[1]), two.dtype
        )
    here.wait()

    @pl.when(owner)
    def _():
        exchange(x_ref, one, s1, r1, None, devices, per_time, False)
        data = one[...]
        total = dot_nn(table_ref[0], data) + dot_nn(table_ref[1], data)
        bins_out[...] = total.astype(HALF_FLOAT)
        exchange(bins_out, two, s2, r2, devices, None, per_bin, True)
        place = pl.ds(pl.multiple_of(me * per_bin, per_bin), per_bin)
        two[place] = bins_out[place]

    exchange(bins_out, two, s2, r2, None, count, per_bin, False)
    spec_ref[...] = dot_nn(move_ref[...], two[...]).astype(HALF_FLOAT)
    base = 0
    for index in range(2):
        local, remote = weight_copies(index)
        local.wait()
        for copy, arrived in remote:
            copy.wait_send()
            arrived.wait_recv()
        target = weights[index][1]

        @pl.loop(0, pieces_list[index])
        def _(one_bin, base=base, target=target):
            place = pl.ds(
                pl.multiple_of(base + one_bin * 2 * devices, 2 * devices), 2 * devices
            )
            rows = spec_ref[place]
            if back:
                real = dot_nt(rows, target[one_bin, 0])
                imag = dot_nt(rows, target[one_bin, 1])
                out = jnp.concatenate(
                    [real[:devices] + imag[devices:], real[devices:] - imag[:devices]]
                )
            else:
                real = dot_nn(rows, target[one_bin, 0])
                imag = dot_nn(rows, target[one_bin, 1])
                out = jnp.concatenate(
                    [real[:devices] - imag[devices:], imag[:devices] + real[devices:]]
                )
            mixed[place] = out.astype(HALF_FLOAT)

        extra = wide[index] - pieces_list[index]
        if extra:
            mixed[
                pl.ds(base + pieces_list[index] * 2 * devices, extra * 2 * devices)
            ] = jnp.zeros((extra * 2 * devices, mixed.shape[1]), mixed.dtype)
        base += wide[index] * 2 * devices

    spread[...] = dot_nn(unmove_ref[...], mixed[...]).astype(HALF_FLOAT)
    exchange(spread, three, s3, r3, count, None, per_bin, True)

    @pl.when(owner)
    def _():
        place = pl.ds(pl.multiple_of(me * per_bin, per_bin), per_bin)
        three[place] = spread[place]
        exchange(spread, three, s3, r3, None, devices, per_bin, False)
        data = three[...]
        total = dot_nn(inverse_ref[0], data) + dot_nn(inverse_ref[1], data)
        four[...] = total
        exchange(four, signal_ref, s4, r4, devices, None, per_time, True)
        place = pl.ds(pl.multiple_of(me * per_time, per_time), per_time)
        signal_ref[place] = four[place]

    exchange(four, signal_ref, s4, r4, None, count, per_time, False)
    drain(x_ref, one, s1, r1, count, per_time)
    drain(spread, three, s3, r3, count, per_bin)

    @pl.when(owner)
    def _():
        drain(bins_out, two, s2, r2, devices, per_bin)
        drain(four, signal_ref, s4, r4, devices, per_time)


def spectral(values, weights, back):
    devices, batches = lax.axis_size("tm"), lax.axis_size("batch")
    pieces_list = tuple(value.shape[1] for value in values)
    count, _, channels = values[0].shape
    wide = [round_up(pieces, 8) for pieces in pieces_list]
    per_time, per_bin = sum(wide), 2 * sum(wide)
    assert count <= devices and per_time % 16 == 0
    packed = jnp.concatenate(
        [
            jnp.pad(value, ((0, 0), (0, room - value.shape[1]), (0, 0)))
            for value, room in zip(values, wide)
        ],
        axis=1,
    ).reshape(count * per_time, channels)
    constants = spectral_constants(devices, pieces_list)
    vmem = pl.BlockSpec(memory_space=pltpu.VMEM)
    hbm = pl.BlockSpec(memory_space=pl.ANY)
    rows_time, rows_bin = devices * per_time, devices * per_bin
    dma = pltpu.SemaphoreType.DMA
    spec, signal = pl.pallas_call(
        functools.partial(spectral_kernel, (devices, batches, count, pieces_list), back),
        out_shape=(
            jax.ShapeDtypeStruct((rows_bin, channels), HALF_FLOAT),
            jax.ShapeDtypeStruct((count * per_time, channels), FLOAT),
        ),
        in_specs=[hbm, hbm, hbm] + [vmem] * 4,
        out_specs=(vmem, vmem),
        scratch_shapes=[
            pltpu.VMEM((rows_time, channels), HALF_FLOAT),
            pltpu.VMEM((rows_bin, channels), HALF_FLOAT),
            pltpu.VMEM((rows_bin, channels), HALF_FLOAT),
            pltpu.VMEM((rows_bin, channels), HALF_FLOAT),
            pltpu.VMEM((rows_bin, channels), HALF_FLOAT),
            pltpu.VMEM((rows_bin, channels), HALF_FLOAT),
            pltpu.VMEM((rows_time, channels), FLOAT),
        ]
        + [
            pltpu.VMEM(
                (weight.shape[0], 2, weight.shape[2] * batches, channels), HALF_FLOAT
            )
            for weight in weights
        ]
        + [dma((devices,))] * 8
        + [dma((2, batches)), dma((2, batches)), dma((3,))],
        compiler_params=pltpu.CompilerParams(
            collective_id=1 if back else 0,
            has_side_effects=True,
            vmem_limit_bytes=60 * 1024 * 1024,
        ),
        cost_estimate=pl.CostEstimate(
            flops=2 * rows_bin * channels * channels * 4,
            bytes_accessed=4 * channels * channels * sum(pieces_list),
            transcendentals=0,
        ),
        name="spectral_back" if back else "spectral_forward",
    )(packed, *weights, *constants)
    signal = signal.reshape(count, per_time, channels)
    specs, signals, offset = [], [], 0
    for pieces, room in zip(pieces_list, wide):
        part = spec[2 * devices * offset : 2 * devices * (offset + pieces)]
        specs.append(part.reshape(pieces, 2, devices, channels)[:, :, :count])
        signals.append(signal[:, offset : offset + pieces])
        offset += room
    return specs, signals


def gradient_kernel(sizes, kinds, *refs):
    groups, members, batches = sizes
    count = len(kinds)
    parts = [refs[i * count : (i + 1) * count] for i in range(17)]
    (wide_refs, narrow_refs, out_refs) = parts[:3]
    (wide_in, narrow_in, narrow_t, send, recv, total) = parts[3:9]
    (sa, ra, sg, rg, sz, rz, sf, rf) = parts[9:17]
    local = refs[17 * count]
    me = lax.axis_index("tm")
    core = lax.axis_index("batch")
    group, member = lax.div(me, members), lax.rem(me, members)
    mates = batches * members
    mine = core * members + member
    cores_per_group = groups // batches

    def place(one_group, one_member, one_core):
        return (one_core, one_group * members + one_member)

    barrier = pltpu.get_barrier_semaphore()
    greeted = 0
    for step in range(1, members):
        for turn in range(batches):
            there = place(
                group, lax.rem(member + step, members), lax.rem(core + turn, batches)
            )
            pl.semaphore_signal(barrier, inc=1, device_id=there, device_id_type=MESH)
            greeted += 1
    for step in range(groups):
        for turn in range(batches):
            if step or turn:
                there = place(lax.rem(group + step, groups), member, lax.rem(core + turn, batches))
                pl.semaphore_signal(barrier, inc=1, device_id=there, device_id_type=MESH)
                greeted += 1
    pl.semaphore_wait(barrier, greeted)

    def inputs(task, step, turn):
        to_member, to_core = lax.rem(member + step, members), lax.rem(core + turn, batches)
        steps = wide_in[task].shape[0]
        half = wide_in[task].shape[3]
        source = wide_refs[task].at[
            pl.ds(to_member * steps, steps), :, pl.ds(pl.multiple_of(to_core * half, half), half)
        ]
        from_member = lax.rem(member + members - step, members)
        from_core = lax.rem(core + batches - turn, batches)
        other = from_core * members + from_member
        there = place(group, to_member, to_core)
        slot = turn * members + step
        if step == 0 and turn == 0:
            return (
                pltpu.make_async_copy(source, wide_in[task].at[:, mine], local.at[2 * task]),
                pltpu.make_async_copy(
                    narrow_refs[task], narrow_in[task].at[mine], local.at[2 * task + 1]
                ),
            )
        return tuple(
            pltpu.make_async_remote_copy(
                src_ref=out,
                dst_ref=into,
                send_sem=ss.at[slot],
                recv_sem=rr.at[slot],
                device_id=there,
                device_id_type=MESH,
            )
            for pick in (mine, other)
            for out, into, ss, rr in (
                (source, wide_in[task].at[:, pick], sa[task], ra[task]),
                (narrow_refs[task], narrow_in[task].at[pick], sg[task], rg[task]),
            )
        )

    pairs = [(step, turn) for step in range(members) for turn in range(batches)]
    for task in range(count):
        for step, turn in pairs:
            for copy in inputs(task, step, turn)[:2]:
                copy.start()

    def chunk(task, to_group, to_core):
        if kinds[task] == "down":
            return send[task].at[:, pl.ds(pl.multiple_of(to_group * 128, 128), 128)]
        half = send[task].shape[1] // batches
        lane = lax.rem(to_group, cores_per_group) * 128
        return send[task].at[
            :,
            pl.ds(pl.multiple_of(to_core * half, half), half),
            pl.ds(pl.multiple_of(lane, 128), 128),
        ]

    def partials(task, step, turn, action):
        to_group, to_core = lax.rem(group + step, groups), lax.rem(core + turn, batches)
        slot = step * batches + turn
        remote = pltpu.make_async_remote_copy(
            src_ref=chunk(task, to_group, to_core),
            dst_ref=recv[task].at[group],
            send_sem=sz[task].at[slot],
            recv_sem=rz[task].at[slot],
            device_id=place(to_group, member, to_core),
            device_id_type=MESH,
        )
        if kinds[task] == "down":
            action(remote)
        else:

            @pl.when(lax.div(to_group, cores_per_group) == core)
            def _():
                action(remote)

    def partials_in(task, step, turn):
        from_group = lax.rem(group + groups - step, groups)
        slot = step * batches + turn
        arrived = pltpu.make_async_remote_copy(
            src_ref=chunk(task, group, core),
            dst_ref=recv[task].at[from_group],
            send_sem=sz[task].at[slot],
            recv_sem=rz[task].at[slot],
            device_id=place(group, member, core),
            device_id_type=MESH,
        )
        if kinds[task] == "down":
            arrived.wait_recv()
        else:
            from_core = lax.rem(core + batches - turn, batches)

            @pl.when(lax.div(group, cores_per_group) == from_core)
            def _():
                arrived.wait_recv()

    def hops(task):
        for step in range(groups):
            for turn in range(batches if kinds[task] == "up" else 1):
                if step or turn:
                    yield step, turn

    for task in range(count):
        for step, turn in pairs:
            copies = inputs(task, step, turn)
            if step == 0 and turn == 0:
                for copy in copies:
                    copy.wait()
            else:
                for copy in copies[2:]:
                    copy.wait_recv()
        rows = narrow_in[task].shape[1]
        narrow_t[task][...] = narrow_in[task][...].reshape(mates * rows, -1).T

        @pl.loop(0, wide_in[task].shape[0])
        def _(one, task=task, rows=rows):
            data = wide_in[task][one].reshape(mates * rows, -1)
            send[task][one] = dot_nn(narrow_t[task][...], data).astype(HALF_FLOAT)

        for step, turn in hops(task):
            partials(task, step, turn, lambda copy: copy.start())
        if kinds[task] == "down":
            recv[task][group] = send[task][:, pl.ds(pl.multiple_of(group * 128, 128), 128)]
        else:
            half = send[task].shape[1] // batches

            @pl.when(lax.div(group, cores_per_group) == core)
            def _(task=task, half=half):
                for lane in range(cores_per_group):

                    @pl.when(lax.rem(group, cores_per_group) == lane)
                    def _():
                        recv[task][group] = send[task][
                            :,
                            pl.ds(pl.multiple_of(core * half, half), half),
                            lane * 128 : lane * 128 + 128,
                        ]

    def final(task, step, start):
        to_member = lax.rem(member + step, members)
        from_member = lax.rem(member + members - step, members)
        steps = total[task].shape[0]
        width = out_refs[task].shape[1]
        pick = member if start else from_member
        return pltpu.make_async_remote_copy(
            src_ref=total[task].at[:, pl.ds(pl.multiple_of(to_member * width, width), width)],
            dst_ref=out_refs[task].at[pl.ds(pick * steps, steps)],
            send_sem=sf[task].at[step],
            recv_sem=rf[task].at[step],
            device_id=place(group, to_member, core),
            device_id_type=MESH,
        )

    for task in range(count):
        for step, turn in hops(task):
            partials_in(task, step, turn)

        @pl.loop(0, total[task].shape[0])
        def _(one, task=task):
            value = recv[task][0, one].astype(FLOAT)
            for other in range(1, groups):
                value = value + recv[task][other, one].astype(FLOAT)
            total[task][one] = value if kinds[task] == "down" else value.T

        for step in range(1, members):
            final(task, step, True).start()
        steps = total[task].shape[0]
        width = out_refs[task].shape[1]
        out_refs[task][pl.ds(member * steps, steps)] = total[task][
            :, pl.ds(pl.multiple_of(member * width, width), width)
        ]

    for task in range(count):
        for step in range(1, members):
            final(task, step, False).wait_recv()
            final(task, step, True).wait_send()
        for step, turn in pairs:
            if step or turn:
                for copy in inputs(task, step, turn)[:2]:
                    copy.wait_send()
        for step, turn in hops(task):
            partials(task, step, turn, lambda copy: copy.wait_send())


def weight_gradients(tasks):
    devices, batches = lax.axis_size("tm"), lax.axis_size("batch")
    channels = tasks[0][1].shape[2]
    groups = channels // 128
    members = devices // groups
    width = channels // devices
    half = channels // batches
    kinds = tuple(task[0] for task in tasks)
    dma = pltpu.SemaphoreType.DMA
    mates = members * batches
    shapes = [[] for _ in range(6)]
    outs = []
    for kind, wide, narrow in tasks:
        steps = wide.shape[0] // members
        rows = wide.shape[1]
        shapes[0].append(pltpu.VMEM((steps, mates, rows, half), HALF_FLOAT))
        shapes[1].append(pltpu.VMEM((mates, rows, channels), HALF_FLOAT))
        shapes[2].append(pltpu.VMEM((channels, mates * rows), HALF_FLOAT))
        shapes[3].append(pltpu.VMEM((steps, channels, half), HALF_FLOAT))
        piece = (128, half) if kind == "down" else (half, 128)
        shapes[4].append(pltpu.VMEM((groups, steps) + piece, HALF_FLOAT))
        shapes[5].append(pltpu.VMEM((steps, 128, half), FLOAT))
        outs.append(jax.ShapeDtypeStruct((wide.shape[0], width, half), FLOAT))
    count = len(tasks)
    sems = [mates] * 4 + [groups * batches] * 2 + [members] * 2
    flops = sum(2 * wide.size * channels for _, wide, _ in tasks)
    return pl.pallas_call(
        functools.partial(gradient_kernel, (groups, members, batches), kinds),
        out_shape=tuple(outs),
        in_specs=[pl.BlockSpec(memory_space=pl.ANY)] * (2 * count),
        out_specs=tuple([pl.BlockSpec(memory_space=pltpu.VMEM)] * count),
        scratch_shapes=[shape for group in shapes for shape in group]
        + [dma((size,)) for size in sems for _ in range(count)]
        + [dma((2 * count,))],
        compiler_params=pltpu.CompilerParams(
            collective_id=2, has_side_effects=True, vmem_limit_bytes=60 * 1024 * 1024
        ),
        cost_estimate=pl.CostEstimate(
            flops=flops, bytes_accessed=8 * flops // channels, transcendentals=0
        ),
        name="weight_gradients",
    )(*[task[1] for task in tasks], *[task[2] for task in tasks])


def spectral_weight_grad(spectrum, grad_mixed):
    real_side = spectrum[:, 0]
    imaginary_side = spectrum[:, 1]
    grad_real = grad_mixed[:, 0]
    grad_imaginary = grad_mixed[:, 1]
    weight_real = jnp.einsum(
        "fbd,fbe->fde", real_side, grad_real, preferred_element_type=FLOAT
    ) + jnp.einsum("fbd,fbe->fde", imaginary_side, grad_imaginary, preferred_element_type=FLOAT)
    weight_imaginary = jnp.einsum(
        "fbd,fbe->fde", real_side, grad_imaginary, preferred_element_type=FLOAT
    ) - jnp.einsum("fbd,fbe->fde", imaginary_side, grad_real, preferred_element_type=FLOAT)
    return jnp.stack([weight_real, weight_imaginary], axis=1)


def extend_series(series_in, rim_width):
    padded = extended_2(series_in, (("tm", 1),), rim_width)
    position = lax.axis_index("tm")
    final_index = lax.axis_size("tm") - 1
    step_count = series_in.shape[1]
    left_rim = jnp.where(
        position == 0,
        jnp.broadcast_to(series_in[:, :1], padded[:, :rim_width].shape),
        padded[:, :rim_width],
    )
    right_rim = jnp.where(
        position == final_index,
        jnp.broadcast_to(series_in[:, -1:], padded[:, rim_width + step_count :].shape),
        padded[:, rim_width + step_count :],
    )
    return jnp.concatenate([left_rim, series_in, right_rim], axis=1)


def band(step_count, rim_width, half_window):
    row = np.arange(step_count)[:, None] + rim_width
    column = np.arange(step_count + 2 * rim_width)[None, :]
    return (np.abs(row - column) <= half_window).astype(HALF_FLOAT)


def seasonal_part(extended, series_in, half_window, rim_width):
    step_count = series_in.shape[1]
    matrix = jnp.asarray(band(step_count, rim_width, half_window))
    running = jnp.einsum("qr,brd->bqd", matrix, extended, preferred_element_type=FLOAT)
    return (series_in.astype(FLOAT) - running / (2 * half_window + 1)).astype(HALF_FLOAT)


def mean_back(grad, half_window, rim_width, is_first, is_final):
    step_count = grad.shape[1]
    matrix = jnp.asarray(band(step_count, rim_width, half_window))
    high = grad.astype(HALF_FLOAT)
    low = (grad - high.astype(FLOAT)).astype(HALF_FLOAT)
    wide = jnp.einsum("qr,bqd->brd", matrix, high, preferred_element_type=FLOAT) + jnp.einsum(
        "qr,bqd->brd", matrix, low, preferred_element_type=FLOAT
    )
    return wide / (2 * half_window + 1)


def batch_split(values, split, join):
    return lax.all_to_all(values, "batch", split_axis=split, concat_axis=join, tiled=True)


def kernel_gradients(tasks):
    batches = lax.axis_size("batch")
    channels = tasks[0][1].shape[2]
    results = []
    if batches == 2 and channels % 256 == 0 and lax.axis_size("tm") % (channels // 128) == 0:
        packed = []
        for kind, wide, narrow in tasks:
            extra = -wide.shape[0] % 16
            wide = jnp.pad(wide, ((0, extra), (0, 0), (0, 0)))
            narrow = jnp.pad(narrow, ((0, extra), (0, 0)))
            packed.append((kind, jnp.transpose(wide, (1, 0, 2)), narrow))
        for (kind, _, _), value in zip(tasks, weight_gradients(packed)):
            results.append(jnp.transpose(value, (0, 2, 1) if kind == "down" else (2, 0, 1)))
        return results
    for kind, wide, narrow in tasks:
        if kind == "down":
            wide, narrow = batch_split(wide, 2, 0), lax.all_gather(narrow, "batch", tiled=True)
            value = jnp.einsum("nkc,nd->kcd", wide, narrow, preferred_element_type=FLOAT)
        else:
            wide, narrow = lax.all_gather(wide, "batch", tiled=True), batch_split(narrow, 1, 0)
            value = jnp.einsum("nd,nkc->dkc", narrow, wide, preferred_element_type=FLOAT)
        results.append(time_sum(value, 2))
    return results


def time_sum(values, dim):
    return lax.psum_scatter(
        values.astype(HALF_FLOAT), "tm", scatter_dimension=dim, tiled=True
    ).astype(FLOAT)


def branch_down(seasonal_low, down_weight, bias_row):
    series_count, step_count, channels = seasonal_low.shape
    kernel = down_weight.shape[0]
    pieces = step_count // kernel
    blocks = seasonal_low.reshape(series_count * pieces, kernel * channels)
    down_act = jnp.tanh(
        jnp.dot(
            blocks, down_weight.reshape(kernel * channels, channels), preferred_element_type=FLOAT
        )
        + bias_row
    )
    return down_act.reshape(series_count, pieces, channels)


def branch_up(seasonal_low, down_act, iso_out, up_weight, bias_rows, gain_row, bias_row):
    series_count, step_count, channels = seasonal_low.shape
    kernel = up_weight.shape[1]
    pieces = step_count // kernel
    iso_act = jnp.tanh(iso_out + bias_rows[0])
    inner_in = iso_act + down_act.astype(HALF_FLOAT).astype(FLOAT)
    inner_low = layer_norm(inner_in, gain_row, bias_row).astype(HALF_FLOAT)
    up_pre = jnp.dot(
        inner_low.reshape(series_count * pieces, channels),
        up_weight.reshape(channels, kernel * channels),
        preferred_element_type=FLOAT,
    )
    up_act = jnp.tanh(up_pre.reshape(series_count, step_count, channels) + bias_rows[1])
    outer_in = up_act + seasonal_low.astype(FLOAT)
    branch_out = layer_norm(outer_in, gain_row, bias_row)
    return branch_out, (iso_act, inner_in, inner_low, up_act, outer_in)


def branch_up_back(grad_out, up_weight, gain_row, bias_row, kept):
    iso_act, inner_in, inner_low, up_act, outer_in = kept
    series_count, step_count, channels = grad_out.shape
    kernel = up_weight.shape[1]
    pieces = step_count // kernel
    normed_out, outer_pull = jax.vjp(layer_norm, outer_in, gain_row, bias_row)
    grad_outer, gain_outer, shift_outer = outer_pull(grad_out)
    grad_up = (grad_outer * (1.0 - up_act * up_act)).astype(HALF_FLOAT)
    up_rows = grad_up.reshape(series_count * pieces, kernel * channels)
    inner_rows = inner_low.reshape(series_count * pieces, channels)
    up_flat = up_weight.reshape(channels, kernel * channels)
    grad_up_weight = ("up", up_rows.reshape(-1, kernel, channels), inner_rows)
    grad_up_bias = jnp.sum(grad_up.astype(FLOAT), axis=(0, 1))
    grad_inner = jnp.einsum("nk,dk->nd", up_rows, up_flat, preferred_element_type=FLOAT).reshape(
        series_count, pieces, channels
    )
    normed_inner, inner_pull = jax.vjp(layer_norm, inner_in, gain_row, bias_row)
    grad_inner_in, gain_inner, shift_inner = inner_pull(grad_inner)
    grad_iso = grad_inner_in * (1.0 - iso_act * iso_act)
    grad_iso_bias = jnp.sum(grad_iso, axis=(0, 1))
    return (
        grad_iso.astype(HALF_FLOAT),
        grad_inner_in,
        grad_outer,
        (
            grad_up_weight,
            grad_iso_bias,
            grad_up_bias,
            gain_outer + gain_inner,
            shift_outer + shift_inner,
        ),
    )


def branch_down_back(grad_signal, grad_inner_in, grad_outer, seasonal_low, down_act, down_weight):
    series_count, step_count, channels = seasonal_low.shape
    kernel = down_weight.shape[0]
    pieces = step_count // kernel
    grad_down = grad_signal + grad_inner_in
    grad_down_pre = (grad_down * (1.0 - down_act * down_act)).astype(HALF_FLOAT)
    down_rows = grad_down_pre.reshape(series_count * pieces, channels)
    down_flat = down_weight.reshape(kernel * channels, channels)
    grad_down_weight = ("down", seasonal_low.reshape(-1, kernel, channels), down_rows)
    grad_down_bias = jnp.sum(grad_down_pre.astype(FLOAT), axis=(0, 1))
    grad_seasonal = (
        jnp.einsum("nd,kd->nk", down_rows, down_flat, preferred_element_type=FLOAT).reshape(
            series_count, step_count, channels
        )
        + grad_outer
    )
    return grad_seasonal, grad_down_weight, grad_down_bias


def batch_split(values, split, join):
    return lax.all_to_all(values, "batch", split_axis=split, concat_axis=join, tiled=True)


def iso_weight_grad(spectrum, grad_mixed):
    return spectral_weight_grad(
        batch_split(spectrum, 3, 2), lax.all_gather(grad_mixed, "batch", axis=2, tiled=True)
    )


def time_sum(values, dim):
    return lax.psum_scatter(
        values.astype(HALF_FLOAT), "tm", scatter_dimension=dim, tiled=True
    ).astype(FLOAT)


def per_device(
    series_in,
    out_cotangent,
    out_mask,
    down_twelve,
    down_sixteen,
    iso_twelve,
    iso_sixteen,
    up_twelve,
    up_sixteen,
    branch_bias,
    merge_weight,
    hidden_weight,
    hidden_bias,
    output_weight,
    head_bias,
    norm_gain,
    norm_shift,
):
    series_dev, step_count, channels = series_in.shape
    row_count = series_dev * step_count
    half_one = down_twelve.shape[0] // 2
    half_two = down_sixteen.shape[0] // 2
    rim_width = max(half_one, half_two)
    biases = branch_bias.astype(FLOAT)
    gains = norm_gain.astype(FLOAT)
    shifts = norm_shift.astype(FLOAT)
    heads = head_bias.astype(FLOAT)
    extended = extend_series(series_in, rim_width)
    seasonal_one = seasonal_part(extended, series_in, half_one, rim_width)
    seasonal_two = seasonal_part(extended, series_in, half_two, rim_width)
    down_one = branch_down(seasonal_one, down_twelve, biases[0])
    down_two = branch_down(seasonal_two, down_sixteen, biases[1])
    iso_weights = (iso_twelve, iso_sixteen)
    spectra, iso_outs = spectral(
        (down_one.astype(HALF_FLOAT), down_two.astype(HALF_FLOAT)), iso_weights, False
    )
    out_one, kept_one = branch_up(
        seasonal_one,
        down_one,
        iso_outs[0],
        up_twelve,
        (biases[2], biases[4]),
        gains[0],
        shifts[0],
    )
    out_two, kept_two = branch_up(
        seasonal_two,
        down_two,
        iso_outs[1],
        up_sixteen,
        (biases[3], biases[5]),
        gains[0],
        shifts[0],
    )
    branch_low = jnp.concatenate(
        [out_one.astype(HALF_FLOAT), out_two.astype(HALF_FLOAT)], axis=2
    ).reshape(row_count, 2 * channels)
    merge_flat = merge_weight.reshape(2 * channels, channels)
    merged = jnp.dot(branch_low, merge_flat, preferred_element_type=FLOAT) + heads[0]
    first_low = layer_norm(merged, gains[1], shifts[1]).astype(HALF_FLOAT)
    hidden_pre = jnp.dot(
        first_low, hidden_weight, preferred_element_type=FLOAT
    ) + hidden_bias.astype(FLOAT)
    hidden_low = jax.nn.gelu(hidden_pre).astype(HALF_FLOAT)
    final_in = merged + (
        jnp.dot(hidden_low, output_weight, preferred_element_type=FLOAT) + heads[1]
    )
    mask_rows = out_mask.astype(FLOAT).reshape(row_count, 1)
    result = (
        (layer_norm(final_in, gains[2], shifts[2]) * mask_rows)
        .astype(HALF_FLOAT)
        .reshape(series_dev, step_count, channels)
    )
    grad_result = out_cotangent.astype(FLOAT).reshape(row_count, channels) * mask_rows
    normed_final, final_pull = jax.vjp(layer_norm, final_in, gains[2], shifts[2])
    grad_final, gain_final, shift_final = final_pull(grad_result)
    grad_feed = grad_final.astype(HALF_FLOAT)
    grad_output_weight = jnp.einsum(
        "nf,nd->fd", hidden_low, grad_feed, preferred_element_type=FLOAT
    )
    grad_output_bias = jnp.sum(grad_feed.astype(FLOAT), axis=0)
    grad_hidden_low = jnp.einsum(
        "nd,fd->nf", grad_feed, output_weight, preferred_element_type=FLOAT
    )
    gelu_value, gelu_pull = jax.vjp(jax.nn.gelu, hidden_pre)
    grad_hidden_pre = gelu_pull(grad_hidden_low)[0].astype(HALF_FLOAT)
    grad_hidden_weight = jnp.einsum(
        "nd,nf->df", first_low, grad_hidden_pre, preferred_element_type=FLOAT
    )
    grad_hidden_bias = jnp.sum(grad_hidden_pre.astype(FLOAT), axis=0)
    grad_first = jnp.einsum(
        "nf,df->nd", grad_hidden_pre, hidden_weight, preferred_element_type=FLOAT
    )
    normed_first, first_pull = jax.vjp(layer_norm, merged, gains[1], shifts[1])
    grad_merged_norm, gain_first, shift_first = first_pull(grad_first)
    grad_merged = (grad_final + grad_merged_norm).astype(HALF_FLOAT)
    grad_merge_bias = jnp.sum(grad_merged.astype(FLOAT), axis=0)
    grad_merge_weight = jnp.einsum(
        "nk,nd->kd", branch_low, grad_merged, preferred_element_type=FLOAT
    ).reshape(2, channels, channels)
    grad_branch = jnp.einsum("nd,kd->nk", grad_merged, merge_flat, preferred_element_type=FLOAT)
    grad_out_one = grad_branch[:, :channels].reshape(series_dev, step_count, channels)
    grad_out_two = grad_branch[:, channels:].reshape(series_dev, step_count, channels)
    iso_one, inner_one, outer_one, terms_one = branch_up_back(
        grad_out_one, up_twelve, gains[0], shifts[0], kept_one
    )
    iso_two, inner_two, outer_two, terms_two = branch_up_back(
        grad_out_two, up_sixteen, gains[0], shifts[0], kept_two
    )
    grads_mixed, grad_signals = spectral((iso_one, iso_two), iso_weights, True)
    grad_iso_one = iso_weight_grad(spectra[0], grads_mixed[0])
    grad_iso_two = iso_weight_grad(spectra[1], grads_mixed[1])
    grad_seasonal_one, grad_down_one, down_bias_one = branch_down_back(
        grad_signals[0], inner_one, outer_one, seasonal_one, down_one, down_twelve
    )
    grad_seasonal_two, grad_down_two, down_bias_two = branch_down_back(
        grad_signals[1], inner_two, outer_two, seasonal_two, down_two, down_sixteen
    )
    position = lax.axis_index("tm")
    final_index = lax.axis_size("tm") - 1
    wide = mean_back(grad_seasonal_one, half_one, rim_width, None, None) + mean_back(
        grad_seasonal_two, half_two, rim_width, None, None
    )
    low_rim = wide[:, :rim_width]
    high_rim = wide[:, rim_width + step_count :]
    forward = [(i, i + 1) for i in range(final_index)]
    from_low = lax.ppermute(high_rim, "tm", forward)
    from_high = lax.ppermute(low_rim, "tm", [(j, i) for i, j in forward])
    edge_low = jnp.where(
        position == 0,
        jnp.pad(jnp.sum(low_rim, axis=1, keepdims=True), ((0, 0), (0, rim_width - 1), (0, 0))),
        from_low,
    )
    edge_high = jnp.where(
        position == final_index,
        jnp.pad(jnp.sum(high_rim, axis=1, keepdims=True), ((0, 0), (rim_width - 1, 0), (0, 0))),
        from_high,
    )
    mean_total = wide[:, rim_width : rim_width + step_count] + jnp.concatenate(
        [
            edge_low,
            jnp.zeros((series_dev, step_count - 2 * rim_width, channels), FLOAT),
            edge_high,
        ],
        axis=1,
    )
    grad_series = (grad_seasonal_one + grad_seasonal_two - mean_total).astype(HALF_FLOAT)
    vectors = jnp.stack(
        [
            down_bias_one,
            down_bias_two,
            terms_one[1],
            terms_two[1],
            terms_one[2],
            terms_two[2],
            terms_one[3] + terms_two[3],
            gain_first,
            gain_final,
            terms_one[4] + terms_two[4],
            shift_first,
            shift_final,
            grad_merge_bias,
            grad_output_bias,
        ]
    )
    devices = lax.axis_size("tm")
    vector_count = vectors.shape[0]
    packed = jnp.concatenate(
        [
            vectors.reshape(vector_count, devices, -1).transpose(1, 0, 2).reshape(devices, -1),
            grad_hidden_bias.reshape(devices, -1),
        ],
        axis=1,
    )
    packed = lax.psum(lax.psum_scatter(packed, "tm", scatter_dimension=0, tiled=True), "batch")[0]
    width = channels // devices
    rows = packed[: vector_count * width].reshape(vector_count, width)
    vector_parts = (
        rows[:6],
        packed[vector_count * width :],
        rows[12:14],
        rows[6:9],
        rows[9:12],
    )
    merge_half = lax.psum_scatter(grad_merge_weight, "batch", scatter_dimension=1, tiled=True)
    hidden_half = lax.psum_scatter(grad_hidden_weight, "batch", scatter_dimension=0, tiled=True)
    output_half = lax.psum_scatter(grad_output_weight, "batch", scatter_dimension=0, tiled=True)
    matrix_parts = (
        *kernel_gradients((terms_one[0], terms_two[0], grad_down_one, grad_down_two)),
        time_sum(merge_half, 2),
        time_sum(hidden_half, 1),
        time_sum(output_half, 1),
    )
    iso_parts = (grad_iso_one, grad_iso_two)
    return (
        result,
        grad_series,
        matrix_parts[2],
        matrix_parts[3],
        iso_parts[0],
        iso_parts[1],
        matrix_parts[0],
        matrix_parts[1],
        vector_parts[0],
        matrix_parts[4],
        matrix_parts[5],
        vector_parts[1],
        matrix_parts[6],
        vector_parts[2],
        vector_parts[3],
        vector_parts[4],
    )


def solution(mesh):
    placed = (
        P("batch", "tm", None),
        P("batch", "tm", None),
        P("batch", "tm"),
        P(),
        P(),
        P("tm", None, "batch", None),
        P("tm", None, "batch", None),
        P(),
        P(),
        P(),
        P(),
        P(),
        P(),
        P(),
        P(),
        P(),
        P(),
    )
    return jax.shard_map(
        per_device,
        mesh=mesh,
        in_specs=placed,
        out_specs=(
            P("batch", "tm", None),
            P("batch", "tm", None),
            P(None, "batch", "tm"),
            P(None, "batch", "tm"),
            P("tm", None, "batch", None),
            P("tm", None, "batch", None),
            P("batch", None, "tm"),
            P("batch", None, "tm"),
            P(None, "tm"),
            P(None, "batch", "tm"),
            P("batch", "tm"),
            P("tm"),
            P("batch", "tm"),
            P(None, "tm"),
            P(None, "tm"),
            P(None, "tm"),
        ),
        check_vma=False,
    )
```

```python
import functools
import math

import jax
import jax.numpy as jnp
import numpy as np
from jax import lax
from jax.experimental import pallas as pl
from jax.experimental.pallas import tpu as pltpu
from jax.sharding import PartitionSpec as P

FLOAT = jnp.float32
HALF_FLOAT = jnp.bfloat16
HIGHEST = lax.Precision.HIGHEST
EPSILON = 1e-05
MESH = pl.DeviceIdType.MESH


def extended_2(block, sides, width):
    for axis, dim in sides:
        count = lax.axis_size(axis)
        forward = [(i, i + 1) for i in range(count - 1)]
        backward = [(target, source) for source, target in forward]
        low = lax.ppermute(
            lax.slice_in_dim(block, block.shape[dim] - width, None, axis=dim), axis, forward
        )
        high = lax.ppermute(lax.slice_in_dim(block, 0, width, axis=dim), axis, backward)
        block = jnp.concatenate([low, block, high], axis=dim)
    return block


def layer_norm(values, gain_row, bias_row):
    center = values - jnp.mean(values, axis=-1, keepdims=True)
    spread = jnp.mean(center * center, axis=-1, keepdims=True)
    return center * lax.rsqrt(spread + EPSILON) * gain_row + bias_row


def round_up(value, multiple):
    return -(-value // multiple) * multiple


def spectral_constants(devices, pieces_list):
    padded = [round_up(pieces, 8) for pieces in pieces_list]
    per_time, per_bin = sum(padded), 2 * sum(padded)
    table = np.zeros((devices, per_bin, devices, per_time), np.float64)
    offset = 0
    for pieces, wide in zip(pieces_list, padded):
        length = devices * pieces
        index = np.arange(length)
        angle = (2.0 * math.pi / length) * (np.outer(index, index) % length)
        factor = 1.0 / math.sqrt(length)
        for part, values in enumerate((np.cos(angle) * factor, -np.sin(angle) * factor)):
            row = 2 * offset + part * wide
            table[:, row : row + pieces, :, offset : offset + pieces] = values.reshape(
                devices, pieces, devices, pieces
            )
        offset += wide
    table = table.reshape(devices * per_bin, devices * per_time).astype(np.float32)
    high = table.astype(HALF_FLOAT)
    low = (table - high.astype(np.float32)).astype(HALF_FLOAT)
    order = []
    offset = 0
    for wide in padded:
        for one_bin in range(wide):
            for part in range(2):
                for series in range(devices):
                    order.append(series * per_bin + 2 * offset + part * wide + one_bin)
        offset += wide
    move = np.zeros((devices * per_bin, devices * per_bin), np.float32)
    move[np.arange(len(order)), order] = 1.0
    move = move.astype(HALF_FLOAT)
    return (
        jnp.asarray(np.stack([high, low])),
        jnp.asarray(np.stack([high.T, low.T])),
        jnp.asarray(move),
        jnp.asarray(np.ascontiguousarray(move.T)),
    )


def dot_nn(left, right):
    return jnp.dot(left, right, preferred_element_type=FLOAT)


def dot_nt(left, right):
    return lax.dot_general(left, right, (((1,), (1,)), ((), ())), preferred_element_type=FLOAT)


def spectral_body(sizes, back, refs, extra):
    devices, batches, count, pieces_list = sizes
    x_ref, w1_ref, w2_ref = refs["x"], refs["weight0"], refs["weight1"]
    table_ref, inverse_ref = refs["table"], refs["inverse"]
    move_ref, unmove_ref = refs["move"], refs["unmove"]
    spec_ref, signal_ref = refs["spec"], refs["signal"]
    (one, two, three, mixed, spread, bins_out, four, w1, w2) = refs["buffers"]
    (s1, r1, s2, r2, s3, r3, s4, r4, ws, wr, own) = refs["sems"]
    me = lax.axis_index("tm")
    mine = lax.axis_index("batch")
    wide = [round_up(pieces, 8) for pieces in pieces_list]
    per_time, per_bin = sum(wide), 2 * sum(wide)
    weights = ((w1_ref, w1), (w2_ref, w2))

    barrier = pltpu.get_barrier_semaphore()

    @pl.loop(1, devices)
    def _(step):
        pl.semaphore_signal(
            barrier, inc=1, device_id=(mine, lax.rem(me + step, devices)), device_id_type=MESH
        )

    for step in range(1, batches):
        pl.semaphore_signal(
            barrier, inc=1, device_id=(lax.rem(mine + step, batches), me), device_id_type=MESH
        )
    pl.semaphore_wait(barrier, devices - 1 + batches - 1 + extra.greet(barrier))

    def exchange(source, target, send_sem, recv_sem, limit_out, limit_in, rows, start):
        def remote(there, here):
            return pltpu.make_async_remote_copy(
                src_ref=source.at[pl.ds(pl.multiple_of(there * rows, rows), rows)],
                dst_ref=target.at[pl.ds(pl.multiple_of(here * rows, rows), rows)],
                send_sem=send_sem.at[there],
                recv_sem=recv_sem.at[here],
                device_id=(mine, there),
                device_id_type=MESH,
            )

        if start:

            @pl.loop(1, devices)
            def _(step):
                there = lax.rem(me + step, devices)

                @pl.when(there < limit_out)
                def _():
                    remote(there, me).start()

        else:

            @pl.loop(1, devices)
            def _(step):
                there = lax.rem(me + step, devices)

                @pl.when(there < limit_in)
                def _():
                    pltpu.make_async_remote_copy(
                        src_ref=source.at[pl.ds(0, rows)],
                        dst_ref=target.at[pl.ds(pl.multiple_of(there * rows, rows), rows)],
                        send_sem=send_sem.at[there],
                        recv_sem=recv_sem.at[there],
                        device_id=(mine, there),
                        device_id_type=MESH,
                    ).wait_recv()

    def drain(source, target, send_sem, recv_sem, limit_out, rows):
        @pl.loop(1, devices)
        def _(step):
            there = lax.rem(me + step, devices)

            @pl.when(there < limit_out)
            def _():
                pltpu.make_async_remote_copy(
                    src_ref=source.at[pl.ds(0, rows)],
                    dst_ref=target.at[pl.ds(0, rows)],
                    send_sem=send_sem.at[there],
                    recv_sem=recv_sem.at[there],
                    device_id=(mine, there),
                    device_id_type=MESH,
                ).wait_send()

    owner = me < count
    exchange(x_ref, one, s1, r1, count, None, per_time, True)

    def weight_copies(index):
        source, target = weights[index]
        rows = source.shape[2]
        place = target.at[:, :, pl.ds(pl.multiple_of(mine * rows, rows), rows)]
        local = pltpu.make_async_copy(source, place, own.at[index])
        remote = []
        for step in range(1, batches):
            there = lax.rem(mine + step, batches)
            back_there = lax.rem(mine + batches - step, batches)
            other = target.at[:, :, pl.ds(pl.multiple_of(back_there * rows, rows), rows)]
            remote.append(
                [
                    pltpu.make_async_remote_copy(
                        src_ref=source,
                        dst_ref=where,
                        send_sem=ws.at[index, step],
                        recv_sem=wr.at[index, step],
                        device_id=(there, me),
                        device_id_type=MESH,
                    )
                    for where in (place, other)
                ]
            )
        return local, remote

    for index in range(2):
        local, remote = weight_copies(index)
        local.start()
        for copy, _unused in remote:
            copy.start()

    here = pltpu.make_async_copy(
        x_ref.at[pl.ds(pl.multiple_of(jnp.minimum(me, count - 1) * per_time, per_time), per_time)],
        one.at[pl.ds(pl.multiple_of(me * per_time, per_time), per_time)],
        own.at[2],
    )
    here.start()
    extra.start()
    if count < devices:
        two[pl.ds(count * per_bin, (devices - count) * per_bin)] = jnp.zeros(
            ((devices - count) * per_bin, two.shape[1]), two.dtype
        )
    here.wait()

    @pl.when(owner)
    def _():
        exchange(x_ref, one, s1, r1, None, devices, per_time, False)
        data = one[...]
        total = dot_nn(table_ref[0], data) + dot_nn(table_ref[1], data)
        bins_out[...] = total.astype(HALF_FLOAT)
        exchange(bins_out, two, s2, r2, devices, None, per_bin, True)
        place = pl.ds(pl.multiple_of(me * per_bin, per_bin), per_bin)
        two[place] = bins_out[place]

    extra.after_bins()
    exchange(bins_out, two, s2, r2, None, count, per_bin, False)
    spec_ref[...] = dot_nn(move_ref[...], two[...]).astype(HALF_FLOAT)
    extra.after_spec()
    base = 0
    for index in range(2):
        local, remote = weight_copies(index)
        local.wait()
        for copy, arrived in remote:
            copy.wait_send()
            arrived.wait_recv()
        target = weights[index][1]

        @pl.loop(0, pieces_list[index])
        def _(one_bin, base=base, target=target):
            place = pl.ds(
                pl.multiple_of(base + one_bin * 2 * devices, 2 * devices), 2 * devices
            )
            rows = spec_ref[place]
            if back:
                real = dot_nt(rows, target[one_bin, 0])
                imag = dot_nt(rows, target[one_bin, 1])
                out = jnp.concatenate(
                    [real[:devices] + imag[devices:], real[devices:] - imag[:devices]]
                )
            else:
                real = dot_nn(rows, target[one_bin, 0])
                imag = dot_nn(rows, target[one_bin, 1])
                out = jnp.concatenate(
                    [real[:devices] - imag[devices:], imag[:devices] + real[devices:]]
                )
            mixed[place] = out.astype(HALF_FLOAT)

        spare = wide[index] - pieces_list[index]
        if spare:
            mixed[
                pl.ds(base + pieces_list[index] * 2 * devices, spare * 2 * devices)
            ] = jnp.zeros((spare * 2 * devices, mixed.shape[1]), mixed.dtype)
        base += wide[index] * 2 * devices

    spread[...] = dot_nn(unmove_ref[...], mixed[...]).astype(HALF_FLOAT)
    exchange(spread, three, s3, r3, count, None, per_bin, True)

    @pl.when(owner)
    def _():
        place = pl.ds(pl.multiple_of(me * per_bin, per_bin), per_bin)
        three[place] = spread[place]
        exchange(spread, three, s3, r3, None, devices, per_bin, False)
        data = three[...]
        total = dot_nn(inverse_ref[0], data) + dot_nn(inverse_ref[1], data)
        four[...] = total
        exchange(four, signal_ref, s4, r4, devices, None, per_time, True)
        place = pl.ds(pl.multiple_of(me * per_time, per_time), per_time)
        signal_ref[place] = four[place]

    extra.after_signal()
    exchange(four, signal_ref, s4, r4, None, count, per_time, False)
    drain(x_ref, one, s1, r1, count, per_time)
    drain(spread, three, s3, r3, count, per_bin)

    @pl.when(owner)
    def _():
        drain(bins_out, two, s2, r2, devices, per_bin)
        drain(four, signal_ref, s4, r4, devices, per_time)

    extra.finish()


class Place:
    def __init__(self, groups, members, batches):
        self.groups, self.members, self.batches = groups, members, batches
        self.me = lax.axis_index("tm")
        self.core = lax.axis_index("batch")
        self.group = lax.div(self.me, members)
        self.member = lax.rem(self.me, members)

    def device(self, group, member, core):
        return (core, group * self.members + member)

    def member_at(self, step):
        return lax.rem(self.member + step + self.members, self.members)

    def group_at(self, step):
        return lax.rem(self.group + step + self.groups, self.groups)

    def core_at(self, step):
        return lax.rem(self.core + step + self.batches, self.batches)

    def greet(self, barrier):
        greeted = 0
        for step in range(self.members):
            for turn in range(self.batches):
                if step or turn:
                    there = self.device(self.group, self.member_at(step), self.core_at(turn))
                    pl.semaphore_signal(barrier, inc=1, device_id=there, device_id_type=MESH)
                    greeted += 1
        for step in range(1, self.groups):
            for turn in range(self.batches):
                there = self.device(self.group_at(step), self.member, self.core_at(turn))
                pl.semaphore_signal(barrier, inc=1, device_id=there, device_id_type=MESH)
                greeted += 1
        return greeted


def send_copy(source, target, send_sem, recv_sem, there):
    return pltpu.make_async_remote_copy(
        src_ref=source,
        dst_ref=target,
        send_sem=send_sem,
        recv_sem=recv_sem,
        device_id=there,
        device_id_type=MESH,
    )


def slab(ref, dim, index, size):
    picks = [slice(None)] * len(ref.shape)
    picks[dim] = pl.ds(pl.multiple_of(index * size, size), size)
    return ref.at[tuple(picks)]


class WideExchange:
    sems = 3

    @staticmethod
    def scratch(place_sizes, wide):
        groups, members, batches = place_sizes
        mates = members * batches
        steps, half = wide.shape[0] // members, wide.shape[2] // batches
        dma = pltpu.SemaphoreType.DMA
        return [dma((mates,)), dma((mates,)), dma((1,))]

    @staticmethod
    def shape(place_sizes, wide):
        groups, members, batches = place_sizes
        return (
            wide.shape[0] // members,
            members * batches,
            wide.shape[1],
            wide.shape[2] // batches,
        )

    def __init__(self, place, source, target, sems):
        self.place, self.source, self.target = place, source, target
        self.send_sem, self.recv_sem, self.local_sem = sems

    def hops(self):
        for step in range(self.place.members):
            for turn in range(self.place.batches):
                if step or turn:
                    yield step, turn

    def out(self, step, turn, pick_step, pick_turn):
        place = self.place
        member, core = place.member_at(step), place.core_at(turn)
        steps, half = self.target.shape[0], self.target.shape[3]
        source = slab(slab(self.source, 0, member, steps), 2, core, half)
        pick = place.core_at(pick_turn) * place.members + place.member_at(pick_step)
        slot = turn * place.members + step
        return send_copy(
            source,
            self.target.at[:, pick],
            self.send_sem.at[slot],
            self.recv_sem.at[slot],
            place.device(place.group, member, core),
        )

    def own(self):
        place = self.place
        steps, half = self.target.shape[0], self.target.shape[3]
        source = slab(slab(self.source, 0, place.member, steps), 2, place.core, half)
        pick = place.core * place.members + place.member
        return pltpu.make_async_copy(source, self.target.at[:, pick], self.local_sem.at[0])

    def start(self):
        self.own().start()
        for step, turn in self.hops():
            self.out(step, turn, 0, 0).start()

    def wait(self):
        self.own().wait()
        for step, turn in self.hops():
            self.out(step, turn, -step, -turn).wait_recv()

    def drain(self):
        for step, turn in self.hops():
            self.out(step, turn, 0, 0).wait_send()


class NarrowGather:
    sems = 5

    @staticmethod
    def scratch(place_sizes, narrow):
        groups, members, batches = place_sizes
        dma = pltpu.SemaphoreType.DMA
        size = members * batches
        return [dma((members,)), dma((members,)), dma((size,)), dma((size,)), dma((1,))]

    def __init__(self, place, source, target, sems):
        self.place, self.source, self.target = place, source, target
        (self.link_send, self.link_recv, self.chip_send, self.chip_recv, self.local_sem) = sems

    def own(self):
        place = self.place
        pick = place.core * place.members + place.member
        return pltpu.make_async_copy(self.source, self.target.at[pick], self.local_sem.at[0])

    def link(self, step, pick_step):
        place = self.place
        pick = place.core * place.members + place.member_at(pick_step)
        return send_copy(
            self.source,
            self.target.at[pick],
            self.link_send.at[step],
            self.link_recv.at[step],
            place.device(place.group, place.member_at(step), place.core),
        )

    def chip(self, step, turn, source_core, target_core):
        place = self.place
        member = place.member_at(-step)
        slot = turn * place.members + step
        source = self.target.at[source_core * place.members + member] if step else self.source
        return send_copy(
            source,
            self.target.at[target_core * place.members + member],
            self.chip_send.at[slot],
            self.chip_recv.at[slot],
            place.device(place.group, place.member, place.core_at(turn)),
        )

    def start(self):
        place = self.place
        self.own().start()
        for step in range(1, place.members):
            self.link(step, 0).start()
        for turn in range(1, place.batches):
            self.chip(0, turn, place.core, place.core).start()

    def forward(self):
        place = self.place
        for step in range(1, place.members):
            self.link(step, -step).wait_recv()
            for turn in range(1, place.batches):
                self.chip(step, turn, place.core, place.core).start()

    def wait(self):
        place = self.place
        self.own().wait()
        for turn in range(1, place.batches):
            other = place.core_at(-turn)
            for step in range(place.members):
                self.chip(step, turn, place.core, other).wait_recv()

    def drain(self):
        place = self.place
        for step in range(1, place.members):
            self.link(step, 0).wait_send()
        for turn in range(1, place.batches):
            for step in range(place.members):
                self.chip(step, turn, place.core, place.core).wait_send()


class KernelProduct:
    sems = 6

    @staticmethod
    def scratch(place_sizes, kind, wide, narrow):
        groups, members, batches = place_sizes
        steps, rows, channels = wide.shape[0] // members, wide.shape[1], wide.shape[2]
        half = channels // batches
        piece = (128, half) if kind == "down" else (half, 128)
        dma = pltpu.SemaphoreType.DMA
        return [
            pltpu.VMEM((channels, members * batches * rows), HALF_FLOAT),
            pltpu.VMEM((steps, channels, half), HALF_FLOAT),
            pltpu.VMEM((groups, steps) + piece, HALF_FLOAT),
            pltpu.VMEM((steps, 128, half), HALF_FLOAT),
            pltpu.VMEM((wide.shape[0], channels // (groups * members), half), HALF_FLOAT),
            dma((groups * batches,)),
            dma((groups * batches,)),
            dma((members,)),
            dma((members,)),
            dma((2,)),
        ]

    def __init__(self, place, kind, wide_in, narrow_in, out, scratch):
        self.place, self.kind, self.wide_in, self.narrow_in, self.out = (
            place,
            kind,
            wide_in,
            narrow_in,
            out,
        )
        (self.narrow_t, self.send, self.recv, self.total, self.gathered) = scratch[:5]
        (self.sz, self.rz, self.sf, self.rf, self.local) = scratch[5:]
        self.cores_per_group = place.groups // place.batches

    def multiply(self):
        mates, rows = self.narrow_in.shape[0], self.narrow_in.shape[1]
        self.narrow_t[...] = self.narrow_in[...].reshape(mates * rows, -1).T

        @pl.loop(0, self.wide_in.shape[0])
        def _(one):
            data = self.wide_in[one].reshape(mates * rows, -1)
            self.send[one] = dot_nn(self.narrow_t[...], data).astype(HALF_FLOAT)

    def chunk(self, group, core):
        if self.kind == "down":
            return slab(self.send, 1, group, 128)
        half = self.send.shape[1] // self.place.batches
        return slab(
            slab(self.send, 1, core, half), 2, lax.rem(group, self.cores_per_group), 128
        )

    def hops(self):
        place = self.place
        for step in range(place.groups):
            for turn in range(place.batches if self.kind == "up" else 1):
                yield step, turn

    def partial(self, step, turn, action):
        place = self.place
        group, core = place.group_at(step), place.core_at(turn)
        slot = step * place.batches + turn
        if step == 0 and turn == 0:
            copy = pltpu.make_async_copy(
                self.chunk(group, core), self.recv.at[place.group], self.local.at[0]
            )
            act = lambda: action(copy, True)
        else:
            copy = send_copy(
                self.chunk(group, core),
                self.recv.at[place.group],
                self.sz.at[slot],
                self.rz.at[slot],
                place.device(group, place.member, core),
            )
            act = lambda: action(copy, False)
        if self.kind == "down":
            act()
        else:
            pl.when(lax.div(group, self.cores_per_group) == place.core)(act)

    def start_partials(self):
        for step, turn in self.hops():
            self.partial(step, turn, lambda copy, local: copy.start())

    def sum_partials(self):
        place = self.place
        for step, turn in self.hops():
            group, core = place.group_at(-step), place.core_at(-turn)
            slot = step * place.batches + turn

            def act(step=step, turn=turn, group=group, slot=slot):
                if step == 0 and turn == 0:
                    pltpu.make_async_copy(
                        self.chunk(place.group, place.core),
                        self.recv.at[place.group],
                        self.local.at[0],
                    ).wait()
                else:
                    send_copy(
                        self.chunk(place.group, place.core),
                        self.recv.at[group],
                        self.sz.at[slot],
                        self.rz.at[slot],
                        place.device(place.group, place.member, place.core),
                    ).wait_recv()

            if self.kind == "down":
                act()
            else:
                pl.when(lax.div(place.group, self.cores_per_group) == core)(act)

        @pl.loop(0, self.total.shape[0])
        def _(one):
            value = self.recv[0, one].astype(FLOAT)
            for other in range(1, place.groups):
                value = value + self.recv[other, one].astype(FLOAT)
            value = value if self.kind == "down" else value.T
            self.total[one] = value.astype(HALF_FLOAT)

    def final(self, step, pick_step):
        place = self.place
        steps, width = self.total.shape[0], self.gathered.shape[1]
        source = slab(self.total, 1, place.member_at(step), width)
        target = slab(self.gathered, 0, place.member_at(pick_step), steps)
        if step == 0:
            return pltpu.make_async_copy(source, target, self.local.at[1])
        return send_copy(
            source,
            target,
            self.sf.at[step],
            self.rf.at[step],
            place.device(place.group, place.member_at(step), place.core),
        )

    def start_final(self):
        for step in range(self.place.members):
            self.final(step, 0).start()

    def finish(self):
        place = self.place
        self.final(0, 0).wait()
        for step in range(1, place.members):
            self.final(step, -step).wait_recv()
        self.out[...] = self.gathered[...].astype(FLOAT)
        for step in range(1, place.members):
            self.final(step, 0).wait_send()
        for step, turn in self.hops():
            if step or turn:
                self.partial(step, turn, lambda copy, local: copy.wait_send())


class MatrixSum:
    sems = 7

    @staticmethod
    def half_shape(place_sizes, kind, value):
        batches = place_sizes[2]
        shape = list(value.shape)
        if kind == "rows":
            shape[0] //= batches
        elif kind == "lanes":
            shape[-1] //= batches
        return tuple(shape)

    @staticmethod
    def piece_shape(place_sizes, kind, value):
        groups, members, batches = place_sizes
        shape = list(MatrixSum.half_shape(place_sizes, kind, value))
        dim = {"rows": 1, "lanes": len(shape) - 2, "whole": 0}[kind]
        shape[dim] //= groups * members
        return tuple(shape)

    @staticmethod
    def scratch(place_sizes, kind, value):
        groups, members, batches = place_sizes
        half = MatrixSum.half_shape(place_sizes, kind, value)
        piece = MatrixSum.piece_shape(place_sizes, kind, value)
        dma = pltpu.SemaphoreType.DMA
        return [
            pltpu.VMEM(half, value.dtype),
            pltpu.VMEM((batches,) + half, value.dtype),
            pltpu.VMEM((members, groups) + piece, value.dtype),
            pltpu.VMEM((groups,) + piece, value.dtype),
            pltpu.VMEM((groups,) + piece, value.dtype),
            dma((batches,)),
            dma((batches,)),
            dma((members * groups,)),
            dma((members * groups,)),
            dma((groups,)),
            dma((groups,)),
            dma((1 + groups,)),
        ]

    def __init__(self, place, kind, source, out, scratch):
        self.place, self.kind, self.source, self.out = place, kind, source, out
        (self.own, self.others, self.by_member, self.sums, self.by_group) = scratch[:5]
        (self.sb, self.rb, self.sm, self.rm, self.sg, self.rg, self.local) = scratch[5:]
        self.piece_dim = {"rows": 1, "lanes": len(self.own.shape) - 2, "whole": 0}[kind]

    def half(self, core):
        if self.kind == "rows":
            return slab(self.source, 0, core, self.own.shape[0])
        if self.kind == "lanes":
            return slab(self.source, len(self.own.shape) - 1, core, self.own.shape[-1])
        return self.source

    def cores(self, step, pick):
        place = self.place
        core = place.core_at(step)
        return send_copy(
            self.half(core),
            self.others.at[pick],
            self.sb.at[step],
            self.rb.at[step],
            place.device(place.group, place.member, core),
        )

    def load(self):
        return pltpu.make_async_copy(self.half(self.place.core), self.own, self.local.at[0])

    def start(self):
        self.load().start()
        for step in range(1, self.place.batches):
            self.cores(step, self.place.core).start()

    def piece(self, group, member):
        size = self.by_member.shape[2 + self.piece_dim]
        return slab(self.own, self.piece_dim, group * self.place.members + member, size)

    def members(self, step, pick_step, group):
        place = self.place
        member = place.member_at(step)
        slot = step * place.groups + group
        target = self.by_member.at[place.member_at(pick_step), group]
        if step == 0:
            return pltpu.make_async_copy(
                self.piece(group, member), target, self.local.at[1 + group]
            )
        return send_copy(
            self.piece(group, member),
            target,
            self.sm.at[slot],
            self.rm.at[slot],
            place.device(place.group, member, place.core),
        )

    def add_cores(self):
        place = self.place
        self.load().wait()
        for step in range(1, place.batches):
            self.cores(step, place.core_at(-step)).wait_recv()
        rows = self.own.shape[0]
        block = max(size for size in (1, 2, 4, 8, 16, 32, 64) if rows % size == 0)

        @pl.loop(0, rows // block)
        def _(index):
            pick = pl.ds(pl.multiple_of(index * block, block), block)
            value = self.own[pick].astype(FLOAT)
            for step in range(1, place.batches):
                value = value + self.others[place.core_at(step), pick].astype(FLOAT)
            self.own[pick] = value.astype(self.own.dtype)

        for step in range(place.members):
            for group in range(place.groups):
                self.members(step, 0, group).start()

    def groups(self, step, pick_step):
        place = self.place
        group = place.group_at(step)
        return send_copy(
            self.sums.at[group],
            self.by_group.at[place.group_at(pick_step)],
            self.sg.at[step],
            self.rg.at[step],
            place.device(group, place.member, place.core),
        )

    def add_members(self):
        place = self.place
        for step in range(place.members):
            for group in range(place.groups):
                if step == 0:
                    self.members(step, 0, group).wait()
                else:
                    self.members(step, -step, group).wait_recv()

        @pl.loop(0, place.groups)
        def _(group):
            value = self.by_member[0, group].astype(FLOAT)
            for other in range(1, place.members):
                value = value + self.by_member[other, group].astype(FLOAT)
            self.sums[group] = value.astype(self.sums.dtype)

        for step in range(1, place.groups):
            self.groups(step, 0).start()
        self.by_group[place.group] = self.sums[place.group]

    def finish(self):
        place = self.place
        for step in range(1, place.groups):
            self.groups(step, -step).wait_recv()
        value = self.by_group[0].astype(FLOAT)
        for other in range(1, place.groups):
            value = value + self.by_group[other].astype(FLOAT)
        self.out[...] = value
        for step in range(1, place.groups):
            self.groups(step, 0).wait_send()
        for step in range(1, place.members):
            for group in range(place.groups):
                self.members(step, 0, group).wait_send()
        for step in range(1, place.batches):
            self.cores(step, place.core).wait_send()


def remote_call(body, inputs, outputs, scratch, collective_id, flops, nbytes, name):
    def kernel(*refs):
        left = list(refs)
        named = {key: left.pop(0) for key in inputs}
        named.update({key: left.pop(0) for key in outputs})
        for key, shapes in scratch.items():
            named[key] = [left.pop(0) for _ in shapes]
        body(named)

    results = pl.pallas_call(
        kernel,
        out_shape=tuple(shape for shape, _ in outputs.values()),
        in_specs=[spec for _, spec in inputs.values()],
        out_specs=tuple(spec for _, spec in outputs.values()),
        scratch_shapes=[shape for shapes in scratch.values() for shape in shapes],
        compiler_params=pltpu.CompilerParams(
            collective_id=collective_id,
            has_side_effects=True,
            vmem_limit_bytes=63 * 1024 * 1024,
        ),
        cost_estimate=pl.CostEstimate(flops=flops, bytes_accessed=nbytes, transcendentals=0),
        name=name,
    )(*[value for value, _ in inputs.values()])
    return dict(zip(outputs, results))


def plane_sizes(channels):
    devices, batches = lax.axis_size("tm"), lax.axis_size("batch")
    groups = channels // 128
    if batches == 2 and channels % 256 == 0 and devices % groups == 0:
        return groups, devices // groups, batches
    return None


def pad_rows(value, dim):
    extra = -value.shape[dim] % 16
    return jnp.pad(value, [(0, extra if i == dim else 0) for i in range(value.ndim)])


VMEM_SPEC = pl.BlockSpec(memory_space=pltpu.VMEM)
HBM_SPEC = pl.BlockSpec(memory_space=pl.ANY)


def down_gradients(sizes, wides, narrows, vectors):
    groups, members, batches = sizes
    half = wides[0].shape[3]
    channels = half * batches
    inputs, outputs, scratch = {}, {}, {}
    for index, (wide, narrow) in enumerate(zip(wides, narrows)):
        steps = wide.shape[0] * members
        shape = jax.ShapeDtypeStruct((steps, wide.shape[2], channels), HALF_FLOAT)
        inputs[f"wide{index}"] = (wide, VMEM_SPEC)
        inputs[f"narrow{index}"] = (narrow, HBM_SPEC)
        outputs[f"out{index}"] = (
            jax.ShapeDtypeStruct((steps, channels // (groups * members), half), FLOAT),
            VMEM_SPEC,
        )
        scratch[f"rows{index}"] = [
            pltpu.VMEM((members * batches,) + narrow.shape, HALF_FLOAT)
        ]
        scratch[f"gather{index}"] = NarrowGather.scratch(sizes, narrow)
        scratch[f"product{index}"] = KernelProduct.scratch(sizes, "down", shape, narrow)
    inputs["vectors"] = (vectors, HBM_SPEC)
    outputs["vector_sum"] = (jax.ShapeDtypeStruct((1,) + vectors.shape[1:], FLOAT), VMEM_SPEC)
    scratch["vector"] = MatrixSum.scratch(sizes, "whole", vectors)

    def body(refs):
        place = Place(*sizes)
        barrier = pltpu.get_barrier_semaphore()
        pl.semaphore_wait(barrier, place.greet(barrier))
        gathers, products = [], []
        for index in range(len(wides)):
            gathers.append(
                NarrowGather(
                    place,
                    refs[f"narrow{index}"],
                    refs[f"rows{index}"][0],
                    refs[f"gather{index}"],
                )
            )
            products.append(
                KernelProduct(
                    place,
                    "down",
                    refs[f"wide{index}"],
                    refs[f"rows{index}"][0],
                    refs[f"out{index}"],
                    refs[f"product{index}"],
                )
            )
        total = MatrixSum(place, "whole", refs["vectors"], refs["vector_sum"], refs["vector"])
        for gather in gathers:
            gather.start()
        total.start()
        for gather in gathers:
            gather.forward()
        for gather, product in zip(gathers, products):
            gather.wait()
            product.multiply()
            product.start_partials()
        total.add_cores()
        total.add_members()
        for product in products:
            product.sum_partials()
            product.start_final()
        total.finish()
        for product in products:
            product.finish()
        for gather in gathers:
            gather.drain()

    flops = sum(2 * wide.size * channels for wide in wides)
    results = remote_call(
        body, inputs, outputs, scratch, 2, flops, 8 * flops // channels, "down_gradients"
    )
    return [results["out0"], results["out1"]], results["vector_sum"]


def iso_gradient_kernel(spec_ref, specs_ref, grad_ref, grads_ref, out_ref):
    devices = spec_ref.shape[0] // 2
    spec, grad, turned = [], [], []
    for own, others, into in ((spec_ref, specs_ref, spec), (grad_ref, grads_ref, grad)):
        into.append(own[...])
        for index in range(others.shape[0]):
            into.append(others[index])
    for value in grad:
        turned.append(jnp.concatenate([value[devices:], -value[:devices]]))
    spec = jnp.concatenate(spec)
    for part, values in enumerate((grad, turned)):
        out_ref[0, part] = lax.dot_general(
            spec,
            jnp.concatenate(values),
            (((0,), (0,)), ((), ())),
            preferred_element_type=FLOAT,
        )


def iso_gradients(spec, specs, grad, grads, first, bins):
    rows, channels = 2 * lax.axis_size("tm"), grad.shape[1]
    half = spec.shape[1]
    others = specs.shape[0]
    return pl.pallas_call(
        iso_gradient_kernel,
        out_shape=jax.ShapeDtypeStruct((bins, 2, half, channels), FLOAT),
        grid=(bins,),
        in_specs=[
            pl.BlockSpec((rows, half), lambda i: (first + i, 0)),
            pl.BlockSpec((others, rows, half), lambda i: (0, first + i, 0)),
            pl.BlockSpec((rows, channels), lambda i: (first + i, 0)),
            pl.BlockSpec((others, rows, channels), lambda i: (0, first + i, 0)),
        ],
        out_specs=pl.BlockSpec((1, 2, half, channels), lambda i: (i, 0, 0, 0)),
        cost_estimate=pl.CostEstimate(
            flops=4 * bins * rows * (1 + others) * half * channels,
            bytes_accessed=8 * bins * half * channels,
            transcendentals=0,
        ),
        name="iso_gradients",
    )(spec, specs, grad, grads)


class Extra:
    def __init__(self, sizes):
        self.sizes = sizes
        self.inputs, self.outputs, self.scratch = {}, {}, {}

    def bind(self, refs):
        self.refs = refs
        self.place = Place(*self.sizes) if self.sizes else None

    def greet(self, barrier):
        return self.place.greet(barrier) if self.sizes else 0

    def start(self):
        pass

    def after_bins(self):
        pass

    def after_spec(self):
        pass

    def after_signal(self):
        pass

    def finish(self):
        pass


class ForwardExtra(Extra):
    def __init__(self, sizes, wides):
        super().__init__(sizes)
        self.count = len(wides) if sizes else 0
        for index in range(self.count):
            self.inputs[f"wide{index}"] = (wides[index], HBM_SPEC)
            self.outputs[f"gathered{index}"] = (
                jax.ShapeDtypeStruct(WideExchange.shape(sizes, wides[index]), HALF_FLOAT),
                HBM_SPEC,
            )
            self.scratch[f"exchange{index}"] = WideExchange.scratch(sizes, wides[index])

    def bind(self, refs):
        super().bind(refs)
        self.exchanges = [
            WideExchange(
                self.place, refs[f"wide{i}"], refs[f"gathered{i}"], refs[f"exchange{i}"]
            )
            for i in range(self.count)
        ]

    def start(self):
        for item in self.exchanges:
            item.start()

    def finish(self):
        for item in self.exchanges:
            item.wait()
            item.drain()


class BackwardExtra(Extra):
    def __init__(self, sizes, spec, wides, narrows, matrices):
        super().__init__(sizes)
        self.batches = lax.axis_size("batch")
        others = jax.ShapeDtypeStruct((self.batches - 1,) + spec.shape, HALF_FLOAT)
        self.inputs["spec_forward"] = (spec, HBM_SPEC)
        self.outputs["specs"] = (others, HBM_SPEC)
        self.outputs["grads"] = (others, HBM_SPEC)
        dma = pltpu.SemaphoreType.DMA
        self.scratch["other_sems"] = [dma((self.batches,))] * 4
        self.count = len(wides) if sizes else 0
        self.kinds = [kind for kind, _ in matrices] if sizes else []
        for i in range(self.count):
            wide, narrow = wides[i], narrows[i]
            groups, members, batches = sizes
            channels = narrow.shape[1]
            self.inputs[f"wide{i}"] = (wide, HBM_SPEC)
            self.inputs[f"narrow{i}"] = (narrow, HBM_SPEC)
            self.outputs[f"up{i}"] = (
                jax.ShapeDtypeStruct(
                    (wide.shape[0], channels // (groups * members), channels // batches), FLOAT
                ),
                VMEM_SPEC,
            )
            self.scratch[f"wide_in{i}"] = [
                pltpu.VMEM(WideExchange.shape(sizes, wide), HALF_FLOAT)
            ]
            self.scratch[f"rows{i}"] = [
                pltpu.VMEM((members * batches,) + narrow.shape, HALF_FLOAT)
            ]
            self.scratch[f"exchange{i}"] = WideExchange.scratch(sizes, wide)
            self.scratch[f"gather{i}"] = NarrowGather.scratch(sizes, narrow)
            self.scratch[f"product{i}"] = KernelProduct.scratch(sizes, "up", wide, narrow)
        for i, kind in enumerate(self.kinds):
            value = matrices[i][1]
            self.inputs[f"matrix{i}"] = (value, HBM_SPEC)
            self.outputs[f"matrix_sum{i}"] = (
                jax.ShapeDtypeStruct(MatrixSum.piece_shape(sizes, kind, value), FLOAT),
                VMEM_SPEC,
            )
            self.scratch[f"sum{i}"] = MatrixSum.scratch(sizes, kind, value)

    def bind(self, refs):
        super().bind(refs)
        self.exchanges, self.gathers, self.products = [], [], []
        for i in range(self.count):
            wide_in, rows = refs[f"wide_in{i}"][0], refs[f"rows{i}"][0]
            self.exchanges.append(
                WideExchange(self.place, refs[f"wide{i}"], wide_in, refs[f"exchange{i}"])
            )
            self.gathers.append(
                NarrowGather(self.place, refs[f"narrow{i}"], rows, refs[f"gather{i}"])
            )
            self.products.append(
                KernelProduct(self.place, "up", wide_in, rows, refs[f"up{i}"], refs[f"product{i}"])
            )
        self.sums = [
            MatrixSum(
                self.place, kind, refs[f"matrix{i}"], refs[f"matrix_sum{i}"], refs[f"sum{i}"]
            )
            for i, kind in enumerate(self.kinds)
        ]

    def other(self, index, turn):
        source, target = (
            (self.refs["spec_forward"], self.refs["specs"]),
            (self.refs["spec"], self.refs["grads"]),
        )[index]
        sems = self.refs["other_sems"]
        core = lax.rem(lax.axis_index("batch") + turn, self.batches)
        return send_copy(
            source,
            target.at[turn - 1],
            sems[2 * index].at[turn],
            sems[2 * index + 1].at[turn],
            (core, lax.axis_index("tm")),
        )

    def start(self):
        for turn in range(1, self.batches):
            self.other(0, turn).start()
        for item in self.gathers + self.exchanges + self.sums:
            item.start()

    def after_bins(self):
        for item in self.gathers:
            item.forward()

    def after_spec(self):
        for turn in range(1, self.batches):
            self.other(1, turn).start()

    def after_signal(self):
        for exchange, gather, product in zip(self.exchanges, self.gathers, self.products):
            exchange.wait()
            gather.wait()
            product.multiply()
            product.start_partials()
        for item in self.sums:
            item.add_cores()

    def finish(self):
        for item in self.sums:
            item.add_members()
        for item in self.products:
            item.sum_partials()
            item.start_final()
        for item in self.sums + self.products:
            item.finish()
        for item in self.exchanges + self.gathers:
            item.drain()
        for index in range(2):
            for turn in range(1, self.batches):
                self.other(index, turn).wait()


def spectral(values, weights, back, extra):
    devices, batches = lax.axis_size("tm"), lax.axis_size("batch")
    pieces_list = tuple(value.shape[1] for value in values)
    count, _, channels = values[0].shape
    wide = [round_up(pieces, 8) for pieces in pieces_list]
    per_time, per_bin = sum(wide), 2 * sum(wide)
    assert count <= devices and per_time % 16 == 0
    packed = jnp.concatenate(
        [
            jnp.pad(value, ((0, 0), (0, room - value.shape[1]), (0, 0)))
            for value, room in zip(values, wide)
        ],
        axis=1,
    ).reshape(count * per_time, channels)
    constants = spectral_constants(devices, pieces_list)
    rows_time, rows_bin = devices * per_time, devices * per_bin
    dma = pltpu.SemaphoreType.DMA
    inputs = {"x": (packed, HBM_SPEC)}
    for index, weight in enumerate(weights):
        inputs[f"weight{index}"] = (weight, HBM_SPEC)
    for key, value in zip(("table", "inverse", "move", "unmove"), constants):
        inputs[key] = (value, VMEM_SPEC)
    outputs = {
        "spec": (jax.ShapeDtypeStruct((rows_bin, channels), HALF_FLOAT), VMEM_SPEC),
        "signal": (jax.ShapeDtypeStruct((count * per_time, channels), FLOAT), VMEM_SPEC),
    }
    scratch = {
        "buffers": [pltpu.VMEM((rows_time, channels), HALF_FLOAT)]
        + [pltpu.VMEM((rows_bin, channels), HALF_FLOAT)] * 5
        + [pltpu.VMEM((rows_time, channels), FLOAT)]
        + [
            pltpu.VMEM((weight.shape[0], 2, weight.shape[2] * batches, channels), HALF_FLOAT)
            for weight in weights
        ],
        "sems": [dma((devices,))] * 8 + [dma((2, batches)), dma((2, batches)), dma((3,))],
    }
    inputs.update(extra.inputs)
    outputs.update(extra.outputs)
    scratch.update(extra.scratch)
    sizes = (devices, batches, count, pieces_list)

    def body(refs):
        extra.bind(refs)
        spectral_body(sizes, back, refs, extra)

    results = remote_call(
        body,
        inputs,
        outputs,
        scratch,
        1 if back else 0,
        2 * rows_bin * channels * channels * 4,
        4 * channels * channels * sum(pieces_list),
        "spectral_back" if back else "spectral_forward",
    )
    signal = results["signal"].reshape(count, per_time, channels)
    signals, offset = [], 0
    for pieces, room in zip(pieces_list, wide):
        signals.append(signal[:, offset : offset + pieces])
        offset += room
    return results, signals


def extend_series(series_in, rim_width):
    padded = extended_2(series_in, (("tm", 1),), rim_width)
    position = lax.axis_index("tm")
    final_index = lax.axis_size("tm") - 1
    step_count = series_in.shape[1]
    left_rim = jnp.where(
        position == 0,
        jnp.broadcast_to(series_in[:, :1], padded[:, :rim_width].shape),
        padded[:, :rim_width],
    )
    right_rim = jnp.where(
        position == final_index,
        jnp.broadcast_to(series_in[:, -1:], padded[:, rim_width + step_count :].shape),
        padded[:, rim_width + step_count :],
    )
    return jnp.concatenate([left_rim, series_in, right_rim], axis=1)


def band(step_count, rim_width, half_window):
    row = np.arange(step_count)[:, None] + rim_width
    column = np.arange(step_count + 2 * rim_width)[None, :]
    return (np.abs(row - column) <= half_window).astype(HALF_FLOAT)


def seasonal_part(extended, series_in, half_window, rim_width):
    step_count = series_in.shape[1]
    matrix = jnp.asarray(band(step_count, rim_width, half_window))
    running = jnp.einsum("qr,brd->bqd", matrix, extended, preferred_element_type=FLOAT)
    return (series_in.astype(FLOAT) - running / (2 * half_window + 1)).astype(HALF_FLOAT)


def mean_back(grad, half_window, rim_width, is_first, is_final):
    step_count = grad.shape[1]
    matrix = jnp.asarray(band(step_count, rim_width, half_window))
    high = grad.astype(HALF_FLOAT)
    low = (grad - high.astype(FLOAT)).astype(HALF_FLOAT)
    wide = jnp.einsum("qr,bqd->brd", matrix, high, preferred_element_type=FLOAT) + jnp.einsum(
        "qr,bqd->brd", matrix, low, preferred_element_type=FLOAT
    )
    return wide / (2 * half_window + 1)


def branch_down(seasonal_low, down_weight, bias_row):
    series_count, step_count, channels = seasonal_low.shape
    kernel = down_weight.shape[0]
    pieces = step_count // kernel
    blocks = seasonal_low.reshape(series_count * pieces, kernel * channels)
    down_act = jnp.tanh(
        jnp.dot(
            blocks, down_weight.reshape(kernel * channels, channels), preferred_element_type=FLOAT
        )
        + bias_row
    )
    return down_act.reshape(series_count, pieces, channels)


def branch_up(seasonal_low, down_act, iso_out, up_weight, bias_rows, gain_row, bias_row):
    series_count, step_count, channels = seasonal_low.shape
    kernel = up_weight.shape[1]
    pieces = step_count // kernel
    iso_act = jnp.tanh(iso_out + bias_rows[0])
    inner_in = iso_act + down_act.astype(HALF_FLOAT).astype(FLOAT)
    inner_low = layer_norm(inner_in, gain_row, bias_row).astype(HALF_FLOAT)
    up_pre = jnp.dot(
        inner_low.reshape(series_count * pieces, channels),
        up_weight.reshape(channels, kernel * channels),
        preferred_element_type=FLOAT,
    )
    up_act = jnp.tanh(up_pre.reshape(series_count, step_count, channels) + bias_rows[1])
    outer_in = up_act + seasonal_low.astype(FLOAT)
    branch_out = layer_norm(outer_in, gain_row, bias_row)
    return branch_out, (iso_act, inner_in, inner_low, up_act, outer_in)


def branch_up_back(grad_out, up_weight, gain_row, bias_row, kept):
    iso_act, inner_in, inner_low, up_act, outer_in = kept
    series_count, step_count, channels = grad_out.shape
    kernel = up_weight.shape[1]
    pieces = step_count // kernel
    normed_out, outer_pull = jax.vjp(layer_norm, outer_in, gain_row, bias_row)
    grad_outer, gain_outer, shift_outer = outer_pull(grad_out)
    grad_up = (grad_outer * (1.0 - up_act * up_act)).astype(HALF_FLOAT)
    up_rows = grad_up.reshape(series_count * pieces, kernel * channels)
    inner_rows = inner_low.reshape(series_count * pieces, channels)
    up_flat = up_weight.reshape(channels, kernel * channels)
    grad_up_weight = ("up", up_rows.reshape(-1, kernel, channels), inner_rows)
    grad_up_bias = jnp.sum(grad_up.astype(FLOAT), axis=(0, 1))
    grad_inner = jnp.einsum("nk,dk->nd", up_rows, up_flat, preferred_element_type=FLOAT).reshape(
        series_count, pieces, channels
    )
    normed_inner, inner_pull = jax.vjp(layer_norm, inner_in, gain_row, bias_row)
    grad_inner_in, gain_inner, shift_inner = inner_pull(grad_inner)
    grad_iso = grad_inner_in * (1.0 - iso_act * iso_act)
    grad_iso_bias = jnp.sum(grad_iso, axis=(0, 1))
    return (
        grad_iso.astype(HALF_FLOAT),
        grad_inner_in,
        grad_outer,
        (
            grad_up_weight,
            grad_iso_bias,
            grad_up_bias,
            gain_outer + gain_inner,
            shift_outer + shift_inner,
        ),
    )


def branch_down_back(grad_signal, grad_inner_in, grad_outer, seasonal_low, down_act, down_weight):
    series_count, step_count, channels = seasonal_low.shape
    kernel = down_weight.shape[0]
    pieces = step_count // kernel
    grad_down = grad_signal + grad_inner_in
    grad_down_pre = (grad_down * (1.0 - down_act * down_act)).astype(HALF_FLOAT)
    down_rows = grad_down_pre.reshape(series_count * pieces, channels)
    down_flat = down_weight.reshape(kernel * channels, channels)
    grad_down_weight = ("down", seasonal_low.reshape(-1, kernel, channels), down_rows)
    grad_down_bias = jnp.sum(grad_down_pre.astype(FLOAT), axis=(0, 1))
    grad_seasonal = (
        jnp.einsum("nd,kd->nk", down_rows, down_flat, preferred_element_type=FLOAT).reshape(
            series_count, step_count, channels
        )
        + grad_outer
    )
    return grad_seasonal, grad_down_weight, grad_down_bias


def batch_split(values, split, join):
    return lax.all_to_all(values, "batch", split_axis=split, concat_axis=join, tiled=True)


def time_sum(values, dim):
    return lax.psum_scatter(
        values.astype(HALF_FLOAT), "tm", scatter_dimension=dim, tiled=True
    ).astype(FLOAT)


def kernel_steps(seasonal, kernel):
    rows = seasonal.reshape(-1, kernel, seasonal.shape[2])
    return pad_rows(jnp.transpose(rows, (1, 0, 2)), 1)


def plain_gradients(wides, narrows, downs):
    results = []
    for wide, narrow, down in zip(wides, narrows, downs):
        if down:
            wide, narrow = batch_split(wide, 2, 1), lax.all_gather(narrow, "batch", tiled=True)
            value = jnp.einsum("knc,nd->kcd", wide, narrow, preferred_element_type=FLOAT)
        else:
            wide = lax.all_gather(wide, "batch", axis=1, tiled=True)
            narrow = batch_split(narrow, 1, 0)
            value = jnp.einsum("nd,knc->dkc", narrow, wide, preferred_element_type=FLOAT)
        results.append(time_sum(value, 2))
    return results


def plain_sums(matrices):
    results = []
    for kind, value in matrices:
        batch_dim, time_dim = (0, 1) if kind == "rows" else (value.ndim - 1, value.ndim - 2)
        value = lax.psum_scatter(
            value.astype(FLOAT), "batch", scatter_dimension=batch_dim, tiled=True
        )
        results.append(time_sum(value, time_dim))
    return results


def per_device(
    series_in,
    out_cotangent,
    out_mask,
    down_twelve,
    down_sixteen,
    iso_twelve,
    iso_sixteen,
    up_twelve,
    up_sixteen,
    branch_bias,
    merge_weight,
    hidden_weight,
    hidden_bias,
    output_weight,
    head_bias,
    norm_gain,
    norm_shift,
):
    series_dev, step_count, channels = series_in.shape
    row_count = series_dev * step_count
    half_one = down_twelve.shape[0] // 2
    half_two = down_sixteen.shape[0] // 2
    rim_width = max(half_one, half_two)
    biases = branch_bias.astype(FLOAT)
    gains = norm_gain.astype(FLOAT)
    shifts = norm_shift.astype(FLOAT)
    heads = head_bias.astype(FLOAT)
    extended = extend_series(series_in, rim_width)
    seasonal_one = seasonal_part(extended, series_in, half_one, rim_width)
    seasonal_two = seasonal_part(extended, series_in, half_two, rim_width)
    down_one = branch_down(seasonal_one, down_twelve, biases[0])
    down_two = branch_down(seasonal_two, down_sixteen, biases[1])
    iso_weights = (iso_twelve, iso_sixteen)
    sizes = plane_sizes(channels)
    seasonal_steps = (
        kernel_steps(seasonal_one, down_twelve.shape[0]),
        kernel_steps(seasonal_two, down_sixteen.shape[0]),
    )
    forward, iso_outs = spectral(
        (down_one.astype(HALF_FLOAT), down_two.astype(HALF_FLOAT)),
        iso_weights,
        False,
        ForwardExtra(sizes, seasonal_steps),
    )
    out_one, kept_one = branch_up(
        seasonal_one,
        down_one,
        iso_outs[0],
        up_twelve,
        (biases[2], biases[4]),
        gains[0],
        shifts[0],
    )
    out_two, kept_two = branch_up(
        seasonal_two,
        down_two,
        iso_outs[1],
        up_sixteen,
        (biases[3], biases[5]),
        gains[0],
        shifts[0],
    )
    branch_low = jnp.concatenate(
        [out_one.astype(HALF_FLOAT), out_two.astype(HALF_FLOAT)], axis=2
    ).reshape(row_count, 2 * channels)
    merge_flat = merge_weight.reshape(2 * channels, channels)
    merged = jnp.dot(branch_low, merge_flat, preferred_element_type=FLOAT) + heads[0]
    first_low = layer_norm(merged, gains[1], shifts[1]).astype(HALF_FLOAT)
    hidden_pre = jnp.dot(
        first_low, hidden_weight, preferred_element_type=FLOAT
    ) + hidden_bias.astype(FLOAT)
    hidden_low = jax.nn.gelu(hidden_pre).astype(HALF_FLOAT)
    final_in = merged + (
        jnp.dot(hidden_low, output_weight, preferred_element_type=FLOAT) + heads[1]
    )
    mask_rows = out_mask.astype(FLOAT).reshape(row_count, 1)
    result = (
        (layer_norm(final_in, gains[2], shifts[2]) * mask_rows)
        .astype(HALF_FLOAT)
        .reshape(series_dev, step_count, channels)
    )
    grad_result = out_cotangent.astype(FLOAT).reshape(row_count, channels) * mask_rows
    normed_final, final_pull = jax.vjp(layer_norm, final_in, gains[2], shifts[2])
    grad_final, gain_final, shift_final = final_pull(grad_result)
    grad_feed = grad_final.astype(HALF_FLOAT)
    grad_output_weight = jnp.einsum(
        "nd,nf->df", grad_feed, hidden_low, preferred_element_type=FLOAT
    ).astype(HALF_FLOAT)
    grad_output_bias = jnp.sum(grad_feed.astype(FLOAT), axis=0)
    grad_hidden_low = jnp.einsum(
        "nd,fd->nf", grad_feed, output_weight, preferred_element_type=FLOAT
    )
    gelu_value, gelu_pull = jax.vjp(jax.nn.gelu, hidden_pre)
    grad_hidden_pre = gelu_pull(grad_hidden_low)[0].astype(HALF_FLOAT)
    grad_hidden_weight = jnp.einsum(
        "nd,nf->df", first_low, grad_hidden_pre, preferred_element_type=FLOAT
    ).astype(HALF_FLOAT)
    grad_hidden_bias = jnp.sum(grad_hidden_pre.astype(FLOAT), axis=0)
    grad_first = jnp.einsum(
        "nf,df->nd", grad_hidden_pre, hidden_weight, preferred_element_type=FLOAT
    )
    normed_first, first_pull = jax.vjp(layer_norm, merged, gains[1], shifts[1])
    grad_merged_norm, gain_first, shift_first = first_pull(grad_first)
    grad_merged = (grad_final + grad_merged_norm).astype(HALF_FLOAT)
    grad_merge_bias = jnp.sum(grad_merged.astype(FLOAT), axis=0)
    grad_merge_weight = jnp.einsum(
        "ne,nkd->ked",
        grad_merged,
        branch_low.reshape(row_count, 2, channels),
        preferred_element_type=FLOAT,
    ).astype(HALF_FLOAT)
    grad_branch = jnp.einsum("nd,kd->nk", grad_merged, merge_flat, preferred_element_type=FLOAT)
    grad_out_one = grad_branch[:, :channels].reshape(series_dev, step_count, channels)
    grad_out_two = grad_branch[:, channels:].reshape(series_dev, step_count, channels)
    iso_one, inner_one, outer_one, terms_one = branch_up_back(
        grad_out_one, up_twelve, gains[0], shifts[0], kept_one
    )
    iso_two, inner_two, outer_two, terms_two = branch_up_back(
        grad_out_two, up_sixteen, gains[0], shifts[0], kept_two
    )
    matrices = (
        ("rows", grad_hidden_weight),
        ("lanes", grad_output_weight),
        ("lanes", grad_merge_weight),
    )
    up_wides = (
        pad_rows(jnp.transpose(terms_one[0][1], (1, 0, 2)), 1),
        pad_rows(jnp.transpose(terms_two[0][1], (1, 0, 2)), 1),
    )
    up_narrows = (pad_rows(terms_one[0][2], 0), pad_rows(terms_two[0][2], 0))
    backward, grad_signals = spectral(
        (iso_one, iso_two),
        iso_weights,
        True,
        BackwardExtra(sizes, forward["spec"], up_wides, up_narrows, matrices),
    )
    half = channels // lax.axis_size("batch")
    core = lax.axis_index("batch")
    spec_half = lax.dynamic_slice_in_dim(forward["spec"], core * half, half, axis=1)
    specs_half = lax.dynamic_slice_in_dim(backward["specs"], core * half, half, axis=2)
    iso_parts, first = [], 0
    for value in (iso_one, iso_two):
        bins = value.shape[1]
        iso_parts.append(
            iso_gradients(
                spec_half, specs_half, backward["spec"], backward["grads"], first, bins
            )
        )
        first += round_up(bins, 8)
    grad_seasonal_one, grad_down_one, down_bias_one = branch_down_back(
        grad_signals[0], inner_one, outer_one, seasonal_one, down_one, down_twelve
    )
    grad_seasonal_two, grad_down_two, down_bias_two = branch_down_back(
        grad_signals[1], inner_two, outer_two, seasonal_two, down_two, down_sixteen
    )
    position = lax.axis_index("tm")
    final_index = lax.axis_size("tm") - 1
    wide = mean_back(grad_seasonal_one, half_one, rim_width, None, None) + mean_back(
        grad_seasonal_two, half_two, rim_width, None, None
    )
    low_rim = wide[:, :rim_width]
    high_rim = wide[:, rim_width + step_count :]
    onward = [(i, i + 1) for i in range(final_index)]
    from_low = lax.ppermute(high_rim, "tm", onward)
    from_high = lax.ppermute(low_rim, "tm", [(j, i) for i, j in onward])
    edge_low = jnp.where(
        position == 0,
        jnp.pad(jnp.sum(low_rim, axis=1, keepdims=True), ((0, 0), (0, rim_width - 1), (0, 0))),
        from_low,
    )
    edge_high = jnp.where(
        position == final_index,
        jnp.pad(jnp.sum(high_rim, axis=1, keepdims=True), ((0, 0), (rim_width - 1, 0), (0, 0))),
        from_high,
    )
    mean_total = wide[:, rim_width : rim_width + step_count] + jnp.concatenate(
        [
            edge_low,
            jnp.zeros((series_dev, step_count - 2 * rim_width, channels), FLOAT),
            edge_high,
        ],
        axis=1,
    )
    grad_series = (grad_seasonal_one + grad_seasonal_two - mean_total).astype(HALF_FLOAT)
    vectors = jnp.stack(
        [
            down_bias_one,
            down_bias_two,
            terms_one[1],
            terms_two[1],
            terms_one[2],
            terms_two[2],
            terms_one[3] + terms_two[3],
            gain_first,
            gain_final,
            terms_one[4] + terms_two[4],
            shift_first,
            shift_final,
            grad_merge_bias,
            grad_output_bias,
        ]
    )
    devices = lax.axis_size("tm")
    vector_count = vectors.shape[0]
    packed = jnp.concatenate(
        [
            vectors.reshape(vector_count, devices, -1).transpose(1, 0, 2).reshape(devices, -1),
            grad_hidden_bias.reshape(devices, -1),
        ],
        axis=1,
    )
    width = channels // devices
    down_narrows = (pad_rows(grad_down_one[2], 0), pad_rows(grad_down_two[2], 0))
    if sizes:
        extent = packed.shape[1]
        packed = jnp.pad(packed, ((0, 0), (0, -extent % 1024))).reshape(devices, -1, 128)
        downs, packed = down_gradients(
            sizes, (forward["gathered0"], forward["gathered1"]), down_narrows, packed
        )
        packed = packed.reshape(-1)[:extent]
        downs = [jnp.transpose(value, (0, 2, 1)) for value in downs]
        ups = [jnp.transpose(backward[key], (2, 0, 1)) for key in ("up0", "up1")]
        sums = [backward[f"matrix_sum{i}"] for i in range(3)]
    else:
        packed = lax.psum(
            lax.psum_scatter(packed, "tm", scatter_dimension=0, tiled=True), "batch"
        )[0]
        downs = plain_gradients(seasonal_steps, down_narrows, (True, True))
        ups = plain_gradients(up_wides, up_narrows, (False, False))
        sums = plain_sums(matrices)
    rows = packed[: vector_count * width].reshape(vector_count, width)
    vector_parts = (
        rows[:6],
        packed[vector_count * width :],
        rows[12:14],
        rows[6:9],
        rows[9:12],
    )
    return (
        result,
        grad_series,
        downs[0],
        downs[1],
        iso_parts[0],
        iso_parts[1],
        ups[0],
        ups[1],
        vector_parts[0],
        jnp.swapaxes(sums[2], 1, 2),
        sums[0],
        vector_parts[1],
        sums[1].T,
        vector_parts[2],
        vector_parts[3],
        vector_parts[4],
    )


def solution(mesh):
    placed = (
        P("batch", "tm", None),
        P("batch", "tm", None),
        P("batch", "tm"),
        P(),
        P(),
        P("tm", None, "batch", None),
        P("tm", None, "batch", None),
        P(),
        P(),
        P(),
        P(),
        P(),
        P(),
        P(),
        P(),
        P(),
        P(),
    )
    return jax.shard_map(
        per_device,
        mesh=mesh,
        in_specs=placed,
        out_specs=(
            P("batch", "tm", None),
            P("batch", "tm", None),
            P(None, "batch", "tm"),
            P(None, "batch", "tm"),
            P("tm", None, "batch", None),
            P("tm", None, "batch", None),
            P("batch", None, "tm"),
            P("batch", None, "tm"),
            P(None, "tm"),
            P(None, "batch", "tm"),
            P("batch", "tm"),
            P("tm"),
            P("batch", "tm"),
            P(None, "tm"),
            P(None, "tm"),
            P(None, "tm"),
        ),
        check_vma=False,
    )
```

```python
import functools
import math

import jax
import jax.numpy as jnp
import numpy as np
from jax import lax
from jax.experimental import pallas as pl
from jax.experimental.pallas import tpu as pltpu
from jax.sharding import PartitionSpec as P

FLOAT = jnp.float32
HALF_FLOAT = jnp.bfloat16
HIGHEST = lax.Precision.HIGHEST
EPSILON = 1e-05
MESH = pl.DeviceIdType.MESH


def layer_norm(values, gain_row, bias_row):
    center = values - jnp.mean(values, axis=-1, keepdims=True)
    spread = jnp.mean(center * center, axis=-1, keepdims=True)
    return center * lax.rsqrt(spread + EPSILON) * gain_row + bias_row


def round_up(value, multiple):
    return -(-value // multiple) * multiple


def spectral_constants(devices, pieces_list):
    padded = [round_up(pieces, 8) for pieces in pieces_list]
    per_time, per_bin = sum(padded), 2 * sum(padded)
    table = np.zeros((devices, per_bin, devices, per_time), np.float64)
    offset = 0
    for pieces, wide in zip(pieces_list, padded):
        length = devices * pieces
        index = np.arange(length)
        angle = (2.0 * math.pi / length) * (np.outer(index, index) % length)
        factor = 1.0 / math.sqrt(length)
        for part, values in enumerate((np.cos(angle) * factor, -np.sin(angle) * factor)):
            row = 2 * offset + part * wide
            table[:, row : row + pieces, :, offset : offset + pieces] = values.reshape(
                devices, pieces, devices, pieces
            )
        offset += wide
    table = table.reshape(devices * per_bin, devices * per_time).astype(np.float32)
    high = table.astype(HALF_FLOAT)
    low = (table - high.astype(np.float32)).astype(HALF_FLOAT)
    order = []
    offset = 0
    for wide in padded:
        for one_bin in range(wide):
            for part in range(2):
                for series in range(devices):
                    order.append(series * per_bin + 2 * offset + part * wide + one_bin)
        offset += wide
    move = np.zeros((devices * per_bin, devices * per_bin), np.float32)
    move[np.arange(len(order)), order] = 1.0
    move = move.astype(HALF_FLOAT)
    return (
        jnp.asarray(np.stack([high, low])),
        jnp.asarray(np.stack([high.T, low.T])),
        jnp.asarray(move),
        jnp.asarray(np.ascontiguousarray(move.T)),
    )


def dot_nn(left, right):
    return jnp.dot(left, right, preferred_element_type=FLOAT)


def dot_nt(left, right):
    return lax.dot_general(left, right, (((1,), (1,)), ((), ())), preferred_element_type=FLOAT)


def spectral_body(sizes, back, refs, extra):
    devices, batches, count, pieces_list = sizes
    x_ref, w1_ref, w2_ref = refs["x"], refs["weight0"], refs["weight1"]
    table_ref, inverse_ref = refs["table"], refs["inverse"]
    move_ref, unmove_ref = refs["move"], refs["unmove"]
    spec_ref, signal_ref = refs["spec"], refs["signal"]
    (one, two, three, mixed, spread, bins_out, four, w1, w2) = refs["buffers"]
    (s1, r1, s2, r2, s3, r3, s4, r4, ws, wr, own) = refs["sems"]
    me = lax.axis_index("tm")
    mine = lax.axis_index("batch")
    wide = [round_up(pieces, 8) for pieces in pieces_list]
    per_time, per_bin = sum(wide), 2 * sum(wide)
    weights = ((w1_ref, w1), (w2_ref, w2))

    barrier = pltpu.get_barrier_semaphore()

    @pl.loop(1, devices)
    def _(step):
        pl.semaphore_signal(
            barrier, inc=1, device_id=(mine, lax.rem(me + step, devices)), device_id_type=MESH
        )

    for step in range(1, batches):
        pl.semaphore_signal(
            barrier, inc=1, device_id=(lax.rem(mine + step, batches), me), device_id_type=MESH
        )
    pl.semaphore_wait(barrier, devices - 1 + batches - 1 + extra.greet(barrier))

    def exchange(source, target, send_sem, recv_sem, limit_out, limit_in, rows, start):
        def remote(there, here):
            return pltpu.make_async_remote_copy(
                src_ref=source.at[pl.ds(pl.multiple_of(there * rows, rows), rows)],
                dst_ref=target.at[pl.ds(pl.multiple_of(here * rows, rows), rows)],
                send_sem=send_sem.at[there],
                recv_sem=recv_sem.at[here],
                device_id=(mine, there),
                device_id_type=MESH,
            )

        if start:

            @pl.loop(1, devices)
            def _(step):
                there = lax.rem(me + step, devices)

                @pl.when(there < limit_out)
                def _():
                    remote(there, me).start()

        else:

            @pl.loop(1, devices)
            def _(step):
                there = lax.rem(me + step, devices)

                @pl.when(there < limit_in)
                def _():
                    pltpu.make_async_remote_copy(
                        src_ref=source.at[pl.ds(0, rows)],
                        dst_ref=target.at[pl.ds(pl.multiple_of(there * rows, rows), rows)],
                        send_sem=send_sem.at[there],
                        recv_sem=recv_sem.at[there],
                        device_id=(mine, there),
                        device_id_type=MESH,
                    ).wait_recv()

    def drain(source, target, send_sem, recv_sem, limit_out, rows):
        @pl.loop(1, devices)
        def _(step):
            there = lax.rem(me + step, devices)

            @pl.when(there < limit_out)
            def _():
                pltpu.make_async_remote_copy(
                    src_ref=source.at[pl.ds(0, rows)],
                    dst_ref=target.at[pl.ds(0, rows)],
                    send_sem=send_sem.at[there],
                    recv_sem=recv_sem.at[there],
                    device_id=(mine, there),
                    device_id_type=MESH,
                ).wait_send()

    owner = me < count
    exchange(x_ref, one, s1, r1, count, None, per_time, True)

    def weight_copies(index):
        source, target = weights[index]
        rows = source.shape[2]
        place = target.at[:, :, pl.ds(pl.multiple_of(mine * rows, rows), rows)]
        local = pltpu.make_async_copy(source, place, own.at[index])
        remote = []
        for step in range(1, batches):
            there = lax.rem(mine + step, batches)
            back_there = lax.rem(mine + batches - step, batches)
            other = target.at[:, :, pl.ds(pl.multiple_of(back_there * rows, rows), rows)]
            remote.append(
                [
                    pltpu.make_async_remote_copy(
                        src_ref=source,
                        dst_ref=where,
                        send_sem=ws.at[index, step],
                        recv_sem=wr.at[index, step],
                        device_id=(there, me),
                        device_id_type=MESH,
                    )
                    for where in (place, other)
                ]
            )
        return local, remote

    for index in range(2):
        local, remote = weight_copies(index)
        local.start()
        for copy, _unused in remote:
            copy.start()

    here = pltpu.make_async_copy(
        x_ref.at[pl.ds(pl.multiple_of(jnp.minimum(me, count - 1) * per_time, per_time), per_time)],
        one.at[pl.ds(pl.multiple_of(me * per_time, per_time), per_time)],
        own.at[2],
    )
    here.start()
    extra.start()
    if count < devices:
        two[pl.ds(count * per_bin, (devices - count) * per_bin)] = jnp.zeros(
            ((devices - count) * per_bin, two.shape[1]), two.dtype
        )
    here.wait()

    @pl.when(owner)
    def _():
        exchange(x_ref, one, s1, r1, None, devices, per_time, False)
        data = one[...]
        total = dot_nn(table_ref[0], data) + dot_nn(table_ref[1], data)
        bins_out[...] = total.astype(HALF_FLOAT)
        exchange(bins_out, two, s2, r2, devices, None, per_bin, True)
        place = pl.ds(pl.multiple_of(me * per_bin, per_bin), per_bin)
        two[place] = bins_out[place]

    extra.after_bins()
    exchange(bins_out, two, s2, r2, None, count, per_bin, False)
    spec_ref[...] = dot_nn(move_ref[...], two[...]).astype(HALF_FLOAT)
    extra.after_spec()
    base = 0
    for index in range(2):
        local, remote = weight_copies(index)
        local.wait()
        for copy, arrived in remote:
            copy.wait_send()
            arrived.wait_recv()
        target = weights[index][1]

        @pl.loop(0, pieces_list[index])
        def _(one_bin, base=base, target=target):
            place = pl.ds(
                pl.multiple_of(base + one_bin * 2 * devices, 2 * devices), 2 * devices
            )
            rows = spec_ref[place]
            if back:
                real = dot_nt(rows, target[one_bin, 0])
                imag = dot_nt(rows, target[one_bin, 1])
                out = jnp.concatenate(
                    [real[:devices] + imag[devices:], real[devices:] - imag[:devices]]
                )
            else:
                real = dot_nn(rows, target[one_bin, 0])
                imag = dot_nn(rows, target[one_bin, 1])
                out = jnp.concatenate(
                    [real[:devices] - imag[devices:], imag[:devices] + real[devices:]]
                )
            mixed[place] = out.astype(HALF_FLOAT)

        spare = wide[index] - pieces_list[index]
        if spare:
            mixed[
                pl.ds(base + pieces_list[index] * 2 * devices, spare * 2 * devices)
            ] = jnp.zeros((spare * 2 * devices, mixed.shape[1]), mixed.dtype)
        base += wide[index] * 2 * devices

    spread[...] = dot_nn(unmove_ref[...], mixed[...]).astype(HALF_FLOAT)
    exchange(spread, three, s3, r3, count, None, per_bin, True)
    extra.after_mixed()

    @pl.when(owner)
    def _():
        place = pl.ds(pl.multiple_of(me * per_bin, per_bin), per_bin)
        three[place] = spread[place]
        exchange(spread, three, s3, r3, None, devices, per_bin, False)
        data = three[...]
        total = dot_nn(inverse_ref[0], data) + dot_nn(inverse_ref[1], data)
        four[...] = total
        exchange(four, signal_ref, s4, r4, devices, None, per_time, True)
        place = pl.ds(pl.multiple_of(me * per_time, per_time), per_time)
        signal_ref[place] = four[place]

    extra.after_signal()
    exchange(four, signal_ref, s4, r4, None, count, per_time, False)
    drain(x_ref, one, s1, r1, count, per_time)
    drain(spread, three, s3, r3, count, per_bin)

    @pl.when(owner)
    def _():
        drain(bins_out, two, s2, r2, devices, per_bin)
        drain(four, signal_ref, s4, r4, devices, per_time)

    extra.finish()


class Place:
    def __init__(self, groups, members, batches):
        self.groups, self.members, self.batches = groups, members, batches
        self.me = lax.axis_index("tm")
        self.core = lax.axis_index("batch")
        self.group = lax.div(self.me, members)
        self.member = lax.rem(self.me, members)

    def device(self, group, member, core):
        return (core, group * self.members + member)

    def member_at(self, step):
        return lax.rem(self.member + step + self.members, self.members)

    def group_at(self, step):
        return lax.rem(self.group + step + self.groups, self.groups)

    def core_at(self, step):
        return lax.rem(self.core + step + self.batches, self.batches)

    def greet(self, barrier):
        greeted = 0
        for step in range(self.members):
            for turn in range(self.batches):
                if step or turn:
                    there = self.device(self.group, self.member_at(step), self.core_at(turn))
                    pl.semaphore_signal(barrier, inc=1, device_id=there, device_id_type=MESH)
                    greeted += 1
        for step in range(1, self.groups):
            for turn in range(self.batches):
                there = self.device(self.group_at(step), self.member, self.core_at(turn))
                pl.semaphore_signal(barrier, inc=1, device_id=there, device_id_type=MESH)
                greeted += 1
        return greeted


def send_copy(source, target, send_sem, recv_sem, there):
    return pltpu.make_async_remote_copy(
        src_ref=source,
        dst_ref=target,
        send_sem=send_sem,
        recv_sem=recv_sem,
        device_id=there,
        device_id_type=MESH,
    )


def slab(ref, dim, index, size):
    picks = [slice(None)] * len(ref.shape)
    picks[dim] = pl.ds(pl.multiple_of(index * size, size), size)
    return ref.at[tuple(picks)]


class WideExchange:
    @staticmethod
    def scratch(place_sizes, wide):
        groups, members, batches = place_sizes
        mates = members * batches
        dma = pltpu.SemaphoreType.DMA
        return [dma((mates,)), dma((mates,)), dma((wide.shape[1] // members,))]

    @staticmethod
    def shape(place_sizes, wide):
        groups, members, batches = place_sizes
        pieces, steps, series, channels = wide.shape
        return (steps // members, members * batches, pieces, series, channels // batches)

    def __init__(self, place, source, target, sems):
        self.place, self.source, self.target = place, source, target
        self.send_sem, self.recv_sem, self.local_sem = sems

    def hops(self):
        for step in range(self.place.members):
            for turn in range(self.place.batches):
                if step or turn:
                    yield step, turn

    def mate(self, step, turn):
        return self.place.core_at(turn) * self.place.members + self.place.member_at(step)

    def piece(self, one, step, turn):
        place = self.place
        steps, half = self.target.shape[0], self.target.shape[4]
        return slab(
            self.source.at[:, place.member_at(step) * steps + one], 2, place.core_at(turn), half
        )

    def own(self, one):
        return pltpu.make_async_copy(
            self.piece(one, 0, 0), self.target.at[one, self.mate(0, 0)], self.local_sem.at[one]
        )

    def whole(self, step, turn, pick):
        slot = turn * self.place.members + step
        block = self.target.at[:, pick]
        return send_copy(
            block,
            block,
            self.send_sem.at[slot],
            self.recv_sem.at[slot],
            self.place.device(
                self.place.group, self.place.member_at(step), self.place.core_at(turn)
            ),
        )

    def units(self):
        return [functools.partial(self.start, one) for one in range(self.target.shape[0])]

    def start(self, one):
        place = self.place
        self.own(one).start()
        for step, turn in self.hops():
            slot = turn * place.members + step
            send_copy(
                self.piece(one, step, turn),
                self.target.at[one, self.mate(0, 0)],
                self.send_sem.at[slot],
                self.recv_sem.at[slot],
                place.device(place.group, place.member_at(step), place.core_at(turn)),
            ).start()

    def wait(self):
        for one in range(self.target.shape[0]):
            self.own(one).wait()
        for step, turn in self.hops():
            self.whole(step, turn, self.mate(-step, -turn)).wait_recv()

    def drain(self):
        for step, turn in self.hops():
            self.whole(step, turn, self.mate(0, 0)).wait_send()


class NarrowGather:
    sems = 5

    @staticmethod
    def scratch(place_sizes, narrow):
        groups, members, batches = place_sizes
        dma = pltpu.SemaphoreType.DMA
        size = members * batches
        return [dma((members,)), dma((members,)), dma((size,)), dma((size,)), dma((1,))]

    def __init__(self, place, source, target, sems):
        self.place, self.source, self.target = place, source, target
        (self.link_send, self.link_recv, self.chip_send, self.chip_recv, self.local_sem) = sems

    def own(self):
        place = self.place
        pick = place.core * place.members + place.member
        return pltpu.make_async_copy(self.source, self.target.at[pick], self.local_sem.at[0])

    def link(self, step, pick_step):
        place = self.place
        pick = place.core * place.members + place.member_at(pick_step)
        return send_copy(
            self.source,
            self.target.at[pick],
            self.link_send.at[step],
            self.link_recv.at[step],
            place.device(place.group, place.member_at(step), place.core),
        )

    def chip(self, step, turn, source_core, target_core):
        place = self.place
        member = place.member_at(-step)
        slot = turn * place.members + step
        source = self.target.at[source_core * place.members + member] if step else self.source
        return send_copy(
            source,
            self.target.at[target_core * place.members + member],
            self.chip_send.at[slot],
            self.chip_recv.at[slot],
            place.device(place.group, place.member, place.core_at(turn)),
        )

    def start(self):
        place = self.place
        self.own().start()
        for step in range(1, place.members):
            self.link(step, 0).start()
        for turn in range(1, place.batches):
            self.chip(0, turn, place.core, place.core).start()

    def forward(self):
        place = self.place
        for step in range(1, place.members):
            self.link(step, -step).wait_recv()
            for turn in range(1, place.batches):
                self.chip(step, turn, place.core, place.core).start()

    def wait(self):
        place = self.place
        self.own().wait()
        for turn in range(1, place.batches):
            other = place.core_at(-turn)
            for step in range(place.members):
                self.chip(step, turn, place.core, other).wait_recv()

    def drain(self):
        place = self.place
        for step in range(1, place.members):
            self.link(step, 0).wait_send()
        for turn in range(1, place.batches):
            for step in range(place.members):
                self.chip(step, turn, place.core, place.core).wait_send()


class KernelProduct:
    sems = 6

    @staticmethod
    def scratch(place_sizes, kind, wide, narrow):
        groups, members, batches = place_sizes
        pieces, kernel, series, channels = wide.shape
        steps, rows = kernel // members, pieces * series
        half = channels // batches
        piece = (128, half) if kind == "down" else (half, 128)
        dma = pltpu.SemaphoreType.DMA
        return [
            pltpu.VMEM((channels, members * batches * rows), HALF_FLOAT),
            pltpu.VMEM((steps, channels, half), HALF_FLOAT),
            pltpu.VMEM((groups, steps) + piece, HALF_FLOAT),
            pltpu.VMEM((steps, 128, half), HALF_FLOAT),
            pltpu.VMEM((kernel, channels // (groups * members), half), HALF_FLOAT),
            dma((groups * batches,)),
            dma((groups * batches,)),
            dma((members,)),
            dma((members,)),
            dma((2,)),
        ]

    def __init__(self, place, kind, wide_in, narrow_in, out, scratch):
        self.place, self.kind, self.wide_in, self.narrow_in, self.out = (
            place,
            kind,
            wide_in,
            narrow_in,
            out,
        )
        (self.narrow_t, self.send, self.recv, self.total, self.gathered) = scratch[:5]
        (self.sz, self.rz, self.sf, self.rf, self.local) = scratch[5:]
        self.cores_per_group = place.groups // place.batches

    def multiply(self):
        mates, rows = self.narrow_in.shape[0], self.narrow_in.shape[1]
        self.narrow_t[...] = self.narrow_in[...].reshape(mates * rows, -1).T

        @pl.loop(0, self.wide_in.shape[0])
        def _(one):
            data = self.wide_in[one].reshape(mates * rows, -1)
            self.send[one] = dot_nn(self.narrow_t[...], data).astype(HALF_FLOAT)

    def chunk(self, group, core):
        if self.kind == "down":
            return slab(self.send, 1, group, 128)
        half = self.send.shape[1] // self.place.batches
        return slab(
            slab(self.send, 1, core, half), 2, lax.rem(group, self.cores_per_group), 128
        )

    def hops(self):
        place = self.place
        for step in range(place.groups):
            for turn in range(place.batches if self.kind == "up" else 1):
                yield step, turn

    def partial(self, step, turn, action):
        place = self.place
        group, core = place.group_at(step), place.core_at(turn)
        slot = step * place.batches + turn
        if step == 0 and turn == 0:
            copy = pltpu.make_async_copy(
                self.chunk(group, core), self.recv.at[place.group], self.local.at[0]
            )
            act = lambda: action(copy, True)
        else:
            copy = send_copy(
                self.chunk(group, core),
                self.recv.at[place.group],
                self.sz.at[slot],
                self.rz.at[slot],
                place.device(group, place.member, core),
            )
            act = lambda: action(copy, False)
        if self.kind == "down":
            act()
        else:
            pl.when(lax.div(group, self.cores_per_group) == place.core)(act)

    def start_partials(self):
        for step, turn in self.hops():
            self.partial(step, turn, lambda copy, local: copy.start())

    def sum_partials(self):
        place = self.place
        for step, turn in self.hops():
            group, core = place.group_at(-step), place.core_at(-turn)
            slot = step * place.batches + turn

            def act(step=step, turn=turn, group=group, slot=slot):
                if step == 0 and turn == 0:
                    pltpu.make_async_copy(
                        self.chunk(place.group, place.core),
                        self.recv.at[place.group],
                        self.local.at[0],
                    ).wait()
                else:
                    send_copy(
                        self.chunk(place.group, place.core),
                        self.recv.at[group],
                        self.sz.at[slot],
                        self.rz.at[slot],
                        place.device(place.group, place.member, place.core),
                    ).wait_recv()

            if self.kind == "down":
                act()
            else:
                pl.when(lax.div(place.group, self.cores_per_group) == core)(act)

        @pl.loop(0, self.total.shape[0])
        def _(one):
            value = self.recv[0, one].astype(FLOAT)
            for other in range(1, place.groups):
                value = value + self.recv[other, one].astype(FLOAT)
            value = value if self.kind == "down" else value.T
            self.total[one] = value.astype(HALF_FLOAT)

    def final(self, step, pick_step):
        place = self.place
        steps, width = self.total.shape[0], self.gathered.shape[1]
        source = slab(self.total, 1, place.member_at(step), width)
        target = slab(self.gathered, 0, place.member_at(pick_step), steps)
        if step == 0:
            return pltpu.make_async_copy(source, target, self.local.at[1])
        return send_copy(
            source,
            target,
            self.sf.at[step],
            self.rf.at[step],
            place.device(place.group, place.member_at(step), place.core),
        )

    def start_final(self):
        for step in range(self.place.members):
            self.final(step, 0).start()

    def finish(self):
        place = self.place
        self.final(0, 0).wait()
        for step in range(1, place.members):
            self.final(step, -step).wait_recv()
        self.out[...] = self.gathered[...].astype(FLOAT)
        for step in range(1, place.members):
            self.final(step, 0).wait_send()
        for step, turn in self.hops():
            if step or turn:
                self.partial(step, turn, lambda copy, local: copy.wait_send())


class MatrixSum:
    sems = 7

    @staticmethod
    def half_shape(place_sizes, kind, value):
        batches = place_sizes[2]
        shape = list(value.shape)
        if kind == "rows":
            shape[0] //= batches
        elif kind == "lanes":
            shape[-1] //= batches
        return tuple(shape)

    @staticmethod
    def piece_shape(place_sizes, kind, value):
        groups, members, batches = place_sizes
        shape = list(MatrixSum.half_shape(place_sizes, kind, value))
        dim = {"rows": 1, "lanes": len(shape) - 2, "whole": 0}[kind]
        shape[dim] //= groups * members
        return tuple(shape)

    @staticmethod
    def scratch(place_sizes, kind, value):
        groups, members, batches = place_sizes
        half = MatrixSum.half_shape(place_sizes, kind, value)
        piece = MatrixSum.piece_shape(place_sizes, kind, value)
        dma = pltpu.SemaphoreType.DMA
        return [
            pltpu.VMEM(half, value.dtype),
            pltpu.VMEM((batches,) + half, value.dtype),
            pltpu.VMEM((members, groups) + piece, value.dtype),
            pltpu.VMEM((groups,) + piece, value.dtype),
            pltpu.VMEM((groups,) + piece, value.dtype),
            dma((batches,)),
            dma((batches,)),
            dma((members * groups,)),
            dma((members * groups,)),
            dma((groups,)),
            dma((groups,)),
            dma((1 + groups,)),
        ]

    def __init__(self, place, kind, source, out, scratch):
        self.place, self.kind, self.source, self.out = place, kind, source, out
        (self.own, self.others, self.by_member, self.sums, self.by_group) = scratch[:5]
        (self.sb, self.rb, self.sm, self.rm, self.sg, self.rg, self.local) = scratch[5:]
        self.piece_dim = {"rows": 1, "lanes": len(self.own.shape) - 2, "whole": 0}[kind]

    def half(self, core):
        if self.kind == "rows":
            return slab(self.source, 0, core, self.own.shape[0])
        if self.kind == "lanes":
            return slab(self.source, len(self.own.shape) - 1, core, self.own.shape[-1])
        return self.source

    def cores(self, step, pick):
        place = self.place
        core = place.core_at(step)
        return send_copy(
            self.half(core),
            self.others.at[pick],
            self.sb.at[step],
            self.rb.at[step],
            place.device(place.group, place.member, core),
        )

    def load(self):
        return pltpu.make_async_copy(self.half(self.place.core), self.own, self.local.at[0])

    def start(self):
        self.load().start()
        for step in range(1, self.place.batches):
            self.cores(step, self.place.core).start()

    def piece(self, group, member):
        size = self.by_member.shape[2 + self.piece_dim]
        return slab(self.own, self.piece_dim, group * self.place.members + member, size)

    def members(self, step, pick_step, group):
        place = self.place
        member = place.member_at(step)
        slot = step * place.groups + group
        target = self.by_member.at[place.member_at(pick_step), group]
        if step == 0:
            return pltpu.make_async_copy(
                self.piece(group, member), target, self.local.at[1 + group]
            )
        return send_copy(
            self.piece(group, member),
            target,
            self.sm.at[slot],
            self.rm.at[slot],
            place.device(place.group, member, place.core),
        )

    def add_cores(self):
        place = self.place
        self.load().wait()
        for step in range(1, place.batches):
            self.cores(step, place.core_at(-step)).wait_recv()
        rows = self.own.shape[0]
        block = max(size for size in (1, 2, 4, 8, 16, 32, 64) if rows % size == 0)

        @pl.loop(0, rows // block)
        def _(index):
            pick = pl.ds(pl.multiple_of(index * block, block), block)
            value = self.own[pick].astype(FLOAT)
            for step in range(1, place.batches):
                value = value + self.others[place.core_at(step), pick].astype(FLOAT)
            self.own[pick] = value.astype(self.own.dtype)

        for step in range(place.members):
            for group in range(place.groups):
                self.members(step, 0, group).start()

    def groups(self, step, pick_step):
        place = self.place
        group = place.group_at(step)
        return send_copy(
            self.sums.at[group],
            self.by_group.at[place.group_at(pick_step)],
            self.sg.at[step],
            self.rg.at[step],
            place.device(group, place.member, place.core),
        )

    def add_members(self):
        place = self.place
        for step in range(place.members):
            for group in range(place.groups):
                if step == 0:
                    self.members(step, 0, group).wait()
                else:
                    self.members(step, -step, group).wait_recv()

        @pl.loop(0, place.groups)
        def _(group):
            value = self.by_member[0, group].astype(FLOAT)
            for other in range(1, place.members):
                value = value + self.by_member[other, group].astype(FLOAT)
            self.sums[group] = value.astype(self.sums.dtype)

        for step in range(1, place.groups):
            self.groups(step, 0).start()
        self.by_group[place.group] = self.sums[place.group]

    def finish(self):
        place = self.place
        for step in range(1, place.groups):
            self.groups(step, -step).wait_recv()
        value = self.by_group[0].astype(FLOAT)
        for other in range(1, place.groups):
            value = value + self.by_group[other].astype(FLOAT)
        self.out[...] = value
        for step in range(1, place.groups):
            self.groups(step, 0).wait_send()
        for step in range(1, place.members):
            for group in range(place.groups):
                self.members(step, 0, group).wait_send()
        for step in range(1, place.batches):
            self.cores(step, place.core).wait_send()


def remote_call(body, inputs, outputs, scratch, collective_id, flops, nbytes, name):
    def kernel(*refs):
        left = list(refs)
        named = {key: left.pop(0) for key in inputs}
        named.update({key: left.pop(0) for key in outputs})
        for key, shapes in scratch.items():
            named[key] = [left.pop(0) for _ in shapes]
        body(named)

    results = pl.pallas_call(
        kernel,
        out_shape=tuple(shape for shape, _ in outputs.values()),
        in_specs=[spec for _, spec in inputs.values()],
        out_specs=tuple(spec for _, spec in outputs.values()),
        scratch_shapes=[shape for shapes in scratch.values() for shape in shapes],
        compiler_params=pltpu.CompilerParams(
            collective_id=collective_id,
            has_side_effects=True,
            vmem_limit_bytes=63 * 1024 * 1024,
        ),
        cost_estimate=pl.CostEstimate(flops=flops, bytes_accessed=nbytes, transcendentals=0),
        name=name,
    )(*[value for value, _ in inputs.values()])
    return dict(zip(outputs, results))


def plane_sizes(channels):
    devices, batches = lax.axis_size("tm"), lax.axis_size("batch")
    groups = channels // 128
    if batches == 2 and channels % 256 == 0 and devices % groups == 0:
        return groups, devices // groups, batches
    return None


VMEM_SPEC = pl.BlockSpec(memory_space=pltpu.VMEM)
HBM_SPEC = pl.BlockSpec(memory_space=pl.ANY)


def down_gradients(sizes, wides, narrows, vectors):
    groups, members, batches = sizes
    half = wides[0].shape[4]
    channels = half * batches
    inputs, outputs, scratch = {}, {}, {}
    for index, (wide, narrow) in enumerate(zip(wides, narrows)):
        steps = wide.shape[0] * members
        shape = jax.ShapeDtypeStruct(
            (wide.shape[2], steps, wide.shape[3], channels), HALF_FLOAT
        )
        inputs[f"wide{index}"] = (wide, VMEM_SPEC)
        inputs[f"narrow{index}"] = (narrow, HBM_SPEC)
        outputs[f"out{index}"] = (
            jax.ShapeDtypeStruct((steps, channels // (groups * members), half), FLOAT),
            VMEM_SPEC,
        )
        scratch[f"rows{index}"] = [
            pltpu.VMEM((members * batches,) + narrow.shape, HALF_FLOAT)
        ]
        scratch[f"gather{index}"] = NarrowGather.scratch(sizes, narrow)
        scratch[f"product{index}"] = KernelProduct.scratch(sizes, "down", shape, narrow)
    inputs["vectors"] = (vectors, HBM_SPEC)
    outputs["vector_sum"] = (jax.ShapeDtypeStruct((1,) + vectors.shape[1:], FLOAT), VMEM_SPEC)
    scratch["vector"] = MatrixSum.scratch(sizes, "whole", vectors)

    def body(refs):
        place = Place(*sizes)
        barrier = pltpu.get_barrier_semaphore()
        pl.semaphore_wait(barrier, place.greet(barrier))
        gathers, products = [], []
        for index in range(len(wides)):
            gathers.append(
                NarrowGather(
                    place,
                    refs[f"narrow{index}"],
                    refs[f"rows{index}"][0],
                    refs[f"gather{index}"],
                )
            )
            products.append(
                KernelProduct(
                    place,
                    "down",
                    refs[f"wide{index}"],
                    refs[f"rows{index}"][0],
                    refs[f"out{index}"],
                    refs[f"product{index}"],
                )
            )
        total = MatrixSum(place, "whole", refs["vectors"], refs["vector_sum"], refs["vector"])
        for gather in gathers:
            gather.start()
        total.start()
        for gather in gathers:
            gather.forward()
        for gather, product in zip(gathers, products):
            gather.wait()
            product.multiply()
            product.start_partials()
        total.add_cores()
        total.add_members()
        for product in products:
            product.sum_partials()
            product.start_final()
        total.finish()
        for product in products:
            product.finish()
        for gather in gathers:
            gather.drain()

    flops = sum(2 * wide.size * channels for wide in wides)
    results = remote_call(
        body, inputs, outputs, scratch, 2, flops, 8 * flops // channels, "down_gradients"
    )
    return [results["out0"], results["out1"]], results["vector_sum"]


def iso_gradient_kernel(spec_ref, specs_ref, grad_ref, grads_ref, out_ref):
    devices = spec_ref.shape[0] // 2
    spec, grad, turned = [], [], []
    for own, others, into in ((spec_ref, specs_ref, spec), (grad_ref, grads_ref, grad)):
        into.append(own[...])
        for index in range(others.shape[0]):
            into.append(others[index])
    for value in grad:
        turned.append(jnp.concatenate([value[devices:], -value[:devices]]))
    spec = jnp.concatenate(spec)
    for part, values in enumerate((grad, turned)):
        out_ref[0, part] = lax.dot_general(
            spec,
            jnp.concatenate(values),
            (((0,), (0,)), ((), ())),
            preferred_element_type=FLOAT,
        )


def iso_gradients(spec, specs, grad, grads, first, bins):
    rows, channels = 2 * lax.axis_size("tm"), grad.shape[1]
    half = spec.shape[1]
    others = specs.shape[0]
    return pl.pallas_call(
        iso_gradient_kernel,
        out_shape=jax.ShapeDtypeStruct((bins, 2, half, channels), FLOAT),
        grid=(bins,),
        in_specs=[
            pl.BlockSpec((rows, half), lambda i: (first + i, 0)),
            pl.BlockSpec((others, rows, half), lambda i: (0, first + i, 0)),
            pl.BlockSpec((rows, channels), lambda i: (first + i, 0)),
            pl.BlockSpec((others, rows, channels), lambda i: (0, first + i, 0)),
        ],
        out_specs=pl.BlockSpec((1, 2, half, channels), lambda i: (i, 0, 0, 0)),
        cost_estimate=pl.CostEstimate(
            flops=4 * bins * rows * (1 + others) * half * channels,
            bytes_accessed=8 * bins * half * channels,
            transcendentals=0,
        ),
        name="iso_gradients",
    )(spec, specs, grad, grads)


class Extra:
    def __init__(self, sizes):
        self.sizes = sizes
        self.inputs, self.outputs, self.scratch = {}, {}, {}

    def bind(self, refs):
        self.refs = refs
        self.place = Place(*self.sizes) if self.sizes else None

    def greet(self, barrier):
        return self.place.greet(barrier) if self.sizes else 0

    def start(self):
        pass

    def after_bins(self):
        pass

    def after_spec(self):
        pass

    def after_mixed(self):
        pass

    def after_signal(self):
        pass

    def finish(self):
        pass

    def run(self, share):
        count = max(1, round(share * self.unit_count))
        for _ in range(min(count, len(self.units))):
            self.units.pop(0)()


class ForwardExtra(Extra):
    def __init__(self, sizes, wides):
        super().__init__(sizes)
        self.count = len(wides) if sizes else 0
        for index in range(self.count):
            self.inputs[f"wide{index}"] = (wides[index], HBM_SPEC)
            self.outputs[f"gathered{index}"] = (
                jax.ShapeDtypeStruct(WideExchange.shape(sizes, wides[index]), HALF_FLOAT),
                HBM_SPEC,
            )
            self.scratch[f"exchange{index}"] = WideExchange.scratch(sizes, wides[index])

    def bind(self, refs):
        super().bind(refs)
        self.exchanges = [
            WideExchange(
                self.place, refs[f"wide{i}"], refs[f"gathered{i}"], refs[f"exchange{i}"]
            )
            for i in range(self.count)
        ]
        self.units = [unit for item in self.exchanges for unit in item.units()]
        self.unit_count = len(self.units)

    def start(self):
        self.run(0.15)

    def after_bins(self):
        self.run(0.55)

    def after_mixed(self):
        self.run(1.0)

    def finish(self):
        for item in self.exchanges:
            item.wait()
            item.drain()


class BackwardExtra(Extra):
    def __init__(self, sizes, spec, wides, narrows, matrices):
        super().__init__(sizes)
        self.batches = lax.axis_size("batch")
        others = jax.ShapeDtypeStruct((self.batches - 1,) + spec.shape, HALF_FLOAT)
        self.inputs["spec_forward"] = (spec, HBM_SPEC)
        self.outputs["specs"] = (others, HBM_SPEC)
        self.outputs["grads"] = (others, HBM_SPEC)
        dma = pltpu.SemaphoreType.DMA
        self.scratch["other_sems"] = [dma((self.batches,))] * 4
        self.count = len(wides) if sizes else 0
        self.kinds = [kind for kind, _ in matrices] if sizes else []
        for i in range(self.count):
            wide, narrow = wides[i], narrows[i]
            groups, members, batches = sizes
            channels = narrow.shape[1]
            self.inputs[f"wide{i}"] = (wide, HBM_SPEC)
            self.inputs[f"narrow{i}"] = (narrow, HBM_SPEC)
            self.outputs[f"up{i}"] = (
                jax.ShapeDtypeStruct(
                    (wide.shape[1], channels // (groups * members), channels // batches), FLOAT
                ),
                VMEM_SPEC,
            )
            self.scratch[f"wide_in{i}"] = [
                pltpu.VMEM(WideExchange.shape(sizes, wide), HALF_FLOAT)
            ]
            self.scratch[f"rows{i}"] = [
                pltpu.VMEM((members * batches,) + narrow.shape, HALF_FLOAT)
            ]
            self.scratch[f"exchange{i}"] = WideExchange.scratch(sizes, wide)
            self.scratch[f"gather{i}"] = NarrowGather.scratch(sizes, narrow)
            self.scratch[f"product{i}"] = KernelProduct.scratch(sizes, "up", wide, narrow)
        for i, kind in enumerate(self.kinds):
            value = matrices[i][1]
            self.inputs[f"matrix{i}"] = (value, HBM_SPEC)
            self.outputs[f"matrix_sum{i}"] = (
                jax.ShapeDtypeStruct(MatrixSum.piece_shape(sizes, kind, value), FLOAT),
                VMEM_SPEC,
            )
            self.scratch[f"sum{i}"] = MatrixSum.scratch(sizes, kind, value)

    def bind(self, refs):
        super().bind(refs)
        self.exchanges, self.gathers, self.products = [], [], []
        for i in range(self.count):
            wide_in, rows = refs[f"wide_in{i}"][0], refs[f"rows{i}"][0]
            self.exchanges.append(
                WideExchange(self.place, refs[f"wide{i}"], wide_in, refs[f"exchange{i}"])
            )
            self.gathers.append(
                NarrowGather(self.place, refs[f"narrow{i}"], rows, refs[f"gather{i}"])
            )
            self.products.append(
                KernelProduct(self.place, "up", wide_in, rows, refs[f"up{i}"], refs[f"product{i}"])
            )
        self.sums = [
            MatrixSum(
                self.place, kind, refs[f"matrix{i}"], refs[f"matrix_sum{i}"], refs[f"sum{i}"]
            )
            for i, kind in enumerate(self.kinds)
        ]

    def other(self, index, turn):
        source, target = (
            (self.refs["spec_forward"], self.refs["specs"]),
            (self.refs["spec"], self.refs["grads"]),
        )[index]
        sems = self.refs["other_sems"]
        core = lax.rem(lax.axis_index("batch") + turn, self.batches)
        return send_copy(
            source,
            target.at[turn - 1],
            sems[2 * index].at[turn],
            sems[2 * index + 1].at[turn],
            (core, lax.axis_index("tm")),
        )

    def start(self):
        self.units = [unit for item in self.exchanges for unit in item.units()]
        self.unit_count = len(self.units)
        for turn in range(1, self.batches):
            self.other(0, turn).start()
        for item in self.gathers + self.sums:
            item.start()

    def after_bins(self):
        self.run(0.6)
        for item in self.gathers:
            item.forward()

    def after_mixed(self):
        self.run(0.3)

    def after_spec(self):
        for turn in range(1, self.batches):
            self.other(1, turn).start()

    def after_signal(self):
        self.run(1.0)
        for exchange, gather, product in zip(self.exchanges, self.gathers, self.products):
            exchange.wait()
            gather.wait()
            product.multiply()
            product.start_partials()
        for item in self.sums:
            item.add_cores()

    def finish(self):
        for item in self.sums:
            item.add_members()
        for item in self.products:
            item.sum_partials()
            item.start_final()
        for item in self.sums + self.products:
            item.finish()
        for item in self.exchanges + self.gathers:
            item.drain()
        for index in range(2):
            for turn in range(1, self.batches):
                self.other(index, turn).wait()


def spectral(values, weights, back, extra):
    devices, batches = lax.axis_size("tm"), lax.axis_size("batch")
    pieces_list = tuple(value.shape[1] for value in values)
    count, _, channels = values[0].shape
    wide = [round_up(pieces, 8) for pieces in pieces_list]
    per_time, per_bin = sum(wide), 2 * sum(wide)
    assert count <= devices and per_time % 16 == 0
    packed = jnp.concatenate(
        [
            jnp.pad(value, ((0, 0), (0, room - value.shape[1]), (0, 0)))
            for value, room in zip(values, wide)
        ],
        axis=1,
    ).reshape(count * per_time, channels)
    constants = spectral_constants(devices, pieces_list)
    rows_time, rows_bin = devices * per_time, devices * per_bin
    dma = pltpu.SemaphoreType.DMA
    inputs = {"x": (packed, HBM_SPEC)}
    for index, weight in enumerate(weights):
        inputs[f"weight{index}"] = (weight, HBM_SPEC)
    for key, value in zip(("table", "inverse", "move", "unmove"), constants):
        inputs[key] = (value, VMEM_SPEC)
    outputs = {
        "spec": (jax.ShapeDtypeStruct((rows_bin, channels), HALF_FLOAT), VMEM_SPEC),
        "signal": (jax.ShapeDtypeStruct((count * per_time, channels), FLOAT), VMEM_SPEC),
    }
    scratch = {
        "buffers": [pltpu.VMEM((rows_time, channels), HALF_FLOAT)]
        + [pltpu.VMEM((rows_bin, channels), HALF_FLOAT)] * 5
        + [pltpu.VMEM((rows_time, channels), FLOAT)]
        + [
            pltpu.VMEM((weight.shape[0], 2, weight.shape[2] * batches, channels), HALF_FLOAT)
            for weight in weights
        ],
        "sems": [dma((devices,))] * 8 + [dma((2, batches)), dma((2, batches)), dma((3,))],
    }
    inputs.update(extra.inputs)
    outputs.update(extra.outputs)
    scratch.update(extra.scratch)
    sizes = (devices, batches, count, pieces_list)

    def body(refs):
        extra.bind(refs)
        spectral_body(sizes, back, refs, extra)

    results = remote_call(
        body,
        inputs,
        outputs,
        scratch,
        1 if back else 0,
        2 * rows_bin * channels * channels * 4,
        4 * channels * channels * sum(pieces_list),
        "spectral_back" if back else "spectral_forward",
    )
    signal = results["signal"].reshape(count, per_time, channels)
    signals, offset = [], 0
    for pieces, room in zip(pieces_list, wide):
        signals.append(signal[:, offset : offset + pieces])
        offset += room
    return results, signals


def by_time(values):
    turned = jnp.swapaxes(values, 0, 1)
    extra = -turned.shape[1] % 16
    return jnp.pad(turned, ((0, 0), (0, extra)) + ((0, 0),) * (turned.ndim - 2))


def by_series(values, count):
    return jnp.swapaxes(values[:, :count], 0, 1)


def neighbours(low_side, high_side):
    count = lax.axis_size("tm")
    onward = [(i, i + 1) for i in range(count - 1)]
    return (
        lax.ppermute(high_side, "tm", onward),
        lax.ppermute(low_side, "tm", [(j, i) for i, j in onward]),
    )


def window_sum(values, first, width, count):
    total, level, size = None, values, 1
    while width:
        if width & 1:
            part = level[first : first + count]
            total = part if total is None else total + part
            first += size
        width >>= 1
        if width:
            level = level[:-size] + level[size:]
            size *= 2
    return total


def seasonal_parts(series, halves, rim):
    steps = series.shape[0]
    before, after = neighbours(series[:rim], series[steps - rim :])
    position = lax.axis_index("tm")
    before = jnp.where(position == 0, jnp.broadcast_to(series[:1], before.shape), before)
    is_final = position == lax.axis_size("tm") - 1
    after = jnp.where(is_final, jnp.broadcast_to(series[-1:], after.shape), after)
    wide = jnp.concatenate([before, series, after]).astype(FLOAT)
    parts = []
    for half in halves:
        mean = window_sum(wide, rim - half, 2 * half + 1, steps) / (2 * half + 1)
        parts.append((series.astype(FLOAT) - mean).astype(HALF_FLOAT))
    return parts


def series_gradient(grads, halves, rim):
    steps = grads[0].shape[0]
    wide = 0.0
    for grad, half in zip(grads, halves):
        padded = jnp.pad(grad, ((2 * rim, 2 * rim), (0, 0), (0, 0)))
        wide = wide + window_sum(padded, rim - half, 2 * half + 1, steps + 2 * rim) / (
            2 * half + 1
        )
    low_rim, high_rim = wide[:rim], wide[rim + steps :]
    before, after = neighbours(low_rim, high_rim)
    position = lax.axis_index("tm")
    is_final = position == lax.axis_size("tm") - 1
    low_sum = jnp.pad(jnp.sum(low_rim, axis=0, keepdims=True), ((0, rim - 1), (0, 0), (0, 0)))
    high_sum = jnp.pad(jnp.sum(high_rim, axis=0, keepdims=True), ((rim - 1, 0), (0, 0), (0, 0)))
    before = jnp.where(position == 0, low_sum, before)
    after = jnp.where(is_final, high_sum, after)
    middle = jnp.zeros((steps - 2 * rim,) + before.shape[1:], FLOAT)
    edges = jnp.concatenate([before, middle, after])
    return (sum(grads) - wide[rim : rim + steps] - edges).astype(HALF_FLOAT)


def step_block(kernel):
    return next(size for size in (4, 3, 2, 1) if kernel % size == 0)


def row_spec(block):
    return pl.BlockSpec(block, lambda i: (0,) * len(block))


def steps_spec(values, block):
    pieces, _, series, channels = values.shape
    return pl.BlockSpec((pieces, block, series, channels), lambda i: (0, i, 0, 0))


def weight_spec(weight, block):
    return pl.BlockSpec((block,) + weight.shape[1:], lambda i: (i, 0, 0))


def local_call(kernel, grid, inputs, outputs, flops, nbytes, name):
    return pl.pallas_call(
        kernel,
        out_shape=tuple(shape for shape, _ in outputs),
        grid=(grid,),
        in_specs=[spec for _, spec in inputs],
        out_specs=tuple(spec for _, spec in outputs),
        compiler_params=pltpu.CompilerParams(vmem_limit_bytes=48 * 1024 * 1024),
        cost_estimate=pl.CostEstimate(
            flops=flops, bytes_accessed=nbytes, transcendentals=0
        ),
        name=name,
    )(*[value for value, _ in inputs])


def down_kernel(x_ref, w_ref, b_ref, out_ref):
    step = pl.program_id(0)

    @pl.when(step == 0)
    def _():
        out_ref[...] = jnp.broadcast_to(b_ref[...], out_ref.shape)

    total = out_ref[...]
    for one in range(w_ref.shape[0]):
        total = total + dot_nn(x_ref[:, one].reshape(total.shape), w_ref[one])
    out_ref[...] = total

    @pl.when(step == pl.num_programs(0) - 1)
    def _():
        out_ref[...] = jnp.tanh(out_ref[...])


def down_layer(seasonal, weight, bias_row):
    pieces, kernel, series, channels = seasonal.shape
    block = step_block(kernel)
    rows = pieces * series
    (down_act,) = local_call(
        down_kernel,
        kernel // block,
        [
            (seasonal, steps_spec(seasonal, block)),
            (weight, weight_spec(weight, block)),
            (bias_row[None], row_spec((1, channels))),
        ],
        [(jax.ShapeDtypeStruct((rows, channels), FLOAT), row_spec((rows, channels)))],
        2 * seasonal.size * channels,
        2 * (seasonal.size + weight.size),
        "down_layer",
    )
    return down_act


def turn_kernel(x_ref, out_ref):
    out_ref[...] = pltpu.einshape("mhd->hmd", x_ref[...])


def kernel_major(weight):
    channels, kernel, outs = weight.shape
    if kernel % 8:
        return jnp.swapaxes(weight, 0, 1)
    block = 64
    (turned,) = local_call(
        turn_kernel,
        channels // block,
        [(weight, pl.BlockSpec((block, kernel, outs), lambda i: (i, 0, 0)))],
        [
            (
                jax.ShapeDtypeStruct((kernel, channels, outs), weight.dtype),
                pl.BlockSpec((kernel, block, outs), lambda i: (0, i, 0)),
            )
        ],
        0,
        4 * weight.size,
        "kernel_major",
    )
    return turned


def normed(values):
    center = values - jnp.mean(values, axis=-1, keepdims=True)
    spread = jnp.mean(center * center, axis=-1, keepdims=True)
    scale = lax.rsqrt(spread + EPSILON)
    return center * scale, scale


def normed_back(grad, hat, scale):
    return (
        grad
        - jnp.mean(grad, axis=-1, keepdims=True)
        - hat * jnp.mean(grad * hat, axis=-1, keepdims=True)
    ) * scale


def up_kernel(inner_ref, x_ref, w_ref, rows_ref, act_ref, out_ref):
    bias_row, gain_row, shift_row = (rows_ref[i : i + 1] for i in range(3))
    inner = inner_ref[...]
    for one in range(w_ref.shape[0]):
        act = jnp.tanh(dot_nn(inner, w_ref[one]) + bias_row)
        hat, _ = normed(act + x_ref[:, one].reshape(act.shape).astype(FLOAT))
        act_ref[:, one] = act.reshape(act_ref.shape[0], act_ref.shape[2], act_ref.shape[3])
        out = (hat * gain_row + shift_row).astype(HALF_FLOAT)
        out_ref[:, one] = out.reshape(out_ref.shape[0], out_ref.shape[2], out_ref.shape[3])


def up_layer(inner, seasonal, weight, bias_row, gain_row, shift_row):
    pieces, kernel, series, channels = seasonal.shape
    block = step_block(kernel)
    rows = jnp.stack([bias_row, gain_row, shift_row])
    return local_call(
        up_kernel,
        kernel // block,
        [
            (inner, row_spec(inner.shape)),
            (seasonal, steps_spec(seasonal, block)),
            (weight, weight_spec(weight, block)),
            (rows, row_spec(rows.shape)),
        ],
        [
            (jax.ShapeDtypeStruct(seasonal.shape, FLOAT), steps_spec(seasonal, block)),
            (jax.ShapeDtypeStruct(seasonal.shape, HALF_FLOAT), steps_spec(seasonal, block)),
        ],
        2 * seasonal.size * channels,
        8 * seasonal.size + 2 * weight.size,
        "up_layer",
    )


def up_back_kernel(
    grad_ref, merge_ref, act_ref, x_ref, w_ref, gain_ref, outer_ref, up_ref, inner_ref, sums_ref
):
    @pl.when(pl.program_id(0) == 0)
    def _():
        inner_ref[...] = jnp.zeros_like(inner_ref)
        sums_ref[...] = jnp.zeros_like(sums_ref)

    shape = inner_ref.shape
    block = (x_ref.shape[0], x_ref.shape[2], x_ref.shape[3])
    gain_row = gain_ref[...]
    total = inner_ref[...]
    sums = [sums_ref[i : i + 1] for i in range(3)]
    for one in range(w_ref.shape[0]):
        grad = dot_nt(grad_ref[:, one].reshape(shape), merge_ref[...])
        act = act_ref[:, one].reshape(shape)
        hat, scale = normed(act + x_ref[:, one].reshape(shape).astype(FLOAT))
        outer = normed_back(grad * gain_row, hat, scale)
        up = (outer * (1.0 - act * act)).astype(HALF_FLOAT)
        total = total + dot_nt(up, w_ref[one])
        outer_ref[:, one] = outer.reshape(block)
        up_ref[:, one] = up.reshape(block)
        for i, value in enumerate((up.astype(FLOAT), grad * hat, grad)):
            sums[i] = sums[i] + jnp.sum(value, axis=0, keepdims=True)
    inner_ref[...] = total
    for i in range(3):
        sums_ref[i : i + 1] = sums[i]


def up_layer_back(grad, merge, act, seasonal, weight, gain_row):
    pieces, kernel, series, channels = seasonal.shape
    block = step_block(kernel)
    rows = pieces * series
    spec = steps_spec(seasonal, block)
    return local_call(
        up_back_kernel,
        kernel // block,
        [
            (grad, spec),
            (merge, row_spec(merge.shape)),
            (act, spec),
            (seasonal, spec),
            (weight, weight_spec(weight, block)),
            (gain_row[None], row_spec((1, channels))),
        ],
        [
            (jax.ShapeDtypeStruct(seasonal.shape, FLOAT), spec),
            (jax.ShapeDtypeStruct(seasonal.shape, HALF_FLOAT), spec),
            (jax.ShapeDtypeStruct((rows, channels), FLOAT), row_spec((rows, channels))),
            (jax.ShapeDtypeStruct((8, channels), FLOAT), row_spec((8, channels))),
        ],
        4 * seasonal.size * channels,
        14 * seasonal.size + 2 * weight.size,
        "up_layer_back",
    )


def down_back_kernel(grad_ref, w_ref, outer_ref, out_ref):
    grad = grad_ref[...]
    block = (out_ref.shape[0], out_ref.shape[2], out_ref.shape[3])
    for one in range(w_ref.shape[0]):
        out_ref[:, one] = dot_nt(grad, w_ref[one]).reshape(block) + outer_ref[:, one]


def down_layer_back(grad, weight, outer):
    pieces, kernel, series, channels = outer.shape
    block = step_block(kernel)
    spec = steps_spec(outer, block)
    (seasonal_grad,) = local_call(
        down_back_kernel,
        kernel // block,
        [(grad, row_spec(grad.shape)), (weight, weight_spec(weight, block)), (outer, spec)],
        [(jax.ShapeDtypeStruct(outer.shape, FLOAT), spec)],
        2 * outer.size * channels,
        8 * outer.size + 2 * weight.size,
        "down_layer_back",
    )
    return seasonal_grad


class Branch:
    def __init__(self, seasonal, down_weight, up_weight, bias_rows, gain_row, shift_row, count):
        steps, series, channels = seasonal.shape
        self.kernel = down_weight.shape[0]
        self.pieces = steps // self.kernel
        self.count, self.series = count, series
        self.seasonal = seasonal.reshape(self.pieces, self.kernel, series, channels)
        self.down_weight, self.up_weight = down_weight, up_weight
        self.bias_rows, self.gain_row, self.shift_row = bias_rows, gain_row, shift_row
        self.down_act = down_layer(self.seasonal, down_weight, bias_rows[0])
        self.down_low = self.down_act.astype(HALF_FLOAT)

    def to_series(self, rows):
        return by_series(rows.reshape(self.pieces, self.series, -1), self.count)

    def from_series(self, values):
        return by_time(values).reshape(self.pieces * self.series, -1)

    def up(self, iso_out):
        self.iso_act = jnp.tanh(self.from_series(iso_out) + self.bias_rows[1])
        self.inner_in = self.iso_act + self.down_low.astype(FLOAT)
        self.inner_low = layer_norm(self.inner_in, self.gain_row, self.shift_row).astype(
            HALF_FLOAT
        )
        self.act, out = up_layer(
            self.inner_low,
            self.seasonal,
            self.up_weight,
            self.bias_rows[2],
            self.gain_row,
            self.shift_row,
        )
        return out.reshape(-1, out.shape[3])

    def up_back(self, grad_merged, merge):
        self.outer, self.grad_up, grad_inner, sums = up_layer_back(
            grad_merged.reshape(self.seasonal.shape),
            merge,
            self.act,
            self.seasonal,
            self.up_weight,
            self.gain_row,
        )
        _, inner_pull = jax.vjp(layer_norm, self.inner_in, self.gain_row, self.shift_row)
        self.grad_inner_in, gain_inner, shift_inner = inner_pull(grad_inner)
        grad_iso = self.grad_inner_in * (1.0 - self.iso_act * self.iso_act)
        self.iso_sum, self.up_sum = jnp.sum(grad_iso, axis=0), sums[0]
        self.gain_sum, self.shift_sum = sums[1] + gain_inner, sums[2] + shift_inner
        return grad_iso.astype(HALF_FLOAT)

    def down_back(self, grad_signal):
        grad_down = self.from_series(grad_signal) + self.grad_inner_in
        self.grad_down = (grad_down * (1.0 - self.down_act * self.down_act)).astype(HALF_FLOAT)
        self.down_sum = jnp.sum(self.grad_down.astype(FLOAT), axis=0)
        grad = down_layer_back(self.grad_down, self.down_weight, self.outer)
        return grad.reshape(-1, self.series, grad.shape[3])


def batch_split(values, split, join):
    return lax.all_to_all(values, "batch", split_axis=split, concat_axis=join, tiled=True)


def time_sum(values, dim):
    return lax.psum_scatter(
        values.astype(HALF_FLOAT), "tm", scatter_dimension=dim, tiled=True
    ).astype(FLOAT)


def plain_gradients(wides, narrows, downs):
    results = []
    for wide, narrow, down in zip(wides, narrows, downs):
        wide = jnp.swapaxes(wide, 0, 1).reshape(wide.shape[1], -1, wide.shape[3])
        if down:
            wide, narrow = batch_split(wide, 2, 1), lax.all_gather(narrow, "batch", tiled=True)
            value = jnp.einsum("knc,nd->kcd", wide, narrow, preferred_element_type=FLOAT)
        else:
            wide = lax.all_gather(wide, "batch", axis=1, tiled=True)
            narrow = batch_split(narrow, 1, 0)
            value = jnp.einsum("nd,knc->dkc", narrow, wide, preferred_element_type=FLOAT)
        results.append(time_sum(value, 2))
    return results


def plain_sums(matrices):
    results = []
    for kind, value in matrices:
        batch_dim, time_dim = (0, 1) if kind == "rows" else (value.ndim - 1, value.ndim - 2)
        value = lax.psum_scatter(
            value.astype(FLOAT), "batch", scatter_dimension=batch_dim, tiled=True
        )
        results.append(time_sum(value, time_dim))
    return results


def per_device(
    series_in,
    out_cotangent,
    out_mask,
    down_twelve,
    down_sixteen,
    iso_twelve,
    iso_sixteen,
    up_twelve,
    up_sixteen,
    branch_bias,
    merge_weight,
    hidden_weight,
    hidden_bias,
    output_weight,
    head_bias,
    norm_gain,
    norm_shift,
):
    series_dev, step_count, channels = series_in.shape
    halves = (down_twelve.shape[0] // 2, down_sixteen.shape[0] // 2)
    rim = max(halves)
    biases = branch_bias.astype(FLOAT)
    gains = norm_gain.astype(FLOAT)
    shifts = norm_shift.astype(FLOAT)
    heads = head_bias.astype(FLOAT)
    seasonals = seasonal_parts(by_time(series_in), halves, rim)
    branches = [
        Branch(
            seasonals[k],
            (down_twelve, down_sixteen)[k],
            kernel_major((up_twelve, up_sixteen)[k]),
            (biases[k], biases[2 + k], biases[4 + k]),
            gains[0],
            shifts[0],
            series_dev,
        )
        for k in range(2)
    ]
    iso_weights = (iso_twelve, iso_sixteen)
    sizes = plane_sizes(channels)
    seasonal_steps = [branch.seasonal for branch in branches]
    forward, iso_outs = spectral(
        [branch.to_series(branch.down_low) for branch in branches],
        iso_weights,
        False,
        ForwardExtra(sizes, seasonal_steps),
    )
    outs = [branch.up(iso_out) for branch, iso_out in zip(branches, iso_outs)]
    row_count = outs[0].shape[0]
    merged = dot_nn(outs[0], merge_weight[0]) + dot_nn(outs[1], merge_weight[1]) + heads[0]
    first_low = layer_norm(merged, gains[1], shifts[1]).astype(HALF_FLOAT)
    hidden_pre = jnp.dot(
        first_low, hidden_weight, preferred_element_type=FLOAT
    ) + hidden_bias.astype(FLOAT)
    hidden_low = jax.nn.gelu(hidden_pre).astype(HALF_FLOAT)
    final_in = merged + (
        jnp.dot(hidden_low, output_weight, preferred_element_type=FLOAT) + heads[1]
    )
    mask_rows = by_time(out_mask.astype(FLOAT)).reshape(row_count, 1)
    result = by_series(
        (layer_norm(final_in, gains[2], shifts[2]) * mask_rows)
        .astype(HALF_FLOAT)
        .reshape(step_count, -1, channels),
        series_dev,
    )
    grad_result = by_time(out_cotangent).astype(FLOAT).reshape(row_count, channels) * mask_rows
    normed_final, final_pull = jax.vjp(layer_norm, final_in, gains[2], shifts[2])
    grad_final, gain_final, shift_final = final_pull(grad_result)
    grad_feed = grad_final.astype(HALF_FLOAT)
    grad_output_weight = jnp.einsum(
        "nd,nf->df", grad_feed, hidden_low, preferred_element_type=FLOAT
    ).astype(HALF_FLOAT)
    grad_output_bias = jnp.sum(grad_feed.astype(FLOAT), axis=0)
    grad_hidden_low = jnp.einsum(
        "nd,fd->nf", grad_feed, output_weight, preferred_element_type=FLOAT
    )
    gelu_value, gelu_pull = jax.vjp(jax.nn.gelu, hidden_pre)
    grad_hidden_pre = gelu_pull(grad_hidden_low)[0].astype(HALF_FLOAT)
    grad_hidden_weight = jnp.einsum(
        "nd,nf->df", first_low, grad_hidden_pre, preferred_element_type=FLOAT
    ).astype(HALF_FLOAT)
    grad_hidden_bias = jnp.sum(grad_hidden_pre.astype(FLOAT), axis=0)
    grad_first = jnp.einsum(
        "nf,df->nd", grad_hidden_pre, hidden_weight, preferred_element_type=FLOAT
    )
    normed_first, first_pull = jax.vjp(layer_norm, merged, gains[1], shifts[1])
    grad_merged_norm, gain_first, shift_first = first_pull(grad_first)
    grad_merged = (grad_final + grad_merged_norm).astype(HALF_FLOAT)
    grad_merge_bias = jnp.sum(grad_merged.astype(FLOAT), axis=0)
    grad_merge_weight = jnp.stack(
        [
            jnp.einsum("ne,nd->ed", grad_merged, out, preferred_element_type=FLOAT)
            for out in outs
        ]
    ).astype(HALF_FLOAT)
    grad_isos = [branches[k].up_back(grad_merged, merge_weight[k]) for k in range(2)]
    matrices = (
        ("rows", grad_hidden_weight),
        ("lanes", grad_output_weight),
        ("lanes", grad_merge_weight),
    )
    up_wides = [branch.grad_up for branch in branches]
    up_narrows = [branch.inner_low for branch in branches]
    backward, grad_signals = spectral(
        [branch.to_series(grad) for branch, grad in zip(branches, grad_isos)],
        iso_weights,
        True,
        BackwardExtra(sizes, forward["spec"], up_wides, up_narrows, matrices),
    )
    half = channels // lax.axis_size("batch")
    core = lax.axis_index("batch")
    spec_half = lax.dynamic_slice_in_dim(forward["spec"], core * half, half, axis=1)
    specs_half = lax.dynamic_slice_in_dim(backward["specs"], core * half, half, axis=2)
    iso_parts, first = [], 0
    for bins in (branches[0].pieces, branches[1].pieces):
        iso_parts.append(
            iso_gradients(
                spec_half, specs_half, backward["spec"], backward["grads"], first, bins
            )
        )
        first += round_up(bins, 8)
    grad_seasonals = [branches[k].down_back(grad_signals[k]) for k in range(2)]
    grad_series = by_series(series_gradient(grad_seasonals, halves, rim), series_dev)
    vectors = jnp.stack(
        [
            branches[0].down_sum,
            branches[1].down_sum,
            branches[0].iso_sum,
            branches[1].iso_sum,
            branches[0].up_sum,
            branches[1].up_sum,
            branches[0].gain_sum + branches[1].gain_sum,
            gain_first,
            gain_final,
            branches[0].shift_sum + branches[1].shift_sum,
            shift_first,
            shift_final,
            grad_merge_bias,
            grad_output_bias,
        ]
    )
    devices = lax.axis_size("tm")
    vector_count = vectors.shape[0]
    packed = jnp.concatenate(
        [
            vectors.reshape(vector_count, devices, -1).transpose(1, 0, 2).reshape(devices, -1),
            grad_hidden_bias.reshape(devices, -1),
        ],
        axis=1,
    )
    width = channels // devices
    down_narrows = [branch.grad_down for branch in branches]
    if sizes:
        extent = packed.shape[1]
        packed = jnp.pad(packed, ((0, 0), (0, -extent % 1024))).reshape(devices, -1, 128)
        downs, packed = down_gradients(
            sizes, (forward["gathered0"], forward["gathered1"]), down_narrows, packed
        )
        packed = packed.reshape(-1)[:extent]
        downs = [jnp.transpose(value, (0, 2, 1)) for value in downs]
        ups = [jnp.transpose(backward[key], (2, 0, 1)) for key in ("up0", "up1")]
        sums = [backward[f"matrix_sum{i}"] for i in range(3)]
    else:
        packed = lax.psum(
            lax.psum_scatter(packed, "tm", scatter_dimension=0, tiled=True), "batch"
        )[0]
        downs = plain_gradients(seasonal_steps, down_narrows, (True, True))
        ups = plain_gradients(up_wides, up_narrows, (False, False))
        sums = plain_sums(matrices)
    rows = packed[: vector_count * width].reshape(vector_count, width)
    vector_parts = (
        rows[:6],
        packed[vector_count * width :],
        rows[12:14],
        rows[6:9],
        rows[9:12],
    )
    return (
        result,
        grad_series,
        downs[0],
        downs[1],
        iso_parts[0],
        iso_parts[1],
        ups[0],
        ups[1],
        vector_parts[0],
        jnp.swapaxes(sums[2], 1, 2),
        sums[0],
        vector_parts[1],
        sums[1].T,
        vector_parts[2],
        vector_parts[3],
        vector_parts[4],
    )


def solution(mesh):
    placed = (
        P("batch", "tm", None),
        P("batch", "tm", None),
        P("batch", "tm"),
        P(),
        P(),
        P("tm", None, "batch", None),
        P("tm", None, "batch", None),
        P(),
        P(),
        P(),
        P(),
        P(),
        P(),
        P(),
        P(),
        P(),
        P(),
    )
    return jax.shard_map(
        per_device,
        mesh=mesh,
        in_specs=placed,
        out_specs=(
            P("batch", "tm", None),
            P("batch", "tm", None),
            P(None, "batch", "tm"),
            P(None, "batch", "tm"),
            P("tm", None, "batch", None),
            P("tm", None, "batch", None),
            P("batch", None, "tm"),
            P("batch", None, "tm"),
            P(None, "tm"),
            P(None, "batch", "tm"),
            P("batch", "tm"),
            P("tm"),
            P("batch", "tm"),
            P(None, "tm"),
            P(None, "tm"),
            P(None, "tm"),
        ),
        check_vma=False,
    )
```

```python
import functools
import math

import jax
import jax.numpy as jnp
import numpy as np
from jax import lax
from jax.experimental import pallas as pl
from jax.experimental.pallas import tpu as pltpu
from jax.sharding import PartitionSpec as P

FLOAT = jnp.float32
HALF_FLOAT = jnp.bfloat16
HIGHEST = lax.Precision.HIGHEST
EPSILON = 1e-05
MESH = pl.DeviceIdType.MESH


def layer_norm(values, gain_row, bias_row):
    center = values - jnp.mean(values, axis=-1, keepdims=True)
    spread = jnp.mean(center * center, axis=-1, keepdims=True)
    return center * lax.rsqrt(spread + EPSILON) * gain_row + bias_row


def round_up(value, multiple):
    return -(-value // multiple) * multiple


def spectral_constants(devices, pieces_list):
    padded = [round_up(pieces, 8) for pieces in pieces_list]
    per_time, per_bin = sum(padded), 2 * sum(padded)
    table = np.zeros((devices, per_bin, devices, per_time), np.float64)
    offset = 0
    for pieces, wide in zip(pieces_list, padded):
        length = devices * pieces
        index = np.arange(length)
        angle = (2.0 * math.pi / length) * (np.outer(index, index) % length)
        factor = 1.0 / math.sqrt(length)
        for part, values in enumerate((np.cos(angle) * factor, -np.sin(angle) * factor)):
            row = 2 * offset + part * wide
            table[:, row : row + pieces, :, offset : offset + pieces] = values.reshape(
                devices, pieces, devices, pieces
            )
        offset += wide
    table = table.reshape(devices * per_bin, devices * per_time).astype(np.float32)
    high = table.astype(HALF_FLOAT)
    low = (table - high.astype(np.float32)).astype(HALF_FLOAT)
    order = []
    offset = 0
    for wide in padded:
        for one_bin in range(wide):
            for part in range(2):
                for series in range(devices):
                    order.append(series * per_bin + 2 * offset + part * wide + one_bin)
        offset += wide
    move = np.zeros((devices * per_bin, devices * per_bin), np.float32)
    move[np.arange(len(order)), order] = 1.0
    move = move.astype(HALF_FLOAT)
    return (
        jnp.asarray(np.stack([high, low])),
        jnp.asarray(np.stack([high.T, low.T])),
        jnp.asarray(move),
        jnp.asarray(np.ascontiguousarray(move.T)),
    )


def dot_nn(left, right):
    return jnp.dot(left, right, preferred_element_type=FLOAT)


def dot_nt(left, right):
    return lax.dot_general(left, right, (((1,), (1,)), ((), ())), preferred_element_type=FLOAT)


def spectral_body(sizes, back, refs, extra):
    devices, batches, count, pieces_list = sizes
    x_ref, w1_ref, w2_ref = refs["x"], refs["weight0"], refs["weight1"]
    table_ref, inverse_ref = refs["table"], refs["inverse"]
    move_ref, unmove_ref = refs["move"], refs["unmove"]
    spec_ref, signal_ref = refs["spec"], refs["signal"]
    (one, two, three, mixed, spread, bins_out, four, w1, w2) = refs["buffers"]
    (s1, r1, s2, r2, s3, r3, s4, r4, ws, wr, own) = refs["sems"]
    me = lax.axis_index("tm")
    mine = lax.axis_index("batch")
    wide = [round_up(pieces, 8) for pieces in pieces_list]
    per_time, per_bin = sum(wide), 2 * sum(wide)
    weights = ((w1_ref, w1), (w2_ref, w2))

    barrier = pltpu.get_barrier_semaphore()

    @pl.loop(1, devices)
    def _(step):
        pl.semaphore_signal(
            barrier, inc=1, device_id=(mine, lax.rem(me + step, devices)), device_id_type=MESH
        )

    for step in range(1, batches):
        pl.semaphore_signal(
            barrier, inc=1, device_id=(lax.rem(mine + step, batches), me), device_id_type=MESH
        )
    pl.semaphore_wait(barrier, devices - 1 + batches - 1 + extra.greet(barrier))

    def exchange(source, target, send_sem, recv_sem, limit_out, limit_in, rows, start):
        def remote(there, here):
            return pltpu.make_async_remote_copy(
                src_ref=source.at[pl.ds(pl.multiple_of(there * rows, rows), rows)],
                dst_ref=target.at[pl.ds(pl.multiple_of(here * rows, rows), rows)],
                send_sem=send_sem.at[there],
                recv_sem=recv_sem.at[here],
                device_id=(mine, there),
                device_id_type=MESH,
            )

        if start:

            @pl.loop(1, devices)
            def _(step):
                there = lax.rem(me + step, devices)

                @pl.when(there < limit_out)
                def _():
                    remote(there, me).start()

        else:

            @pl.loop(1, devices)
            def _(step):
                there = lax.rem(me + step, devices)

                @pl.when(there < limit_in)
                def _():
                    pltpu.make_async_remote_copy(
                        src_ref=source.at[pl.ds(0, rows)],
                        dst_ref=target.at[pl.ds(pl.multiple_of(there * rows, rows), rows)],
                        send_sem=send_sem.at[there],
                        recv_sem=recv_sem.at[there],
                        device_id=(mine, there),
                        device_id_type=MESH,
                    ).wait_recv()

    def drain(source, target, send_sem, recv_sem, limit_out, rows):
        @pl.loop(1, devices)
        def _(step):
            there = lax.rem(me + step, devices)

            @pl.when(there < limit_out)
            def _():
                pltpu.make_async_remote_copy(
                    src_ref=source.at[pl.ds(0, rows)],
                    dst_ref=target.at[pl.ds(0, rows)],
                    send_sem=send_sem.at[there],
                    recv_sem=recv_sem.at[there],
                    device_id=(mine, there),
                    device_id_type=MESH,
                ).wait_send()

    owner = me < count
    exchange(x_ref, one, s1, r1, count, None, per_time, True)

    def weight_copies(index):
        source, target = weights[index]
        rows = source.shape[2]
        place = target.at[:, :, pl.ds(pl.multiple_of(mine * rows, rows), rows)]
        local = pltpu.make_async_copy(source, place, own.at[index])
        remote = []
        for step in range(1, batches):
            there = lax.rem(mine + step, batches)
            back_there = lax.rem(mine + batches - step, batches)
            other = target.at[:, :, pl.ds(pl.multiple_of(back_there * rows, rows), rows)]
            remote.append(
                [
                    pltpu.make_async_remote_copy(
                        src_ref=source,
                        dst_ref=where,
                        send_sem=ws.at[index, step],
                        recv_sem=wr.at[index, step],
                        device_id=(there, me),
                        device_id_type=MESH,
                    )
                    for where in (place, other)
                ]
            )
        return local, remote

    for index in range(2):
        local, remote = weight_copies(index)
        local.start()
        for copy, _unused in remote:
            copy.start()

    here = pltpu.make_async_copy(
        x_ref.at[pl.ds(pl.multiple_of(jnp.minimum(me, count - 1) * per_time, per_time), per_time)],
        one.at[pl.ds(pl.multiple_of(me * per_time, per_time), per_time)],
        own.at[2],
    )
    here.start()
    extra.start()
    if count < devices:
        two[pl.ds(count * per_bin, (devices - count) * per_bin)] = jnp.zeros(
            ((devices - count) * per_bin, two.shape[1]), two.dtype
        )
    here.wait()

    @pl.when(owner)
    def _():
        exchange(x_ref, one, s1, r1, None, devices, per_time, False)
        data = one[...]
        total = dot_nn(table_ref[0], data) + dot_nn(table_ref[1], data)
        bins_out[...] = total.astype(HALF_FLOAT)
        exchange(bins_out, two, s2, r2, devices, None, per_bin, True)
        place = pl.ds(pl.multiple_of(me * per_bin, per_bin), per_bin)
        two[place] = bins_out[place]

    extra.after_bins()
    exchange(bins_out, two, s2, r2, None, count, per_bin, False)
    spec_ref[...] = dot_nn(move_ref[...], two[...]).astype(HALF_FLOAT)
    extra.after_spec()
    base = 0
    for index in range(2):
        local, remote = weight_copies(index)
        local.wait()
        for copy, arrived in remote:
            copy.wait_send()
            arrived.wait_recv()
        target = weights[index][1]

        @pl.loop(0, pieces_list[index])
        def _(one_bin, base=base, target=target):
            place = pl.ds(
                pl.multiple_of(base + one_bin * 2 * devices, 2 * devices), 2 * devices
            )
            rows = spec_ref[place]
            if back:
                real = dot_nt(rows, target[one_bin, 0])
                imag = dot_nt(rows, target[one_bin, 1])
                out = jnp.concatenate(
                    [real[:devices] + imag[devices:], real[devices:] - imag[:devices]]
                )
            else:
                real = dot_nn(rows, target[one_bin, 0])
                imag = dot_nn(rows, target[one_bin, 1])
                out = jnp.concatenate(
                    [real[:devices] - imag[devices:], imag[:devices] + real[devices:]]
                )
            mixed[place] = out.astype(HALF_FLOAT)

        spare = wide[index] - pieces_list[index]
        if spare:
            mixed[
                pl.ds(base + pieces_list[index] * 2 * devices, spare * 2 * devices)
            ] = jnp.zeros((spare * 2 * devices, mixed.shape[1]), mixed.dtype)
        base += wide[index] * 2 * devices

    spread[...] = dot_nn(unmove_ref[...], mixed[...]).astype(HALF_FLOAT)
    exchange(spread, three, s3, r3, count, None, per_bin, True)
    extra.after_mixed()

    @pl.when(owner)
    def _():
        place = pl.ds(pl.multiple_of(me * per_bin, per_bin), per_bin)
        three[place] = spread[place]
        exchange(spread, three, s3, r3, None, devices, per_bin, False)
        data = three[...]
        total = dot_nn(inverse_ref[0], data) + dot_nn(inverse_ref[1], data)
        four[...] = total
        exchange(four, signal_ref, s4, r4, devices, None, per_time, True)
        place = pl.ds(pl.multiple_of(me * per_time, per_time), per_time)
        signal_ref[place] = four[place]

    extra.after_signal()
    exchange(four, signal_ref, s4, r4, None, count, per_time, False)
    drain(x_ref, one, s1, r1, count, per_time)
    drain(spread, three, s3, r3, count, per_bin)

    @pl.when(owner)
    def _():
        drain(bins_out, two, s2, r2, devices, per_bin)
        drain(four, signal_ref, s4, r4, devices, per_time)

    extra.finish()


class Place:
    def __init__(self, groups, members, batches):
        self.groups, self.members, self.batches = groups, members, batches
        self.me = lax.axis_index("tm")
        self.core = lax.axis_index("batch")
        self.group = lax.div(self.me, members)
        self.member = lax.rem(self.me, members)

    def device(self, group, member, core):
        return (core, group * self.members + member)

    def member_at(self, step):
        return lax.rem(self.member + step + self.members, self.members)

    def group_at(self, step):
        return lax.rem(self.group + step + self.groups, self.groups)

    def core_at(self, step):
        return lax.rem(self.core + step + self.batches, self.batches)

    def greet(self, barrier):
        greeted = 0
        for step in range(self.members):
            for turn in range(self.batches):
                if step or turn:
                    there = self.device(self.group, self.member_at(step), self.core_at(turn))
                    pl.semaphore_signal(barrier, inc=1, device_id=there, device_id_type=MESH)
                    greeted += 1
        for step in range(1, self.groups):
            for turn in range(self.batches):
                there = self.device(self.group_at(step), self.member, self.core_at(turn))
                pl.semaphore_signal(barrier, inc=1, device_id=there, device_id_type=MESH)
                greeted += 1
        return greeted


def send_copy(source, target, send_sem, recv_sem, there):
    return pltpu.make_async_remote_copy(
        src_ref=source,
        dst_ref=target,
        send_sem=send_sem,
        recv_sem=recv_sem,
        device_id=there,
        device_id_type=MESH,
    )


def slab(ref, dim, index, size):
    picks = [slice(None)] * len(ref.shape)
    picks[dim] = pl.ds(pl.multiple_of(index * size, size), size)
    return ref.at[tuple(picks)]


class WideExchange:
    @staticmethod
    def scratch(place_sizes, wide):
        groups, members, batches = place_sizes
        mates = members * batches
        dma = pltpu.SemaphoreType.DMA
        return [dma((mates,)), dma((mates,)), dma((wide.shape[1] // members,))]

    @staticmethod
    def shape(place_sizes, wide):
        groups, members, batches = place_sizes
        pieces, steps, series, channels = wide.shape
        return (steps // members, members * batches, pieces, series, channels // batches)

    def __init__(self, place, source, target, sems):
        self.place, self.source, self.target = place, source, target
        self.send_sem, self.recv_sem, self.local_sem = sems

    def hops(self):
        for step in range(self.place.members):
            for turn in range(self.place.batches):
                if step or turn:
                    yield step, turn

    def mate(self, step, turn):
        return self.place.core_at(turn) * self.place.members + self.place.member_at(step)

    def piece(self, one, step, turn):
        place = self.place
        steps, half = self.target.shape[0], self.target.shape[4]
        return slab(
            self.source.at[:, place.member_at(step) * steps + one], 2, place.core_at(turn), half
        )

    def own(self, one):
        return pltpu.make_async_copy(
            self.piece(one, 0, 0), self.target.at[one, self.mate(0, 0)], self.local_sem.at[one]
        )

    def whole(self, step, turn, pick):
        slot = turn * self.place.members + step
        block = self.target.at[:, pick]
        return send_copy(
            block,
            block,
            self.send_sem.at[slot],
            self.recv_sem.at[slot],
            self.place.device(
                self.place.group, self.place.member_at(step), self.place.core_at(turn)
            ),
        )

    def units(self):
        return [functools.partial(self.start, one) for one in range(self.target.shape[0])]

    def start(self, one):
        place = self.place
        self.own(one).start()
        for step, turn in self.hops():
            slot = turn * place.members + step
            send_copy(
                self.piece(one, step, turn),
                self.target.at[one, self.mate(0, 0)],
                self.send_sem.at[slot],
                self.recv_sem.at[slot],
                place.device(place.group, place.member_at(step), place.core_at(turn)),
            ).start()

    def wait(self):
        for one in range(self.target.shape[0]):
            self.own(one).wait()
        for step, turn in self.hops():
            self.whole(step, turn, self.mate(-step, -turn)).wait_recv()

    def drain(self):
        for step, turn in self.hops():
            self.whole(step, turn, self.mate(0, 0)).wait_send()


class NarrowGather:
    sems = 5

    @staticmethod
    def scratch(place_sizes, narrow):
        groups, members, batches = place_sizes
        dma = pltpu.SemaphoreType.DMA
        size = members * batches
        return [dma((members,)), dma((members,)), dma((size,)), dma((size,)), dma((1,))]

    def __init__(self, place, source, target, sems):
        self.place, self.source, self.target = place, source, target
        (self.link_send, self.link_recv, self.chip_send, self.chip_recv, self.local_sem) = sems

    def own(self):
        place = self.place
        pick = place.core * place.members + place.member
        return pltpu.make_async_copy(self.source, self.target.at[pick], self.local_sem.at[0])

    def link(self, step, pick_step):
        place = self.place
        pick = place.core * place.members + place.member_at(pick_step)
        return send_copy(
            self.source,
            self.target.at[pick],
            self.link_send.at[step],
            self.link_recv.at[step],
            place.device(place.group, place.member_at(step), place.core),
        )

    def chip(self, step, turn, source_core, target_core):
        place = self.place
        member = place.member_at(-step)
        slot = turn * place.members + step
        source = self.target.at[source_core * place.members + member] if step else self.source
        return send_copy(
            source,
            self.target.at[target_core * place.members + member],
            self.chip_send.at[slot],
            self.chip_recv.at[slot],
            place.device(place.group, place.member, place.core_at(turn)),
        )

    def start(self):
        place = self.place
        self.own().start()
        for step in range(1, place.members):
            self.link(step, 0).start()
        for turn in range(1, place.batches):
            self.chip(0, turn, place.core, place.core).start()

    def forward(self):
        place = self.place
        for step in range(1, place.members):
            self.link(step, -step).wait_recv()
            for turn in range(1, place.batches):
                self.chip(step, turn, place.core, place.core).start()

    def wait(self):
        place = self.place
        self.own().wait()
        for turn in range(1, place.batches):
            other = place.core_at(-turn)
            for step in range(place.members):
                self.chip(step, turn, place.core, other).wait_recv()

    def drain(self):
        place = self.place
        for step in range(1, place.members):
            self.link(step, 0).wait_send()
        for turn in range(1, place.batches):
            for step in range(place.members):
                self.chip(step, turn, place.core, place.core).wait_send()


class KernelProduct:
    sems = 6

    @staticmethod
    def scratch(place_sizes, kind, wide, narrow):
        groups, members, batches = place_sizes
        pieces, kernel, series, channels = wide.shape
        steps, rows = kernel // members, pieces * series
        half = channels // batches
        piece = (128, half) if kind == "down" else (half, 128)
        dma = pltpu.SemaphoreType.DMA
        return [
            pltpu.VMEM((channels, members * batches * rows), HALF_FLOAT),
            pltpu.VMEM((steps, channels, half), HALF_FLOAT),
            pltpu.VMEM((groups, steps) + piece, HALF_FLOAT),
            pltpu.VMEM((steps, 128, half), HALF_FLOAT),
            pltpu.VMEM((kernel, channels // (groups * members), half), HALF_FLOAT),
            dma((groups * batches,)),
            dma((groups * batches,)),
            dma((members,)),
            dma((members,)),
            dma((2,)),
        ]

    def __init__(self, place, kind, wide_in, narrow_in, out, scratch):
        self.place, self.kind, self.wide_in, self.narrow_in, self.out = (
            place,
            kind,
            wide_in,
            narrow_in,
            out,
        )
        (self.narrow_t, self.send, self.recv, self.total, self.gathered) = scratch[:5]
        (self.sz, self.rz, self.sf, self.rf, self.local) = scratch[5:]
        self.cores_per_group = place.groups // place.batches

    def multiply(self):
        mates, rows = self.narrow_in.shape[0], self.narrow_in.shape[1]
        self.narrow_t[...] = self.narrow_in[...].reshape(mates * rows, -1).T

        @pl.loop(0, self.wide_in.shape[0])
        def _(one):
            data = self.wide_in[one].reshape(mates * rows, -1)
            self.send[one] = dot_nn(self.narrow_t[...], data).astype(HALF_FLOAT)

    def chunk(self, group, core):
        if self.kind == "down":
            return slab(self.send, 1, group, 128)
        half = self.send.shape[1] // self.place.batches
        return slab(
            slab(self.send, 1, core, half), 2, lax.rem(group, self.cores_per_group), 128
        )

    def hops(self):
        place = self.place
        for step in range(place.groups):
            for turn in range(place.batches if self.kind == "up" else 1):
                yield step, turn

    def partial(self, step, turn, action):
        place = self.place
        group, core = place.group_at(step), place.core_at(turn)
        slot = step * place.batches + turn
        if step == 0 and turn == 0:
            copy = pltpu.make_async_copy(
                self.chunk(group, core), self.recv.at[place.group], self.local.at[0]
            )
            act = lambda: action(copy, True)
        else:
            copy = send_copy(
                self.chunk(group, core),
                self.recv.at[place.group],
                self.sz.at[slot],
                self.rz.at[slot],
                place.device(group, place.member, core),
            )
            act = lambda: action(copy, False)
        if self.kind == "down":
            act()
        else:
            pl.when(lax.div(group, self.cores_per_group) == place.core)(act)

    def start_partials(self):
        for step, turn in self.hops():
            self.partial(step, turn, lambda copy, local: copy.start())

    def sum_partials(self):
        place = self.place
        for step, turn in self.hops():
            group, core = place.group_at(-step), place.core_at(-turn)
            slot = step * place.batches + turn

            def act(step=step, turn=turn, group=group, slot=slot):
                if step == 0 and turn == 0:
                    pltpu.make_async_copy(
                        self.chunk(place.group, place.core),
                        self.recv.at[place.group],
                        self.local.at[0],
                    ).wait()
                else:
                    send_copy(
                        self.chunk(place.group, place.core),
                        self.recv.at[group],
                        self.sz.at[slot],
                        self.rz.at[slot],
                        place.device(place.group, place.member, place.core),
                    ).wait_recv()

            if self.kind == "down":
                act()
            else:
                pl.when(lax.div(place.group, self.cores_per_group) == core)(act)

        @pl.loop(0, self.total.shape[0])
        def _(one):
            value = self.recv[0, one].astype(FLOAT)
            for other in range(1, place.groups):
                value = value + self.recv[other, one].astype(FLOAT)
            value = value if self.kind == "down" else value.T
            self.total[one] = value.astype(HALF_FLOAT)

    def final(self, step, pick_step):
        place = self.place
        steps, width = self.total.shape[0], self.gathered.shape[1]
        source = slab(self.total, 1, place.member_at(step), width)
        target = slab(self.gathered, 0, place.member_at(pick_step), steps)
        if step == 0:
            return pltpu.make_async_copy(source, target, self.local.at[1])
        return send_copy(
            source,
            target,
            self.sf.at[step],
            self.rf.at[step],
            place.device(place.group, place.member_at(step), place.core),
        )

    def start_final(self):
        for step in range(self.place.members):
            self.final(step, 0).start()

    def finish(self):
        place = self.place
        self.final(0, 0).wait()
        for step in range(1, place.members):
            self.final(step, -step).wait_recv()
        self.out[...] = self.gathered[...].astype(FLOAT)
        for step in range(1, place.members):
            self.final(step, 0).wait_send()
        for step, turn in self.hops():
            if step or turn:
                self.partial(step, turn, lambda copy, local: copy.wait_send())


class MatrixSum:
    sems = 7

    @staticmethod
    def half_shape(place_sizes, kind, value):
        batches = place_sizes[2]
        shape = list(value.shape)
        if kind == "rows":
            shape[0] //= batches
        elif kind == "lanes":
            shape[-1] //= batches
        return tuple(shape)

    @staticmethod
    def piece_shape(place_sizes, kind, value):
        groups, members, batches = place_sizes
        shape = list(MatrixSum.half_shape(place_sizes, kind, value))
        dim = {"rows": 1, "lanes": len(shape) - 2, "whole": 0}[kind]
        shape[dim] //= groups * members
        return tuple(shape)

    @staticmethod
    def scratch(place_sizes, kind, value):
        groups, members, batches = place_sizes
        half = MatrixSum.half_shape(place_sizes, kind, value)
        piece = MatrixSum.piece_shape(place_sizes, kind, value)
        dma = pltpu.SemaphoreType.DMA
        return [
            pltpu.VMEM(half, value.dtype),
            pltpu.VMEM((batches,) + half, value.dtype),
            pltpu.VMEM((members, groups) + piece, value.dtype),
            pltpu.VMEM((groups,) + piece, value.dtype),
            pltpu.VMEM((groups,) + piece, value.dtype),
            dma((batches,)),
            dma((batches,)),
            dma((members * groups,)),
            dma((members * groups,)),
            dma((groups,)),
            dma((groups,)),
            dma((1 + groups,)),
        ]

    def __init__(self, place, kind, source, out, scratch):
        self.place, self.kind, self.source, self.out = place, kind, source, out
        (self.own, self.others, self.by_member, self.sums, self.by_group) = scratch[:5]
        (self.sb, self.rb, self.sm, self.rm, self.sg, self.rg, self.local) = scratch[5:]
        self.piece_dim = {"rows": 1, "lanes": len(self.own.shape) - 2, "whole": 0}[kind]

    def half(self, core):
        if self.kind == "rows":
            return slab(self.source, 0, core, self.own.shape[0])
        if self.kind == "lanes":
            return slab(self.source, len(self.own.shape) - 1, core, self.own.shape[-1])
        return self.source

    def cores(self, step, pick):
        place = self.place
        core = place.core_at(step)
        return send_copy(
            self.half(core),
            self.others.at[pick],
            self.sb.at[step],
            self.rb.at[step],
            place.device(place.group, place.member, core),
        )

    def load(self):
        return pltpu.make_async_copy(self.half(self.place.core), self.own, self.local.at[0])

    def start(self):
        self.load().start()
        for step in range(1, self.place.batches):
            self.cores(step, self.place.core).start()

    def piece(self, group, member):
        size = self.by_member.shape[2 + self.piece_dim]
        return slab(self.own, self.piece_dim, group * self.place.members + member, size)

    def members(self, step, pick_step, group):
        place = self.place
        member = place.member_at(step)
        slot = step * place.groups + group
        target = self.by_member.at[place.member_at(pick_step), group]
        if step == 0:
            return pltpu.make_async_copy(
                self.piece(group, member), target, self.local.at[1 + group]
            )
        return send_copy(
            self.piece(group, member),
            target,
            self.sm.at[slot],
            self.rm.at[slot],
            place.device(place.group, member, place.core),
        )

    def add_cores(self):
        place = self.place
        self.load().wait()
        for step in range(1, place.batches):
            self.cores(step, place.core_at(-step)).wait_recv()
        rows = self.own.shape[0]
        block = max(size for size in (1, 2, 4, 8, 16, 32, 64) if rows % size == 0)

        @pl.loop(0, rows // block)
        def _(index):
            pick = pl.ds(pl.multiple_of(index * block, block), block)
            value = self.own[pick].astype(FLOAT)
            for step in range(1, place.batches):
                value = value + self.others[place.core_at(step), pick].astype(FLOAT)
            self.own[pick] = value.astype(self.own.dtype)

        for step in range(place.members):
            for group in range(place.groups):
                self.members(step, 0, group).start()

    def groups(self, step, pick_step):
        place = self.place
        group = place.group_at(step)
        return send_copy(
            self.sums.at[group],
            self.by_group.at[place.group_at(pick_step)],
            self.sg.at[step],
            self.rg.at[step],
            place.device(group, place.member, place.core),
        )

    def add_members(self):
        place = self.place
        for step in range(place.members):
            for group in range(place.groups):
                if step == 0:
                    self.members(step, 0, group).wait()
                else:
                    self.members(step, -step, group).wait_recv()

        @pl.loop(0, place.groups)
        def _(group):
            value = self.by_member[0, group].astype(FLOAT)
            for other in range(1, place.members):
                value = value + self.by_member[other, group].astype(FLOAT)
            self.sums[group] = value.astype(self.sums.dtype)

        for step in range(1, place.groups):
            self.groups(step, 0).start()
        self.by_group[place.group] = self.sums[place.group]

    def finish(self):
        place = self.place
        for step in range(1, place.groups):
            self.groups(step, -step).wait_recv()
        value = self.by_group[0].astype(FLOAT)
        for other in range(1, place.groups):
            value = value + self.by_group[other].astype(FLOAT)
        self.out[...] = value
        for step in range(1, place.groups):
            self.groups(step, 0).wait_send()
        for step in range(1, place.members):
            for group in range(place.groups):
                self.members(step, 0, group).wait_send()
        for step in range(1, place.batches):
            self.cores(step, place.core).wait_send()


def remote_call(body, inputs, outputs, scratch, collective_id, flops, nbytes, name):
    def kernel(*refs):
        left = list(refs)
        named = {key: left.pop(0) for key in inputs}
        named.update({key: left.pop(0) for key in outputs})
        for key, shapes in scratch.items():
            named[key] = [left.pop(0) for _ in shapes]
        body(named)

    results = pl.pallas_call(
        kernel,
        out_shape=tuple(shape for shape, _ in outputs.values()),
        in_specs=[spec for _, spec in inputs.values()],
        out_specs=tuple(spec for _, spec in outputs.values()),
        scratch_shapes=[shape for shapes in scratch.values() for shape in shapes],
        compiler_params=pltpu.CompilerParams(
            collective_id=collective_id,
            has_side_effects=True,
            vmem_limit_bytes=63 * 1024 * 1024,
        ),
        cost_estimate=pl.CostEstimate(flops=flops, bytes_accessed=nbytes, transcendentals=0),
        name=name,
    )(*[value for value, _ in inputs.values()])
    return dict(zip(outputs, results))


def plane_sizes(channels):
    devices, batches = lax.axis_size("tm"), lax.axis_size("batch")
    groups = channels // 128
    if batches == 2 and channels % 256 == 0 and devices % groups == 0:
        return groups, devices // groups, batches
    return None


VMEM_SPEC = pl.BlockSpec(memory_space=pltpu.VMEM)
HBM_SPEC = pl.BlockSpec(memory_space=pl.ANY)


class SeriesGradient:
    @staticmethod
    def scratch(weights, outers, rim):
        steps, series, channels = outers[0].shape
        lead = 2 * rim + 8
        dma = pltpu.SemaphoreType.DMA
        rims = (rim, series, channels)
        return (
            [pltpu.VMEM(weight.shape, HALF_FLOAT) for weight in weights]
            + [pltpu.VMEM((steps + 2 * lead, series, channels), FLOAT) for _ in outers]
            + [pltpu.VMEM((channels // 128, steps * series, 128), FLOAT)]
            + [pltpu.VMEM(rims, FLOAT) for _ in range(4)]
            + [dma((4,)), dma((2,)), dma((2,))]
        )

    def __init__(self, weights, outers, out, scratch, halves, rim):
        self.weights, self.outers, self.out = weights, outers, out
        self.halves, self.rim = halves, rim
        count = len(weights)
        self.held, self.grads = scratch[:count], scratch[count : 2 * count]
        (self.result, self.low, self.high, self.before, self.after) = scratch[
            2 * count : 2 * count + 5
        ]
        (self.local, self.send, self.recv) = scratch[2 * count + 5 :]
        self.steps = outers[0].shape[0]
        self.series = outers[0].shape[1]
        self.lead = 2 * rim + 8
        self.me, self.core = lax.axis_index("tm"), lax.axis_index("batch")
        self.last = lax.axis_size("tm") - 1

    def greet(self, barrier):
        @pl.when(self.me > 0)
        def _():
            pl.semaphore_signal(
                barrier, inc=1, device_id=(self.core, self.me - 1), device_id_type=MESH
            )

        @pl.when(self.me < self.last)
        def _():
            pl.semaphore_signal(
                barrier, inc=1, device_id=(self.core, self.me + 1), device_id_type=MESH
            )

        return jnp.where(self.me > 0, 1, 0) + jnp.where(self.me < self.last, 1, 0)

    def loads(self, index):
        return (
            pltpu.make_async_copy(
                self.weights[index], self.held[index], self.local.at[2 * index]
            ),
            pltpu.make_async_copy(
                self.outers[index],
                self.grads[index].at[pl.ds(self.lead, self.steps)],
                self.local.at[2 * index + 1],
            ),
        )

    def start(self):
        for index in range(len(self.held)):
            for copy in self.loads(index):
                copy.start()
            grads = self.grads[index]
            zero = jnp.zeros((self.lead,) + grads.shape[1:], FLOAT)
            grads[: self.lead] = zero
            grads[self.lead + self.steps :] = zero

    def through_down(self, index, grad):
        for copy in self.loads(index):
            copy.wait()
        kernel = self.held[index].shape[0]
        pieces = self.steps // kernel
        grads = self.grads[index]

        @pl.loop(0, kernel)
        def _(one):
            value = dot_nt(grad, self.held[index][one])
            for piece in range(pieces):
                row = self.lead + piece * kernel + one
                grads[row] = (
                    grads[row] + value[piece * self.series : (piece + 1) * self.series]
                )

    def store(self, place, value, add=False):
        for lane in range(self.result.shape[0]):
            part = value[:, lane * 128 : lane * 128 + 128]
            self.result[lane, place] = self.result[lane, place] - part if add else part

    def adjoint(self):
        def means(index, sums):
            out, total = [], 0.0
            for grads, half, value in zip(self.grads, self.halves, sums):
                high = grads[index + (self.lead - self.rim + half)]
                low = grads[index + (self.lead - self.rim - half - 1)]
                value = value + high - low
                out.append(value)
                total = total + value * (1.0 / (2 * half + 1))
            return tuple(out), total

        def low_step(index, sums):
            sums, total = means(index, sums)
            self.low[index] = total
            return sums

        def step(index, sums):
            sums, total = means(index + self.rim, sums)
            value = self.grads[0][self.lead + index] + self.grads[1][self.lead + index]
            place = pl.ds(pl.multiple_of(index * self.series, self.series), self.series)
            self.store(place, value - total)
            return sums

        def high_step(index, sums):
            sums, total = means(index + (self.rim + self.steps), sums)
            self.high[index] = total
            return sums

        zero = jnp.zeros(self.low.shape[1:], FLOAT)
        sums = lax.fori_loop(0, self.rim, low_step, (zero, zero))
        sums = lax.fori_loop(0, self.steps, step, sums)
        lax.fori_loop(0, self.rim, high_step, sums)

    def edge(self, up):
        source, target = (self.high, self.before) if up else (self.low, self.after)
        index = 0 if up else 1
        return send_copy(
            source,
            target,
            self.send.at[index],
            self.recv.at[index],
            (self.core, self.me + 1 if up else self.me - 1),
        )

    def send_edges(self):
        pl.when(self.me < self.last)(lambda: self.edge(True).start())
        pl.when(self.me > 0)(lambda: self.edge(False).start())

    def finish(self):
        series = self.series
        rows, end = self.rim * series, self.steps * series

        @pl.when(self.me > 0)
        def _():
            self.edge(True).wait_recv()
            self.store(pl.ds(0, rows), self.before[...].reshape(rows, -1), True)

        @pl.when(self.me == 0)
        def _():
            total = self.low[0]
            for index in range(1, self.rim):
                total = total + self.low[index]
            self.store(pl.ds(0, series), total, True)

        @pl.when(self.me < self.last)
        def _():
            self.edge(False).wait_recv()
            self.store(pl.ds(end - rows, rows), self.after[...].reshape(rows, -1), True)

        @pl.when(self.me == self.last)
        def _():
            total = self.high[0]
            for index in range(1, self.rim):
                total = total + self.high[index]
            self.store(pl.ds(end - series, series), total, True)

        for one in range(self.out.shape[0]):
            for lane in range(self.result.shape[0]):
                value = self.result[lane, pl.ds(one, self.steps, stride=series), :]
                self.out[one, :, lane * 128 : lane * 128 + 128] = value.astype(HALF_FLOAT)
        pl.when(self.me < self.last)(lambda: self.edge(True).wait_send())
        pl.when(self.me > 0)(lambda: self.edge(False).wait_send())


def down_gradients(sizes, wides, narrows, vectors, weights, outers, halves, rim, count):
    groups, members, batches = sizes
    half = wides[0].shape[4]
    channels = half * batches
    inputs, outputs, scratch = {}, {}, {}
    for index, (wide, narrow) in enumerate(zip(wides, narrows)):
        steps = wide.shape[0] * members
        shape = jax.ShapeDtypeStruct(
            (wide.shape[2], steps, wide.shape[3], channels), HALF_FLOAT
        )
        inputs[f"wide{index}"] = (wide, VMEM_SPEC)
        inputs[f"narrow{index}"] = (narrow, HBM_SPEC)
        outputs[f"out{index}"] = (
            jax.ShapeDtypeStruct((steps, channels // (groups * members), half), FLOAT),
            VMEM_SPEC,
        )
        scratch[f"rows{index}"] = [
            pltpu.VMEM((members * batches,) + narrow.shape, HALF_FLOAT)
        ]
        scratch[f"gather{index}"] = NarrowGather.scratch(sizes, narrow)
        scratch[f"product{index}"] = KernelProduct.scratch(sizes, "down", shape, narrow)
    for index in range(len(wides)):
        inputs[f"weight{index}"] = (weights[index], HBM_SPEC)
        inputs[f"outer{index}"] = (outers[index], HBM_SPEC)
    scratch["series"] = SeriesGradient.scratch(weights, outers, rim)
    outputs["grad_series"] = (
        jax.ShapeDtypeStruct((count, outers[0].shape[0], channels), HALF_FLOAT),
        VMEM_SPEC,
    )
    inputs["vectors"] = (vectors, HBM_SPEC)
    outputs["vector_sum"] = (jax.ShapeDtypeStruct((1,) + vectors.shape[1:], FLOAT), VMEM_SPEC)
    scratch["vector"] = MatrixSum.scratch(sizes, "whole", vectors)

    def body(refs):
        place = Place(*sizes)
        back = SeriesGradient(
            [refs[f"weight{index}"] for index in range(len(wides))],
            [refs[f"outer{index}"] for index in range(len(wides))],
            refs["grad_series"],
            refs["series"],
            halves,
            rim,
        )
        barrier = pltpu.get_barrier_semaphore()
        pl.semaphore_wait(barrier, place.greet(barrier) + back.greet(barrier))
        gathers, products = [], []
        for index in range(len(wides)):
            gathers.append(
                NarrowGather(
                    place,
                    refs[f"narrow{index}"],
                    refs[f"rows{index}"][0],
                    refs[f"gather{index}"],
                )
            )
            products.append(
                KernelProduct(
                    place,
                    "down",
                    refs[f"wide{index}"],
                    refs[f"rows{index}"][0],
                    refs[f"out{index}"],
                    refs[f"product{index}"],
                )
            )
        total = MatrixSum(place, "whole", refs["vectors"], refs["vector_sum"], refs["vector"])
        for gather in gathers:
            gather.start()
        total.start()
        back.start()
        for gather in gathers:
            gather.forward()
        for gather, product in zip(gathers, products):
            gather.wait()
            product.multiply()
            product.start_partials()
        total.add_cores()
        mine = place.core * members + place.member
        for index in range(len(wides)):
            back.through_down(index, refs[f"rows{index}"][0][mine])
        total.add_members()
        back.adjoint()
        back.send_edges()
        for product in products:
            product.sum_partials()
            product.start_final()
        total.finish()
        back.finish()
        for product in products:
            product.finish()
        for gather in gathers:
            gather.drain()

    flops = sum(2 * wide.size * channels for wide in wides)
    results = remote_call(
        body, inputs, outputs, scratch, 2, flops, 8 * flops // channels, "down_gradients"
    )
    return [results["out0"], results["out1"]], results["vector_sum"], results["grad_series"]


def iso_gradient_kernel(spec_ref, specs_ref, grad_ref, grads_ref, out_ref):
    devices = spec_ref.shape[0] // 2
    spec, grad, turned = [], [], []
    for own, others, into in ((spec_ref, specs_ref, spec), (grad_ref, grads_ref, grad)):
        into.append(own[...])
        for index in range(others.shape[0]):
            into.append(others[index])
    for value in grad:
        turned.append(jnp.concatenate([value[devices:], -value[:devices]]))
    spec = jnp.concatenate(spec)
    for part, values in enumerate((grad, turned)):
        out_ref[0, part] = lax.dot_general(
            spec,
            jnp.concatenate(values),
            (((0,), (0,)), ((), ())),
            preferred_element_type=FLOAT,
        )


def iso_gradients(spec, specs, grad, grads, first, bins):
    rows, channels = 2 * lax.axis_size("tm"), grad.shape[1]
    half = spec.shape[1]
    others = specs.shape[0]
    return pl.pallas_call(
        iso_gradient_kernel,
        out_shape=jax.ShapeDtypeStruct((bins, 2, half, channels), FLOAT),
        grid=(bins,),
        in_specs=[
            pl.BlockSpec((rows, half), lambda i: (first + i, 0)),
            pl.BlockSpec((others, rows, half), lambda i: (0, first + i, 0)),
            pl.BlockSpec((rows, channels), lambda i: (first + i, 0)),
            pl.BlockSpec((others, rows, channels), lambda i: (0, first + i, 0)),
        ],
        out_specs=pl.BlockSpec((1, 2, half, channels), lambda i: (i, 0, 0, 0)),
        cost_estimate=pl.CostEstimate(
            flops=4 * bins * rows * (1 + others) * half * channels,
            bytes_accessed=8 * bins * half * channels,
            transcendentals=0,
        ),
        name="iso_gradients",
    )(spec, specs, grad, grads)


class Extra:
    def __init__(self, sizes):
        self.sizes = sizes
        self.inputs, self.outputs, self.scratch = {}, {}, {}

    def bind(self, refs):
        self.refs = refs
        self.place = Place(*self.sizes) if self.sizes else None

    def greet(self, barrier):
        return self.place.greet(barrier) if self.sizes else 0

    def start(self):
        pass

    def after_bins(self):
        pass

    def after_spec(self):
        pass

    def after_mixed(self):
        pass

    def after_signal(self):
        pass

    def finish(self):
        pass

    def run(self, share):
        count = max(1, round(share * self.unit_count))
        for _ in range(min(count, len(self.units))):
            self.units.pop(0)()


class ForwardExtra(Extra):
    def __init__(self, sizes, wides):
        super().__init__(sizes)
        self.count = len(wides) if sizes else 0
        for index in range(self.count):
            self.inputs[f"wide{index}"] = (wides[index], HBM_SPEC)
            self.outputs[f"gathered{index}"] = (
                jax.ShapeDtypeStruct(WideExchange.shape(sizes, wides[index]), HALF_FLOAT),
                HBM_SPEC,
            )
            self.scratch[f"exchange{index}"] = WideExchange.scratch(sizes, wides[index])

    def bind(self, refs):
        super().bind(refs)
        self.exchanges = [
            WideExchange(
                self.place, refs[f"wide{i}"], refs[f"gathered{i}"], refs[f"exchange{i}"]
            )
            for i in range(self.count)
        ]
        self.units = [unit for item in self.exchanges for unit in item.units()]
        self.unit_count = len(self.units)

    def start(self):
        self.run(0.15)

    def after_bins(self):
        self.run(0.55)

    def after_mixed(self):
        self.run(1.0)

    def finish(self):
        for item in self.exchanges:
            item.wait()
            item.drain()


class BackwardExtra(Extra):
    def __init__(self, sizes, spec, wides, narrows, matrices):
        super().__init__(sizes)
        self.batches = lax.axis_size("batch")
        others = jax.ShapeDtypeStruct((self.batches - 1,) + spec.shape, HALF_FLOAT)
        self.inputs["spec_forward"] = (spec, HBM_SPEC)
        self.outputs["specs"] = (others, HBM_SPEC)
        self.outputs["grads"] = (others, HBM_SPEC)
        dma = pltpu.SemaphoreType.DMA
        self.scratch["other_sems"] = [dma((self.batches,))] * 4
        self.count = len(wides) if sizes else 0
        self.kinds = [kind for kind, _ in matrices] if sizes else []
        for i in range(self.count):
            wide, narrow = wides[i], narrows[i]
            groups, members, batches = sizes
            channels = narrow.shape[1]
            self.inputs[f"wide{i}"] = (wide, HBM_SPEC)
            self.inputs[f"narrow{i}"] = (narrow, HBM_SPEC)
            self.outputs[f"up{i}"] = (
                jax.ShapeDtypeStruct(
                    (wide.shape[1], channels // (groups * members), channels // batches), FLOAT
                ),
                VMEM_SPEC,
            )
            self.scratch[f"wide_in{i}"] = [
                pltpu.VMEM(WideExchange.shape(sizes, wide), HALF_FLOAT)
            ]
            self.scratch[f"rows{i}"] = [
                pltpu.VMEM((members * batches,) + narrow.shape, HALF_FLOAT)
            ]
            self.scratch[f"exchange{i}"] = WideExchange.scratch(sizes, wide)
            self.scratch[f"gather{i}"] = NarrowGather.scratch(sizes, narrow)
            self.scratch[f"product{i}"] = KernelProduct.scratch(sizes, "up", wide, narrow)
        for i, kind in enumerate(self.kinds):
            value = matrices[i][1]
            self.inputs[f"matrix{i}"] = (value, HBM_SPEC)
            self.outputs[f"matrix_sum{i}"] = (
                jax.ShapeDtypeStruct(MatrixSum.piece_shape(sizes, kind, value), FLOAT),
                VMEM_SPEC,
            )
            self.scratch[f"sum{i}"] = MatrixSum.scratch(sizes, kind, value)

    def bind(self, refs):
        super().bind(refs)
        self.exchanges, self.gathers, self.products = [], [], []
        for i in range(self.count):
            wide_in, rows = refs[f"wide_in{i}"][0], refs[f"rows{i}"][0]
            self.exchanges.append(
                WideExchange(self.place, refs[f"wide{i}"], wide_in, refs[f"exchange{i}"])
            )
            self.gathers.append(
                NarrowGather(self.place, refs[f"narrow{i}"], rows, refs[f"gather{i}"])
            )
            self.products.append(
                KernelProduct(self.place, "up", wide_in, rows, refs[f"up{i}"], refs[f"product{i}"])
            )
        self.sums = [
            MatrixSum(
                self.place, kind, refs[f"matrix{i}"], refs[f"matrix_sum{i}"], refs[f"sum{i}"]
            )
            for i, kind in enumerate(self.kinds)
        ]

    def other(self, index, turn):
        source, target = (
            (self.refs["spec_forward"], self.refs["specs"]),
            (self.refs["spec"], self.refs["grads"]),
        )[index]
        sems = self.refs["other_sems"]
        core = lax.rem(lax.axis_index("batch") + turn, self.batches)
        return send_copy(
            source,
            target.at[turn - 1],
            sems[2 * index].at[turn],
            sems[2 * index + 1].at[turn],
            (core, lax.axis_index("tm")),
        )

    def start(self):
        self.units = [unit for item in self.exchanges for unit in item.units()]
        self.unit_count = len(self.units)
        for turn in range(1, self.batches):
            self.other(0, turn).start()
        for item in self.gathers + self.sums:
            item.start()

    def after_bins(self):
        self.run(0.6)
        for item in self.gathers:
            item.forward()

    def after_mixed(self):
        self.run(0.3)

    def after_spec(self):
        for turn in range(1, self.batches):
            self.other(1, turn).start()

    def after_signal(self):
        self.run(1.0)
        for exchange, gather, product in zip(self.exchanges, self.gathers, self.products):
            exchange.wait()
            gather.wait()
            product.multiply()
            product.start_partials()
        for item in self.sums:
            item.add_cores()

    def finish(self):
        for item in self.sums:
            item.add_members()
        for item in self.products:
            item.sum_partials()
            item.start_final()
        for item in self.sums + self.products:
            item.finish()
        for item in self.exchanges + self.gathers:
            item.drain()
        for index in range(2):
            for turn in range(1, self.batches):
                self.other(index, turn).wait()


def spectral(values, weights, back, extra):
    devices, batches = lax.axis_size("tm"), lax.axis_size("batch")
    pieces_list = tuple(value.shape[1] for value in values)
    count, _, channels = values[0].shape
    wide = [round_up(pieces, 8) for pieces in pieces_list]
    per_time, per_bin = sum(wide), 2 * sum(wide)
    assert count <= devices and per_time % 16 == 0
    packed = jnp.concatenate(
        [
            jnp.pad(value, ((0, 0), (0, room - value.shape[1]), (0, 0)))
            for value, room in zip(values, wide)
        ],
        axis=1,
    ).reshape(count * per_time, channels)
    constants = spectral_constants(devices, pieces_list)
    rows_time, rows_bin = devices * per_time, devices * per_bin
    dma = pltpu.SemaphoreType.DMA
    inputs = {"x": (packed, HBM_SPEC)}
    for index, weight in enumerate(weights):
        inputs[f"weight{index}"] = (weight, HBM_SPEC)
    for key, value in zip(("table", "inverse", "move", "unmove"), constants):
        inputs[key] = (value, VMEM_SPEC)
    outputs = {
        "spec": (jax.ShapeDtypeStruct((rows_bin, channels), HALF_FLOAT), VMEM_SPEC),
        "signal": (jax.ShapeDtypeStruct((count * per_time, channels), FLOAT), VMEM_SPEC),
    }
    scratch = {
        "buffers": [pltpu.VMEM((rows_time, channels), HALF_FLOAT)]
        + [pltpu.VMEM((rows_bin, channels), HALF_FLOAT)] * 5
        + [pltpu.VMEM((rows_time, channels), FLOAT)]
        + [
            pltpu.VMEM((weight.shape[0], 2, weight.shape[2] * batches, channels), HALF_FLOAT)
            for weight in weights
        ],
        "sems": [dma((devices,))] * 8 + [dma((2, batches)), dma((2, batches)), dma((3,))],
    }
    inputs.update(extra.inputs)
    outputs.update(extra.outputs)
    scratch.update(extra.scratch)
    sizes = (devices, batches, count, pieces_list)

    def body(refs):
        extra.bind(refs)
        spectral_body(sizes, back, refs, extra)

    results = remote_call(
        body,
        inputs,
        outputs,
        scratch,
        1 if back else 0,
        2 * rows_bin * channels * channels * 4,
        4 * channels * channels * sum(pieces_list),
        "spectral_back" if back else "spectral_forward",
    )
    signal = results["signal"].reshape(count, per_time, channels)
    signals, offset = [], 0
    for pieces, room in zip(pieces_list, wide):
        signals.append(signal[:, offset : offset + pieces])
        offset += room
    return results, signals


def by_time(values):
    turned = jnp.swapaxes(values, 0, 1)
    extra = -turned.shape[1] % 16
    return jnp.pad(turned, ((0, 0), (0, extra)) + ((0, 0),) * (turned.ndim - 2))


def by_series(values, count):
    return jnp.swapaxes(values[:, :count], 0, 1)


def neighbours(low_side, high_side):
    count = lax.axis_size("tm")
    onward = [(i, i + 1) for i in range(count - 1)]
    return (
        lax.ppermute(high_side, "tm", onward),
        lax.ppermute(low_side, "tm", [(j, i) for i, j in onward]),
    )


def window_sum(values, first, width, count):
    total, level, size = None, values, 1
    while width:
        if width & 1:
            part = level[first : first + count]
            total = part if total is None else total + part
            first += size
        width >>= 1
        if width:
            level = level[:-size] + level[size:]
            size *= 2
    return total


def seasonal_parts(series, halves, rim):
    steps = series.shape[0]
    before, after = neighbours(series[:rim], series[steps - rim :])
    position = lax.axis_index("tm")
    before = jnp.where(position == 0, jnp.broadcast_to(series[:1], before.shape), before)
    is_final = position == lax.axis_size("tm") - 1
    after = jnp.where(is_final, jnp.broadcast_to(series[-1:], after.shape), after)
    wide = jnp.concatenate([before, series, after]).astype(FLOAT)
    parts = []
    for half in halves:
        mean = window_sum(wide, rim - half, 2 * half + 1, steps) / (2 * half + 1)
        parts.append((series.astype(FLOAT) - mean).astype(HALF_FLOAT))
    return parts


def series_gradient(grads, halves, rim):
    steps = grads[0].shape[0]
    wide = 0.0
    for grad, half in zip(grads, halves):
        padded = jnp.pad(grad, ((2 * rim, 2 * rim), (0, 0), (0, 0)))
        wide = wide + window_sum(padded, rim - half, 2 * half + 1, steps + 2 * rim) / (
            2 * half + 1
        )
    low_rim, high_rim = wide[:rim], wide[rim + steps :]
    before, after = neighbours(low_rim, high_rim)
    position = lax.axis_index("tm")
    is_final = position == lax.axis_size("tm") - 1
    low_sum = jnp.pad(jnp.sum(low_rim, axis=0, keepdims=True), ((0, rim - 1), (0, 0), (0, 0)))
    high_sum = jnp.pad(jnp.sum(high_rim, axis=0, keepdims=True), ((rim - 1, 0), (0, 0), (0, 0)))
    before = jnp.where(position == 0, low_sum, before)
    after = jnp.where(is_final, high_sum, after)
    middle = jnp.zeros((steps - 2 * rim,) + before.shape[1:], FLOAT)
    edges = jnp.concatenate([before, middle, after])
    return (sum(grads) - wide[rim : rim + steps] - edges).astype(HALF_FLOAT)


def step_block(kernel):
    return next(size for size in (4, 3, 2, 1) if kernel % size == 0)


def row_spec(block):
    return pl.BlockSpec(block, lambda i: (0,) * len(block))


def steps_spec(values, block):
    pieces, _, series, channels = values.shape
    return pl.BlockSpec((pieces, block, series, channels), lambda i: (0, i, 0, 0))


def weight_spec(weight, block):
    return pl.BlockSpec((block,) + weight.shape[1:], lambda i: (i, 0, 0))


def local_call(kernel, grid, inputs, outputs, flops, nbytes, name):
    return pl.pallas_call(
        kernel,
        out_shape=tuple(shape for shape, _ in outputs),
        grid=(grid,),
        in_specs=[spec for _, spec in inputs],
        out_specs=tuple(spec for _, spec in outputs),
        compiler_params=pltpu.CompilerParams(vmem_limit_bytes=48 * 1024 * 1024),
        cost_estimate=pl.CostEstimate(
            flops=flops, bytes_accessed=nbytes, transcendentals=0
        ),
        name=name,
    )(*[value for value, _ in inputs])


def down_kernel(x_ref, w_ref, b_ref, out_ref):
    step = pl.program_id(0)

    @pl.when(step == 0)
    def _():
        out_ref[...] = jnp.broadcast_to(b_ref[...], out_ref.shape)

    total = out_ref[...]
    for one in range(w_ref.shape[0]):
        total = total + dot_nn(x_ref[:, one].reshape(total.shape), w_ref[one])
    out_ref[...] = total

    @pl.when(step == pl.num_programs(0) - 1)
    def _():
        out_ref[...] = jnp.tanh(out_ref[...])


def down_layer(seasonal, weight, bias_row):
    pieces, kernel, series, channels = seasonal.shape
    block = step_block(kernel)
    rows = pieces * series
    (down_act,) = local_call(
        down_kernel,
        kernel // block,
        [
            (seasonal, steps_spec(seasonal, block)),
            (weight, weight_spec(weight, block)),
            (bias_row[None], row_spec((1, channels))),
        ],
        [(jax.ShapeDtypeStruct((rows, channels), FLOAT), row_spec((rows, channels)))],
        2 * seasonal.size * channels,
        2 * (seasonal.size + weight.size),
        "down_layer",
    )
    return down_act


def turn_kernel(x_ref, out_ref):
    out_ref[...] = pltpu.einshape("mhd->hmd", x_ref[...])


def kernel_major(weight):
    channels, kernel, outs = weight.shape
    if kernel % 8:
        return jnp.swapaxes(weight, 0, 1)
    block = 64
    (turned,) = local_call(
        turn_kernel,
        channels // block,
        [(weight, pl.BlockSpec((block, kernel, outs), lambda i: (i, 0, 0)))],
        [
            (
                jax.ShapeDtypeStruct((kernel, channels, outs), weight.dtype),
                pl.BlockSpec((kernel, block, outs), lambda i: (0, i, 0)),
            )
        ],
        0,
        4 * weight.size,
        "kernel_major",
    )
    return turned


def normed(values):
    center = values - jnp.mean(values, axis=-1, keepdims=True)
    spread = jnp.mean(center * center, axis=-1, keepdims=True)
    scale = lax.rsqrt(spread + EPSILON)
    return center * scale, scale


def normed_back(grad, hat, scale):
    return (
        grad
        - jnp.mean(grad, axis=-1, keepdims=True)
        - hat * jnp.mean(grad * hat, axis=-1, keepdims=True)
    ) * scale


def up_kernel(inner_ref, x_ref, w_ref, rows_ref, act_ref, out_ref):
    bias_row, gain_row, shift_row = (rows_ref[i : i + 1] for i in range(3))
    inner = inner_ref[...]
    for one in range(w_ref.shape[0]):
        act = jnp.tanh(dot_nn(inner, w_ref[one]) + bias_row)
        hat, _ = normed(act + x_ref[:, one].reshape(act.shape).astype(FLOAT))
        act_ref[:, one] = act.reshape(act_ref.shape[0], act_ref.shape[2], act_ref.shape[3])
        out = (hat * gain_row + shift_row).astype(HALF_FLOAT)
        out_ref[:, one] = out.reshape(out_ref.shape[0], out_ref.shape[2], out_ref.shape[3])


def up_layer(inner, seasonal, weight, bias_row, gain_row, shift_row):
    pieces, kernel, series, channels = seasonal.shape
    block = step_block(kernel)
    rows = jnp.stack([bias_row, gain_row, shift_row])
    return local_call(
        up_kernel,
        kernel // block,
        [
            (inner, row_spec(inner.shape)),
            (seasonal, steps_spec(seasonal, block)),
            (weight, weight_spec(weight, block)),
            (rows, row_spec(rows.shape)),
        ],
        [
            (jax.ShapeDtypeStruct(seasonal.shape, FLOAT), steps_spec(seasonal, block)),
            (jax.ShapeDtypeStruct(seasonal.shape, HALF_FLOAT), steps_spec(seasonal, block)),
        ],
        2 * seasonal.size * channels,
        8 * seasonal.size + 2 * weight.size,
        "up_layer",
    )


def up_back_kernel(
    grad_ref, merge_ref, act_ref, x_ref, w_ref, gain_ref, outer_ref, up_ref, inner_ref, sums_ref
):
    @pl.when(pl.program_id(0) == 0)
    def _():
        inner_ref[...] = jnp.zeros_like(inner_ref)
        sums_ref[...] = jnp.zeros_like(sums_ref)

    shape = inner_ref.shape
    block = (x_ref.shape[0], x_ref.shape[2], x_ref.shape[3])
    gain_row = gain_ref[...]
    total = inner_ref[...]
    sums = [sums_ref[i : i + 1] for i in range(3)]
    for one in range(w_ref.shape[0]):
        grad = dot_nt(grad_ref[:, one].reshape(shape), merge_ref[...])
        act = act_ref[:, one].reshape(shape)
        hat, scale = normed(act + x_ref[:, one].reshape(shape).astype(FLOAT))
        outer = normed_back(grad * gain_row, hat, scale)
        up = (outer * (1.0 - act * act)).astype(HALF_FLOAT)
        total = total + dot_nt(up, w_ref[one])
        outer_ref[:, one] = outer.reshape(block)
        up_ref[:, one] = up.reshape(block)
        for i, value in enumerate((up.astype(FLOAT), grad * hat, grad)):
            sums[i] = sums[i] + jnp.sum(value, axis=0, keepdims=True)
    inner_ref[...] = total
    for i in range(3):
        sums_ref[i : i + 1] = sums[i]


def up_layer_back(grad, merge, act, seasonal, weight, gain_row):
    pieces, kernel, series, channels = seasonal.shape
    block = step_block(kernel)
    rows = pieces * series
    spec = steps_spec(seasonal, block)
    return local_call(
        up_back_kernel,
        kernel // block,
        [
            (grad, spec),
            (merge, row_spec(merge.shape)),
            (act, spec),
            (seasonal, spec),
            (weight, weight_spec(weight, block)),
            (gain_row[None], row_spec((1, channels))),
        ],
        [
            (jax.ShapeDtypeStruct(seasonal.shape, FLOAT), spec),
            (jax.ShapeDtypeStruct(seasonal.shape, HALF_FLOAT), spec),
            (jax.ShapeDtypeStruct((rows, channels), FLOAT), row_spec((rows, channels))),
            (jax.ShapeDtypeStruct((8, channels), FLOAT), row_spec((8, channels))),
        ],
        4 * seasonal.size * channels,
        14 * seasonal.size + 2 * weight.size,
        "up_layer_back",
    )


def down_back_kernel(grad_ref, w_ref, outer_ref, out_ref):
    grad = grad_ref[...]
    block = (out_ref.shape[0], out_ref.shape[2], out_ref.shape[3])
    for one in range(w_ref.shape[0]):
        out_ref[:, one] = dot_nt(grad, w_ref[one]).reshape(block) + outer_ref[:, one]


def down_layer_back(grad, weight, outer):
    pieces, kernel, series, channels = outer.shape
    block = step_block(kernel)
    spec = steps_spec(outer, block)
    (seasonal_grad,) = local_call(
        down_back_kernel,
        kernel // block,
        [(grad, row_spec(grad.shape)), (weight, weight_spec(weight, block)), (outer, spec)],
        [(jax.ShapeDtypeStruct(outer.shape, FLOAT), spec)],
        2 * outer.size * channels,
        8 * outer.size + 2 * weight.size,
        "down_layer_back",
    )
    return seasonal_grad


class Branch:
    def __init__(self, seasonal, down_weight, up_weight, bias_rows, gain_row, shift_row, count):
        steps, series, channels = seasonal.shape
        self.kernel = down_weight.shape[0]
        self.pieces = steps // self.kernel
        self.count, self.series = count, series
        self.seasonal = seasonal.reshape(self.pieces, self.kernel, series, channels)
        self.down_weight, self.up_weight = down_weight, up_weight
        self.bias_rows, self.gain_row, self.shift_row = bias_rows, gain_row, shift_row
        self.down_act = down_layer(self.seasonal, down_weight, bias_rows[0])
        self.down_low = self.down_act.astype(HALF_FLOAT)

    def to_series(self, rows):
        return by_series(rows.reshape(self.pieces, self.series, -1), self.count)

    def from_series(self, values):
        return by_time(values).reshape(self.pieces * self.series, -1)

    def up(self, iso_out):
        self.iso_act = jnp.tanh(self.from_series(iso_out) + self.bias_rows[1])
        self.inner_in = self.iso_act + self.down_low.astype(FLOAT)
        self.inner_low = layer_norm(self.inner_in, self.gain_row, self.shift_row).astype(
            HALF_FLOAT
        )
        self.act, out = up_layer(
            self.inner_low,
            self.seasonal,
            self.up_weight,
            self.bias_rows[2],
            self.gain_row,
            self.shift_row,
        )
        return out.reshape(-1, out.shape[3])

    def up_back(self, grad_merged, merge):
        self.outer, self.grad_up, grad_inner, sums = up_layer_back(
            grad_merged.reshape(self.seasonal.shape),
            merge,
            self.act,
            self.seasonal,
            self.up_weight,
            self.gain_row,
        )
        _, inner_pull = jax.vjp(layer_norm, self.inner_in, self.gain_row, self.shift_row)
        self.grad_inner_in, gain_inner, shift_inner = inner_pull(grad_inner)
        grad_iso = self.grad_inner_in * (1.0 - self.iso_act * self.iso_act)
        self.iso_sum, self.up_sum = jnp.sum(grad_iso, axis=0), sums[0]
        self.gain_sum, self.shift_sum = sums[1] + gain_inner, sums[2] + shift_inner
        return grad_iso.astype(HALF_FLOAT)

    def down_back(self, grad_signal):
        grad_down = self.from_series(grad_signal) + self.grad_inner_in
        self.grad_down = (grad_down * (1.0 - self.down_act * self.down_act)).astype(HALF_FLOAT)
        self.down_sum = jnp.sum(self.grad_down.astype(FLOAT), axis=0)

    def seasonal_back(self):
        grad = down_layer_back(self.grad_down, self.down_weight, self.outer)
        return grad.reshape(-1, self.series, grad.shape[3])


def batch_split(values, split, join):
    return lax.all_to_all(values, "batch", split_axis=split, concat_axis=join, tiled=True)


def time_sum(values, dim):
    return lax.psum_scatter(
        values.astype(HALF_FLOAT), "tm", scatter_dimension=dim, tiled=True
    ).astype(FLOAT)


def plain_gradients(wides, narrows, downs):
    results = []
    for wide, narrow, down in zip(wides, narrows, downs):
        wide = jnp.swapaxes(wide, 0, 1).reshape(wide.shape[1], -1, wide.shape[3])
        if down:
            wide, narrow = batch_split(wide, 2, 1), lax.all_gather(narrow, "batch", tiled=True)
            value = jnp.einsum("knc,nd->kcd", wide, narrow, preferred_element_type=FLOAT)
        else:
            wide = lax.all_gather(wide, "batch", axis=1, tiled=True)
            narrow = batch_split(narrow, 1, 0)
            value = jnp.einsum("nd,knc->dkc", narrow, wide, preferred_element_type=FLOAT)
        results.append(time_sum(value, 2))
    return results


def plain_sums(matrices):
    results = []
    for kind, value in matrices:
        batch_dim, time_dim = (0, 1) if kind == "rows" else (value.ndim - 1, value.ndim - 2)
        value = lax.psum_scatter(
            value.astype(FLOAT), "batch", scatter_dimension=batch_dim, tiled=True
        )
        results.append(time_sum(value, time_dim))
    return results


def per_device(
    series_in,
    out_cotangent,
    out_mask,
    down_twelve,
    down_sixteen,
    iso_twelve,
    iso_sixteen,
    up_twelve,
    up_sixteen,
    branch_bias,
    merge_weight,
    hidden_weight,
    hidden_bias,
    output_weight,
    head_bias,
    norm_gain,
    norm_shift,
):
    series_dev, step_count, channels = series_in.shape
    halves = (down_twelve.shape[0] // 2, down_sixteen.shape[0] // 2)
    rim = max(halves)
    biases = branch_bias.astype(FLOAT)
    gains = norm_gain.astype(FLOAT)
    shifts = norm_shift.astype(FLOAT)
    heads = head_bias.astype(FLOAT)
    seasonals = seasonal_parts(by_time(series_in), halves, rim)
    branches = [
        Branch(
            seasonals[k],
            (down_twelve, down_sixteen)[k],
            kernel_major((up_twelve, up_sixteen)[k]),
            (biases[k], biases[2 + k], biases[4 + k]),
            gains[0],
            shifts[0],
            series_dev,
        )
        for k in range(2)
    ]
    iso_weights = (iso_twelve, iso_sixteen)
    sizes = plane_sizes(channels)
    seasonal_steps = [branch.seasonal for branch in branches]
    forward, iso_outs = spectral(
        [branch.to_series(branch.down_low) for branch in branches],
        iso_weights,
        False,
        ForwardExtra(sizes, seasonal_steps),
    )
    outs = [branch.up(iso_out) for branch, iso_out in zip(branches, iso_outs)]
    row_count = outs[0].shape[0]
    merged = dot_nn(outs[0], merge_weight[0]) + dot_nn(outs[1], merge_weight[1]) + heads[0]
    first_low = layer_norm(merged, gains[1], shifts[1]).astype(HALF_FLOAT)
    hidden_pre = jnp.dot(
        first_low, hidden_weight, preferred_element_type=FLOAT
    ) + hidden_bias.astype(FLOAT)
    hidden_low = jax.nn.gelu(hidden_pre).astype(HALF_FLOAT)
    final_in = merged + (
        jnp.dot(hidden_low, output_weight, preferred_element_type=FLOAT) + heads[1]
    )
    mask_rows = by_time(out_mask.astype(FLOAT)).reshape(row_count, 1)
    result = by_series(
        (layer_norm(final_in, gains[2], shifts[2]) * mask_rows)
        .astype(HALF_FLOAT)
        .reshape(step_count, -1, channels),
        series_dev,
    )
    grad_result = by_time(out_cotangent).astype(FLOAT).reshape(row_count, channels) * mask_rows
    normed_final, final_pull = jax.vjp(layer_norm, final_in, gains[2], shifts[2])
    grad_final, gain_final, shift_final = final_pull(grad_result)
    grad_feed = grad_final.astype(HALF_FLOAT)
    grad_output_weight = jnp.einsum(
        "nd,nf->df", grad_feed, hidden_low, preferred_element_type=FLOAT
    ).astype(HALF_FLOAT)
    grad_output_bias = jnp.sum(grad_feed.astype(FLOAT), axis=0)
    grad_hidden_low = jnp.einsum(
        "nd,fd->nf", grad_feed, output_weight, preferred_element_type=FLOAT
    )
    gelu_value, gelu_pull = jax.vjp(jax.nn.gelu, hidden_pre)
    grad_hidden_pre = gelu_pull(grad_hidden_low)[0].astype(HALF_FLOAT)
    grad_hidden_weight = jnp.einsum(
        "nd,nf->df", first_low, grad_hidden_pre, preferred_element_type=FLOAT
    ).astype(HALF_FLOAT)
    grad_hidden_bias = jnp.sum(grad_hidden_pre.astype(FLOAT), axis=0)
    grad_first = jnp.einsum(
        "nf,df->nd", grad_hidden_pre, hidden_weight, preferred_element_type=FLOAT
    )
    normed_first, first_pull = jax.vjp(layer_norm, merged, gains[1], shifts[1])
    grad_merged_norm, gain_first, shift_first = first_pull(grad_first)
    grad_merged = (grad_final + grad_merged_norm).astype(HALF_FLOAT)
    grad_merge_bias = jnp.sum(grad_merged.astype(FLOAT), axis=0)
    grad_merge_weight = jnp.stack(
        [
            jnp.einsum("ne,nd->ed", grad_merged, out, preferred_element_type=FLOAT)
            for out in outs
        ]
    ).astype(HALF_FLOAT)
    grad_isos = [branches[k].up_back(grad_merged, merge_weight[k]) for k in range(2)]
    matrices = (
        ("rows", grad_hidden_weight),
        ("lanes", grad_output_weight),
        ("lanes", grad_merge_weight),
    )
    up_wides = [branch.grad_up for branch in branches]
    up_narrows = [branch.inner_low for branch in branches]
    backward, grad_signals = spectral(
        [branch.to_series(grad) for branch, grad in zip(branches, grad_isos)],
        iso_weights,
        True,
        BackwardExtra(sizes, forward["spec"], up_wides, up_narrows, matrices),
    )
    half = channels // lax.axis_size("batch")
    core = lax.axis_index("batch")
    spec_half = lax.dynamic_slice_in_dim(forward["spec"], core * half, half, axis=1)
    specs_half = lax.dynamic_slice_in_dim(backward["specs"], core * half, half, axis=2)
    iso_parts, first = [], 0
    for bins in (branches[0].pieces, branches[1].pieces):
        iso_parts.append(
            iso_gradients(
                spec_half, specs_half, backward["spec"], backward["grads"], first, bins
            )
        )
        first += round_up(bins, 8)
    for k in range(2):
        branches[k].down_back(grad_signals[k])
    vectors = jnp.stack(
        [
            branches[0].down_sum,
            branches[1].down_sum,
            branches[0].iso_sum,
            branches[1].iso_sum,
            branches[0].up_sum,
            branches[1].up_sum,
            branches[0].gain_sum + branches[1].gain_sum,
            gain_first,
            gain_final,
            branches[0].shift_sum + branches[1].shift_sum,
            shift_first,
            shift_final,
            grad_merge_bias,
            grad_output_bias,
        ]
    )
    devices = lax.axis_size("tm")
    vector_count = vectors.shape[0]
    packed = jnp.concatenate(
        [
            vectors.reshape(vector_count, devices, -1).transpose(1, 0, 2).reshape(devices, -1),
            grad_hidden_bias.reshape(devices, -1),
        ],
        axis=1,
    )
    width = channels // devices
    down_narrows = [branch.grad_down for branch in branches]
    if sizes:
        extent = packed.shape[1]
        packed = jnp.pad(packed, ((0, 0), (0, -extent % 1024))).reshape(devices, -1, 128)
        downs, packed, grad_series = down_gradients(
            sizes,
            (forward["gathered0"], forward["gathered1"]),
            down_narrows,
            packed,
            (down_twelve, down_sixteen),
            [branch.outer.reshape(step_count, -1, channels) for branch in branches],
            halves,
            rim,
            series_dev,
        )
        packed = packed.reshape(-1)[:extent]
        downs = [jnp.transpose(value, (0, 2, 1)) for value in downs]
        ups = [jnp.transpose(backward[key], (2, 0, 1)) for key in ("up0", "up1")]
        sums = [backward[f"matrix_sum{i}"] for i in range(3)]
    else:
        packed = lax.psum(
            lax.psum_scatter(packed, "tm", scatter_dimension=0, tiled=True), "batch"
        )[0]
        grad_seasonals = [branch.seasonal_back() for branch in branches]
        grad_series = by_series(series_gradient(grad_seasonals, halves, rim), series_dev)
        downs = plain_gradients(seasonal_steps, down_narrows, (True, True))
        ups = plain_gradients(up_wides, up_narrows, (False, False))
        sums = plain_sums(matrices)
    rows = packed[: vector_count * width].reshape(vector_count, width)
    vector_parts = (
        rows[:6],
        packed[vector_count * width :],
        rows[12:14],
        rows[6:9],
        rows[9:12],
    )
    return (
        result,
        grad_series,
        downs[0],
        downs[1],
        iso_parts[0],
        iso_parts[1],
        ups[0],
        ups[1],
        vector_parts[0],
        jnp.swapaxes(sums[2], 1, 2),
        sums[0],
        vector_parts[1],
        sums[1].T,
        vector_parts[2],
        vector_parts[3],
        vector_parts[4],
    )


def solution(mesh):
    placed = (
        P("batch", "tm", None),
        P("batch", "tm", None),
        P("batch", "tm"),
        P(),
        P(),
        P("tm", None, "batch", None),
        P("tm", None, "batch", None),
        P(),
        P(),
        P(),
        P(),
        P(),
        P(),
        P(),
        P(),
        P(),
        P(),
    )
    return jax.shard_map(
        per_device,
        mesh=mesh,
        in_specs=placed,
        out_specs=(
            P("batch", "tm", None),
            P("batch", "tm", None),
            P(None, "batch", "tm"),
            P(None, "batch", "tm"),
            P("tm", None, "batch", None),
            P("tm", None, "batch", None),
            P("batch", None, "tm"),
            P("batch", None, "tm"),
            P(None, "tm"),
            P(None, "batch", "tm"),
            P("batch", "tm"),
            P("tm"),
            P("batch", "tm"),
            P(None, "tm"),
            P(None, "tm"),
            P(None, "tm"),
        ),
        check_vma=False,
    )
```

```python
import functools
import math

import jax
import jax.numpy as jnp
import numpy as np
from jax import lax
from jax.experimental import pallas as pl
from jax.experimental.pallas import tpu as pltpu
from jax.sharding import PartitionSpec as P

FLOAT = jnp.float32
HALF_FLOAT = jnp.bfloat16
HIGHEST = lax.Precision.HIGHEST
EPSILON = 1e-05
MESH = pl.DeviceIdType.MESH


def layer_norm(values, gain_row, bias_row):
    center = values - jnp.mean(values, axis=-1, keepdims=True)
    spread = jnp.mean(center * center, axis=-1, keepdims=True)
    return center * lax.rsqrt(spread + EPSILON) * gain_row + bias_row


def round_up(value, multiple):
    return -(-value // multiple) * multiple


def spectral_constants(devices, pieces_list):
    padded = [round_up(pieces, 8) for pieces in pieces_list]
    per_time, per_bin = sum(padded), 2 * sum(padded)
    table = np.zeros((devices, per_bin, devices, per_time), np.float64)
    offset = 0
    for pieces, wide in zip(pieces_list, padded):
        length = devices * pieces
        index = np.arange(length)
        angle = (2.0 * math.pi / length) * (np.outer(index, index) % length)
        factor = 1.0 / math.sqrt(length)
        for part, values in enumerate((np.cos(angle) * factor, -np.sin(angle) * factor)):
            row = 2 * offset + part * wide
            table[:, row : row + pieces, :, offset : offset + pieces] = values.reshape(
                devices, pieces, devices, pieces
            )
        offset += wide
    table = table.reshape(devices * per_bin, devices * per_time).astype(np.float32)
    high = table.astype(HALF_FLOAT)
    low = (table - high.astype(np.float32)).astype(HALF_FLOAT)
    order = []
    offset = 0
    for wide in padded:
        for one_bin in range(wide):
            for part in range(2):
                for series in range(devices):
                    order.append(series * per_bin + 2 * offset + part * wide + one_bin)
        offset += wide
    move = np.zeros((devices * per_bin, devices * per_bin), np.float32)
    move[np.arange(len(order)), order] = 1.0
    move = move.astype(HALF_FLOAT)
    return (
        jnp.asarray(np.stack([high, low])),
        jnp.asarray(np.stack([high.T, low.T])),
        jnp.asarray(move),
        jnp.asarray(np.ascontiguousarray(move.T)),
    )


def dot_nn(left, right):
    return jnp.dot(left, right, preferred_element_type=FLOAT)


def dot_nt(left, right):
    return lax.dot_general(left, right, (((1,), (1,)), ((), ())), preferred_element_type=FLOAT)


def spectral_body(sizes, back, refs, extra):
    devices, batches, count, pieces_list = sizes
    w1_ref, w2_ref = refs["weight0"], refs["weight1"]
    table_ref, inverse_ref = refs["table"], refs["inverse"]
    move_ref, unmove_ref = refs["move"], refs["unmove"]
    spec_ref, signal_ref = refs["spec"], refs["signal"]
    (one, two, three, mixed, spread, bins_out, four, w1, w2) = refs["buffers"]
    (s1, r1, s2, r2, s3, r3, s4, r4, ws, wr, own) = refs["sems"]
    me = lax.axis_index("tm")
    mine = lax.axis_index("batch")
    wide = [round_up(pieces, 8) for pieces in pieces_list]
    per_time, per_bin = sum(wide), 2 * sum(wide)
    weights = ((w1_ref, w1), (w2_ref, w2))

    barrier = pltpu.get_barrier_semaphore()

    @pl.loop(1, devices)
    def _(step):
        pl.semaphore_signal(
            barrier, inc=1, device_id=(mine, lax.rem(me + step, devices)), device_id_type=MESH
        )

    for step in range(1, batches):
        pl.semaphore_signal(
            barrier, inc=1, device_id=(lax.rem(mine + step, batches), me), device_id_type=MESH
        )
    pl.semaphore_wait(barrier, devices - 1 + batches - 1 + extra.greet(barrier))

    def exchange(source, target, send_sem, recv_sem, limit_out, limit_in, rows, start):
        def remote(there, here):
            return pltpu.make_async_remote_copy(
                src_ref=source.at[pl.ds(pl.multiple_of(there * rows, rows), rows)],
                dst_ref=target.at[pl.ds(pl.multiple_of(here * rows, rows), rows)],
                send_sem=send_sem.at[there],
                recv_sem=recv_sem.at[here],
                device_id=(mine, there),
                device_id_type=MESH,
            )

        if start:

            @pl.loop(1, devices)
            def _(step):
                there = lax.rem(me + step, devices)

                @pl.when(there < limit_out)
                def _():
                    remote(there, me).start()

        else:

            @pl.loop(1, devices)
            def _(step):
                there = lax.rem(me + step, devices)

                @pl.when(there < limit_in)
                def _():
                    pltpu.make_async_remote_copy(
                        src_ref=source.at[pl.ds(0, rows)],
                        dst_ref=target.at[pl.ds(pl.multiple_of(there * rows, rows), rows)],
                        send_sem=send_sem.at[there],
                        recv_sem=recv_sem.at[there],
                        device_id=(mine, there),
                        device_id_type=MESH,
                    ).wait_recv()

    def drain(source, target, send_sem, recv_sem, limit_out, rows):
        @pl.loop(1, devices)
        def _(step):
            there = lax.rem(me + step, devices)

            @pl.when(there < limit_out)
            def _():
                pltpu.make_async_remote_copy(
                    src_ref=source.at[pl.ds(0, rows)],
                    dst_ref=target.at[pl.ds(0, rows)],
                    send_sem=send_sem.at[there],
                    recv_sem=recv_sem.at[there],
                    device_id=(mine, there),
                    device_id_type=MESH,
                ).wait_send()

    owner = me < count

    def weight_copies(index):
        source, target = weights[index]
        rows = source.shape[2]
        place = target.at[:, :, pl.ds(pl.multiple_of(mine * rows, rows), rows)]
        local = pltpu.make_async_copy(source, place, own.at[index])
        remote = []
        for step in range(1, batches):
            there = lax.rem(mine + step, batches)
            back_there = lax.rem(mine + batches - step, batches)
            other = target.at[:, :, pl.ds(pl.multiple_of(back_there * rows, rows), rows)]
            remote.append(
                [
                    pltpu.make_async_remote_copy(
                        src_ref=source,
                        dst_ref=where,
                        send_sem=ws.at[index, step],
                        recv_sem=wr.at[index, step],
                        device_id=(there, me),
                        device_id_type=MESH,
                    )
                    for where in (place, other)
                ]
            )
        return local, remote

    for index in range(2):
        local, remote = weight_copies(index)
        local.start()
        for copy, _unused in remote:
            copy.start()

    x_ref = extra.prepare()
    exchange(x_ref, one, s1, r1, count, None, per_time, True)
    here = pltpu.make_async_copy(
        x_ref.at[pl.ds(pl.multiple_of(jnp.minimum(me, count - 1) * per_time, per_time), per_time)],
        one.at[pl.ds(pl.multiple_of(me * per_time, per_time), per_time)],
        own.at[2],
    )
    here.start()
    extra.start()
    if count < devices:
        two[pl.ds(count * per_bin, (devices - count) * per_bin)] = jnp.zeros(
            ((devices - count) * per_bin, two.shape[1]), two.dtype
        )
    here.wait()

    @pl.when(owner)
    def _():
        exchange(x_ref, one, s1, r1, None, devices, per_time, False)
        data = one[...]
        total = dot_nn(table_ref[0], data) + dot_nn(table_ref[1], data)
        bins_out[...] = total.astype(HALF_FLOAT)
        exchange(bins_out, two, s2, r2, devices, None, per_bin, True)
        place = pl.ds(pl.multiple_of(me * per_bin, per_bin), per_bin)
        two[place] = bins_out[place]

    extra.after_bins()
    exchange(bins_out, two, s2, r2, None, count, per_bin, False)
    spec_ref[...] = dot_nn(move_ref[...], two[...]).astype(HALF_FLOAT)
    extra.after_spec()
    base = 0
    for index in range(2):
        local, remote = weight_copies(index)
        local.wait()
        for copy, arrived in remote:
            copy.wait_send()
            arrived.wait_recv()
        target = weights[index][1]

        @pl.loop(0, pieces_list[index])
        def _(one_bin, base=base, target=target):
            place = pl.ds(
                pl.multiple_of(base + one_bin * 2 * devices, 2 * devices), 2 * devices
            )
            rows = spec_ref[place]
            if back:
                real = dot_nt(rows, target[one_bin, 0])
                imag = dot_nt(rows, target[one_bin, 1])
                out = jnp.concatenate(
                    [real[:devices] + imag[devices:], real[devices:] - imag[:devices]]
                )
            else:
                real = dot_nn(rows, target[one_bin, 0])
                imag = dot_nn(rows, target[one_bin, 1])
                out = jnp.concatenate(
                    [real[:devices] - imag[devices:], imag[:devices] + real[devices:]]
                )
            mixed[place] = out.astype(HALF_FLOAT)

        spare = wide[index] - pieces_list[index]
        if spare:
            mixed[
                pl.ds(base + pieces_list[index] * 2 * devices, spare * 2 * devices)
            ] = jnp.zeros((spare * 2 * devices, mixed.shape[1]), mixed.dtype)
        base += wide[index] * 2 * devices

    spread[...] = dot_nn(unmove_ref[...], mixed[...]).astype(HALF_FLOAT)
    exchange(spread, three, s3, r3, count, None, per_bin, True)
    extra.after_mixed()

    @pl.when(owner)
    def _():
        place = pl.ds(pl.multiple_of(me * per_bin, per_bin), per_bin)
        three[place] = spread[place]
        exchange(spread, three, s3, r3, None, devices, per_bin, False)
        data = three[...]
        total = dot_nn(inverse_ref[0], data) + dot_nn(inverse_ref[1], data)
        four[...] = total.astype(HALF_FLOAT)
        exchange(four, signal_ref, s4, r4, devices, None, per_time, True)
        place = pl.ds(pl.multiple_of(me * per_time, per_time), per_time)
        signal_ref[place] = four[place]

    extra.after_signal()
    exchange(four, signal_ref, s4, r4, None, count, per_time, False)
    drain(x_ref, one, s1, r1, count, per_time)
    drain(spread, three, s3, r3, count, per_bin)

    @pl.when(owner)
    def _():
        drain(bins_out, two, s2, r2, devices, per_bin)
        drain(four, signal_ref, s4, r4, devices, per_time)

    extra.finish()


class Place:
    def __init__(self, groups, members, batches):
        self.groups, self.members, self.batches = groups, members, batches
        self.me = lax.axis_index("tm")
        self.core = lax.axis_index("batch")
        self.group = lax.div(self.me, members)
        self.member = lax.rem(self.me, members)

    def device(self, group, member, core):
        return (core, group * self.members + member)

    def member_at(self, step):
        return lax.rem(self.member + step + self.members, self.members)

    def group_at(self, step):
        return lax.rem(self.group + step + self.groups, self.groups)

    def core_at(self, step):
        return lax.rem(self.core + step + self.batches, self.batches)

    def greet(self, barrier):
        greeted = 0
        for step in range(self.members):
            for turn in range(self.batches):
                if step or turn:
                    there = self.device(self.group, self.member_at(step), self.core_at(turn))
                    pl.semaphore_signal(barrier, inc=1, device_id=there, device_id_type=MESH)
                    greeted += 1
        for step in range(1, self.groups):
            for turn in range(self.batches):
                there = self.device(self.group_at(step), self.member, self.core_at(turn))
                pl.semaphore_signal(barrier, inc=1, device_id=there, device_id_type=MESH)
                greeted += 1
        return greeted


class VectorSum:
    @staticmethod
    def scratch(place_sizes, value):
        dma = pltpu.SemaphoreType.DMA
        groups, members, batches = place_sizes
        parts = [pltpu.VMEM(value.shape, value.dtype)]
        for size in (batches, members, groups):
            parts += [pltpu.VMEM((size,) + value.shape, value.dtype), dma((size,)), dma((size,))]
        return parts + [pltpu.VMEM(value.shape, value.dtype) for _ in range(2)]

    def __init__(self, place, source, out, scratch):
        self.place, self.source, self.out = place, source, out
        self.stages = [scratch[1 + 3 * k : 4 + 3 * k] for k in range(3)]
        self.values = [source, scratch[10], scratch[11]]

    def copy(self, stage, step, back):
        place = self.place
        held, send, recv = self.stages[stage]
        picks = [place.core_at, place.member_at, place.group_at]
        to = [place.core, place.member, place.group]
        to[stage] = picks[stage](step)
        return send_copy(
            self.values[stage],
            held.at[picks[stage](-step) if back else picks[stage](0)],
            send.at[step],
            recv.at[step],
            place.device(to[2], to[1], to[0]),
        )

    def start(self, stage):
        for step in range(1, self.stages[stage][0].shape[0]):
            self.copy(stage, step, False).start()

    def add(self, stage):
        held = self.stages[stage][0]
        value = self.values[stage][...]
        picks = [self.place.core_at, self.place.member_at, self.place.group_at]
        held[picks[stage](0)] = value
        for step in range(1, held.shape[0]):
            self.copy(stage, step, True).wait_recv()
        total = held[0]
        for index in range(1, held.shape[0]):
            total = total + held[index]
        target = self.out if stage == 2 else self.values[stage + 1]
        target[...] = total
        if stage < 2:
            self.start(stage + 1)

    def drain(self):
        for stage in range(3):
            for step in range(1, self.stages[stage][0].shape[0]):
                self.copy(stage, step, False).wait_send()


def send_copy(source, target, send_sem, recv_sem, there):
    return pltpu.make_async_remote_copy(
        src_ref=source,
        dst_ref=target,
        send_sem=send_sem,
        recv_sem=recv_sem,
        device_id=there,
        device_id_type=MESH,
    )


def slab(ref, dim, index, size):
    picks = [slice(None)] * len(ref.shape)
    picks[dim] = pl.ds(pl.multiple_of(index * size, size), size)
    return ref.at[tuple(picks)]


class WideExchange:
    @staticmethod
    def scratch(place_sizes, wide):
        groups, members, batches = place_sizes
        mates = members * batches
        dma = pltpu.SemaphoreType.DMA
        return [dma((mates,)), dma((mates,)), dma((wide.shape[1] // members,))]

    @staticmethod
    def shape(place_sizes, wide):
        groups, members, batches = place_sizes
        pieces, steps, series, channels = wide.shape
        return (steps // members, members * batches, pieces, series, channels // batches)

    def __init__(self, place, source, target, sems):
        self.place, self.source, self.target = place, source, target
        self.send_sem, self.recv_sem, self.local_sem = sems

    def hops(self):
        for step in range(self.place.members):
            for turn in range(self.place.batches):
                if step or turn:
                    yield step, turn

    def mate(self, step, turn):
        return self.place.core_at(turn) * self.place.members + self.place.member_at(step)

    def piece(self, one, step, turn):
        place = self.place
        steps, half = self.target.shape[0], self.target.shape[4]
        return slab(
            self.source.at[:, place.member_at(step) * steps + one], 2, place.core_at(turn), half
        )

    def own(self, one):
        return pltpu.make_async_copy(
            self.piece(one, 0, 0), self.target.at[one, self.mate(0, 0)], self.local_sem.at[one]
        )

    def whole(self, step, turn, pick):
        slot = turn * self.place.members + step
        block = self.target.at[:, pick]
        return send_copy(
            block,
            block,
            self.send_sem.at[slot],
            self.recv_sem.at[slot],
            self.place.device(
                self.place.group, self.place.member_at(step), self.place.core_at(turn)
            ),
        )

    def units(self):
        return [functools.partial(self.start, one) for one in range(self.target.shape[0])]

    def start(self, one):
        place = self.place
        self.own(one).start()
        for step, turn in self.hops():
            slot = turn * place.members + step
            send_copy(
                self.piece(one, step, turn),
                self.target.at[one, self.mate(0, 0)],
                self.send_sem.at[slot],
                self.recv_sem.at[slot],
                place.device(place.group, place.member_at(step), place.core_at(turn)),
            ).start()

    def wait(self):
        for one in range(self.target.shape[0]):
            self.own(one).wait()
        for step, turn in self.hops():
            self.whole(step, turn, self.mate(-step, -turn)).wait_recv()

    def drain(self):
        for step, turn in self.hops():
            self.whole(step, turn, self.mate(0, 0)).wait_send()


class NarrowGather:
    sems = 5

    @staticmethod
    def scratch(place_sizes, narrow):
        groups, members, batches = place_sizes
        dma = pltpu.SemaphoreType.DMA
        size = members * batches
        return [dma((members,)), dma((members,)), dma((size,)), dma((size,)), dma((1,))]

    def __init__(self, place, source, target, sems):
        self.place, self.source, self.target = place, source, target
        (self.link_send, self.link_recv, self.chip_send, self.chip_recv, self.local_sem) = sems

    def own(self):
        place = self.place
        pick = place.core * place.members + place.member
        return pltpu.make_async_copy(self.source, self.target.at[pick], self.local_sem.at[0])

    def link(self, step, pick_step):
        place = self.place
        pick = place.core * place.members + place.member_at(pick_step)
        return send_copy(
            self.source,
            self.target.at[pick],
            self.link_send.at[step],
            self.link_recv.at[step],
            place.device(place.group, place.member_at(step), place.core),
        )

    def chip(self, step, turn, source_core, target_core):
        place = self.place
        member = place.member_at(-step)
        slot = turn * place.members + step
        source = self.target.at[source_core * place.members + member] if step else self.source
        return send_copy(
            source,
            self.target.at[target_core * place.members + member],
            self.chip_send.at[slot],
            self.chip_recv.at[slot],
            place.device(place.group, place.member, place.core_at(turn)),
        )

    def start(self):
        place = self.place
        self.own().start()
        for step in range(1, place.members):
            self.link(step, 0).start()
        for turn in range(1, place.batches):
            self.chip(0, turn, place.core, place.core).start()

    def forward(self):
        place = self.place
        for step in range(1, place.members):
            self.link(step, -step).wait_recv()
            for turn in range(1, place.batches):
                self.chip(step, turn, place.core, place.core).start()

    def wait(self):
        place = self.place
        self.own().wait()
        for turn in range(1, place.batches):
            other = place.core_at(-turn)
            for step in range(place.members):
                self.chip(step, turn, place.core, other).wait_recv()

    def drain(self):
        place = self.place
        for step in range(1, place.members):
            self.link(step, 0).wait_send()
        for turn in range(1, place.batches):
            for step in range(place.members):
                self.chip(step, turn, place.core, place.core).wait_send()


class KernelProduct:
    sems = 6

    @staticmethod
    def scratch(place_sizes, kind, wide, narrow):
        groups, members, batches = place_sizes
        pieces, kernel, series, channels = wide.shape
        steps, rows = kernel // members, pieces * series
        half = channels // batches
        piece = (128, half) if kind == "down" else (half, 128)
        dma = pltpu.SemaphoreType.DMA
        return [
            pltpu.VMEM((channels, members * batches * rows), HALF_FLOAT),
            pltpu.VMEM((steps, channels, half), HALF_FLOAT),
            pltpu.VMEM((groups, steps) + piece, HALF_FLOAT),
            pltpu.VMEM((steps, 128, half), HALF_FLOAT),
            pltpu.VMEM((kernel, channels // (groups * members), half), HALF_FLOAT),
            dma((groups * batches,)),
            dma((groups * batches,)),
            dma((members,)),
            dma((members,)),
            dma((2,)),
        ]

    def __init__(self, place, kind, wide_in, narrow_in, out, scratch):
        self.place, self.kind, self.wide_in, self.narrow_in, self.out = (
            place,
            kind,
            wide_in,
            narrow_in,
            out,
        )
        (self.narrow_t, self.send, self.recv, self.total, self.gathered) = scratch[:5]
        (self.sz, self.rz, self.sf, self.rf, self.local) = scratch[5:]
        self.cores_per_group = place.groups // place.batches

    def multiply(self):
        mates, rows = self.narrow_in.shape[0], self.narrow_in.shape[1]
        self.narrow_t[...] = self.narrow_in[...].reshape(mates * rows, -1).T

        @pl.loop(0, self.wide_in.shape[0])
        def _(one):
            data = self.wide_in[one].reshape(mates * rows, -1)
            self.send[one] = dot_nn(self.narrow_t[...], data).astype(HALF_FLOAT)

    def chunk(self, group, core):
        if self.kind == "down":
            return slab(self.send, 1, group, 128)
        half = self.send.shape[1] // self.place.batches
        return slab(
            slab(self.send, 1, core, half), 2, lax.rem(group, self.cores_per_group), 128
        )

    def hops(self):
        place = self.place
        for step in range(place.groups):
            for turn in range(place.batches if self.kind == "up" else 1):
                yield step, turn

    def partial(self, step, turn, action):
        place = self.place
        group, core = place.group_at(step), place.core_at(turn)
        slot = step * place.batches + turn
        if step == 0 and turn == 0:
            copy = pltpu.make_async_copy(
                self.chunk(group, core), self.recv.at[place.group], self.local.at[0]
            )
            act = lambda: action(copy, True)
        else:
            copy = send_copy(
                self.chunk(group, core),
                self.recv.at[place.group],
                self.sz.at[slot],
                self.rz.at[slot],
                place.device(group, place.member, core),
            )
            act = lambda: action(copy, False)
        if self.kind == "down":
            act()
        else:
            pl.when(lax.div(group, self.cores_per_group) == place.core)(act)

    def start_partials(self):
        for step, turn in self.hops():
            self.partial(step, turn, lambda copy, local: copy.start())

    def sum_partials(self):
        place = self.place
        for step, turn in self.hops():
            group, core = place.group_at(-step), place.core_at(-turn)
            slot = step * place.batches + turn

            def act(step=step, turn=turn, group=group, slot=slot):
                if step == 0 and turn == 0:
                    pltpu.make_async_copy(
                        self.chunk(place.group, place.core),
                        self.recv.at[place.group],
                        self.local.at[0],
                    ).wait()
                else:
                    send_copy(
                        self.chunk(place.group, place.core),
                        self.recv.at[group],
                        self.sz.at[slot],
                        self.rz.at[slot],
                        place.device(place.group, place.member, place.core),
                    ).wait_recv()

            if self.kind == "down":
                act()
            else:
                pl.when(lax.div(place.group, self.cores_per_group) == core)(act)

        @pl.loop(0, self.total.shape[0])
        def _(one):
            value = self.recv[0, one].astype(FLOAT)
            for other in range(1, place.groups):
                value = value + self.recv[other, one].astype(FLOAT)
            value = value if self.kind == "down" else value.T
            self.total[one] = value.astype(HALF_FLOAT)

    def final(self, step, pick_step):
        place = self.place
        steps, width = self.total.shape[0], self.gathered.shape[1]
        source = slab(self.total, 1, place.member_at(step), width)
        target = slab(self.gathered, 0, place.member_at(pick_step), steps)
        if step == 0:
            return pltpu.make_async_copy(source, target, self.local.at[1])
        return send_copy(
            source,
            target,
            self.sf.at[step],
            self.rf.at[step],
            place.device(place.group, place.member_at(step), place.core),
        )

    def start_final(self):
        for step in range(self.place.members):
            self.final(step, 0).start()

    def finish(self):
        place = self.place
        self.final(0, 0).wait()
        for step in range(1, place.members):
            self.final(step, -step).wait_recv()
        self.out[...] = self.gathered[...].astype(FLOAT)
        for step in range(1, place.members):
            self.final(step, 0).wait_send()
        for step, turn in self.hops():
            if step or turn:
                self.partial(step, turn, lambda copy, local: copy.wait_send())


class MatrixSum:
    sems = 7

    @staticmethod
    def half_shape(place_sizes, kind, value):
        batches = place_sizes[2]
        shape = list(value.shape)
        if kind == "rows":
            shape[0] //= batches
        elif kind == "lanes":
            shape[-1] //= batches
        return tuple(shape)

    @staticmethod
    def piece_shape(place_sizes, kind, value):
        groups, members, batches = place_sizes
        shape = list(MatrixSum.half_shape(place_sizes, kind, value))
        dim = {"rows": 1, "lanes": len(shape) - 2, "whole": 0}[kind]
        shape[dim] //= groups * members
        return tuple(shape)

    @staticmethod
    def scratch(place_sizes, kind, value):
        groups, members, batches = place_sizes
        half = MatrixSum.half_shape(place_sizes, kind, value)
        piece = MatrixSum.piece_shape(place_sizes, kind, value)
        dma = pltpu.SemaphoreType.DMA
        return [
            pltpu.VMEM(half, value.dtype),
            pltpu.VMEM((batches,) + half, value.dtype),
            pltpu.VMEM((members, groups) + piece, value.dtype),
            pltpu.VMEM((groups,) + piece, value.dtype),
            pltpu.VMEM((groups,) + piece, value.dtype),
            dma((batches,)),
            dma((batches,)),
            dma((members * groups,)),
            dma((members * groups,)),
            dma((groups,)),
            dma((groups,)),
            dma((1 + groups,)),
        ]

    def __init__(self, place, kind, source, out, scratch):
        self.place, self.kind, self.source, self.out = place, kind, source, out
        (self.own, self.others, self.by_member, self.sums, self.by_group) = scratch[:5]
        (self.sb, self.rb, self.sm, self.rm, self.sg, self.rg, self.local) = scratch[5:]
        self.piece_dim = {"rows": 1, "lanes": len(self.own.shape) - 2, "whole": 0}[kind]

    def half(self, core):
        if self.kind == "rows":
            return slab(self.source, 0, core, self.own.shape[0])
        if self.kind == "lanes":
            return slab(self.source, len(self.own.shape) - 1, core, self.own.shape[-1])
        return self.source

    def cores(self, step, pick):
        place = self.place
        core = place.core_at(step)
        return send_copy(
            self.half(core),
            self.others.at[pick],
            self.sb.at[step],
            self.rb.at[step],
            place.device(place.group, place.member, core),
        )

    def load(self):
        return pltpu.make_async_copy(self.half(self.place.core), self.own, self.local.at[0])

    def start(self):
        self.load().start()
        for step in range(1, self.place.batches):
            self.cores(step, self.place.core).start()

    def piece(self, group, member):
        size = self.by_member.shape[2 + self.piece_dim]
        return slab(self.own, self.piece_dim, group * self.place.members + member, size)

    def members(self, step, pick_step, group):
        place = self.place
        member = place.member_at(step)
        slot = step * place.groups + group
        target = self.by_member.at[place.member_at(pick_step), group]
        if step == 0:
            return pltpu.make_async_copy(
                self.piece(group, member), target, self.local.at[1 + group]
            )
        return send_copy(
            self.piece(group, member),
            target,
            self.sm.at[slot],
            self.rm.at[slot],
            place.device(place.group, member, place.core),
        )

    def add_cores(self):
        place = self.place
        self.load().wait()
        for step in range(1, place.batches):
            self.cores(step, place.core_at(-step)).wait_recv()
        rows = self.own.shape[0]
        block = max(size for size in (1, 2, 4, 8, 16, 32, 64) if rows % size == 0)

        @pl.loop(0, rows // block)
        def _(index):
            pick = pl.ds(pl.multiple_of(index * block, block), block)
            value = self.own[pick].astype(FLOAT)
            for step in range(1, place.batches):
                value = value + self.others[place.core_at(step), pick].astype(FLOAT)
            self.own[pick] = value.astype(self.own.dtype)

        for step in range(place.members):
            for group in range(place.groups):
                self.members(step, 0, group).start()

    def groups(self, step, pick_step):
        place = self.place
        group = place.group_at(step)
        return send_copy(
            self.sums.at[group],
            self.by_group.at[place.group_at(pick_step)],
            self.sg.at[step],
            self.rg.at[step],
            place.device(group, place.member, place.core),
        )

    def add_members(self):
        place = self.place
        for step in range(place.members):
            for group in range(place.groups):
                if step == 0:
                    self.members(step, 0, group).wait()
                else:
                    self.members(step, -step, group).wait_recv()

        @pl.loop(0, place.groups)
        def _(group):
            value = self.by_member[0, group].astype(FLOAT)
            for other in range(1, place.members):
                value = value + self.by_member[other, group].astype(FLOAT)
            self.sums[group] = value.astype(self.sums.dtype)

        for step in range(1, place.groups):
            self.groups(step, 0).start()
        self.by_group[place.group] = self.sums[place.group]

    def finish(self):
        place = self.place
        for step in range(1, place.groups):
            self.groups(step, -step).wait_recv()
        value = self.by_group[0].astype(FLOAT)
        for other in range(1, place.groups):
            value = value + self.by_group[other].astype(FLOAT)
        self.out[...] = value
        for step in range(1, place.groups):
            self.groups(step, 0).wait_send()
        for step in range(1, place.members):
            for group in range(place.groups):
                self.members(step, 0, group).wait_send()
        for step in range(1, place.batches):
            self.cores(step, place.core).wait_send()


def remote_call(body, inputs, outputs, scratch, collective_id, flops, nbytes, name):
    def kernel(*refs):
        left = list(refs)
        named = {key: left.pop(0) for key in inputs}
        named.update({key: left.pop(0) for key in outputs})
        for key, shapes in scratch.items():
            named[key] = [left.pop(0) for _ in shapes]
        body(named)

    results = pl.pallas_call(
        kernel,
        out_shape=tuple(shape for shape, _ in outputs.values()),
        in_specs=[spec for _, spec in inputs.values()],
        out_specs=tuple(spec for _, spec in outputs.values()),
        scratch_shapes=[shape for shapes in scratch.values() for shape in shapes],
        compiler_params=pltpu.CompilerParams(
            collective_id=collective_id,
            has_side_effects=True,
            vmem_limit_bytes=63 * 1024 * 1024,
        ),
        cost_estimate=pl.CostEstimate(flops=flops, bytes_accessed=nbytes, transcendentals=0),
        name=name,
    )(*[value for value, _ in inputs.values()])
    return dict(zip(outputs, results))


def plane_sizes(channels):
    devices, batches = lax.axis_size("tm"), lax.axis_size("batch")
    groups = channels // 128
    if batches == 2 and channels % 256 == 0 and devices % groups == 0:
        return groups, devices // groups, batches
    return None


VMEM_SPEC = pl.BlockSpec(memory_space=pltpu.VMEM)
HBM_SPEC = pl.BlockSpec(memory_space=pl.ANY)


class SeriesGradient:
    @staticmethod
    def scratch(weights, outers, rim):
        steps, series, channels = outers[0].shape
        lead = 2 * rim + 8
        dma = pltpu.SemaphoreType.DMA
        rims = (rim, series, channels)
        return (
            [pltpu.VMEM(weight.shape, HALF_FLOAT) for weight in weights]
            + [pltpu.VMEM((steps + 2 * lead, series, channels), FLOAT) for _ in outers]
            + [pltpu.VMEM((channels // 128, steps * series, 128), FLOAT)]
            + [pltpu.VMEM(rims, FLOAT) for _ in range(4)]
            + [dma((4,)), dma((2,)), dma((2,))]
        )

    def __init__(self, weights, outers, out, scratch, halves, rim):
        self.weights, self.outers, self.out = weights, outers, out
        self.halves, self.rim = halves, rim
        count = len(weights)
        self.held, self.grads = scratch[:count], scratch[count : 2 * count]
        (self.result, self.low, self.high, self.before, self.after) = scratch[
            2 * count : 2 * count + 5
        ]
        (self.local, self.send, self.recv) = scratch[2 * count + 5 :]
        self.steps = outers[0].shape[0]
        self.series = outers[0].shape[1]
        self.lead = 2 * rim + 8
        self.me, self.core = lax.axis_index("tm"), lax.axis_index("batch")
        self.last = lax.axis_size("tm") - 1

    def greet(self, barrier):
        @pl.when(self.me > 0)
        def _():
            pl.semaphore_signal(
                barrier, inc=1, device_id=(self.core, self.me - 1), device_id_type=MESH
            )

        @pl.when(self.me < self.last)
        def _():
            pl.semaphore_signal(
                barrier, inc=1, device_id=(self.core, self.me + 1), device_id_type=MESH
            )

        return jnp.where(self.me > 0, 1, 0) + jnp.where(self.me < self.last, 1, 0)

    def loads(self, index):
        return (
            pltpu.make_async_copy(
                self.weights[index], self.held[index], self.local.at[2 * index]
            ),
            pltpu.make_async_copy(
                self.outers[index],
                self.grads[index].at[pl.ds(self.lead, self.steps)],
                self.local.at[2 * index + 1],
            ),
        )

    def start(self):
        for index in range(len(self.held)):
            for copy in self.loads(index):
                copy.start()
            grads = self.grads[index]
            zero = jnp.zeros((self.lead,) + grads.shape[1:], FLOAT)
            grads[: self.lead] = zero
            grads[self.lead + self.steps :] = zero

    def through_down(self, index, grad):
        for copy in self.loads(index):
            copy.wait()
        kernel = self.held[index].shape[0]
        pieces = self.steps // kernel
        grads = self.grads[index]

        @pl.loop(0, kernel)
        def _(one):
            value = dot_nt(grad, self.held[index][one])
            for piece in range(pieces):
                row = self.lead + piece * kernel + one
                grads[row] = (
                    grads[row] + value[piece * self.series : (piece + 1) * self.series]
                )

    def store(self, place, value, add=False):
        for lane in range(self.result.shape[0]):
            part = value[:, lane * 128 : lane * 128 + 128]
            self.result[lane, place] = self.result[lane, place] - part if add else part

    def adjoint(self):
        def means(index, sums):
            out, total = [], 0.0
            for grads, half, value in zip(self.grads, self.halves, sums):
                high = grads[index + (self.lead - self.rim + half)]
                low = grads[index + (self.lead - self.rim - half - 1)]
                value = value + high - low
                out.append(value)
                total = total + value * (1.0 / (2 * half + 1))
            return tuple(out), total

        def low_step(index, sums):
            sums, total = means(index, sums)
            self.low[index] = total
            return sums

        def step(index, sums):
            sums, total = means(index + self.rim, sums)
            value = self.grads[0][self.lead + index] + self.grads[1][self.lead + index]
            place = pl.ds(pl.multiple_of(index * self.series, self.series), self.series)
            self.store(place, value - total)
            return sums

        def high_step(index, sums):
            sums, total = means(index + (self.rim + self.steps), sums)
            self.high[index] = total
            return sums

        zero = jnp.zeros(self.low.shape[1:], FLOAT)
        sums = lax.fori_loop(0, self.rim, low_step, (zero, zero))
        sums = lax.fori_loop(0, self.steps, step, sums)
        lax.fori_loop(0, self.rim, high_step, sums)

    def edge(self, up):
        source, target = (self.high, self.before) if up else (self.low, self.after)
        index = 0 if up else 1
        return send_copy(
            source,
            target,
            self.send.at[index],
            self.recv.at[index],
            (self.core, self.me + 1 if up else self.me - 1),
        )

    def send_edges(self):
        pl.when(self.me < self.last)(lambda: self.edge(True).start())
        pl.when(self.me > 0)(lambda: self.edge(False).start())

    def finish(self):
        series = self.series
        rows, end = self.rim * series, self.steps * series

        @pl.when(self.me > 0)
        def _():
            self.edge(True).wait_recv()
            self.store(pl.ds(0, rows), self.before[...].reshape(rows, -1), True)

        @pl.when(self.me == 0)
        def _():
            total = self.low[0]
            for index in range(1, self.rim):
                total = total + self.low[index]
            self.store(pl.ds(0, series), total, True)

        @pl.when(self.me < self.last)
        def _():
            self.edge(False).wait_recv()
            self.store(pl.ds(end - rows, rows), self.after[...].reshape(rows, -1), True)

        @pl.when(self.me == self.last)
        def _():
            total = self.high[0]
            for index in range(1, self.rim):
                total = total + self.high[index]
            self.store(pl.ds(end - series, series), total, True)

        for one in range(self.out.shape[0]):
            for lane in range(self.result.shape[0]):
                value = self.result[lane, pl.ds(one, self.steps, stride=series), :]
                self.out[one, :, lane * 128 : lane * 128 + 128] = value.astype(HALF_FLOAT)
        pl.when(self.me < self.last)(lambda: self.edge(True).wait_send())
        pl.when(self.me > 0)(lambda: self.edge(False).wait_send())


def down_gradients(sizes, wides, narrows, vectors, weights, outers, halves, rim, count, matrix):
    groups, members, batches = sizes
    half = wides[0].shape[4]
    channels = half * batches
    inputs, outputs, scratch = {}, {}, {}
    for index, (wide, narrow) in enumerate(zip(wides, narrows)):
        steps = wide.shape[0] * members
        shape = jax.ShapeDtypeStruct(
            (wide.shape[2], steps, wide.shape[3], channels), HALF_FLOAT
        )
        inputs[f"wide{index}"] = (wide, VMEM_SPEC)
        inputs[f"narrow{index}"] = (narrow, HBM_SPEC)
        outputs[f"out{index}"] = (
            jax.ShapeDtypeStruct((steps, channels // (groups * members), half), FLOAT),
            VMEM_SPEC,
        )
        scratch[f"rows{index}"] = [
            pltpu.VMEM((members * batches,) + narrow.shape, HALF_FLOAT)
        ]
        scratch[f"gather{index}"] = NarrowGather.scratch(sizes, narrow)
        scratch[f"product{index}"] = KernelProduct.scratch(sizes, "down", shape, narrow)
    for index in range(len(wides)):
        inputs[f"weight{index}"] = (weights[index], HBM_SPEC)
        inputs[f"outer{index}"] = (outers[index], HBM_SPEC)
    scratch["series"] = SeriesGradient.scratch(weights, outers, rim)
    outputs["grad_series"] = (
        jax.ShapeDtypeStruct((count, outers[0].shape[0], channels), HALF_FLOAT),
        VMEM_SPEC,
    )
    kind, value = matrix
    inputs["matrix"] = (value, HBM_SPEC)
    outputs["matrix_sum"] = (
        jax.ShapeDtypeStruct(MatrixSum.piece_shape(sizes, kind, value), FLOAT),
        VMEM_SPEC,
    )
    scratch["matrix_parts"] = MatrixSum.scratch(sizes, kind, value)
    inputs["vectors"] = (vectors, VMEM_SPEC)
    outputs["vector_sum"] = (jax.ShapeDtypeStruct(vectors.shape, FLOAT), VMEM_SPEC)
    scratch["vector"] = VectorSum.scratch(sizes, vectors)

    def body(refs):
        place = Place(*sizes)
        back = SeriesGradient(
            [refs[f"weight{index}"] for index in range(len(wides))],
            [refs[f"outer{index}"] for index in range(len(wides))],
            refs["grad_series"],
            refs["series"],
            halves,
            rim,
        )
        barrier = pltpu.get_barrier_semaphore()
        pl.semaphore_wait(barrier, place.greet(barrier) + back.greet(barrier))
        gathers, products = [], []
        for index in range(len(wides)):
            gathers.append(
                NarrowGather(
                    place,
                    refs[f"narrow{index}"],
                    refs[f"rows{index}"][0],
                    refs[f"gather{index}"],
                )
            )
            products.append(
                KernelProduct(
                    place,
                    "down",
                    refs[f"wide{index}"],
                    refs[f"rows{index}"][0],
                    refs[f"out{index}"],
                    refs[f"product{index}"],
                )
            )
        total = VectorSum(place, refs["vectors"], refs["vector_sum"], refs["vector"])
        dense = MatrixSum(place, kind, refs["matrix"], refs["matrix_sum"], refs["matrix_parts"])
        for gather in gathers:
            gather.start()
        dense.start()
        total.start(0)
        back.start()
        for gather in gathers:
            gather.forward()
        for gather, product in zip(gathers, products):
            gather.wait()
            product.multiply()
            product.start_partials()
        dense.add_cores()
        total.add(0)
        mine = place.core * members + place.member
        for index in range(len(wides)):
            back.through_down(index, refs[f"rows{index}"][0][mine])
        dense.add_members()
        total.add(1)
        back.adjoint()
        back.send_edges()
        for product in products:
            product.sum_partials()
            product.start_final()
        dense.finish()
        total.add(2)
        back.finish()
        for product in products:
            product.finish()
        for gather in gathers:
            gather.drain()
        total.drain()

    flops = sum(2 * wide.size * channels for wide in wides)
    results = remote_call(
        body, inputs, outputs, scratch, 2, flops, 8 * flops // channels, "down_gradients"
    )
    return (
        [results["out0"], results["out1"]],
        results["vector_sum"],
        results["grad_series"],
        results["matrix_sum"],
    )


def iso_gradient_kernel(lane_ref, spec_ref, specs_ref, grad_ref, grads_ref, out_ref):
    devices = spec_ref.shape[0] // 2
    spec, grad, turned = [], [], []
    for own, others, into in ((spec_ref, specs_ref, spec), (grad_ref, grads_ref, grad)):
        into.append(own[...])
        for index in range(others.shape[0]):
            into.append(others[index])
    for value in grad:
        turned.append(jnp.concatenate([value[devices:], -value[:devices]]))
    spec = jnp.concatenate(spec)
    for part, values in enumerate((grad, turned)):
        out_ref[0, part] = lax.dot_general(
            spec,
            jnp.concatenate(values),
            (((0,), (0,)), ((), ())),
            preferred_element_type=FLOAT,
        )


def iso_gradients(spec, specs, grad, grads, first, bins):
    rows, channels = 2 * lax.axis_size("tm"), grad.shape[1]
    half = channels // lax.axis_size("batch")
    others = specs.shape[0]
    core = lax.axis_index("batch")
    if half % 128:
        spec = lax.dynamic_slice_in_dim(spec, core * half, half, axis=1)
        specs = lax.dynamic_slice_in_dim(specs, core * half, half, axis=2)
        core = 0
    return pl.pallas_call(
        iso_gradient_kernel,
        out_shape=jax.ShapeDtypeStruct((bins, 2, half, channels), FLOAT),
        grid_spec=pltpu.PrefetchScalarGridSpec(
            num_scalar_prefetch=1,
            grid=(bins,),
            in_specs=[
                pl.BlockSpec((rows, half), lambda i, lane: (first + i, lane[0])),
                pl.BlockSpec((others, rows, half), lambda i, lane: (0, first + i, lane[0])),
                pl.BlockSpec((rows, channels), lambda i, lane: (first + i, 0)),
                pl.BlockSpec((others, rows, channels), lambda i, lane: (0, first + i, 0)),
            ],
            out_specs=pl.BlockSpec((1, 2, half, channels), lambda i, lane: (i, 0, 0, 0)),
        ),
        cost_estimate=pl.CostEstimate(
            flops=4 * bins * rows * (1 + others) * half * channels,
            bytes_accessed=8 * bins * half * channels,
            transcendentals=0,
        ),
        name="iso_gradients",
    )(jnp.full((1,), core, jnp.int32), spec, specs, grad, grads)


class Extra:
    def __init__(self, sizes):
        self.sizes = sizes
        self.inputs, self.outputs, self.scratch = {}, {}, {}

    def bind(self, refs):
        self.refs = refs
        self.place = Place(*self.sizes) if self.sizes else None

    def greet(self, barrier):
        return self.place.greet(barrier) if self.sizes else 0

    def prepare(self):
        return self.refs["x"]

    def start(self):
        pass

    def after_bins(self):
        pass

    def after_spec(self):
        pass

    def after_mixed(self):
        pass

    def after_signal(self):
        pass

    def finish(self):
        pass

    def run(self, share):
        count = max(1, round(share * self.unit_count))
        for _ in range(min(count, len(self.units))):
            self.units.pop(0)()


class Turn:
    block = 64

    @staticmethod
    def scratch(weight):
        channels, kernel, outs = weight.shape
        dma = pltpu.SemaphoreType.DMA
        return [
            pltpu.VMEM((2, Turn.block, kernel, outs), HALF_FLOAT),
            pltpu.VMEM((2, kernel, Turn.block, outs), HALF_FLOAT),
            dma((2,)),
            dma((2,)),
        ]

    def __init__(self, source, target, scratch):
        self.source, self.target = source, target
        self.read, self.turned, self.in_sem, self.out_sem = scratch
        self.total = source.shape[0] // self.block
        self.done = 0

    def load(self, index, slot):
        place = pl.ds(pl.multiple_of(index * self.block, self.block), self.block)
        return pltpu.make_async_copy(
            self.source.at[place], self.read.at[slot], self.in_sem.at[slot]
        )

    def store(self, index, slot):
        place = pl.ds(pl.multiple_of(index * self.block, self.block), self.block)
        return pltpu.make_async_copy(
            self.turned.at[slot], self.target.at[:, place], self.out_sem.at[slot]
        )

    def start(self):
        self.load(0, 0).start()

    def run(self, share):
        first, self.done = self.done, min(self.total, self.done + math.ceil(share * self.total))

        @pl.loop(first, self.done)
        def _(index):
            slot = lax.rem(index, 2)
            self.load(index, slot).wait()

            @pl.when(index + 1 < self.total)
            def _():
                self.load(index + 1, 1 - slot).start()

            @pl.when(index >= 2)
            def _():
                self.store(index - 2, slot).wait()

            self.turned[slot] = pltpu.einshape("mhd->hmd", self.read[slot])
            self.store(index, slot).start()

    def finish(self):
        self.run(1.0)
        for index in range(max(0, self.total - 2), self.total):
            self.store(index, index % 2).wait()


def by_piece(signal, rows, count):
    per_time = signal.shape[0] // count
    width = rows.shape[1] // per_time
    for lane in range(rows.shape[0]):
        value = signal[:, lane * 128 : lane * 128 + 128]
        rows[lane, : signal.shape[0], :] = value.astype(FLOAT)
        if width > count:
            rows[lane, signal.shape[0] :, :] = jnp.zeros(
                (rows.shape[1] - signal.shape[0], 128), FLOAT
            )

    def piece(index):
        return jnp.concatenate(
            [rows[lane, pl.ds(index, width, stride=per_time), :] for lane in range(rows.shape[0])],
            axis=1,
        )

    return lambda first, size: jnp.concatenate([piece(first + i) for i in range(size)])


class Front:
    halo = 16

    @staticmethod
    def scratch(series, weights, per_time, rim):
        count, steps, channels = series.shape
        wide, lanes = round_up(count, 16), channels // 128
        rows = max(steps // weight.shape[0] for weight in weights) * wide
        dma = pltpu.SemaphoreType.DMA
        return (
            [pltpu.VMEM(weight.shape, HALF_FLOAT) for weight in weights]
            + [
                pltpu.VMEM(series.shape, HALF_FLOAT),
                pltpu.VMEM((count, Front.halo, channels), HALF_FLOAT),
                pltpu.VMEM((count, Front.halo, channels), HALF_FLOAT),
                pltpu.VMEM((lanes, (steps + 2 * rim + 1) * wide, 128), FLOAT),
                pltpu.VMEM((lanes, per_time * wide, 128), FLOAT),
                pltpu.VMEM((rows, channels), FLOAT),
                pltpu.VMEM((count * per_time, channels), HALF_FLOAT),
            ]
            + [dma((1 + len(weights),)), dma((2,)), dma((2,))]
        )

    def __init__(self, source, weights, bias, seasonals, acts, scratch, halves, rim):
        self.source, self.weights, self.bias = source, weights, bias
        self.seasonals, self.acts, self.halves, self.rim = seasonals, acts, halves, rim
        self.held = scratch[: len(weights)]
        (self.series, self.before, self.after, self.wide, self.rows, self.total, self.x) = (
            scratch[len(weights) : len(weights) + 7]
        )
        (self.local, self.send, self.recv) = scratch[len(weights) + 7 :]
        self.count, self.steps, _ = source.shape
        self.width = seasonals[0].shape[2]
        self.me, self.core = lax.axis_index("tm"), lax.axis_index("batch")
        self.last = lax.axis_size("tm") - 1

    def loads(self):
        return [pltpu.make_async_copy(self.source, self.series, self.local.at[0])] + [
            pltpu.make_async_copy(weight, held, self.local.at[1 + index])
            for index, (weight, held) in enumerate(zip(self.weights, self.held))
        ]

    def edge(self, up):
        first = self.steps - self.halo if up else 0
        index = 0 if up else 1
        return send_copy(
            self.source.at[:, pl.ds(first, self.halo)],
            self.before if up else self.after,
            self.send.at[index],
            self.recv.at[index],
            (self.core, self.me + 1 if up else self.me - 1),
        )

    def start(self):
        pl.when(self.me < self.last)(lambda: self.edge(True).start())
        pl.when(self.me > 0)(lambda: self.edge(False).start())
        for copy in self.loads():
            copy.start()

    def spread(self, values, first, count):
        for lane in range(self.wide.shape[0]):
            self.wide[lane, pl.ds(first, count, stride=self.width), :] = values[
                :, lane * 128 : lane * 128 + 128
            ]

    def step(self, index):
        place = pl.ds(pl.multiple_of(index * self.width, self.width), self.width)
        return jnp.concatenate(
            [self.wide[lane, place, :] for lane in range(self.wide.shape[0])], axis=1
        )

    def repeat(self, index, first):
        value = self.step(index)
        for row in range(self.rim):
            place = pl.ds((first + row) * self.width, self.width)
            for lane in range(self.wide.shape[0]):
                self.wide[lane, place, :] = value[:, lane * 128 : lane * 128 + 128]

    def layers(self, ready):
        rim, steps, width = self.rim, self.steps, self.width
        self.wide[...] = jnp.zeros_like(self.wide)
        copies = self.loads()
        copies[0].wait()
        for one in range(self.count):
            self.spread(self.series[one].astype(FLOAT), rim * width + one, steps)

        @pl.when(self.me > 0)
        def _():
            self.edge(True).wait_recv()
            for one in range(self.count):
                self.spread(self.before[one].astype(FLOAT)[self.halo - rim :], one, rim)

        @pl.when(self.me < self.last)
        def _():
            self.edge(False).wait_recv()
            for one in range(self.count):
                first = (rim + steps) * width + one
                self.spread(self.after[one].astype(FLOAT)[:rim], first, rim)

        pl.when(self.me == 0)(lambda: self.repeat(rim, 0))
        pl.when(self.me == self.last)(lambda: self.repeat(rim + steps - 1, rim + steps))
        sums = []
        for half in self.halves:
            value = self.step(rim - half)
            for index in range(rim - half + 1, rim + half + 1):
                value = value + self.step(index)
            sums.append(value)

        def move(index, sums):
            here, later = self.step(index + rim), []
            for seasonal, half, value in zip(self.seasonals, self.halves, sums):
                kernel = seasonal.shape[1]
                part = here - value * (1.0 / (2 * half + 1))
                seasonal[lax.div(index, kernel), lax.rem(index, kernel)] = part.astype(
                    HALF_FLOAT
                )
                later.append(
                    value + self.step(index + rim + half + 1) - self.step(index + rim - half)
                )
            return tuple(later)

        lax.fori_loop(0, steps, move, tuple(sums))
        ready()
        self.rows[...] = jnp.zeros_like(self.rows)
        base = 0
        for index, (seasonal, held, act) in enumerate(zip(self.seasonals, self.held, self.acts)):
            copies[1 + index].wait()
            count = act.shape[0]
            total = self.total.at[pl.ds(0, count)]
            total[...] = jnp.broadcast_to(self.bias[index : index + 1], total.shape)

            @pl.loop(0, seasonal.shape[1])
            def _(one, total=total, seasonal=seasonal, held=held):
                total[...] += dot_nn(seasonal[:, one].reshape(total.shape), held[one])

            value = jnp.tanh(total[...])
            act[...] = value
            value = value.astype(HALF_FLOAT).astype(FLOAT)
            for lane in range(self.rows.shape[0]):
                self.rows[lane, pl.ds(base * width, count), :] = value[
                    :, lane * 128 : lane * 128 + 128
                ]
            base += round_up(count // width, 8)
        per_time = self.x.shape[0] // self.count
        for one in range(self.count):
            for lane in range(self.rows.shape[0]):
                value = self.rows[lane, pl.ds(one, per_time, stride=width), :]
                self.x[
                    one * per_time : (one + 1) * per_time, lane * 128 : lane * 128 + 128
                ] = value.astype(HALF_FLOAT)

    def finish(self):
        pl.when(self.me < self.last)(lambda: self.edge(True).wait_send())
        pl.when(self.me > 0)(lambda: self.edge(False).wait_send())

    def turn(self, source):
        return pltpu.make_async_copy(source, self.series, self.local.at[0])

    def turned(self, source, target):
        self.turn(source).wait()
        for one in range(self.count):
            self.spread(self.series[one].astype(FLOAT), self.rim * self.width + one, self.steps)

        @pl.loop(0, self.steps)
        def _(index):
            target[index] = self.step(index + self.rim).astype(HALF_FLOAT)


class ForwardExtra(Extra):
    def __init__(self, sizes, wides, weights, front):
        super().__init__(sizes)
        self.front = front
        if front:
            series, cotangent, down_weights, bias, per_time, halves, rim = front
            count, steps, channels = series.shape
            series_rows = round_up(count, 16)
            self.inputs["series"] = (series, HBM_SPEC)
            self.inputs["down_bias"] = (bias, VMEM_SPEC)
            for index, weight in enumerate(down_weights):
                kernel = weight.shape[0]
                self.inputs[f"down{index}"] = (weight, HBM_SPEC)
                self.outputs[f"seasonal{index}"] = (
                    jax.ShapeDtypeStruct(
                        (steps // kernel, kernel, series_rows, channels), HALF_FLOAT
                    ),
                    VMEM_SPEC,
                )
                self.outputs[f"down_act{index}"] = (
                    jax.ShapeDtypeStruct((steps // kernel * series_rows, channels), FLOAT),
                    VMEM_SPEC,
                )
                rows = self.outputs[f"down_act{index}"][0].shape
                self.outputs[f"iso_act{index}"] = (
                    jax.ShapeDtypeStruct(rows, FLOAT),
                    VMEM_SPEC,
                )
                self.outputs[f"inner{index}"] = (
                    jax.ShapeDtypeStruct(rows, HALF_FLOAT),
                    VMEM_SPEC,
                )
            self.inputs["cotangent"] = (cotangent, HBM_SPEC)
            self.outputs["cotangent_steps"] = (
                jax.ShapeDtypeStruct((steps, series_rows, channels), HALF_FLOAT),
                VMEM_SPEC,
            )
            self.scratch["front"] = Front.scratch(series, down_weights, per_time, rim)
            wides = [self.outputs[f"seasonal{index}"][0] for index in range(len(down_weights))]
        self.turn_count = len(weights)
        for index, weight in enumerate(weights):
            channels, kernel, outs = weight.shape
            self.inputs[f"turn{index}"] = (weight, HBM_SPEC)
            self.outputs[f"turned{index}"] = (
                jax.ShapeDtypeStruct((kernel, channels, outs), HALF_FLOAT),
                HBM_SPEC,
            )
            self.scratch[f"turning{index}"] = Turn.scratch(weight)
        self.count = len(wides) if sizes else 0
        for index in range(self.count):
            if not front:
                self.inputs[f"wide{index}"] = (wides[index], HBM_SPEC)
            self.outputs[f"gathered{index}"] = (
                jax.ShapeDtypeStruct(WideExchange.shape(sizes, wides[index]), HALF_FLOAT),
                HBM_SPEC,
            )
            self.scratch[f"exchange{index}"] = WideExchange.scratch(sizes, wides[index])

    def bind(self, refs):
        super().bind(refs)
        self.exchanges = [
            WideExchange(
                self.place,
                refs[f"seasonal{i}" if self.front else f"wide{i}"],
                refs[f"gathered{i}"],
                refs[f"exchange{i}"],
            )
            for i in range(self.count)
        ]
        self.units = [unit for item in self.exchanges for unit in item.units()]
        self.unit_count = len(self.units)
        self.turns = [
            Turn(refs[f"turn{i}"], refs[f"turned{i}"], refs[f"turning{i}"])
            for i in range(self.turn_count)
        ]

    def inner(self):
        refs, base = self.refs, 0
        count = self.front[0].shape[0]
        rows = by_piece(refs["signal"], self.layers.rows, count)
        table = refs["down_bias"]
        for index in range(self.count):
            act_ref = refs[f"iso_act{index}"]
            pieces = act_ref.shape[0] // self.layers.width
            act = jnp.tanh(rows(base, pieces) + table[2 + index : 3 + index])
            down = refs[f"down_act{index}"][...].astype(HALF_FLOAT).astype(FLOAT)
            hat, _ = normed(act + down)
            act_ref[...] = act
            out = hat * table[8:9] + table[11:12]
            refs[f"inner{index}"][...] = out.astype(HALF_FLOAT)
            base += round_up(pieces, 8)

    def prepare(self):
        for item in self.turns:
            item.start()
        if not self.front:
            return super().prepare()
        refs, count = self.refs, self.count
        halves, rim = self.front[5:]
        self.layers = Front(
            refs["series"],
            [refs[f"down{i}"] for i in range(count)],
            refs["down_bias"],
            [refs[f"seasonal{i}"] for i in range(count)],
            [refs[f"down_act{i}"] for i in range(count)],
            refs["front"],
            halves,
            rim,
        )
        self.layers.start()
        self.layers.layers(functools.partial(self.run, 0.3))
        return self.layers.x

    def start(self):
        self.run(0.15)
        if self.front:
            self.layers.turn(self.refs["cotangent"]).start()
        for item in self.turns:
            item.run(0.25)

    def after_bins(self):
        self.run(0.55)
        if self.front:
            self.layers.turned(self.refs["cotangent"], self.refs["cotangent_steps"])
        for item in self.turns:
            item.run(0.25)

    def after_mixed(self):
        self.run(1.0)
        for item in self.turns:
            item.run(0.375)

    def after_signal(self):
        for item in self.turns:
            item.run(0.125)

    def finish(self):
        if self.front:
            self.inner()
            self.layers.finish()
        for item in self.turns:
            item.finish()
        for item in self.exchanges:
            item.wait()
            item.drain()


class BackwardExtra(Extra):
    def __init__(self, sizes, spec, wides, narrows, matrices, inners, acts, counts):
        super().__init__(sizes)
        self.counts = counts
        if sizes:
            for i, (inner, act) in enumerate(zip(inners, acts)):
                self.inputs[f"inner_grad{i}"] = (inner, VMEM_SPEC)
                self.inputs[f"act{i}"] = (act, VMEM_SPEC)
                self.outputs[f"down_grad{i}"] = (
                    jax.ShapeDtypeStruct(act.shape, HALF_FLOAT),
                    VMEM_SPEC,
                )
            channels = spec.shape[1]
            self.outputs["down_sums"] = (jax.ShapeDtypeStruct((8, channels), FLOAT), VMEM_SPEC)
            per_time, width = counts[1:]
            self.scratch["piece_rows"] = [
                pltpu.VMEM((channels // 128, per_time * width, 128), FLOAT)
            ]
        self.batches = lax.axis_size("batch")
        others = jax.ShapeDtypeStruct((self.batches - 1,) + spec.shape, HALF_FLOAT)
        self.inputs["spec_forward"] = (spec, HBM_SPEC)
        self.outputs["specs"] = (others, HBM_SPEC)
        self.outputs["grads"] = (others, HBM_SPEC)
        dma = pltpu.SemaphoreType.DMA
        self.scratch["other_sems"] = [dma((self.batches,))] * 4
        self.count = len(wides) if sizes else 0
        self.kinds = [kind for kind, _ in matrices] if sizes else []
        for i in range(self.count):
            wide, narrow = wides[i], narrows[i]
            groups, members, batches = sizes
            channels = narrow.shape[1]
            self.inputs[f"wide{i}"] = (wide, HBM_SPEC)
            self.inputs[f"narrow{i}"] = (narrow, HBM_SPEC)
            self.outputs[f"up{i}"] = (
                jax.ShapeDtypeStruct(
                    (wide.shape[1], channels // (groups * members), channels // batches), FLOAT
                ),
                VMEM_SPEC,
            )
            self.scratch[f"wide_in{i}"] = [
                pltpu.VMEM(WideExchange.shape(sizes, wide), HALF_FLOAT)
            ]
            self.scratch[f"rows{i}"] = [
                pltpu.VMEM((members * batches,) + narrow.shape, HALF_FLOAT)
            ]
            self.scratch[f"exchange{i}"] = WideExchange.scratch(sizes, wide)
            self.scratch[f"gather{i}"] = NarrowGather.scratch(sizes, narrow)
            self.scratch[f"product{i}"] = KernelProduct.scratch(sizes, "up", wide, narrow)
        for i, kind in enumerate(self.kinds):
            value = matrices[i][1]
            self.inputs[f"matrix{i}"] = (value, HBM_SPEC)
            self.outputs[f"matrix_sum{i}"] = (
                jax.ShapeDtypeStruct(MatrixSum.piece_shape(sizes, kind, value), FLOAT),
                VMEM_SPEC,
            )
            self.scratch[f"sum{i}"] = MatrixSum.scratch(sizes, kind, value)

    def bind(self, refs):
        super().bind(refs)
        self.exchanges, self.gathers, self.products = [], [], []
        for i in range(self.count):
            wide_in, rows = refs[f"wide_in{i}"][0], refs[f"rows{i}"][0]
            self.exchanges.append(
                WideExchange(self.place, refs[f"wide{i}"], wide_in, refs[f"exchange{i}"])
            )
            self.gathers.append(
                NarrowGather(self.place, refs[f"narrow{i}"], rows, refs[f"gather{i}"])
            )
            self.products.append(
                KernelProduct(self.place, "up", wide_in, rows, refs[f"up{i}"], refs[f"product{i}"])
            )
        self.sums = [
            MatrixSum(
                self.place, kind, refs[f"matrix{i}"], refs[f"matrix_sum{i}"], refs[f"sum{i}"]
            )
            for i, kind in enumerate(self.kinds)
        ]

    def other(self, index, turn):
        source, target = (
            (self.refs["spec_forward"], self.refs["specs"]),
            (self.refs["spec"], self.refs["grads"]),
        )[index]
        sems = self.refs["other_sems"]
        core = lax.rem(lax.axis_index("batch") + turn, self.batches)
        return send_copy(
            source,
            target.at[turn - 1],
            sems[2 * index].at[turn],
            sems[2 * index + 1].at[turn],
            (core, lax.axis_index("tm")),
        )

    def start(self):
        self.units = [unit for item in self.exchanges for unit in item.units()]
        self.unit_count = len(self.units)
        for turn in range(1, self.batches):
            self.other(0, turn).start()
        for item in self.gathers + self.sums:
            item.start()

    def after_bins(self):
        self.run(0.6)
        for item in self.gathers:
            item.forward()

    def after_mixed(self):
        self.run(0.3)
        if self.count:
            self.multiply(0)

    def after_spec(self):
        for turn in range(1, self.batches):
            self.other(1, turn).start()

    def multiply(self, index):
        self.exchanges[index].wait()
        self.gathers[index].wait()
        self.products[index].multiply()
        self.products[index].start_partials()

    def after_signal(self):
        self.run(1.0)
        for index in range(1, self.count):
            self.multiply(index)
        for item in self.sums:
            item.add_cores()

    def down_grads(self):
        refs, base = self.refs, 0
        count, _, width = self.counts
        rows = by_piece(refs["signal"], refs["piece_rows"][0], count)
        refs["down_sums"][...] = jnp.zeros_like(refs["down_sums"])
        for index in range(self.count):
            act = refs[f"act{index}"][...]
            pieces = act.shape[0] // width
            grad = rows(base, pieces) + refs[f"inner_grad{index}"][...]
            grad = (grad * (1.0 - act * act)).astype(HALF_FLOAT)
            refs[f"down_grad{index}"][...] = grad
            refs["down_sums"][index : index + 1] = jnp.sum(
                grad.astype(FLOAT), axis=0, keepdims=True
            )
            base += round_up(pieces, 8)

    def finish(self):
        if self.count:
            self.down_grads()
        for item in self.sums:
            item.add_members()
        for item in self.products:
            item.sum_partials()
            item.start_final()
        for item in self.sums + self.products:
            item.finish()
        for item in self.exchanges + self.gathers:
            item.drain()
        for index in range(2):
            for turn in range(1, self.batches):
                self.other(index, turn).wait()


def spectral(values, shapes, weights, back, extra):
    devices, batches = lax.axis_size("tm"), lax.axis_size("batch")
    pieces_list = tuple(shape[1] for shape in shapes)
    count, _, channels = shapes[0]
    wide = [round_up(pieces, 8) for pieces in pieces_list]
    per_time, per_bin = sum(wide), 2 * sum(wide)
    assert count <= devices and per_time % 16 == 0
    inputs = {}
    if values:
        packed = jnp.concatenate(
            [
                jnp.pad(value, ((0, 0), (0, room - value.shape[1]), (0, 0)))
                for value, room in zip(values, wide)
            ],
            axis=1,
        ).reshape(count * per_time, channels)
        inputs["x"] = (packed, HBM_SPEC)
    constants = spectral_constants(devices, pieces_list)
    rows_time, rows_bin = devices * per_time, devices * per_bin
    dma = pltpu.SemaphoreType.DMA
    for index, weight in enumerate(weights):
        inputs[f"weight{index}"] = (weight, HBM_SPEC)
    for key, value in zip(("table", "inverse", "move", "unmove"), constants):
        inputs[key] = (value, VMEM_SPEC)
    outputs = {
        "spec": (jax.ShapeDtypeStruct((rows_bin, channels), HALF_FLOAT), VMEM_SPEC),
        "signal": (jax.ShapeDtypeStruct((count * per_time, channels), HALF_FLOAT), VMEM_SPEC),
    }
    scratch = {
        "buffers": [pltpu.VMEM((rows_time, channels), HALF_FLOAT)]
        + [pltpu.VMEM((rows_bin, channels), HALF_FLOAT)] * 5
        + [pltpu.VMEM((rows_time, channels), HALF_FLOAT)]
        + [
            pltpu.VMEM((weight.shape[0], 2, weight.shape[2] * batches, channels), HALF_FLOAT)
            for weight in weights
        ],
        "sems": [dma((devices,))] * 8 + [dma((2, batches)), dma((2, batches)), dma((3,))],
    }
    inputs.update(extra.inputs)
    outputs.update(extra.outputs)
    scratch.update(extra.scratch)
    sizes = (devices, batches, count, pieces_list)

    def body(refs):
        extra.bind(refs)
        spectral_body(sizes, back, refs, extra)

    results = remote_call(
        body,
        inputs,
        outputs,
        scratch,
        1 if back else 0,
        2 * rows_bin * channels * channels * 4,
        4 * channels * channels * sum(pieces_list),
        "spectral_back" if back else "spectral_forward",
    )
    signal = results["signal"].reshape(count, per_time, channels)
    signals, offset = [], 0
    for pieces, room in zip(pieces_list, wide):
        signals.append(signal[:, offset : offset + pieces])
        offset += room
    return results, signals


def gelu_pair(value):
    slope = math.sqrt(2.0 / math.pi)
    square = value * value
    bent = jnp.tanh(slope * value * (1.0 + 0.044715 * square))
    rise = 0.5 * (1.0 + bent)
    turn = 0.5 * slope * value * (1.0 - bent * bent) * (1.0 + 3.0 * 0.044715 * square)
    return (value * rise).astype(HALF_FLOAT), (rise + turn).astype(HALF_FLOAT)


def by_time(values):
    turned = jnp.swapaxes(values, 0, 1)
    extra = -turned.shape[1] % 16
    return jnp.pad(turned, ((0, 0), (0, extra)) + ((0, 0),) * (turned.ndim - 2))


def by_series(values, count):
    return jnp.swapaxes(values[:, :count], 0, 1)


def neighbours(low_side, high_side):
    count = lax.axis_size("tm")
    onward = [(i, i + 1) for i in range(count - 1)]
    return (
        lax.ppermute(high_side, "tm", onward),
        lax.ppermute(low_side, "tm", [(j, i) for i, j in onward]),
    )


def window_sum(values, first, width, count):
    total, level, size = None, values, 1
    while width:
        if width & 1:
            part = level[first : first + count]
            total = part if total is None else total + part
            first += size
        width >>= 1
        if width:
            level = level[:-size] + level[size:]
            size *= 2
    return total


def seasonal_parts(series, halves, rim):
    steps = series.shape[0]
    before, after = neighbours(series[:rim], series[steps - rim :])
    position = lax.axis_index("tm")
    before = jnp.where(position == 0, jnp.broadcast_to(series[:1], before.shape), before)
    is_final = position == lax.axis_size("tm") - 1
    after = jnp.where(is_final, jnp.broadcast_to(series[-1:], after.shape), after)
    wide = jnp.concatenate([before, series, after]).astype(FLOAT)
    parts = []
    for half in halves:
        mean = window_sum(wide, rim - half, 2 * half + 1, steps) / (2 * half + 1)
        parts.append((series.astype(FLOAT) - mean).astype(HALF_FLOAT))
    return parts


def series_gradient(grads, halves, rim):
    steps = grads[0].shape[0]
    wide = 0.0
    for grad, half in zip(grads, halves):
        padded = jnp.pad(grad, ((2 * rim, 2 * rim), (0, 0), (0, 0)))
        wide = wide + window_sum(padded, rim - half, 2 * half + 1, steps + 2 * rim) / (
            2 * half + 1
        )
    low_rim, high_rim = wide[:rim], wide[rim + steps :]
    before, after = neighbours(low_rim, high_rim)
    position = lax.axis_index("tm")
    is_final = position == lax.axis_size("tm") - 1
    low_sum = jnp.pad(jnp.sum(low_rim, axis=0, keepdims=True), ((0, rim - 1), (0, 0), (0, 0)))
    high_sum = jnp.pad(jnp.sum(high_rim, axis=0, keepdims=True), ((rim - 1, 0), (0, 0), (0, 0)))
    before = jnp.where(position == 0, low_sum, before)
    after = jnp.where(is_final, high_sum, after)
    middle = jnp.zeros((steps - 2 * rim,) + before.shape[1:], FLOAT)
    edges = jnp.concatenate([before, middle, after])
    return (sum(grads) - wide[rim : rim + steps] - edges).astype(HALF_FLOAT)


def step_block(kernel):
    return next(size for size in (4, 3, 2, 1) if kernel % size == 0)


def row_spec(block):
    return pl.BlockSpec(block, lambda i: (0,) * len(block))


def steps_spec(values, block):
    pieces, _, series, channels = values.shape
    return pl.BlockSpec((pieces, block, series, channels), lambda i: (0, i, 0, 0))


def weight_spec(weight, block):
    return pl.BlockSpec((block,) + weight.shape[1:], lambda i: (i, 0, 0))


def local_call(kernel, grid, inputs, outputs, flops, nbytes, name):
    return pl.pallas_call(
        kernel,
        out_shape=tuple(shape for shape, _ in outputs),
        grid=(grid,),
        in_specs=[spec for _, spec in inputs],
        out_specs=tuple(spec for _, spec in outputs),
        compiler_params=pltpu.CompilerParams(vmem_limit_bytes=48 * 1024 * 1024),
        cost_estimate=pl.CostEstimate(
            flops=flops, bytes_accessed=nbytes, transcendentals=0
        ),
        name=name,
    )(*[value for value, _ in inputs])


def down_kernel(x_ref, w_ref, b_ref, out_ref):
    step = pl.program_id(0)

    @pl.when(step == 0)
    def _():
        out_ref[...] = jnp.broadcast_to(b_ref[...], out_ref.shape)

    total = out_ref[...]
    for one in range(w_ref.shape[0]):
        total = total + dot_nn(x_ref[:, one].reshape(total.shape), w_ref[one])
    out_ref[...] = total

    @pl.when(step == pl.num_programs(0) - 1)
    def _():
        out_ref[...] = jnp.tanh(out_ref[...])


def down_layer(seasonal, weight, bias_row):
    pieces, kernel, series, channels = seasonal.shape
    block = step_block(kernel)
    rows = pieces * series
    (down_act,) = local_call(
        down_kernel,
        kernel // block,
        [
            (seasonal, steps_spec(seasonal, block)),
            (weight, weight_spec(weight, block)),
            (bias_row[None], row_spec((1, channels))),
        ],
        [(jax.ShapeDtypeStruct((rows, channels), FLOAT), row_spec((rows, channels)))],
        2 * seasonal.size * channels,
        2 * (seasonal.size + weight.size),
        "down_layer",
    )
    return down_act


def normed(values):
    center = values - jnp.mean(values, axis=-1, keepdims=True)
    spread = jnp.mean(center * center, axis=-1, keepdims=True)
    scale = lax.rsqrt(spread + EPSILON)
    return center * scale, scale


def normed_back(grad, hat, scale):
    return (
        grad
        - jnp.mean(grad, axis=-1, keepdims=True)
        - hat * jnp.mean(grad * hat, axis=-1, keepdims=True)
    ) * scale


def up_kernel(picks, inner_ref, x_ref, w_ref, rows_ref, act_ref, out_ref):
    bias_row, gain_row, shift_row = (rows_ref[i : i + 1] for i in picks)
    inner = inner_ref[...]
    for one in range(w_ref.shape[0]):
        act = jnp.tanh(dot_nn(inner, w_ref[one]) + bias_row)
        hat, _ = normed(act + x_ref[:, one].reshape(act.shape).astype(FLOAT))
        act_ref[:, one] = act.reshape(act_ref.shape[0], act_ref.shape[2], act_ref.shape[3])
        out = (hat * gain_row + shift_row).astype(HALF_FLOAT)
        out_ref[:, one] = out.reshape(out_ref.shape[0], out_ref.shape[2], out_ref.shape[3])


def up_layer(inner, seasonal, weight, rows, picks):
    pieces, kernel, series, channels = seasonal.shape
    block = step_block(kernel)
    return local_call(
        functools.partial(up_kernel, picks),
        kernel // block,
        [
            (inner, row_spec(inner.shape)),
            (seasonal, steps_spec(seasonal, block)),
            (weight, weight_spec(weight, block)),
            (rows, row_spec(rows.shape)),
        ],
        [
            (jax.ShapeDtypeStruct(seasonal.shape, FLOAT), steps_spec(seasonal, block)),
            (jax.ShapeDtypeStruct(seasonal.shape, HALF_FLOAT), steps_spec(seasonal, block)),
        ],
        2 * seasonal.size * channels,
        8 * seasonal.size + 2 * weight.size,
        "up_layer",
    )


def up_back_kernel(
    grad_ref, merge_ref, act_ref, x_ref, w_ref, gain_ref, outer_ref, up_ref, inner_ref, sums_ref
):
    @pl.when(pl.program_id(0) == 0)
    def _():
        inner_ref[...] = jnp.zeros_like(inner_ref)
        sums_ref[...] = jnp.zeros_like(sums_ref)

    shape = inner_ref.shape
    block = (x_ref.shape[0], x_ref.shape[2], x_ref.shape[3])
    gain_row = gain_ref[8:9]
    total = inner_ref[...]
    sums = [sums_ref[i : i + 1] for i in range(3)]
    for one in range(w_ref.shape[0]):
        grad = dot_nt(grad_ref[:, one].reshape(shape), merge_ref[0])
        act = act_ref[:, one].reshape(shape)
        hat, scale = normed(act + x_ref[:, one].reshape(shape).astype(FLOAT))
        outer = normed_back(grad * gain_row, hat, scale)
        up = (outer * (1.0 - act * act)).astype(HALF_FLOAT)
        total = total + dot_nt(up, w_ref[one])
        outer_ref[:, one] = outer.reshape(block)
        up_ref[:, one] = up.reshape(block)
        for i, value in enumerate((up.astype(FLOAT), grad * hat, grad)):
            sums[i] = sums[i] + jnp.sum(value, axis=0, keepdims=True)
    inner_ref[...] = total
    for i in range(3):
        sums_ref[i : i + 1] = sums[i]


def up_layer_back(grad, merge, index, act, seasonal, weight, table):
    pieces, kernel, series, channels = seasonal.shape
    block = step_block(kernel)
    rows = pieces * series
    spec = steps_spec(seasonal, block)
    return local_call(
        up_back_kernel,
        kernel // block,
        [
            (grad, spec),
            (merge, pl.BlockSpec((1,) + merge.shape[1:], lambda i: (index, 0, 0))),
            (act, spec),
            (seasonal, spec),
            (weight, weight_spec(weight, block)),
            (table, row_spec(table.shape)),
        ],
        [
            (jax.ShapeDtypeStruct(seasonal.shape, FLOAT), spec),
            (jax.ShapeDtypeStruct(seasonal.shape, HALF_FLOAT), spec),
            (jax.ShapeDtypeStruct((rows, channels), FLOAT), row_spec((rows, channels))),
            (jax.ShapeDtypeStruct((8, channels), FLOAT), row_spec((8, channels))),
        ],
        4 * seasonal.size * channels,
        14 * seasonal.size + 2 * weight.size,
        "up_layer_back",
    )


def down_back_kernel(grad_ref, w_ref, outer_ref, out_ref):
    grad = grad_ref[...]
    block = (out_ref.shape[0], out_ref.shape[2], out_ref.shape[3])
    for one in range(w_ref.shape[0]):
        out_ref[:, one] = dot_nt(grad, w_ref[one]).reshape(block) + outer_ref[:, one]


def down_layer_back(grad, weight, outer):
    pieces, kernel, series, channels = outer.shape
    block = step_block(kernel)
    spec = steps_spec(outer, block)
    (seasonal_grad,) = local_call(
        down_back_kernel,
        kernel // block,
        [(grad, row_spec(grad.shape)), (weight, weight_spec(weight, block)), (outer, spec)],
        [(jax.ShapeDtypeStruct(outer.shape, FLOAT), spec)],
        2 * outer.size * channels,
        8 * outer.size + 2 * weight.size,
        "down_layer_back",
    )
    return seasonal_grad


class Branch:
    def __init__(self, index, shape, down_weight, table):
        self.index, self.table = index, table
        self.count, steps, channels = shape
        self.kernel = down_weight.shape[0]
        self.pieces = steps // self.kernel
        self.series = round_up(self.count, 16)
        self.down_weight = down_weight
        self.gain_row, self.shift_row = table[8], table[11]

    def down(self, seasonal, down_act=None):
        self.seasonal = seasonal.reshape(self.pieces, self.kernel, self.series, -1)
        if down_act is None:
            down_act = down_layer(self.seasonal, self.down_weight, self.table[self.index])
        self.down_act = down_act
        self.down_low = down_act.astype(HALF_FLOAT)

    def to_series(self, rows):
        return by_series(rows.reshape(self.pieces, self.series, -1), self.count)

    def from_series(self, values):
        return by_time(values).reshape(self.pieces * self.series, -1)

    def inner(self, iso_out):
        act = jnp.tanh(self.from_series(iso_out).astype(FLOAT) + self.table[2 + self.index])
        inner_in = act + self.down_low.astype(FLOAT)
        return act, layer_norm(inner_in, self.gain_row, self.shift_row).astype(HALF_FLOAT)

    def up(self, iso_act, inner_low, up_weight):
        self.up_weight, self.iso_act, self.inner_low = up_weight, iso_act, inner_low
        self.act, out = up_layer(
            inner_low, self.seasonal, up_weight, self.table, (4 + self.index, 8, 11)
        )
        return out.reshape(-1, out.shape[3])

    def up_back(self, grad_merged, merge):
        self.outer, self.grad_up, grad_inner, sums = up_layer_back(
            grad_merged.reshape(self.seasonal.shape),
            merge,
            self.index,
            self.act,
            self.seasonal,
            self.up_weight,
            self.table,
        )
        inner_in = self.iso_act + self.down_low.astype(FLOAT)
        _, inner_pull = jax.vjp(layer_norm, inner_in, self.gain_row, self.shift_row)
        self.grad_inner_in, gain_inner, shift_inner = inner_pull(grad_inner)
        grad_iso = self.grad_inner_in * (1.0 - self.iso_act * self.iso_act)
        self.iso_sum, self.up_sum = jnp.sum(grad_iso, axis=0), sums[0]
        self.gain_sum, self.shift_sum = sums[1] + gain_inner, sums[2] + shift_inner
        return grad_iso.astype(HALF_FLOAT)

    def down_back(self, grad_signal):
        grad_down = self.from_series(grad_signal).astype(FLOAT) + self.grad_inner_in
        self.grad_down = (grad_down * (1.0 - self.down_act * self.down_act)).astype(HALF_FLOAT)
        return jnp.sum(self.grad_down.astype(FLOAT), axis=0)

    def seasonal_back(self):
        grad = down_layer_back(self.grad_down, self.down_weight, self.outer)
        return grad.reshape(-1, self.series, grad.shape[3])


def batch_split(values, split, join):
    return lax.all_to_all(values, "batch", split_axis=split, concat_axis=join, tiled=True)


def time_sum(values, dim):
    return lax.psum_scatter(
        values.astype(HALF_FLOAT), "tm", scatter_dimension=dim, tiled=True
    ).astype(FLOAT)


def plain_gradients(wides, narrows, downs):
    results = []
    for wide, narrow, down in zip(wides, narrows, downs):
        wide = jnp.swapaxes(wide, 0, 1).reshape(wide.shape[1], -1, wide.shape[3])
        if down:
            wide, narrow = batch_split(wide, 2, 1), lax.all_gather(narrow, "batch", tiled=True)
            value = jnp.einsum("knc,nd->kcd", wide, narrow, preferred_element_type=FLOAT)
        else:
            wide = lax.all_gather(wide, "batch", axis=1, tiled=True)
            narrow = batch_split(narrow, 1, 0)
            value = jnp.einsum("nd,knc->dkc", narrow, wide, preferred_element_type=FLOAT)
        results.append(time_sum(value, 2))
    return results


def plain_sums(matrices):
    results = []
    for kind, value in matrices:
        batch_dim, time_dim = (0, 1) if kind == "rows" else (value.ndim - 1, value.ndim - 2)
        value = lax.psum_scatter(
            value.astype(FLOAT), "batch", scatter_dimension=batch_dim, tiled=True
        )
        results.append(time_sum(value, time_dim))
    return results


def per_device(
    series_in,
    out_cotangent,
    out_mask,
    down_twelve,
    down_sixteen,
    iso_twelve,
    iso_sixteen,
    up_twelve,
    up_sixteen,
    branch_bias,
    merge_weight,
    hidden_weight,
    hidden_bias,
    output_weight,
    head_bias,
    norm_gain,
    norm_shift,
):
    series_dev, step_count, channels = series_in.shape
    halves = (down_twelve.shape[0] // 2, down_sixteen.shape[0] // 2)
    rim = max(halves)
    hidden_rows = hidden_bias.reshape(-1, channels)
    table = jnp.concatenate([branch_bias, head_bias, norm_gain, norm_shift, hidden_rows])
    table = jnp.pad(table, ((0, -table.shape[0] % 8), (0, 0))).astype(FLOAT)
    heads, gains, shifts = table[6:8], table[8:11], table[11:14]
    down_weights = (down_twelve, down_sixteen)
    branches = [
        Branch(k, series_in.shape, down_weights[k], table) for k in range(2)
    ]
    iso_weights = (iso_twelve, iso_sixteen)
    sizes = plane_sizes(channels)
    up_weights = [up_twelve, up_sixteen]
    turns = [weight for weight in up_weights if weight.shape[1] % 8 == 0]
    shapes = [(series_dev, branch.pieces, channels) for branch in branches]
    if sizes:
        per_time = sum(round_up(branch.pieces, 8) for branch in branches)
        values, wides = None, []
        front = (series_in, out_cotangent, down_weights, table, per_time, halves, rim)
    else:
        for branch, seasonal in zip(branches, seasonal_parts(by_time(series_in), halves, rim)):
            branch.down(seasonal)
        values = [branch.to_series(branch.down_low) for branch in branches]
        wides = [branch.seasonal for branch in branches]
        front = None
    forward, iso_outs = spectral(
        values, shapes, iso_weights, False, ForwardExtra(sizes, wides, turns, front)
    )
    if sizes:
        for k in range(2):
            branches[k].down(forward[f"seasonal{k}"], forward[f"down_act{k}"])
        inners = [(forward[f"iso_act{k}"], forward[f"inner{k}"]) for k in range(2)]
        cotangent = forward["cotangent_steps"]
    else:
        inners = [branches[k].inner(iso_outs[k]) for k in range(2)]
        cotangent = by_time(out_cotangent)
    turned = [forward[f"turned{i}"] for i in range(len(turns))]
    up_weights = [
        jnp.swapaxes(weight, 0, 1) if weight.shape[1] % 8 else turned.pop(0)
        for weight in up_weights
    ]
    outs = [
        branch.up(*inner, weight)
        for branch, inner, weight in zip(branches, inners, up_weights)
    ]
    row_count = outs[0].shape[0]
    merged = dot_nn(outs[0], merge_weight[0]) + dot_nn(outs[1], merge_weight[1]) + heads[0]
    first_low = layer_norm(merged, gains[1], shifts[1]).astype(HALF_FLOAT)
    hidden_pre = jnp.dot(
        first_low, hidden_weight, preferred_element_type=FLOAT
    ) + table[14 : 14 + hidden_rows.shape[0]].reshape(-1)
    hidden_low, hidden_slope = gelu_pair(hidden_pre)
    final_in = merged + (
        jnp.dot(hidden_low, output_weight, preferred_element_type=FLOAT) + heads[1]
    )
    mask_rows = by_time(out_mask.astype(FLOAT)).reshape(row_count, 1)
    result = by_series(
        (layer_norm(final_in, gains[2], shifts[2]) * mask_rows)
        .astype(HALF_FLOAT)
        .reshape(step_count, -1, channels),
        series_dev,
    )
    grad_result = cotangent.astype(FLOAT).reshape(row_count, channels) * mask_rows
    normed_final, final_pull = jax.vjp(layer_norm, final_in, gains[2], shifts[2])
    grad_final, gain_final, shift_final = final_pull(grad_result)
    grad_feed = grad_final.astype(HALF_FLOAT)
    grad_output_weight = jnp.einsum(
        "nd,nf->df", grad_feed, hidden_low, preferred_element_type=FLOAT
    ).astype(HALF_FLOAT)
    grad_output_bias = jnp.sum(grad_feed.astype(FLOAT), axis=0)
    grad_hidden_low = jnp.einsum(
        "nd,fd->nf", grad_feed, output_weight, preferred_element_type=FLOAT
    )
    grad_hidden_pre = (grad_hidden_low * hidden_slope.astype(FLOAT)).astype(HALF_FLOAT)
    grad_hidden_weight = jnp.einsum(
        "nd,nf->df", first_low, grad_hidden_pre, preferred_element_type=FLOAT
    ).astype(HALF_FLOAT)
    grad_hidden_bias = jnp.sum(grad_hidden_pre.astype(FLOAT), axis=0)
    grad_first = jnp.einsum(
        "nf,df->nd", grad_hidden_pre, hidden_weight, preferred_element_type=FLOAT
    )
    normed_first, first_pull = jax.vjp(layer_norm, merged, gains[1], shifts[1])
    grad_merged_norm, gain_first, shift_first = first_pull(grad_first)
    grad_merged = (grad_final + grad_merged_norm).astype(HALF_FLOAT)
    grad_merge_bias = jnp.sum(grad_merged.astype(FLOAT), axis=0)
    grad_merge_weight = jnp.stack(
        [
            jnp.einsum("ne,nd->ed", grad_merged, out, preferred_element_type=FLOAT)
            for out in outs
        ]
    ).astype(HALF_FLOAT)
    grad_isos = [branches[k].up_back(grad_merged, merge_weight) for k in range(2)]
    matrices = (
        ("rows", grad_hidden_weight),
        ("lanes", grad_merge_weight),
        ("lanes", grad_output_weight),
    )
    up_wides = [branch.grad_up for branch in branches]
    up_narrows = [branch.inner_low for branch in branches]
    backward, grad_signals = spectral(
        [branch.to_series(grad) for branch, grad in zip(branches, grad_isos)],
        shapes,
        iso_weights,
        True,
        BackwardExtra(
            sizes,
            forward["spec"],
            up_wides,
            up_narrows,
            matrices[:2],
            [branch.grad_inner_in for branch in branches],
            [branch.down_act for branch in branches],
            (
                series_dev,
                sum(round_up(branch.pieces, 8) for branch in branches),
                branches[0].series,
            ),
        ),
    )
    iso_parts, first = [], 0
    for bins in (branches[0].pieces, branches[1].pieces):
        iso_parts.append(
            iso_gradients(
                forward["spec"],
                backward["specs"],
                backward["spec"],
                backward["grads"],
                first,
                bins,
            )
        )
        first += round_up(bins, 8)
    if sizes:
        down_sums = backward["down_sums"][:2]
        down_narrows = [backward["down_grad0"], backward["down_grad1"]]
    else:
        down_sums = jnp.stack([branches[k].down_back(grad_signals[k]) for k in range(2)])
        down_narrows = [branch.grad_down for branch in branches]
    one, two = branches
    singles = (one.iso_sum, two.iso_sum, one.up_sum, two.up_sum)
    singles += (one.gain_sum + two.gain_sum, gain_first, gain_final)
    singles += (one.shift_sum + two.shift_sum, shift_first, shift_final)
    singles += (grad_merge_bias, grad_output_bias)
    vectors = jnp.concatenate(
        [down_sums] + [row[None] for row in singles] + [grad_hidden_bias.reshape(-1, channels)]
    )
    vectors = jnp.pad(vectors, ((0, -vectors.shape[0] % 8), (0, 0)))
    if sizes:
        downs, vectors, grad_series, last_sum = down_gradients(
            sizes,
            (forward["gathered0"], forward["gathered1"]),
            down_narrows,
            vectors,
            (down_twelve, down_sixteen),
            [branch.outer.reshape(step_count, -1, channels) for branch in branches],
            halves,
            rim,
            series_dev,
            matrices[2],
        )
        downs = [jnp.transpose(value, (0, 2, 1)) for value in downs]
        ups = [jnp.transpose(backward[key], (2, 0, 1)) for key in ("up0", "up1")]
        sums = [backward["matrix_sum0"], backward["matrix_sum1"], last_sum]
    else:
        vectors = lax.psum(vectors, ("tm", "batch"))
        grad_seasonals = [branch.seasonal_back() for branch in branches]
        grad_series = by_series(series_gradient(grad_seasonals, halves, rim), series_dev)
        downs = plain_gradients(wides, down_narrows, (True, True))
        ups = plain_gradients(up_wides, up_narrows, (False, False))
        sums = plain_sums(matrices)
    me, devices = lax.axis_index("tm"), lax.axis_size("tm")
    width = channels // devices
    rows = lax.dynamic_slice_in_dim(vectors[:14], me * width, width, axis=1)
    hidden_width = hidden_bias.shape[0] // devices
    hidden_sum = vectors[14 : 14 + hidden_rows.shape[0]].reshape(-1)
    vector_parts = (
        rows[:6],
        lax.dynamic_slice_in_dim(hidden_sum, me * hidden_width, hidden_width),
        rows[12:14],
        rows[6:9],
        rows[9:12],
    )
    return (
        result,
        grad_series,
        downs[0],
        downs[1],
        iso_parts[0],
        iso_parts[1],
        ups[0],
        ups[1],
        vector_parts[0],
        jnp.swapaxes(sums[1], 1, 2),
        sums[0],
        vector_parts[1],
        sums[2].T,
        vector_parts[2],
        vector_parts[3],
        vector_parts[4],
    )


def solution(mesh):
    placed = (
        P("batch", "tm", None),
        P("batch", "tm", None),
        P("batch", "tm"),
        P(),
        P(),
        P("tm", None, "batch", None),
        P("tm", None, "batch", None),
        P(),
        P(),
        P(),
        P(),
        P(),
        P(),
        P(),
        P(),
        P(),
        P(),
    )
    return jax.shard_map(
        per_device,
        mesh=mesh,
        in_specs=placed,
        out_specs=(
            P("batch", "tm", None),
            P("batch", "tm", None),
            P(None, "batch", "tm"),
            P(None, "batch", "tm"),
            P("tm", None, "batch", None),
            P("tm", None, "batch", None),
            P("batch", None, "tm"),
            P("batch", None, "tm"),
            P(None, "tm"),
            P(None, "batch", "tm"),
            P("batch", "tm"),
            P("tm"),
            P("batch", "tm"),
            P(None, "tm"),
            P(None, "tm"),
            P(None, "tm"),
        ),
        check_vma=False,
    )
```

```python
import functools
import math

import jax
import jax.numpy as jnp
import numpy as np
from jax import lax
from jax.experimental import pallas as pl
from jax.experimental.pallas import tpu as pltpu
from jax.sharding import PartitionSpec as P

FLOAT = jnp.float32
HALF_FLOAT = jnp.bfloat16
HIGHEST = lax.Precision.HIGHEST
EPSILON = 1e-05
MESH = pl.DeviceIdType.MESH


def layer_norm(values, gain_row, bias_row):
    center = values - jnp.mean(values, axis=-1, keepdims=True)
    spread = jnp.mean(center * center, axis=-1, keepdims=True)
    return center * lax.rsqrt(spread + EPSILON) * gain_row + bias_row


def round_up(value, multiple):
    return -(-value // multiple) * multiple


def spectral_constants(devices, pieces_list):
    padded = [round_up(pieces, 8) for pieces in pieces_list]
    per_time, per_bin = sum(padded), 2 * sum(padded)
    table = np.zeros((devices, per_bin, devices, per_time), np.float64)
    offset = 0
    for pieces, wide in zip(pieces_list, padded):
        length = devices * pieces
        index = np.arange(length)
        angle = (2.0 * math.pi / length) * (np.outer(index, index) % length)
        factor = 1.0 / math.sqrt(length)
        for part, values in enumerate((np.cos(angle) * factor, -np.sin(angle) * factor)):
            row = 2 * offset + part * wide
            table[:, row : row + pieces, :, offset : offset + pieces] = values.reshape(
                devices, pieces, devices, pieces
            )
        offset += wide
    table = table.reshape(devices * per_bin, devices * per_time).astype(np.float32)
    high = table.astype(HALF_FLOAT)
    low = (table - high.astype(np.float32)).astype(HALF_FLOAT)
    order = []
    offset = 0
    for wide in padded:
        for one_bin in range(wide):
            for part in range(2):
                for series in range(devices):
                    order.append(series * per_bin + 2 * offset + part * wide + one_bin)
        offset += wide
    move = np.zeros((devices * per_bin, devices * per_bin), np.float32)
    move[np.arange(len(order)), order] = 1.0
    move = move.astype(HALF_FLOAT)
    return (
        jnp.asarray(np.stack([high, low])),
        jnp.asarray(np.stack([high.T, low.T])),
        jnp.asarray(move),
        jnp.asarray(np.ascontiguousarray(move.T)),
    )


def dot_nn(left, right):
    return jnp.dot(left, right, preferred_element_type=FLOAT)


def dot_nt(left, right):
    return lax.dot_general(left, right, (((1,), (1,)), ((), ())), preferred_element_type=FLOAT)


def spectral_body(sizes, back, refs, extra):
    devices, batches, count, pieces_list = sizes
    w1_ref, w2_ref = refs["weight0"], refs["weight1"]
    table_ref, inverse_ref = refs["table"], refs["inverse"]
    move_ref, unmove_ref = refs["move"], refs["unmove"]
    spec_ref, signal_ref = refs["spec"], refs["signal"]
    (one, two, three, mixed, spread, bins_out, four, w1, w2) = refs["buffers"]
    (s1, r1, s2, r2, s3, r3, s4, r4, ws, wr, own) = refs["sems"]
    me = lax.axis_index("tm")
    mine = lax.axis_index("batch")
    wide = [round_up(pieces, 8) for pieces in pieces_list]
    per_time, per_bin = sum(wide), 2 * sum(wide)
    weights = ((w1_ref, w1), (w2_ref, w2))

    barrier = pltpu.get_barrier_semaphore()

    @pl.loop(1, devices)
    def _(step):
        pl.semaphore_signal(
            barrier, inc=1, device_id=(mine, lax.rem(me + step, devices)), device_id_type=MESH
        )

    for step in range(1, batches):
        pl.semaphore_signal(
            barrier, inc=1, device_id=(lax.rem(mine + step, batches), me), device_id_type=MESH
        )
    pl.semaphore_wait(barrier, devices - 1 + batches - 1 + extra.greet(barrier))

    def exchange(source, target, send_sem, recv_sem, limit_out, limit_in, rows, start):
        def remote(there, here):
            return pltpu.make_async_remote_copy(
                src_ref=source.at[pl.ds(pl.multiple_of(there * rows, rows), rows)],
                dst_ref=target.at[pl.ds(pl.multiple_of(here * rows, rows), rows)],
                send_sem=send_sem.at[there],
                recv_sem=recv_sem.at[here],
                device_id=(mine, there),
                device_id_type=MESH,
            )

        if start:

            @pl.loop(1, devices)
            def _(step):
                there = lax.rem(me + step, devices)

                @pl.when(there < limit_out)
                def _():
                    remote(there, me).start()

        else:

            @pl.loop(1, devices)
            def _(step):
                there = lax.rem(me + step, devices)

                @pl.when(there < limit_in)
                def _():
                    pltpu.make_async_remote_copy(
                        src_ref=source.at[pl.ds(0, rows)],
                        dst_ref=target.at[pl.ds(pl.multiple_of(there * rows, rows), rows)],
                        send_sem=send_sem.at[there],
                        recv_sem=recv_sem.at[there],
                        device_id=(mine, there),
                        device_id_type=MESH,
                    ).wait_recv()

    def drain(source, target, send_sem, recv_sem, limit_out, rows):
        @pl.loop(1, devices)
        def _(step):
            there = lax.rem(me + step, devices)

            @pl.when(there < limit_out)
            def _():
                pltpu.make_async_remote_copy(
                    src_ref=source.at[pl.ds(0, rows)],
                    dst_ref=target.at[pl.ds(0, rows)],
                    send_sem=send_sem.at[there],
                    recv_sem=recv_sem.at[there],
                    device_id=(mine, there),
                    device_id_type=MESH,
                ).wait_send()

    owner = me < count

    def weight_copies(index):
        source, target = weights[index]
        rows = source.shape[2]
        place = target.at[:, :, pl.ds(pl.multiple_of(mine * rows, rows), rows)]
        local = pltpu.make_async_copy(source, place, own.at[index])
        remote = []
        for step in range(1, batches):
            there = lax.rem(mine + step, batches)
            back_there = lax.rem(mine + batches - step, batches)
            other = target.at[:, :, pl.ds(pl.multiple_of(back_there * rows, rows), rows)]
            remote.append(
                [
                    pltpu.make_async_remote_copy(
                        src_ref=source,
                        dst_ref=where,
                        send_sem=ws.at[index, step],
                        recv_sem=wr.at[index, step],
                        device_id=(there, me),
                        device_id_type=MESH,
                    )
                    for where in (place, other)
                ]
            )
        return local, remote

    for index in range(2):
        local, remote = weight_copies(index)
        local.start()
        for copy, _unused in remote:
            copy.start()

    x_ref = extra.prepare()
    exchange(x_ref, one, s1, r1, count, None, per_time, True)
    here = pltpu.make_async_copy(
        x_ref.at[pl.ds(pl.multiple_of(jnp.minimum(me, count - 1) * per_time, per_time), per_time)],
        one.at[pl.ds(pl.multiple_of(me * per_time, per_time), per_time)],
        own.at[2],
    )
    here.start()
    extra.start()
    if count < devices:
        two[pl.ds(count * per_bin, (devices - count) * per_bin)] = jnp.zeros(
            ((devices - count) * per_bin, two.shape[1]), two.dtype
        )
    here.wait()

    @pl.when(owner)
    def _():
        exchange(x_ref, one, s1, r1, None, devices, per_time, False)
        data = one[...]
        total = dot_nn(table_ref[0], data) + dot_nn(table_ref[1], data)
        bins_out[...] = total.astype(HALF_FLOAT)
        exchange(bins_out, two, s2, r2, devices, None, per_bin, True)
        place = pl.ds(pl.multiple_of(me * per_bin, per_bin), per_bin)
        two[place] = bins_out[place]

    extra.after_bins()
    exchange(bins_out, two, s2, r2, None, count, per_bin, False)
    spec_ref[...] = dot_nn(move_ref[...], two[...]).astype(HALF_FLOAT)
    extra.after_spec()
    base = 0
    for index in range(2):
        local, remote = weight_copies(index)
        local.wait()
        for copy, arrived in remote:
            copy.wait_send()
            arrived.wait_recv()
        target = weights[index][1]

        @pl.loop(0, pieces_list[index])
        def _(one_bin, base=base, target=target):
            place = pl.ds(
                pl.multiple_of(base + one_bin * 2 * devices, 2 * devices), 2 * devices
            )
            rows = spec_ref[place]
            if back:
                real = dot_nt(rows, target[one_bin, 0])
                imag = dot_nt(rows, target[one_bin, 1])
                out = jnp.concatenate(
                    [real[:devices] + imag[devices:], real[devices:] - imag[:devices]]
                )
            else:
                real = dot_nn(rows, target[one_bin, 0])
                imag = dot_nn(rows, target[one_bin, 1])
                out = jnp.concatenate(
                    [real[:devices] - imag[devices:], imag[:devices] + real[devices:]]
                )
            mixed[place] = out.astype(HALF_FLOAT)

        spare = wide[index] - pieces_list[index]
        if spare:
            mixed[
                pl.ds(base + pieces_list[index] * 2 * devices, spare * 2 * devices)
            ] = jnp.zeros((spare * 2 * devices, mixed.shape[1]), mixed.dtype)
        base += wide[index] * 2 * devices

    spread[...] = dot_nn(unmove_ref[...], mixed[...]).astype(HALF_FLOAT)
    exchange(spread, three, s3, r3, count, None, per_bin, True)
    extra.after_mixed()

    @pl.when(owner)
    def _():
        place = pl.ds(pl.multiple_of(me * per_bin, per_bin), per_bin)
        three[place] = spread[place]
        exchange(spread, three, s3, r3, None, devices, per_bin, False)
        data = three[...]
        total = dot_nn(inverse_ref[0], data) + dot_nn(inverse_ref[1], data)
        four[...] = total.astype(HALF_FLOAT)
        exchange(four, signal_ref, s4, r4, devices, None, per_time, True)
        place = pl.ds(pl.multiple_of(me * per_time, per_time), per_time)
        signal_ref[place] = four[place]

    extra.after_signal()
    exchange(four, signal_ref, s4, r4, None, count, per_time, False)
    drain(x_ref, one, s1, r1, count, per_time)
    drain(spread, three, s3, r3, count, per_bin)

    @pl.when(owner)
    def _():
        drain(bins_out, two, s2, r2, devices, per_bin)
        drain(four, signal_ref, s4, r4, devices, per_time)

    extra.finish()


class Place:
    def __init__(self, groups, members, batches):
        self.groups, self.members, self.batches = groups, members, batches
        self.me = lax.axis_index("tm")
        self.core = lax.axis_index("batch")
        self.group = lax.div(self.me, members)
        self.member = lax.rem(self.me, members)

    def device(self, group, member, core):
        return (core, group * self.members + member)

    def member_at(self, step):
        return lax.rem(self.member + step + self.members, self.members)

    def group_at(self, step):
        return lax.rem(self.group + step + self.groups, self.groups)

    def core_at(self, step):
        return lax.rem(self.core + step + self.batches, self.batches)

    def greet(self, barrier):
        greeted = 0
        for step in range(self.members):
            for turn in range(self.batches):
                if step or turn:
                    there = self.device(self.group, self.member_at(step), self.core_at(turn))
                    pl.semaphore_signal(barrier, inc=1, device_id=there, device_id_type=MESH)
                    greeted += 1
        for step in range(1, self.groups):
            for turn in range(self.batches):
                there = self.device(self.group_at(step), self.member, self.core_at(turn))
                pl.semaphore_signal(barrier, inc=1, device_id=there, device_id_type=MESH)
                greeted += 1
        return greeted


class VectorSum:
    @staticmethod
    def scratch(place_sizes, value):
        dma = pltpu.SemaphoreType.DMA
        groups, members, batches = place_sizes
        parts = [pltpu.VMEM(value.shape, value.dtype)]
        for size in (batches, members, groups):
            parts += [pltpu.VMEM((size,) + value.shape, value.dtype), dma((size,)), dma((size,))]
        return parts + [pltpu.VMEM(value.shape, value.dtype) for _ in range(2)]

    def __init__(self, place, source, out, scratch):
        self.place, self.source, self.out = place, source, out
        self.stages = [scratch[1 + 3 * k : 4 + 3 * k] for k in range(3)]
        self.values = [source, scratch[10], scratch[11]]

    def copy(self, stage, step, back):
        place = self.place
        held, send, recv = self.stages[stage]
        picks = [place.core_at, place.member_at, place.group_at]
        to = [place.core, place.member, place.group]
        to[stage] = picks[stage](step)
        return send_copy(
            self.values[stage],
            held.at[picks[stage](-step) if back else picks[stage](0)],
            send.at[step],
            recv.at[step],
            place.device(to[2], to[1], to[0]),
        )

    def start(self, stage):
        for step in range(1, self.stages[stage][0].shape[0]):
            self.copy(stage, step, False).start()

    def add(self, stage):
        held = self.stages[stage][0]
        value = self.values[stage][...]
        picks = [self.place.core_at, self.place.member_at, self.place.group_at]
        held[picks[stage](0)] = value
        for step in range(1, held.shape[0]):
            self.copy(stage, step, True).wait_recv()
        total = held[0]
        for index in range(1, held.shape[0]):
            total = total + held[index]
        target = self.out if stage == 2 else self.values[stage + 1]
        target[...] = total
        if stage < 2:
            self.start(stage + 1)

    def drain(self):
        for stage in range(3):
            for step in range(1, self.stages[stage][0].shape[0]):
                self.copy(stage, step, False).wait_send()


def send_copy(source, target, send_sem, recv_sem, there):
    return pltpu.make_async_remote_copy(
        src_ref=source,
        dst_ref=target,
        send_sem=send_sem,
        recv_sem=recv_sem,
        device_id=there,
        device_id_type=MESH,
    )


def slab(ref, dim, index, size):
    picks = [slice(None)] * len(ref.shape)
    picks[dim] = pl.ds(pl.multiple_of(index * size, size), size)
    return ref.at[tuple(picks)]


class WideExchange:
    @staticmethod
    def scratch(place_sizes, wide):
        groups, members, batches = place_sizes
        mates = members * batches
        dma = pltpu.SemaphoreType.DMA
        return [dma((mates,)), dma((mates,)), dma((wide.shape[1] // members,))]

    @staticmethod
    def shape(place_sizes, wide):
        groups, members, batches = place_sizes
        pieces, steps, series, channels = wide.shape
        return (steps // members, members * batches, pieces, series, channels // batches)

    def __init__(self, place, source, target, sems):
        self.place, self.source, self.target = place, source, target
        self.send_sem, self.recv_sem, self.local_sem = sems

    def hops(self):
        for step in range(self.place.members):
            for turn in range(self.place.batches):
                if step or turn:
                    yield step, turn

    def mate(self, step, turn):
        return self.place.core_at(turn) * self.place.members + self.place.member_at(step)

    def piece(self, one, step, turn):
        place = self.place
        steps, half = self.target.shape[0], self.target.shape[4]
        return slab(
            self.source.at[:, place.member_at(step) * steps + one], 2, place.core_at(turn), half
        )

    def own(self, one):
        return pltpu.make_async_copy(
            self.piece(one, 0, 0), self.target.at[one, self.mate(0, 0)], self.local_sem.at[one]
        )

    def whole(self, step, turn, pick):
        slot = turn * self.place.members + step
        block = self.target.at[:, pick]
        return send_copy(
            block,
            block,
            self.send_sem.at[slot],
            self.recv_sem.at[slot],
            self.place.device(
                self.place.group, self.place.member_at(step), self.place.core_at(turn)
            ),
        )

    def units(self):
        return [functools.partial(self.start, one) for one in range(self.target.shape[0])]

    def start(self, one):
        place = self.place
        self.own(one).start()
        for step, turn in self.hops():
            slot = turn * place.members + step
            send_copy(
                self.piece(one, step, turn),
                self.target.at[one, self.mate(0, 0)],
                self.send_sem.at[slot],
                self.recv_sem.at[slot],
                place.device(place.group, place.member_at(step), place.core_at(turn)),
            ).start()

    def wait(self):
        for one in range(self.target.shape[0]):
            self.own(one).wait()
        for step, turn in self.hops():
            self.whole(step, turn, self.mate(-step, -turn)).wait_recv()

    def drain(self):
        for step, turn in self.hops():
            self.whole(step, turn, self.mate(0, 0)).wait_send()


class NarrowGather:
    sems = 5

    @staticmethod
    def scratch(place_sizes, narrow):
        groups, members, batches = place_sizes
        dma = pltpu.SemaphoreType.DMA
        size = members * batches
        return [dma((members,)), dma((members,)), dma((size,)), dma((size,)), dma((1,))]

    def __init__(self, place, source, target, sems):
        self.place, self.source, self.target = place, source, target
        (self.link_send, self.link_recv, self.chip_send, self.chip_recv, self.local_sem) = sems

    def own(self):
        place = self.place
        pick = place.core * place.members + place.member
        return pltpu.make_async_copy(self.source, self.target.at[pick], self.local_sem.at[0])

    def link(self, step, pick_step):
        place = self.place
        pick = place.core * place.members + place.member_at(pick_step)
        return send_copy(
            self.source,
            self.target.at[pick],
            self.link_send.at[step],
            self.link_recv.at[step],
            place.device(place.group, place.member_at(step), place.core),
        )

    def chip(self, step, turn, source_core, target_core):
        place = self.place
        member = place.member_at(-step)
        slot = turn * place.members + step
        source = self.target.at[source_core * place.members + member] if step else self.source
        return send_copy(
            source,
            self.target.at[target_core * place.members + member],
            self.chip_send.at[slot],
            self.chip_recv.at[slot],
            place.device(place.group, place.member, place.core_at(turn)),
        )

    def start(self):
        place = self.place
        self.own().start()
        for step in range(1, place.members):
            self.link(step, 0).start()
        for turn in range(1, place.batches):
            self.chip(0, turn, place.core, place.core).start()

    def forward(self):
        place = self.place
        for step in range(1, place.members):
            self.link(step, -step).wait_recv()
            for turn in range(1, place.batches):
                self.chip(step, turn, place.core, place.core).start()

    def wait(self):
        place = self.place
        self.own().wait()
        for turn in range(1, place.batches):
            other = place.core_at(-turn)
            for step in range(place.members):
                self.chip(step, turn, place.core, other).wait_recv()

    def drain(self):
        place = self.place
        for step in range(1, place.members):
            self.link(step, 0).wait_send()
        for turn in range(1, place.batches):
            for step in range(place.members):
                self.chip(step, turn, place.core, place.core).wait_send()


class KernelProduct:
    sems = 6

    @staticmethod
    def scratch(place_sizes, kind, wide, narrow):
        groups, members, batches = place_sizes
        pieces, kernel, series, channels = wide.shape
        steps, rows = kernel // members, pieces * series
        half = channels // batches
        piece = (128, half) if kind == "down" else (half, 128)
        dma = pltpu.SemaphoreType.DMA
        return [
            pltpu.VMEM((channels, members * batches * rows), HALF_FLOAT),
            pltpu.VMEM((steps, channels, half), HALF_FLOAT),
            pltpu.VMEM((groups, steps) + piece, HALF_FLOAT),
            pltpu.VMEM((steps, 128, half), HALF_FLOAT),
            pltpu.VMEM((kernel, channels // (groups * members), half), HALF_FLOAT),
            dma((groups * batches,)),
            dma((groups * batches,)),
            dma((members,)),
            dma((members,)),
            dma((2,)),
        ]

    def __init__(self, place, kind, wide_in, narrow_in, out, scratch):
        self.place, self.kind, self.wide_in, self.narrow_in, self.out = (
            place,
            kind,
            wide_in,
            narrow_in,
            out,
        )
        (self.narrow_t, self.send, self.recv, self.total, self.gathered) = scratch[:5]
        (self.sz, self.rz, self.sf, self.rf, self.local) = scratch[5:]
        self.cores_per_group = place.groups // place.batches

    def multiply(self):
        mates, rows = self.narrow_in.shape[0], self.narrow_in.shape[1]
        self.narrow_t[...] = self.narrow_in[...].reshape(mates * rows, -1).T

        @pl.loop(0, self.wide_in.shape[0])
        def _(one):
            data = self.wide_in[one].reshape(mates * rows, -1)
            self.send[one] = dot_nn(self.narrow_t[...], data).astype(HALF_FLOAT)

    def chunk(self, group, core):
        if self.kind == "down":
            return slab(self.send, 1, group, 128)
        half = self.send.shape[1] // self.place.batches
        return slab(
            slab(self.send, 1, core, half), 2, lax.rem(group, self.cores_per_group), 128
        )

    def hops(self):
        place = self.place
        for step in range(place.groups):
            for turn in range(place.batches if self.kind == "up" else 1):
                yield step, turn

    def partial(self, step, turn, action):
        place = self.place
        group, core = place.group_at(step), place.core_at(turn)
        slot = step * place.batches + turn
        if step == 0 and turn == 0:
            copy = pltpu.make_async_copy(
                self.chunk(group, core), self.recv.at[place.group], self.local.at[0]
            )
            act = lambda: action(copy, True)
        else:
            copy = send_copy(
                self.chunk(group, core),
                self.recv.at[place.group],
                self.sz.at[slot],
                self.rz.at[slot],
                place.device(group, place.member, core),
            )
            act = lambda: action(copy, False)
        if self.kind == "down":
            act()
        else:
            pl.when(lax.div(group, self.cores_per_group) == place.core)(act)

    def start_partials(self):
        for step, turn in self.hops():
            self.partial(step, turn, lambda copy, local: copy.start())

    def sum_partials(self):
        place = self.place
        for step, turn in self.hops():
            group, core = place.group_at(-step), place.core_at(-turn)
            slot = step * place.batches + turn

            def act(step=step, turn=turn, group=group, slot=slot):
                if step == 0 and turn == 0:
                    pltpu.make_async_copy(
                        self.chunk(place.group, place.core),
                        self.recv.at[place.group],
                        self.local.at[0],
                    ).wait()
                else:
                    send_copy(
                        self.chunk(place.group, place.core),
                        self.recv.at[group],
                        self.sz.at[slot],
                        self.rz.at[slot],
                        place.device(place.group, place.member, place.core),
                    ).wait_recv()

            if self.kind == "down":
                act()
            else:
                pl.when(lax.div(place.group, self.cores_per_group) == core)(act)

        @pl.loop(0, self.total.shape[0])
        def _(one):
            value = self.recv[0, one].astype(FLOAT)
            for other in range(1, place.groups):
                value = value + self.recv[other, one].astype(FLOAT)
            value = value if self.kind == "down" else value.T
            self.total[one] = value.astype(HALF_FLOAT)

    def final(self, step, pick_step):
        place = self.place
        steps, width = self.total.shape[0], self.gathered.shape[1]
        source = slab(self.total, 1, place.member_at(step), width)
        target = slab(self.gathered, 0, place.member_at(pick_step), steps)
        if step == 0:
            return pltpu.make_async_copy(source, target, self.local.at[1])
        return send_copy(
            source,
            target,
            self.sf.at[step],
            self.rf.at[step],
            place.device(place.group, place.member_at(step), place.core),
        )

    def start_final(self):
        for step in range(self.place.members):
            self.final(step, 0).start()

    def finish(self):
        place = self.place
        self.final(0, 0).wait()
        for step in range(1, place.members):
            self.final(step, -step).wait_recv()
        self.out[...] = self.gathered[...].astype(FLOAT)
        for step in range(1, place.members):
            self.final(step, 0).wait_send()
        for step, turn in self.hops():
            if step or turn:
                self.partial(step, turn, lambda copy, local: copy.wait_send())


class MatrixSum:
    sems = 7

    @staticmethod
    def half_shape(place_sizes, kind, value):
        batches = place_sizes[2]
        shape = list(value.shape)
        if kind == "rows":
            shape[0] //= batches
        elif kind == "lanes":
            shape[-1] //= batches
        return tuple(shape)

    @staticmethod
    def piece_shape(place_sizes, kind, value):
        groups, members, batches = place_sizes
        shape = list(MatrixSum.half_shape(place_sizes, kind, value))
        dim = {"rows": 1, "lanes": len(shape) - 2, "whole": 0}[kind]
        shape[dim] //= groups * members
        return tuple(shape)

    @staticmethod
    def scratch(place_sizes, kind, value):
        groups, members, batches = place_sizes
        half = MatrixSum.half_shape(place_sizes, kind, value)
        piece = MatrixSum.piece_shape(place_sizes, kind, value)
        dma = pltpu.SemaphoreType.DMA
        return [
            pltpu.VMEM(half, value.dtype),
            pltpu.VMEM((batches,) + half, value.dtype),
            pltpu.VMEM((members, groups) + piece, value.dtype),
            pltpu.VMEM((groups,) + piece, value.dtype),
            pltpu.VMEM((groups,) + piece, value.dtype),
            dma((batches,)),
            dma((batches,)),
            dma((members * groups,)),
            dma((members * groups,)),
            dma((groups,)),
            dma((groups,)),
            dma((1 + groups,)),
        ]

    def __init__(self, place, kind, source, out, scratch):
        self.place, self.kind, self.source, self.out = place, kind, source, out
        (self.own, self.others, self.by_member, self.sums, self.by_group) = scratch[:5]
        (self.sb, self.rb, self.sm, self.rm, self.sg, self.rg, self.local) = scratch[5:]
        self.piece_dim = {"rows": 1, "lanes": len(self.own.shape) - 2, "whole": 0}[kind]

    def half(self, core):
        if self.kind == "rows":
            return slab(self.source, 0, core, self.own.shape[0])
        if self.kind == "lanes":
            return slab(self.source, len(self.own.shape) - 1, core, self.own.shape[-1])
        return self.source

    def cores(self, step, pick):
        place = self.place
        core = place.core_at(step)
        return send_copy(
            self.half(core),
            self.others.at[pick],
            self.sb.at[step],
            self.rb.at[step],
            place.device(place.group, place.member, core),
        )

    def load(self):
        return pltpu.make_async_copy(self.half(self.place.core), self.own, self.local.at[0])

    def start(self):
        self.load().start()
        for step in range(1, self.place.batches):
            self.cores(step, self.place.core).start()

    def piece(self, group, member):
        size = self.by_member.shape[2 + self.piece_dim]
        return slab(self.own, self.piece_dim, group * self.place.members + member, size)

    def members(self, step, pick_step, group):
        place = self.place
        member = place.member_at(step)
        slot = step * place.groups + group
        target = self.by_member.at[place.member_at(pick_step), group]
        if step == 0:
            return pltpu.make_async_copy(
                self.piece(group, member), target, self.local.at[1 + group]
            )
        return send_copy(
            self.piece(group, member),
            target,
            self.sm.at[slot],
            self.rm.at[slot],
            place.device(place.group, member, place.core),
        )

    def add_cores(self):
        place = self.place
        self.load().wait()
        for step in range(1, place.batches):
            self.cores(step, place.core_at(-step)).wait_recv()
        rows = self.own.shape[0]
        block = max(size for size in (1, 2, 4, 8, 16, 32, 64) if rows % size == 0)

        @pl.loop(0, rows // block)
        def _(index):
            pick = pl.ds(pl.multiple_of(index * block, block), block)
            value = self.own[pick].astype(FLOAT)
            for step in range(1, place.batches):
                value = value + self.others[place.core_at(step), pick].astype(FLOAT)
            self.own[pick] = value.astype(self.own.dtype)

        for step in range(place.members):
            for group in range(place.groups):
                self.members(step, 0, group).start()

    def groups(self, step, pick_step):
        place = self.place
        group = place.group_at(step)
        return send_copy(
            self.sums.at[group],
            self.by_group.at[place.group_at(pick_step)],
            self.sg.at[step],
            self.rg.at[step],
            place.device(group, place.member, place.core),
        )

    def add_members(self):
        place = self.place
        for step in range(place.members):
            for group in range(place.groups):
                if step == 0:
                    self.members(step, 0, group).wait()
                else:
                    self.members(step, -step, group).wait_recv()

        @pl.loop(0, place.groups)
        def _(group):
            value = self.by_member[0, group].astype(FLOAT)
            for other in range(1, place.members):
                value = value + self.by_member[other, group].astype(FLOAT)
            self.sums[group] = value.astype(self.sums.dtype)

        for step in range(1, place.groups):
            self.groups(step, 0).start()
        self.by_group[place.group] = self.sums[place.group]

    def finish(self):
        place = self.place
        for step in range(1, place.groups):
            self.groups(step, -step).wait_recv()
        value = self.by_group[0].astype(FLOAT)
        for other in range(1, place.groups):
            value = value + self.by_group[other].astype(FLOAT)
        self.out[...] = value
        for step in range(1, place.groups):
            self.groups(step, 0).wait_send()
        for step in range(1, place.members):
            for group in range(place.groups):
                self.members(step, 0, group).wait_send()
        for step in range(1, place.batches):
            self.cores(step, place.core).wait_send()


def remote_call(body, inputs, outputs, scratch, collective_id, flops, nbytes, name):
    def kernel(*refs):
        left = list(refs)
        named = {key: left.pop(0) for key in inputs}
        named.update({key: left.pop(0) for key in outputs})
        for key, shapes in scratch.items():
            named[key] = [left.pop(0) for _ in shapes]
        body(named)

    results = pl.pallas_call(
        kernel,
        out_shape=tuple(shape for shape, _ in outputs.values()),
        in_specs=[spec for _, spec in inputs.values()],
        out_specs=tuple(spec for _, spec in outputs.values()),
        scratch_shapes=[shape for shapes in scratch.values() for shape in shapes],
        compiler_params=pltpu.CompilerParams(
            collective_id=collective_id,
            has_side_effects=True,
            vmem_limit_bytes=63 * 1024 * 1024,
        ),
        cost_estimate=pl.CostEstimate(flops=flops, bytes_accessed=nbytes, transcendentals=0),
        name=name,
    )(*[value for value, _ in inputs.values()])
    return dict(zip(outputs, results))


def plane_sizes(channels):
    devices, batches = lax.axis_size("tm"), lax.axis_size("batch")
    groups = channels // 128
    if batches == 2 and channels % 256 == 0 and devices % groups == 0:
        return groups, devices // groups, batches
    return None


VMEM_SPEC = pl.BlockSpec(memory_space=pltpu.VMEM)
HBM_SPEC = pl.BlockSpec(memory_space=pl.ANY)


class SeriesGradient:
    @staticmethod
    def scratch(weights, outers, rim):
        steps, series, channels = outers[0].shape
        lead = 2 * rim + 8
        dma = pltpu.SemaphoreType.DMA
        rims = (rim, series, channels)
        return (
            [pltpu.VMEM(weight.shape, HALF_FLOAT) for weight in weights]
            + [pltpu.VMEM((steps + 2 * lead, series, channels), FLOAT) for _ in outers]
            + [pltpu.VMEM((channels // 128, steps * series, 128), FLOAT)]
            + [pltpu.VMEM(rims, FLOAT) for _ in range(4)]
            + [dma((4,)), dma((2,)), dma((2,))]
        )

    def __init__(self, weights, outers, out, scratch, halves, rim):
        self.weights, self.outers, self.out = weights, outers, out
        self.halves, self.rim = halves, rim
        count = len(weights)
        self.held, self.grads = scratch[:count], scratch[count : 2 * count]
        (self.result, self.low, self.high, self.before, self.after) = scratch[
            2 * count : 2 * count + 5
        ]
        (self.local, self.send, self.recv) = scratch[2 * count + 5 :]
        self.steps = outers[0].shape[0]
        self.series = outers[0].shape[1]
        self.lead = 2 * rim + 8
        self.me, self.core = lax.axis_index("tm"), lax.axis_index("batch")
        self.last = lax.axis_size("tm") - 1

    def greet(self, barrier):
        @pl.when(self.me > 0)
        def _():
            pl.semaphore_signal(
                barrier, inc=1, device_id=(self.core, self.me - 1), device_id_type=MESH
            )

        @pl.when(self.me < self.last)
        def _():
            pl.semaphore_signal(
                barrier, inc=1, device_id=(self.core, self.me + 1), device_id_type=MESH
            )

        return jnp.where(self.me > 0, 1, 0) + jnp.where(self.me < self.last, 1, 0)

    def loads(self, index):
        return (
            pltpu.make_async_copy(
                self.weights[index], self.held[index], self.local.at[2 * index]
            ),
            pltpu.make_async_copy(
                self.outers[index],
                self.grads[index].at[pl.ds(self.lead, self.steps)],
                self.local.at[2 * index + 1],
            ),
        )

    def start(self):
        for index in range(len(self.held)):
            for copy in self.loads(index):
                copy.start()
            grads = self.grads[index]
            zero = jnp.zeros((self.lead,) + grads.shape[1:], FLOAT)
            grads[: self.lead] = zero
            grads[self.lead + self.steps :] = zero

    def through_down(self, index, grad):
        for copy in self.loads(index):
            copy.wait()
        kernel = self.held[index].shape[0]
        pieces = self.steps // kernel
        grads = self.grads[index]

        @pl.loop(0, kernel)
        def _(one):
            value = dot_nt(grad, self.held[index][one])
            for piece in range(pieces):
                row = self.lead + piece * kernel + one
                grads[row] = (
                    grads[row] + value[piece * self.series : (piece + 1) * self.series]
                )

    def store(self, place, value, add=False):
        for lane in range(self.result.shape[0]):
            part = value[:, lane * 128 : lane * 128 + 128]
            self.result[lane, place] = self.result[lane, place] - part if add else part

    def adjoint(self):
        def means(index, sums):
            out, total = [], 0.0
            for grads, half, value in zip(self.grads, self.halves, sums):
                high = grads[index + (self.lead - self.rim + half)]
                low = grads[index + (self.lead - self.rim - half - 1)]
                value = value + high - low
                out.append(value)
                total = total + value * (1.0 / (2 * half + 1))
            return tuple(out), total

        def low_step(index, sums):
            sums, total = means(index, sums)
            self.low[index] = total
            return sums

        def step(index, sums):
            sums, total = means(index + self.rim, sums)
            value = self.grads[0][self.lead + index] + self.grads[1][self.lead + index]
            place = pl.ds(pl.multiple_of(index * self.series, self.series), self.series)
            self.store(place, value - total)
            return sums

        def high_step(index, sums):
            sums, total = means(index + (self.rim + self.steps), sums)
            self.high[index] = total
            return sums

        zero = jnp.zeros(self.low.shape[1:], FLOAT)
        sums = lax.fori_loop(0, self.rim, low_step, (zero, zero))
        sums = lax.fori_loop(0, self.steps, step, sums)
        lax.fori_loop(0, self.rim, high_step, sums)

    def edge(self, up):
        source, target = (self.high, self.before) if up else (self.low, self.after)
        index = 0 if up else 1
        return send_copy(
            source,
            target,
            self.send.at[index],
            self.recv.at[index],
            (self.core, self.me + 1 if up else self.me - 1),
        )

    def send_edges(self):
        pl.when(self.me < self.last)(lambda: self.edge(True).start())
        pl.when(self.me > 0)(lambda: self.edge(False).start())

    def finish(self):
        series = self.series
        rows, end = self.rim * series, self.steps * series

        @pl.when(self.me > 0)
        def _():
            self.edge(True).wait_recv()
            self.store(pl.ds(0, rows), self.before[...].reshape(rows, -1), True)

        @pl.when(self.me == 0)
        def _():
            total = self.low[0]
            for index in range(1, self.rim):
                total = total + self.low[index]
            self.store(pl.ds(0, series), total, True)

        @pl.when(self.me < self.last)
        def _():
            self.edge(False).wait_recv()
            self.store(pl.ds(end - rows, rows), self.after[...].reshape(rows, -1), True)

        @pl.when(self.me == self.last)
        def _():
            total = self.high[0]
            for index in range(1, self.rim):
                total = total + self.high[index]
            self.store(pl.ds(end - series, series), total, True)

        for one in range(self.out.shape[0]):
            for lane in range(self.result.shape[0]):
                value = self.result[lane, pl.ds(one, self.steps, stride=series), :]
                self.out[one, :, lane * 128 : lane * 128 + 128] = value.astype(HALF_FLOAT)
        pl.when(self.me < self.last)(lambda: self.edge(True).wait_send())
        pl.when(self.me > 0)(lambda: self.edge(False).wait_send())


def down_gradients(sizes, wides, narrows, vectors, weights, outers, halves, rim, count, matrices):
    groups, members, batches = sizes
    half = wides[0].shape[4]
    channels = half * batches
    inputs, outputs, scratch = {}, {}, {}
    for index, (wide, narrow) in enumerate(zip(wides, narrows)):
        steps = wide.shape[0] * members
        shape = jax.ShapeDtypeStruct(
            (wide.shape[2], steps, wide.shape[3], channels), HALF_FLOAT
        )
        inputs[f"wide{index}"] = (wide, VMEM_SPEC)
        inputs[f"narrow{index}"] = (narrow, HBM_SPEC)
        outputs[f"out{index}"] = (
            jax.ShapeDtypeStruct((steps, channels // (groups * members), half), FLOAT),
            VMEM_SPEC,
        )
        scratch[f"rows{index}"] = [
            pltpu.VMEM((members * batches,) + narrow.shape, HALF_FLOAT)
        ]
        scratch[f"gather{index}"] = NarrowGather.scratch(sizes, narrow)
        scratch[f"product{index}"] = KernelProduct.scratch(sizes, "down", shape, narrow)
    for index in range(len(wides)):
        inputs[f"weight{index}"] = (weights[index], HBM_SPEC)
        inputs[f"outer{index}"] = (outers[index], HBM_SPEC)
    scratch["series"] = SeriesGradient.scratch(weights, outers, rim)
    outputs["grad_series"] = (
        jax.ShapeDtypeStruct((count, outers[0].shape[0], channels), HALF_FLOAT),
        VMEM_SPEC,
    )
    for index, (kind, value) in enumerate(matrices):
        inputs[f"matrix{index}"] = (value, HBM_SPEC)
        outputs[f"matrix_sum{index}"] = (
            jax.ShapeDtypeStruct(MatrixSum.piece_shape(sizes, kind, value), FLOAT),
            VMEM_SPEC,
        )
        scratch[f"parts{index}"] = MatrixSum.scratch(sizes, kind, value)
    inputs["vectors"] = (vectors, VMEM_SPEC)
    outputs["vector_sum"] = (jax.ShapeDtypeStruct(vectors.shape, FLOAT), VMEM_SPEC)
    scratch["vector"] = VectorSum.scratch(sizes, vectors)

    def body(refs):
        place = Place(*sizes)
        back = SeriesGradient(
            [refs[f"weight{index}"] for index in range(len(wides))],
            [refs[f"outer{index}"] for index in range(len(wides))],
            refs["grad_series"],
            refs["series"],
            halves,
            rim,
        )
        barrier = pltpu.get_barrier_semaphore()
        pl.semaphore_wait(barrier, place.greet(barrier) + back.greet(barrier))
        gathers, products = [], []
        for index in range(len(wides)):
            gathers.append(
                NarrowGather(
                    place,
                    refs[f"narrow{index}"],
                    refs[f"rows{index}"][0],
                    refs[f"gather{index}"],
                )
            )
            products.append(
                KernelProduct(
                    place,
                    "down",
                    refs[f"wide{index}"],
                    refs[f"rows{index}"][0],
                    refs[f"out{index}"],
                    refs[f"product{index}"],
                )
            )
        total = VectorSum(place, refs["vectors"], refs["vector_sum"], refs["vector"])
        sums = [
            MatrixSum(
                place, kind, refs[f"matrix{i}"], refs[f"matrix_sum{i}"], refs[f"parts{i}"]
            )
            for i, (kind, _) in enumerate(matrices)
        ]
        order = list(range(len(wides)))[::-1]
        for index in order:
            gathers[index].start()
        for item in sums:
            item.start()
        total.start(0)
        back.start()
        for index in order:
            gathers[index].forward()
            gathers[index].wait()
            products[index].multiply()
            products[index].start_partials()
        for item in sums:
            item.add_cores()
        total.add(0)
        mine = place.core * members + place.member
        for index in range(len(wides)):
            back.through_down(index, refs[f"rows{index}"][0][mine])
        for item in sums:
            item.add_members()
        total.add(1)
        back.adjoint()
        back.send_edges()
        for index in order:
            products[index].sum_partials()
            products[index].start_final()
        for item in sums:
            item.finish()
        total.add(2)
        back.finish()
        for product in products:
            product.finish()
        for gather in gathers:
            gather.drain()
        total.drain()

    flops = sum(2 * wide.size * channels for wide in wides)
    results = remote_call(
        body, inputs, outputs, scratch, 2, flops, 8 * flops // channels, "down_gradients"
    )
    return (
        [results["out0"], results["out1"]],
        results["vector_sum"],
        results["grad_series"],
        [results[f"matrix_sum{index}"] for index in range(len(matrices))],
    )


def iso_gradient_kernel(lane_ref, spec_ref, specs_ref, grad_ref, grads_ref, out_ref):
    bins, _, half, channels = out_ref.shape
    rows = spec_ref.shape[0] // bins
    devices = rows // 2
    for one in range(bins):
        place = slice(one * rows, (one + 1) * rows)
        spec = [spec_ref[place]] + [specs_ref[i, place] for i in range(specs_ref.shape[0])]
        grad = [grad_ref[place]] + [grads_ref[i, place] for i in range(grads_ref.shape[0])]
        turned = [jnp.concatenate([value[devices:], -value[:devices]]) for value in grad]
        both = jnp.concatenate([jnp.concatenate(grad), jnp.concatenate(turned)], axis=1)
        value = lax.dot_general(
            jnp.concatenate(spec), both, (((0,), (0,)), ((), ())), preferred_element_type=FLOAT
        )
        out_ref[one, 0] = value[:, :channels]
        out_ref[one, 1] = value[:, channels:]


def iso_gradients(spec, specs, grad, grads, first, bins):
    rows, channels = 2 * lax.axis_size("tm"), grad.shape[1]
    half = channels // lax.axis_size("batch")
    others = specs.shape[0]
    block = 2 if bins % 2 == 0 and first % 2 == 0 else 1
    rows, first = rows * block, first // block
    core = lax.axis_index("batch")
    if half % 128:
        spec = lax.dynamic_slice_in_dim(spec, core * half, half, axis=1)
        specs = lax.dynamic_slice_in_dim(specs, core * half, half, axis=2)
        core = 0
    return pl.pallas_call(
        iso_gradient_kernel,
        out_shape=jax.ShapeDtypeStruct((bins, 2, half, channels), FLOAT),
        grid_spec=pltpu.PrefetchScalarGridSpec(
            num_scalar_prefetch=1,
            grid=(bins // block,),
            in_specs=[
                pl.BlockSpec((rows, half), lambda i, lane: (first + i, lane[0])),
                pl.BlockSpec((others, rows, half), lambda i, lane: (0, first + i, lane[0])),
                pl.BlockSpec((rows, channels), lambda i, lane: (first + i, 0)),
                pl.BlockSpec((others, rows, channels), lambda i, lane: (0, first + i, 0)),
            ],
            out_specs=pl.BlockSpec((block, 2, half, channels), lambda i, lane: (i, 0, 0, 0)),
        ),
        cost_estimate=pl.CostEstimate(
            flops=4 * (bins // block) * rows * (1 + others) * half * channels,
            bytes_accessed=8 * bins * half * channels,
            transcendentals=0,
        ),
        name="iso_gradients",
    )(jnp.full((1,), core, jnp.int32), spec, specs, grad, grads)


class RowProducts:
    @staticmethod
    def scratch(jobs):
        rows, channels = jobs[0][0].shape
        most = max(sum(right.shape[1] for right in rights) for _, rights in jobs)
        return [
            pltpu.VMEM((rows, channels), HALF_FLOAT),
            pltpu.VMEM((channels, rows), HALF_FLOAT),
            pltpu.VMEM((rows, most), HALF_FLOAT),
            pltpu.SemaphoreType.DMA((1 + max(len(rights) for _, rights in jobs),)),
        ]

    def __init__(self, jobs, scratch):
        self.jobs = jobs
        self.left, self.turned, self.right, self.sem = scratch
        self.next = 0

    def copies(self, index):
        left, rights, _ = self.jobs[index]
        copies = [pltpu.make_async_copy(left, self.left, self.sem.at[0])]
        for k, right in enumerate(rights):
            width = right.shape[1]
            target = self.right.at[:, pl.ds(k * width, width)]
            copies.append(pltpu.make_async_copy(right, target, self.sem.at[1 + k]))
        return copies

    def load(self):
        if self.next < len(self.jobs):
            for copy in self.copies(self.next):
                copy.start()

    def run(self):
        index, self.next = self.next, self.next + 1
        for copy in self.copies(index):
            copy.wait()
        self.turned[...] = self.left[...].T
        out = self.jobs[index][2]
        channels = self.left.shape[1]
        width = sum(right.shape[1] for right in self.jobs[index][1])
        for k in range(width // channels):
            chunk = pl.ds(k * channels, channels)
            value = dot_nn(self.turned[...], self.right[:, chunk]).astype(HALF_FLOAT)
            if len(out.shape) == 3:
                out[k] = value
            else:
                out[:, chunk] = value
        self.load()


class Extra:
    def __init__(self, sizes):
        self.sizes = sizes
        self.inputs, self.outputs, self.scratch = {}, {}, {}

    def bind(self, refs):
        self.refs = refs
        self.place = Place(*self.sizes) if self.sizes else None

    def greet(self, barrier):
        return self.place.greet(barrier) if self.sizes else 0

    def prepare(self):
        return self.refs["x"]

    def start(self):
        pass

    def after_bins(self):
        pass

    def after_spec(self):
        pass

    def after_mixed(self):
        pass

    def after_signal(self):
        pass

    def finish(self):
        pass

    def run(self, share):
        count = max(1, round(share * self.unit_count))
        for _ in range(min(count, len(self.units))):
            self.units.pop(0)()


class Turn:
    block = 64

    @staticmethod
    def scratch(weight):
        channels, kernel, outs = weight.shape
        dma = pltpu.SemaphoreType.DMA
        return [
            pltpu.VMEM((2, Turn.block, kernel, outs), HALF_FLOAT),
            pltpu.VMEM((2, kernel, Turn.block, outs), HALF_FLOAT),
            dma((2,)),
            dma((2,)),
        ]

    def __init__(self, source, target, scratch):
        self.source, self.target = source, target
        self.read, self.turned, self.in_sem, self.out_sem = scratch
        self.total = source.shape[0] // self.block
        self.done = 0

    def load(self, index, slot):
        place = pl.ds(pl.multiple_of(index * self.block, self.block), self.block)
        return pltpu.make_async_copy(
            self.source.at[place], self.read.at[slot], self.in_sem.at[slot]
        )

    def store(self, index, slot):
        place = pl.ds(pl.multiple_of(index * self.block, self.block), self.block)
        return pltpu.make_async_copy(
            self.turned.at[slot], self.target.at[:, place], self.out_sem.at[slot]
        )

    def start(self):
        self.load(0, 0).start()

    def run(self, share):
        first, self.done = self.done, min(self.total, self.done + math.ceil(share * self.total))

        @pl.loop(first, self.done)
        def _(index):
            slot = lax.rem(index, 2)
            self.load(index, slot).wait()

            @pl.when(index + 1 < self.total)
            def _():
                self.load(index + 1, 1 - slot).start()

            @pl.when(index >= 2)
            def _():
                self.store(index - 2, slot).wait()

            self.turned[slot] = pltpu.einshape("mhd->hmd", self.read[slot])
            self.store(index, slot).start()

    def finish(self):
        self.run(1.0)
        for index in range(max(0, self.total - 2), self.total):
            self.store(index, index % 2).wait()


def by_piece(signal, rows, count):
    per_time = signal.shape[0] // count
    width = rows.shape[1] // per_time
    for lane in range(rows.shape[0]):
        value = signal[:, lane * 128 : lane * 128 + 128]
        rows[lane, : signal.shape[0], :] = value.astype(FLOAT)
        if width > count:
            rows[lane, signal.shape[0] :, :] = jnp.zeros(
                (rows.shape[1] - signal.shape[0], 128), FLOAT
            )

    def piece(index):
        return jnp.concatenate(
            [rows[lane, pl.ds(index, width, stride=per_time), :] for lane in range(rows.shape[0])],
            axis=1,
        )

    return lambda first, size: jnp.concatenate([piece(first + i) for i in range(size)])


class Front:
    halo = 16

    @staticmethod
    def scratch(series, weights, per_time, rim):
        count, steps, channels = series.shape
        wide, lanes = round_up(count, 16), channels // 128
        rows = max(steps // weight.shape[0] for weight in weights) * wide
        dma = pltpu.SemaphoreType.DMA
        return (
            [pltpu.VMEM(weight.shape, HALF_FLOAT) for weight in weights]
            + [
                pltpu.VMEM(series.shape, HALF_FLOAT),
                pltpu.VMEM((count, Front.halo, channels), HALF_FLOAT),
                pltpu.VMEM((count, Front.halo, channels), HALF_FLOAT),
                pltpu.VMEM((lanes, (steps + 2 * rim + 1) * wide, 128), FLOAT),
                pltpu.VMEM((lanes, per_time * wide, 128), FLOAT),
                pltpu.VMEM((rows, channels), FLOAT),
                pltpu.VMEM((count * per_time, channels), HALF_FLOAT),
            ]
            + [dma((1 + len(weights),)), dma((2,)), dma((2,))]
        )

    def __init__(self, source, weights, bias, seasonals, acts, scratch, halves, rim):
        self.source, self.weights, self.bias = source, weights, bias
        self.seasonals, self.acts, self.halves, self.rim = seasonals, acts, halves, rim
        self.held = scratch[: len(weights)]
        (self.series, self.before, self.after, self.wide, self.rows, self.total, self.x) = (
            scratch[len(weights) : len(weights) + 7]
        )
        (self.local, self.send, self.recv) = scratch[len(weights) + 7 :]
        self.count, self.steps, _ = source.shape
        self.width = seasonals[0].shape[2]
        self.me, self.core = lax.axis_index("tm"), lax.axis_index("batch")
        self.last = lax.axis_size("tm") - 1

    def loads(self):
        return [pltpu.make_async_copy(self.source, self.series, self.local.at[0])] + [
            pltpu.make_async_copy(weight, held, self.local.at[1 + index])
            for index, (weight, held) in enumerate(zip(self.weights, self.held))
        ]

    def edge(self, up):
        first = self.steps - self.halo if up else 0
        index = 0 if up else 1
        return send_copy(
            self.source.at[:, pl.ds(first, self.halo)],
            self.before if up else self.after,
            self.send.at[index],
            self.recv.at[index],
            (self.core, self.me + 1 if up else self.me - 1),
        )

    def start(self):
        pl.when(self.me < self.last)(lambda: self.edge(True).start())
        pl.when(self.me > 0)(lambda: self.edge(False).start())
        for copy in self.loads():
            copy.start()

    def spread(self, values, first, count):
        for lane in range(self.wide.shape[0]):
            self.wide[lane, pl.ds(first, count, stride=self.width), :] = values[
                :, lane * 128 : lane * 128 + 128
            ]

    def step(self, index):
        place = pl.ds(pl.multiple_of(index * self.width, self.width), self.width)
        return jnp.concatenate(
            [self.wide[lane, place, :] for lane in range(self.wide.shape[0])], axis=1
        )

    def repeat(self, index, first):
        value = self.step(index)
        for row in range(self.rim):
            place = pl.ds((first + row) * self.width, self.width)
            for lane in range(self.wide.shape[0]):
                self.wide[lane, place, :] = value[:, lane * 128 : lane * 128 + 128]

    def layers(self, ready):
        rim, steps, width = self.rim, self.steps, self.width
        self.wide[...] = jnp.zeros_like(self.wide)
        copies = self.loads()
        copies[0].wait()
        for one in range(self.count):
            self.spread(self.series[one].astype(FLOAT), rim * width + one, steps)

        @pl.when(self.me > 0)
        def _():
            self.edge(True).wait_recv()
            for one in range(self.count):
                self.spread(self.before[one].astype(FLOAT)[self.halo - rim :], one, rim)

        @pl.when(self.me < self.last)
        def _():
            self.edge(False).wait_recv()
            for one in range(self.count):
                first = (rim + steps) * width + one
                self.spread(self.after[one].astype(FLOAT)[:rim], first, rim)

        pl.when(self.me == 0)(lambda: self.repeat(rim, 0))
        pl.when(self.me == self.last)(lambda: self.repeat(rim + steps - 1, rim + steps))
        sums = []
        for half in self.halves:
            value = self.step(rim - half)
            for index in range(rim - half + 1, rim + half + 1):
                value = value + self.step(index)
            sums.append(value)

        def move(index, sums):
            here, later = self.step(index + rim), []
            for seasonal, half, value in zip(self.seasonals, self.halves, sums):
                kernel = seasonal.shape[1]
                part = here - value * (1.0 / (2 * half + 1))
                seasonal[lax.div(index, kernel), lax.rem(index, kernel)] = part.astype(
                    HALF_FLOAT
                )
                later.append(
                    value + self.step(index + rim + half + 1) - self.step(index + rim - half)
                )
            return tuple(later)

        lax.fori_loop(0, steps, move, tuple(sums))
        ready()
        self.rows[...] = jnp.zeros_like(self.rows)
        base = 0
        for index, (seasonal, held, act) in enumerate(zip(self.seasonals, self.held, self.acts)):
            copies[1 + index].wait()
            count = act.shape[0]
            total = self.total.at[pl.ds(0, count)]
            total[...] = jnp.broadcast_to(self.bias[index : index + 1], total.shape)

            @pl.loop(0, seasonal.shape[1])
            def _(one, total=total, seasonal=seasonal, held=held):
                total[...] += dot_nn(seasonal[:, one].reshape(total.shape), held[one])

            value = jnp.tanh(total[...])
            act[...] = value
            value = value.astype(HALF_FLOAT).astype(FLOAT)
            for lane in range(self.rows.shape[0]):
                self.rows[lane, pl.ds(base * width, count), :] = value[
                    :, lane * 128 : lane * 128 + 128
                ]
            base += round_up(count // width, 8)
        per_time = self.x.shape[0] // self.count
        for one in range(self.count):
            for lane in range(self.rows.shape[0]):
                value = self.rows[lane, pl.ds(one, per_time, stride=width), :]
                self.x[
                    one * per_time : (one + 1) * per_time, lane * 128 : lane * 128 + 128
                ] = value.astype(HALF_FLOAT)

    def finish(self):
        pl.when(self.me < self.last)(lambda: self.edge(True).wait_send())
        pl.when(self.me > 0)(lambda: self.edge(False).wait_send())

    def turn(self, source):
        return pltpu.make_async_copy(source, self.series, self.local.at[0])

    def turned(self, source, target):
        self.turn(source).wait()
        for one in range(self.count):
            self.spread(self.series[one].astype(FLOAT), self.rim * self.width + one, self.steps)

        @pl.loop(0, self.steps)
        def _(index):
            target[index] = self.step(index + self.rim).astype(HALF_FLOAT)


class ForwardExtra(Extra):
    def __init__(self, sizes, wides, weights, front):
        super().__init__(sizes)
        self.front = front
        if front:
            series, cotangent, down_weights, bias, per_time, halves, rim = front
            count, steps, channels = series.shape
            series_rows = round_up(count, 16)
            self.inputs["series"] = (series, HBM_SPEC)
            self.inputs["down_bias"] = (bias, VMEM_SPEC)
            for index, weight in enumerate(down_weights):
                kernel = weight.shape[0]
                self.inputs[f"down{index}"] = (weight, HBM_SPEC)
                self.outputs[f"seasonal{index}"] = (
                    jax.ShapeDtypeStruct(
                        (steps // kernel, kernel, series_rows, channels), HALF_FLOAT
                    ),
                    VMEM_SPEC,
                )
                self.outputs[f"down_act{index}"] = (
                    jax.ShapeDtypeStruct((steps // kernel * series_rows, channels), FLOAT),
                    VMEM_SPEC,
                )
                rows = self.outputs[f"down_act{index}"][0].shape
                self.outputs[f"iso_act{index}"] = (
                    jax.ShapeDtypeStruct(rows, FLOAT),
                    VMEM_SPEC,
                )
                self.outputs[f"inner{index}"] = (
                    jax.ShapeDtypeStruct(rows, HALF_FLOAT),
                    VMEM_SPEC,
                )
            self.inputs["cotangent"] = (cotangent, HBM_SPEC)
            self.outputs["cotangent_steps"] = (
                jax.ShapeDtypeStruct((steps, series_rows, channels), HALF_FLOAT),
                VMEM_SPEC,
            )
            self.scratch["front"] = Front.scratch(series, down_weights, per_time, rim)
            wides = [self.outputs[f"seasonal{index}"][0] for index in range(len(down_weights))]
        self.turn_count = len(weights)
        for index, weight in enumerate(weights):
            channels, kernel, outs = weight.shape
            self.inputs[f"turn{index}"] = (weight, HBM_SPEC)
            self.outputs[f"turned{index}"] = (
                jax.ShapeDtypeStruct((kernel, channels, outs), HALF_FLOAT),
                HBM_SPEC,
            )
            self.scratch[f"turning{index}"] = Turn.scratch(weight)
        self.count = len(wides) if sizes else 0
        for index in range(self.count):
            if not front:
                self.inputs[f"wide{index}"] = (wides[index], HBM_SPEC)
            self.outputs[f"gathered{index}"] = (
                jax.ShapeDtypeStruct(WideExchange.shape(sizes, wides[index]), HALF_FLOAT),
                HBM_SPEC,
            )
            self.scratch[f"exchange{index}"] = WideExchange.scratch(sizes, wides[index])

    def bind(self, refs):
        super().bind(refs)
        self.exchanges = [
            WideExchange(
                self.place,
                refs[f"seasonal{i}" if self.front else f"wide{i}"],
                refs[f"gathered{i}"],
                refs[f"exchange{i}"],
            )
            for i in range(self.count)
        ]
        self.units = [unit for item in self.exchanges for unit in item.units()]
        self.unit_count = len(self.units)
        self.turns = [
            Turn(refs[f"turn{i}"], refs[f"turned{i}"], refs[f"turning{i}"])
            for i in range(self.turn_count)
        ]

    def inner(self):
        refs, base = self.refs, 0
        count = self.front[0].shape[0]
        rows = by_piece(refs["signal"], self.layers.rows, count)
        table = refs["down_bias"]
        for index in range(self.count):
            act_ref = refs[f"iso_act{index}"]
            pieces = act_ref.shape[0] // self.layers.width
            act = jnp.tanh(rows(base, pieces) + table[2 + index : 3 + index])
            down = refs[f"down_act{index}"][...].astype(HALF_FLOAT).astype(FLOAT)
            hat, _ = normed(act + down)
            act_ref[...] = act
            out = hat * table[8:9] + table[11:12]
            refs[f"inner{index}"][...] = out.astype(HALF_FLOAT)
            base += round_up(pieces, 8)

    def prepare(self):
        for item in self.turns:
            item.start()
        if not self.front:
            return super().prepare()
        refs, count = self.refs, self.count
        halves, rim = self.front[5:]
        self.layers = Front(
            refs["series"],
            [refs[f"down{i}"] for i in range(count)],
            refs["down_bias"],
            [refs[f"seasonal{i}"] for i in range(count)],
            [refs[f"down_act{i}"] for i in range(count)],
            refs["front"],
            halves,
            rim,
        )
        self.layers.start()
        self.layers.layers(functools.partial(self.run, 0.3))
        return self.layers.x

    def start(self):
        self.run(0.15)
        if self.front:
            self.layers.turn(self.refs["cotangent"]).start()
        for item in self.turns:
            item.run(0.25)

    def after_bins(self):
        self.run(0.55)
        if self.front:
            self.layers.turned(self.refs["cotangent"], self.refs["cotangent_steps"])
        for item in self.turns:
            item.run(0.25)

    def after_mixed(self):
        self.run(1.0)
        for item in self.turns:
            item.run(0.375)

    def after_signal(self):
        for item in self.turns:
            item.run(0.125)

    def finish(self):
        if self.front:
            self.inner()
            self.layers.finish()
        for item in self.turns:
            item.finish()
        for item in self.exchanges:
            item.wait()
            item.drain()


class BackwardExtra(Extra):
    def __init__(self, sizes, spec, wides, narrows, jobs, inners, acts, counts):
        super().__init__(sizes)
        self.counts = counts
        if sizes:
            for i, (inner, act) in enumerate(zip(inners, acts)):
                self.inputs[f"inner_grad{i}"] = (inner, VMEM_SPEC)
                self.inputs[f"act{i}"] = (act, VMEM_SPEC)
                self.outputs[f"down_grad{i}"] = (
                    jax.ShapeDtypeStruct(act.shape, HALF_FLOAT),
                    VMEM_SPEC,
                )
            channels = spec.shape[1]
            self.outputs["down_sums"] = (jax.ShapeDtypeStruct((8, channels), FLOAT), VMEM_SPEC)
            per_time, width = counts[1:]
            self.scratch["piece_rows"] = [
                pltpu.VMEM((channels // 128, per_time * width, 128), FLOAT)
            ]
        self.batches = lax.axis_size("batch")
        others = jax.ShapeDtypeStruct((self.batches - 1,) + spec.shape, HALF_FLOAT)
        self.inputs["spec_forward"] = (spec, HBM_SPEC)
        self.outputs["specs"] = (others, HBM_SPEC)
        self.outputs["grads"] = (others, HBM_SPEC)
        dma = pltpu.SemaphoreType.DMA
        self.scratch["other_sems"] = [dma((self.batches,))] * 4
        self.count = len(wides) if sizes else 0
        self.job_sizes = [len(rights) for _, rights, _ in jobs] if sizes else []
        if sizes:
            for i, (left, rights, shape) in enumerate(jobs):
                self.inputs[f"left{i}"] = (left, HBM_SPEC)
                for k, right in enumerate(rights):
                    self.inputs[f"right{i}_{k}"] = (right, HBM_SPEC)
                self.outputs[f"matrix{i}"] = (
                    jax.ShapeDtypeStruct(shape, HALF_FLOAT),
                    VMEM_SPEC,
                )
            self.scratch["row_products"] = RowProducts.scratch(
                [(left, rights) for left, rights, _ in jobs]
            )
        for i in range(self.count):
            wide, narrow = wides[i], narrows[i]
            groups, members, batches = sizes
            channels = narrow.shape[1]
            self.inputs[f"wide{i}"] = (wide, HBM_SPEC)
            self.inputs[f"narrow{i}"] = (narrow, HBM_SPEC)
            self.outputs[f"up{i}"] = (
                jax.ShapeDtypeStruct(
                    (wide.shape[1], channels // (groups * members), channels // batches), FLOAT
                ),
                VMEM_SPEC,
            )
            self.scratch[f"wide_in{i}"] = [
                pltpu.VMEM(WideExchange.shape(sizes, wide), HALF_FLOAT)
            ]
            self.scratch[f"rows{i}"] = [
                pltpu.VMEM((members * batches,) + narrow.shape, HALF_FLOAT)
            ]
            self.scratch[f"exchange{i}"] = WideExchange.scratch(sizes, wide)
            self.scratch[f"gather{i}"] = NarrowGather.scratch(sizes, narrow)
            self.scratch[f"product{i}"] = KernelProduct.scratch(sizes, "up", wide, narrow)

    def bind(self, refs):
        super().bind(refs)
        self.exchanges, self.gathers, self.products = [], [], []
        for i in range(self.count):
            wide_in, rows = refs[f"wide_in{i}"][0], refs[f"rows{i}"][0]
            self.exchanges.append(
                WideExchange(self.place, refs[f"wide{i}"], wide_in, refs[f"exchange{i}"])
            )
            self.gathers.append(
                NarrowGather(self.place, refs[f"narrow{i}"], rows, refs[f"gather{i}"])
            )
            self.products.append(
                KernelProduct(self.place, "up", wide_in, rows, refs[f"up{i}"], refs[f"product{i}"])
            )
        jobs = [
            (
                refs[f"left{i}"],
                [refs[f"right{i}_{k}"] for k in range(size)],
                refs[f"matrix{i}"],
            )
            for i, size in enumerate(self.job_sizes)
        ]
        self.row_products = RowProducts(jobs, refs["row_products"]) if jobs else None

    def other(self, index, turn):
        source, target = (
            (self.refs["spec_forward"], self.refs["specs"]),
            (self.refs["spec"], self.refs["grads"]),
        )[index]
        sems = self.refs["other_sems"]
        core = lax.rem(lax.axis_index("batch") + turn, self.batches)
        return send_copy(
            source,
            target.at[turn - 1],
            sems[2 * index].at[turn],
            sems[2 * index + 1].at[turn],
            (core, lax.axis_index("tm")),
        )

    def start(self):
        self.units = [unit for item in self.exchanges[::-1] for unit in item.units()]
        self.unit_count = len(self.units)
        for turn in range(1, self.batches):
            self.other(0, turn).start()
        for item in self.gathers:
            item.start()
        if self.row_products:
            self.row_products.load()

    def after_bins(self):
        self.run(0.6)
        for item in self.gathers:
            item.forward()
        if self.row_products:
            self.row_products.run()

    def after_mixed(self):
        self.run(0.3)
        if self.count:
            self.multiply(self.count - 1)

    def after_spec(self):
        for turn in range(1, self.batches):
            self.other(1, turn).start()

    def multiply(self, index):
        self.exchanges[index].wait()
        self.gathers[index].wait()
        self.products[index].multiply()
        self.products[index].start_partials()

    def after_signal(self):
        self.run(1.0)
        for index in range(self.count - 1):
            self.multiply(index)

    def down_grads(self):
        refs, base = self.refs, 0
        count, _, width = self.counts
        rows = by_piece(refs["signal"], refs["piece_rows"][0], count)
        refs["down_sums"][...] = jnp.zeros_like(refs["down_sums"])
        for index in range(self.count):
            act = refs[f"act{index}"][...]
            pieces = act.shape[0] // width
            grad = rows(base, pieces) + refs[f"inner_grad{index}"][...]
            grad = (grad * (1.0 - act * act)).astype(HALF_FLOAT)
            refs[f"down_grad{index}"][...] = grad
            refs["down_sums"][index : index + 1] = jnp.sum(
                grad.astype(FLOAT), axis=0, keepdims=True
            )
            base += round_up(pieces, 8)

    def finish(self):
        if self.count:
            self.down_grads()
            for _ in range(1, len(self.job_sizes)):
                self.row_products.run()
        for item in self.products[::-1]:
            item.sum_partials()
            item.start_final()
        for item in self.products:
            item.finish()
        for item in self.exchanges + self.gathers:
            item.drain()
        for index in range(2):
            for turn in range(1, self.batches):
                self.other(index, turn).wait()


def spectral(values, shapes, weights, back, extra):
    devices, batches = lax.axis_size("tm"), lax.axis_size("batch")
    pieces_list = tuple(shape[1] for shape in shapes)
    count, _, channels = shapes[0]
    wide = [round_up(pieces, 8) for pieces in pieces_list]
    per_time, per_bin = sum(wide), 2 * sum(wide)
    assert count <= devices and per_time % 16 == 0
    inputs = {}
    if values:
        packed = jnp.concatenate(
            [
                jnp.pad(value, ((0, 0), (0, room - value.shape[1]), (0, 0)))
                for value, room in zip(values, wide)
            ],
            axis=1,
        ).reshape(count * per_time, channels)
        inputs["x"] = (packed, HBM_SPEC)
    constants = spectral_constants(devices, pieces_list)
    rows_time, rows_bin = devices * per_time, devices * per_bin
    dma = pltpu.SemaphoreType.DMA
    for index, weight in enumerate(weights):
        inputs[f"weight{index}"] = (weight, HBM_SPEC)
    for key, value in zip(("table", "inverse", "move", "unmove"), constants):
        inputs[key] = (value, VMEM_SPEC)
    outputs = {
        "spec": (jax.ShapeDtypeStruct((rows_bin, channels), HALF_FLOAT), VMEM_SPEC),
        "signal": (jax.ShapeDtypeStruct((count * per_time, channels), HALF_FLOAT), VMEM_SPEC),
    }
    scratch = {
        "buffers": [pltpu.VMEM((rows_time, channels), HALF_FLOAT)]
        + [pltpu.VMEM((rows_bin, channels), HALF_FLOAT)] * 5
        + [pltpu.VMEM((rows_time, channels), HALF_FLOAT)]
        + [
            pltpu.VMEM((weight.shape[0], 2, weight.shape[2] * batches, channels), HALF_FLOAT)
            for weight in weights
        ],
        "sems": [dma((devices,))] * 8 + [dma((2, batches)), dma((2, batches)), dma((3,))],
    }
    inputs.update(extra.inputs)
    outputs.update(extra.outputs)
    scratch.update(extra.scratch)
    sizes = (devices, batches, count, pieces_list)

    def body(refs):
        extra.bind(refs)
        spectral_body(sizes, back, refs, extra)

    results = remote_call(
        body,
        inputs,
        outputs,
        scratch,
        1 if back else 0,
        2 * rows_bin * channels * channels * 4,
        4 * channels * channels * sum(pieces_list),
        "spectral_back" if back else "spectral_forward",
    )
    signal = results["signal"].reshape(count, per_time, channels)
    signals, offset = [], 0
    for pieces, room in zip(pieces_list, wide):
        signals.append(signal[:, offset : offset + pieces])
        offset += room
    return results, signals


def gelu_pair(value):
    slope = math.sqrt(2.0 / math.pi)
    square = value * value
    bent = jnp.tanh(slope * value * (1.0 + 0.044715 * square))
    rise = 0.5 * (1.0 + bent)
    turn = 0.5 * slope * value * (1.0 - bent * bent) * (1.0 + 3.0 * 0.044715 * square)
    return (value * rise).astype(HALF_FLOAT), (rise + turn).astype(HALF_FLOAT)


def by_time(values):
    turned = jnp.swapaxes(values, 0, 1)
    extra = -turned.shape[1] % 16
    return jnp.pad(turned, ((0, 0), (0, extra)) + ((0, 0),) * (turned.ndim - 2))


def by_series(values, count):
    return jnp.swapaxes(values[:, :count], 0, 1)


def neighbours(low_side, high_side):
    count = lax.axis_size("tm")
    onward = [(i, i + 1) for i in range(count - 1)]
    return (
        lax.ppermute(high_side, "tm", onward),
        lax.ppermute(low_side, "tm", [(j, i) for i, j in onward]),
    )


def window_sum(values, first, width, count):
    total, level, size = None, values, 1
    while width:
        if width & 1:
            part = level[first : first + count]
            total = part if total is None else total + part
            first += size
        width >>= 1
        if width:
            level = level[:-size] + level[size:]
            size *= 2
    return total


def seasonal_parts(series, halves, rim):
    steps = series.shape[0]
    before, after = neighbours(series[:rim], series[steps - rim :])
    position = lax.axis_index("tm")
    before = jnp.where(position == 0, jnp.broadcast_to(series[:1], before.shape), before)
    is_final = position == lax.axis_size("tm") - 1
    after = jnp.where(is_final, jnp.broadcast_to(series[-1:], after.shape), after)
    wide = jnp.concatenate([before, series, after]).astype(FLOAT)
    parts = []
    for half in halves:
        mean = window_sum(wide, rim - half, 2 * half + 1, steps) / (2 * half + 1)
        parts.append((series.astype(FLOAT) - mean).astype(HALF_FLOAT))
    return parts


def series_gradient(grads, halves, rim):
    steps = grads[0].shape[0]
    wide = 0.0
    for grad, half in zip(grads, halves):
        padded = jnp.pad(grad, ((2 * rim, 2 * rim), (0, 0), (0, 0)))
        wide = wide + window_sum(padded, rim - half, 2 * half + 1, steps + 2 * rim) / (
            2 * half + 1
        )
    low_rim, high_rim = wide[:rim], wide[rim + steps :]
    before, after = neighbours(low_rim, high_rim)
    position = lax.axis_index("tm")
    is_final = position == lax.axis_size("tm") - 1
    low_sum = jnp.pad(jnp.sum(low_rim, axis=0, keepdims=True), ((0, rim - 1), (0, 0), (0, 0)))
    high_sum = jnp.pad(jnp.sum(high_rim, axis=0, keepdims=True), ((rim - 1, 0), (0, 0), (0, 0)))
    before = jnp.where(position == 0, low_sum, before)
    after = jnp.where(is_final, high_sum, after)
    middle = jnp.zeros((steps - 2 * rim,) + before.shape[1:], FLOAT)
    edges = jnp.concatenate([before, middle, after])
    return (sum(grads) - wide[rim : rim + steps] - edges).astype(HALF_FLOAT)


def step_block(kernel):
    return next(size for size in (4, 3, 2, 1) if kernel % size == 0)


def row_spec(block):
    return pl.BlockSpec(block, lambda i: (0,) * len(block))


def steps_spec(values, block):
    pieces, _, series, channels = values.shape
    return pl.BlockSpec((pieces, block, series, channels), lambda i: (0, i, 0, 0))


def weight_spec(weight, block):
    return pl.BlockSpec((block,) + weight.shape[1:], lambda i: (i, 0, 0))


def local_call(kernel, grid, inputs, outputs, flops, nbytes, name):
    return pl.pallas_call(
        kernel,
        out_shape=tuple(shape for shape, _ in outputs),
        grid=(grid,),
        in_specs=[spec for _, spec in inputs],
        out_specs=tuple(spec for _, spec in outputs),
        compiler_params=pltpu.CompilerParams(vmem_limit_bytes=48 * 1024 * 1024),
        cost_estimate=pl.CostEstimate(
            flops=flops, bytes_accessed=nbytes, transcendentals=0
        ),
        name=name,
    )(*[value for value, _ in inputs])


def down_kernel(x_ref, w_ref, b_ref, out_ref):
    step = pl.program_id(0)

    @pl.when(step == 0)
    def _():
        out_ref[...] = jnp.broadcast_to(b_ref[...], out_ref.shape)

    total = out_ref[...]
    for one in range(w_ref.shape[0]):
        total = total + dot_nn(x_ref[:, one].reshape(total.shape), w_ref[one])
    out_ref[...] = total

    @pl.when(step == pl.num_programs(0) - 1)
    def _():
        out_ref[...] = jnp.tanh(out_ref[...])


def down_layer(seasonal, weight, bias_row):
    pieces, kernel, series, channels = seasonal.shape
    block = step_block(kernel)
    rows = pieces * series
    (down_act,) = local_call(
        down_kernel,
        kernel // block,
        [
            (seasonal, steps_spec(seasonal, block)),
            (weight, weight_spec(weight, block)),
            (bias_row[None], row_spec((1, channels))),
        ],
        [(jax.ShapeDtypeStruct((rows, channels), FLOAT), row_spec((rows, channels)))],
        2 * seasonal.size * channels,
        2 * (seasonal.size + weight.size),
        "down_layer",
    )
    return down_act


def normed(values):
    center = values - jnp.mean(values, axis=-1, keepdims=True)
    spread = jnp.mean(center * center, axis=-1, keepdims=True)
    scale = lax.rsqrt(spread + EPSILON)
    return center * scale, scale


def normed_back(grad, hat, scale):
    return (
        grad
        - jnp.mean(grad, axis=-1, keepdims=True)
        - hat * jnp.mean(grad * hat, axis=-1, keepdims=True)
    ) * scale


def up_kernel(picks, inner_ref, x_ref, w_ref, rows_ref, act_ref, out_ref):
    bias_row, gain_row, shift_row = (rows_ref[i : i + 1] for i in picks)
    inner = inner_ref[...]
    for one in range(w_ref.shape[0]):
        act = jnp.tanh(dot_nn(inner, w_ref[one]) + bias_row)
        hat, _ = normed(act + x_ref[:, one].reshape(act.shape).astype(FLOAT))
        act_ref[:, one] = act.reshape(act_ref.shape[0], act_ref.shape[2], act_ref.shape[3])
        out = (hat * gain_row + shift_row).astype(HALF_FLOAT)
        out_ref[:, one] = out.reshape(out_ref.shape[0], out_ref.shape[2], out_ref.shape[3])


def up_layer(inner, seasonal, weight, rows, picks):
    pieces, kernel, series, channels = seasonal.shape
    block = step_block(kernel)
    return local_call(
        functools.partial(up_kernel, picks),
        kernel // block,
        [
            (inner, row_spec(inner.shape)),
            (seasonal, steps_spec(seasonal, block)),
            (weight, weight_spec(weight, block)),
            (rows, row_spec(rows.shape)),
        ],
        [
            (jax.ShapeDtypeStruct(seasonal.shape, FLOAT), steps_spec(seasonal, block)),
            (jax.ShapeDtypeStruct(seasonal.shape, HALF_FLOAT), steps_spec(seasonal, block)),
        ],
        2 * seasonal.size * channels,
        8 * seasonal.size + 2 * weight.size,
        "up_layer",
    )


def up_back_kernel(
    grad_ref, merge_ref, act_ref, x_ref, w_ref, gain_ref, outer_ref, up_ref, inner_ref, sums_ref
):
    @pl.when(pl.program_id(0) == 0)
    def _():
        inner_ref[...] = jnp.zeros_like(inner_ref)
        sums_ref[...] = jnp.zeros_like(sums_ref)

    shape = inner_ref.shape
    block = (x_ref.shape[0], x_ref.shape[2], x_ref.shape[3])
    gain_row = gain_ref[8:9]
    total = inner_ref[...]
    sums = [sums_ref[i : i + 1] for i in range(3)]
    for one in range(w_ref.shape[0]):
        grad = dot_nt(grad_ref[:, one].reshape(shape), merge_ref[0])
        act = act_ref[:, one].reshape(shape)
        hat, scale = normed(act + x_ref[:, one].reshape(shape).astype(FLOAT))
        outer = normed_back(grad * gain_row, hat, scale)
        up = (outer * (1.0 - act * act)).astype(HALF_FLOAT)
        total = total + dot_nt(up, w_ref[one])
        outer_ref[:, one] = outer.reshape(block)
        up_ref[:, one] = up.reshape(block)
        for i, value in enumerate((up.astype(FLOAT), grad * hat, grad)):
            sums[i] = sums[i] + jnp.sum(value, axis=0, keepdims=True)
    inner_ref[...] = total
    for i in range(3):
        sums_ref[i : i + 1] = sums[i]


def up_layer_back(grad, merge, index, act, seasonal, weight, table):
    pieces, kernel, series, channels = seasonal.shape
    block = step_block(kernel)
    rows = pieces * series
    spec = steps_spec(seasonal, block)
    return local_call(
        up_back_kernel,
        kernel // block,
        [
            (grad, spec),
            (merge, pl.BlockSpec((1,) + merge.shape[1:], lambda i: (index, 0, 0))),
            (act, spec),
            (seasonal, spec),
            (weight, weight_spec(weight, block)),
            (table, row_spec(table.shape)),
        ],
        [
            (jax.ShapeDtypeStruct(seasonal.shape, FLOAT), spec),
            (jax.ShapeDtypeStruct(seasonal.shape, HALF_FLOAT), spec),
            (jax.ShapeDtypeStruct((rows, channels), FLOAT), row_spec((rows, channels))),
            (jax.ShapeDtypeStruct((8, channels), FLOAT), row_spec((8, channels))),
        ],
        4 * seasonal.size * channels,
        14 * seasonal.size + 2 * weight.size,
        "up_layer_back",
    )


def head_kernel(
    one_ref,
    two_ref,
    cot_ref,
    mask_ref,
    table_ref,
    bias_ref,
    merge_ref,
    hidden_w_ref,
    output_w_ref,
    result_ref,
    first_ref,
    hidden_ref,
    grad_hidden_ref,
    feed_ref,
    merged_ref,
    sums_ref,
    hidden_sums_ref,
    slope_ref,
    rows_ref,
):
    @pl.when(pl.program_id(0) == 0)
    def _():
        sums_ref[...] = jnp.zeros_like(sums_ref)
        hidden_sums_ref[...] = jnp.zeros_like(hidden_sums_ref)

    channels = one_ref.shape[1]
    chunks = [pl.ds(k * channels, channels) for k in range(hidden_ref.shape[1] // channels)]
    gain_first, gain_final = table_ref[9:10], table_ref[10:11]
    merged = dot_nn(one_ref[...], merge_ref[0]) + dot_nn(two_ref[...], merge_ref[1])
    merged = merged + table_ref[6:7]
    hat_first, scale_first = normed(merged)
    first = (hat_first * gain_first + table_ref[12:13]).astype(HALF_FLOAT)
    first_ref[...] = first
    final = merged + table_ref[7:8]
    for chunk in chunks:
        value = dot_nn(first, hidden_w_ref[:, chunk]) + bias_ref[:, chunk]
        hidden, slope = gelu_pair(value)
        hidden_ref[:, chunk] = hidden
        slope_ref[:, chunk] = slope
        final = final + dot_nn(hidden, output_w_ref[chunk])
    hat_final, scale_final = normed(final)
    mask = mask_ref[...]
    result = (hat_final * gain_final + table_ref[13:14]) * mask
    for lane in range(rows_ref.shape[0]):
        rows_ref[lane] = result[:, lane * 128 : lane * 128 + 128]
    count, steps = result_ref.shape[0], result_ref.shape[1]
    series = rows_ref.shape[1] // steps
    for one in range(count):
        for lane in range(rows_ref.shape[0]):
            value = rows_ref[lane, pl.ds(one, steps, stride=series), :]
            result_ref[one, :, lane * 128 : lane * 128 + 128] = value.astype(HALF_FLOAT)
    grad = cot_ref[...].astype(FLOAT) * mask
    grad_final = normed_back(grad * gain_final, hat_final, scale_final)
    feed = grad_final.astype(HALF_FLOAT)
    feed_ref[...] = feed
    grad_first = jnp.zeros_like(merged)
    for chunk in chunks:
        value = dot_nt(feed, output_w_ref[chunk]) * slope_ref[:, chunk].astype(FLOAT)
        value = value.astype(HALF_FLOAT)
        grad_hidden_ref[:, chunk] = value
        hidden_sums_ref[0:1, chunk] += jnp.sum(value.astype(FLOAT), axis=0, keepdims=True)
        grad_first = grad_first + dot_nt(value, hidden_w_ref[:, chunk])
    grad_merged = grad_final + normed_back(grad_first * gain_first, hat_first, scale_first)
    low = grad_merged.astype(HALF_FLOAT)
    merged_ref[...] = low
    parts = (
        grad_first * hat_first,
        grad * hat_final,
        grad_first,
        grad,
        low.astype(FLOAT),
        feed.astype(FLOAT),
    )
    for row, value in enumerate(parts):
        sums_ref[row : row + 1] += jnp.sum(value, axis=0, keepdims=True)


def head(outs, cotangent, mask_rows, table, bias, merge, hidden_w, output_w, count):
    total, channels = outs[0].shape
    steps = cotangent.shape[0]
    series = total // steps
    block_steps = 16
    rows, hidden = block_steps * series, hidden_w.shape[1]
    block, wide = (
        pl.BlockSpec((rows, channels), lambda i: (i, 0)),
        pl.BlockSpec((rows, hidden), lambda i: (i, 0)),
    )
    low, low_wide = (
        jax.ShapeDtypeStruct((total, channels), HALF_FLOAT),
        jax.ShapeDtypeStruct((total, hidden), HALF_FLOAT),
    )

    def held(value):
        return pl.BlockSpec(value.shape, lambda i: (0,) * value.ndim)

    return pl.pallas_call(
        head_kernel,
        out_shape=(
            jax.ShapeDtypeStruct((count, steps, channels), HALF_FLOAT),
            low,
            low_wide,
            low_wide,
            low,
            low,
            jax.ShapeDtypeStruct((8, channels), FLOAT),
            jax.ShapeDtypeStruct((8, hidden), FLOAT),
        ),
        grid=(steps // block_steps,),
        in_specs=[
            block,
            block,
            block,
            pl.BlockSpec((rows, 1), lambda i: (i, 0)),
            held(table),
            held(bias),
            held(merge),
            held(hidden_w),
            held(output_w),
        ],
        out_specs=(
            pl.BlockSpec((count, block_steps, channels), lambda i: (0, i, 0)),
            block,
            wide,
            wide,
            block,
            block,
            pl.BlockSpec((8, channels), lambda i: (0, 0)),
            pl.BlockSpec((8, hidden), lambda i: (0, 0)),
        ),
        scratch_shapes=[
            pltpu.VMEM((rows, hidden), HALF_FLOAT),
            pltpu.VMEM((channels // 128, rows, 128), FLOAT),
        ],
        compiler_params=pltpu.CompilerParams(vmem_limit_bytes=56 * 1024 * 1024),
        cost_estimate=pl.CostEstimate(
            flops=2 * total * channels * (4 * channels + 4 * hidden),
            bytes_accessed=total * (14 * channels + 4 * hidden),
            transcendentals=total * hidden,
        ),
        name="head",
    )(
        outs[0],
        outs[1],
        cotangent.reshape(total, channels),
        mask_rows,
        table,
        bias,
        merge,
        hidden_w,
        output_w,
    )


def down_back_kernel(grad_ref, w_ref, outer_ref, out_ref):
    grad = grad_ref[...]
    block = (out_ref.shape[0], out_ref.shape[2], out_ref.shape[3])
    for one in range(w_ref.shape[0]):
        out_ref[:, one] = dot_nt(grad, w_ref[one]).reshape(block) + outer_ref[:, one]


def down_layer_back(grad, weight, outer):
    pieces, kernel, series, channels = outer.shape
    block = step_block(kernel)
    spec = steps_spec(outer, block)
    (seasonal_grad,) = local_call(
        down_back_kernel,
        kernel // block,
        [(grad, row_spec(grad.shape)), (weight, weight_spec(weight, block)), (outer, spec)],
        [(jax.ShapeDtypeStruct(outer.shape, FLOAT), spec)],
        2 * outer.size * channels,
        8 * outer.size + 2 * weight.size,
        "down_layer_back",
    )
    return seasonal_grad


class Branch:
    def __init__(self, index, shape, down_weight, table):
        self.index, self.table = index, table
        self.count, steps, channels = shape
        self.kernel = down_weight.shape[0]
        self.pieces = steps // self.kernel
        self.series = round_up(self.count, 16)
        self.down_weight = down_weight
        self.gain_row, self.shift_row = table[8], table[11]

    def down(self, seasonal, down_act=None):
        self.seasonal = seasonal.reshape(self.pieces, self.kernel, self.series, -1)
        if down_act is None:
            down_act = down_layer(self.seasonal, self.down_weight, self.table[self.index])
        self.down_act = down_act
        self.down_low = down_act.astype(HALF_FLOAT)

    def to_series(self, rows):
        return by_series(rows.reshape(self.pieces, self.series, -1), self.count)

    def from_series(self, values):
        return by_time(values).reshape(self.pieces * self.series, -1)

    def inner(self, iso_out):
        act = jnp.tanh(self.from_series(iso_out).astype(FLOAT) + self.table[2 + self.index])
        inner_in = act + self.down_low.astype(FLOAT)
        return act, layer_norm(inner_in, self.gain_row, self.shift_row).astype(HALF_FLOAT)

    def up(self, iso_act, inner_low, up_weight):
        self.up_weight, self.iso_act, self.inner_low = up_weight, iso_act, inner_low
        self.act, out = up_layer(
            inner_low, self.seasonal, up_weight, self.table, (4 + self.index, 8, 11)
        )
        return out.reshape(-1, out.shape[3])

    def up_back(self, grad_merged, merge):
        self.outer, self.grad_up, grad_inner, sums = up_layer_back(
            grad_merged.reshape(self.seasonal.shape),
            merge,
            self.index,
            self.act,
            self.seasonal,
            self.up_weight,
            self.table,
        )
        inner_in = self.iso_act + self.down_low.astype(FLOAT)
        _, inner_pull = jax.vjp(layer_norm, inner_in, self.gain_row, self.shift_row)
        self.grad_inner_in, gain_inner, shift_inner = inner_pull(grad_inner)
        grad_iso = self.grad_inner_in * (1.0 - self.iso_act * self.iso_act)
        self.iso_sum, self.up_sum = jnp.sum(grad_iso, axis=0), sums[0]
        self.gain_sum, self.shift_sum = sums[1] + gain_inner, sums[2] + shift_inner
        return grad_iso.astype(HALF_FLOAT)

    def down_back(self, grad_signal):
        grad_down = self.from_series(grad_signal).astype(FLOAT) + self.grad_inner_in
        self.grad_down = (grad_down * (1.0 - self.down_act * self.down_act)).astype(HALF_FLOAT)
        return jnp.sum(self.grad_down.astype(FLOAT), axis=0)

    def seasonal_back(self):
        grad = down_layer_back(self.grad_down, self.down_weight, self.outer)
        return grad.reshape(-1, self.series, grad.shape[3])


def batch_split(values, split, join):
    return lax.all_to_all(values, "batch", split_axis=split, concat_axis=join, tiled=True)


def time_sum(values, dim):
    return lax.psum_scatter(
        values.astype(HALF_FLOAT), "tm", scatter_dimension=dim, tiled=True
    ).astype(FLOAT)


def plain_gradients(wides, narrows, downs):
    results = []
    for wide, narrow, down in zip(wides, narrows, downs):
        wide = jnp.swapaxes(wide, 0, 1).reshape(wide.shape[1], -1, wide.shape[3])
        if down:
            wide, narrow = batch_split(wide, 2, 1), lax.all_gather(narrow, "batch", tiled=True)
            value = jnp.einsum("knc,nd->kcd", wide, narrow, preferred_element_type=FLOAT)
        else:
            wide = lax.all_gather(wide, "batch", axis=1, tiled=True)
            narrow = batch_split(narrow, 1, 0)
            value = jnp.einsum("nd,knc->dkc", narrow, wide, preferred_element_type=FLOAT)
        results.append(time_sum(value, 2))
    return results


def plain_sums(matrices):
    results = []
    for kind, value in matrices:
        batch_dim, time_dim = (0, 1) if kind == "rows" else (value.ndim - 1, value.ndim - 2)
        value = lax.psum_scatter(
            value.astype(FLOAT), "batch", scatter_dimension=batch_dim, tiled=True
        )
        results.append(time_sum(value, time_dim))
    return results


def per_device(
    series_in,
    out_cotangent,
    out_mask,
    down_twelve,
    down_sixteen,
    iso_twelve,
    iso_sixteen,
    up_twelve,
    up_sixteen,
    branch_bias,
    merge_weight,
    hidden_weight,
    hidden_bias,
    output_weight,
    head_bias,
    norm_gain,
    norm_shift,
):
    series_dev, step_count, channels = series_in.shape
    halves = (down_twelve.shape[0] // 2, down_sixteen.shape[0] // 2)
    rim = max(halves)
    hidden_rows = hidden_bias.reshape(-1, channels)
    table = jnp.concatenate([branch_bias, head_bias, norm_gain, norm_shift, hidden_rows])
    table = jnp.pad(table, ((0, -table.shape[0] % 8), (0, 0))).astype(FLOAT)
    down_weights = (down_twelve, down_sixteen)
    branches = [
        Branch(k, series_in.shape, down_weights[k], table) for k in range(2)
    ]
    iso_weights = (iso_twelve, iso_sixteen)
    sizes = plane_sizes(channels)
    up_weights = [up_twelve, up_sixteen]
    turns = [weight for weight in up_weights if weight.shape[1] % 8 == 0]
    shapes = [(series_dev, branch.pieces, channels) for branch in branches]
    if sizes:
        per_time = sum(round_up(branch.pieces, 8) for branch in branches)
        values, wides = None, []
        front = (series_in, out_cotangent, down_weights, table, per_time, halves, rim)
    else:
        for branch, seasonal in zip(branches, seasonal_parts(by_time(series_in), halves, rim)):
            branch.down(seasonal)
        values = [branch.to_series(branch.down_low) for branch in branches]
        wides = [branch.seasonal for branch in branches]
        front = None
    forward, iso_outs = spectral(
        values, shapes, iso_weights, False, ForwardExtra(sizes, wides, turns, front)
    )
    if sizes:
        for k in range(2):
            branches[k].down(forward[f"seasonal{k}"], forward[f"down_act{k}"])
        inners = [(forward[f"iso_act{k}"], forward[f"inner{k}"]) for k in range(2)]
        cotangent = forward["cotangent_steps"]
    else:
        inners = [branches[k].inner(iso_outs[k]) for k in range(2)]
        cotangent = by_time(out_cotangent)
    turned = [forward[f"turned{i}"] for i in range(len(turns))]
    up_weights = [
        jnp.swapaxes(weight, 0, 1) if weight.shape[1] % 8 else turned.pop(0)
        for weight in up_weights
    ]
    outs = [
        branch.up(*inner, weight)
        for branch, inner, weight in zip(branches, inners, up_weights)
    ]
    row_count = outs[0].shape[0]
    mask_rows = by_time(out_mask.astype(FLOAT)).reshape(row_count, 1)
    hidden_row = table[14 : 14 + hidden_rows.shape[0]].reshape(1, -1)
    result, first_low, hidden_low, grad_hidden_pre, grad_feed, grad_merged, sums, hidden_sums = head(
        outs,
        cotangent,
        mask_rows,
        table,
        hidden_row,
        merge_weight,
        hidden_weight,
        output_weight,
        series_dev,
    )
    gain_first, gain_final, shift_first, shift_final = (sums[k] for k in range(4))
    grad_merge_bias, grad_output_bias, grad_hidden_bias = sums[4], sums[5], hidden_sums[0]
    hidden_size = hidden_low.shape[1]
    jobs = (
        (first_low, [grad_hidden_pre], (channels, hidden_size)),
        (grad_feed, [hidden_low], (channels, hidden_size)),
        (grad_merged, outs, (2, channels, channels)),
    )
    job_kinds = ("rows", "lanes", "lanes")
    grad_isos = [branches[k].up_back(grad_merged, merge_weight) for k in range(2)]
    up_wides = [branch.grad_up for branch in branches]
    up_narrows = [branch.inner_low for branch in branches]
    backward, grad_signals = spectral(
        [branch.to_series(grad) for branch, grad in zip(branches, grad_isos)],
        shapes,
        iso_weights,
        True,
        BackwardExtra(
            sizes,
            forward["spec"],
            up_wides,
            up_narrows,
            jobs,
            [branch.grad_inner_in for branch in branches],
            [branch.down_act for branch in branches],
            (
                series_dev,
                sum(round_up(branch.pieces, 8) for branch in branches),
                branches[0].series,
            ),
        ),
    )
    iso_parts, first = [], 0
    for bins in (branches[0].pieces, branches[1].pieces):
        iso_parts.append(
            iso_gradients(
                forward["spec"],
                backward["specs"],
                backward["spec"],
                backward["grads"],
                first,
                bins,
            )
        )
        first += round_up(bins, 8)
    if sizes:
        matrices = [(kind, backward[f"matrix{i}"]) for i, kind in enumerate(job_kinds)]
        down_sums = backward["down_sums"][:2]
        down_narrows = [backward["down_grad0"], backward["down_grad1"]]
    else:
        matrices = []
        for kind, (left, rights, shape) in zip(job_kinds, jobs):
            values = [
                jnp.einsum("nd,nf->df", left, right, preferred_element_type=FLOAT)
                for right in rights
            ]
            matrices.append((kind, jnp.stack(values).astype(HALF_FLOAT).reshape(shape)))
        down_sums = jnp.stack([branches[k].down_back(grad_signals[k]) for k in range(2)])
        down_narrows = [branch.grad_down for branch in branches]
    one, two = branches
    singles = (one.iso_sum, two.iso_sum, one.up_sum, two.up_sum)
    singles += (one.gain_sum + two.gain_sum, gain_first, gain_final)
    singles += (one.shift_sum + two.shift_sum, shift_first, shift_final)
    singles += (grad_merge_bias, grad_output_bias)
    vectors = jnp.concatenate(
        [down_sums] + [row[None] for row in singles] + [grad_hidden_bias.reshape(-1, channels)]
    )
    vectors = jnp.pad(vectors, ((0, -vectors.shape[0] % 8), (0, 0)))
    if sizes:
        downs, vectors, grad_series, sums = down_gradients(
            sizes,
            (forward["gathered0"], forward["gathered1"]),
            down_narrows,
            vectors,
            (down_twelve, down_sixteen),
            [branch.outer.reshape(step_count, -1, channels) for branch in branches],
            halves,
            rim,
            series_dev,
            matrices,
        )
        downs = [jnp.transpose(value, (0, 2, 1)) for value in downs]
        ups = [jnp.transpose(backward[key], (2, 0, 1)) for key in ("up0", "up1")]
    else:
        vectors = lax.psum(vectors, ("tm", "batch"))
        grad_seasonals = [branch.seasonal_back() for branch in branches]
        grad_series = by_series(series_gradient(grad_seasonals, halves, rim), series_dev)
        downs = plain_gradients(wides, down_narrows, (True, True))
        ups = plain_gradients(up_wides, up_narrows, (False, False))
        sums = plain_sums(matrices)
    me, devices = lax.axis_index("tm"), lax.axis_size("tm")
    width = channels // devices
    rows = lax.dynamic_slice_in_dim(vectors[:14], me * width, width, axis=1)
    hidden_width = hidden_bias.shape[0] // devices
    hidden_sum = vectors[14 : 14 + hidden_rows.shape[0]].reshape(-1)
    vector_parts = (
        rows[:6],
        lax.dynamic_slice_in_dim(hidden_sum, me * hidden_width, hidden_width),
        rows[12:14],
        rows[6:9],
        rows[9:12],
    )
    return (
        result,
        grad_series,
        downs[0],
        downs[1],
        iso_parts[0],
        iso_parts[1],
        ups[0],
        ups[1],
        vector_parts[0],
        jnp.swapaxes(sums[2], 1, 2),
        sums[0],
        vector_parts[1],
        sums[1].T,
        vector_parts[2],
        vector_parts[3],
        vector_parts[4],
    )


def solution(mesh):
    placed = (
        P("batch", "tm", None),
        P("batch", "tm", None),
        P("batch", "tm"),
        P(),
        P(),
        P("tm", None, "batch", None),
        P("tm", None, "batch", None),
        P(),
        P(),
        P(),
        P(),
        P(),
        P(),
        P(),
        P(),
        P(),
        P(),
    )
    return jax.shard_map(
        per_device,
        mesh=mesh,
        in_specs=placed,
        out_specs=(
            P("batch", "tm", None),
            P("batch", "tm", None),
            P(None, "batch", "tm"),
            P(None, "batch", "tm"),
            P("tm", None, "batch", None),
            P("tm", None, "batch", None),
            P("batch", None, "tm"),
            P("batch", None, "tm"),
            P(None, "tm"),
            P(None, "batch", "tm"),
            P("batch", "tm"),
            P("tm"),
            P("batch", "tm"),
            P(None, "tm"),
            P(None, "tm"),
            P(None, "tm"),
        ),
        check_vma=False,
    )
```

```python
import functools
import math

import jax
import jax.numpy as jnp
import numpy as np
from jax import lax
from jax.experimental import pallas as pl
from jax.experimental.pallas import tpu as pltpu
from jax.sharding import PartitionSpec as P

FLOAT = jnp.float32
HALF_FLOAT = jnp.bfloat16
HIGHEST = lax.Precision.HIGHEST
EPSILON = 1e-05
MESH = pl.DeviceIdType.MESH


def layer_norm(values, gain_row, bias_row):
    center = values - jnp.mean(values, axis=-1, keepdims=True)
    spread = jnp.mean(center * center, axis=-1, keepdims=True)
    return center * lax.rsqrt(spread + EPSILON) * gain_row + bias_row


def round_up(value, multiple):
    return -(-value // multiple) * multiple


def spectral_constants(devices, pieces_list):
    padded = [round_up(pieces, 8) for pieces in pieces_list]
    per_time, per_bin = sum(padded), 2 * sum(padded)
    table = np.zeros((devices, per_bin, devices, per_time), np.float64)
    offset = 0
    for pieces, wide in zip(pieces_list, padded):
        length = devices * pieces
        index = np.arange(length)
        angle = (2.0 * math.pi / length) * (np.outer(index, index) % length)
        factor = 1.0 / math.sqrt(length)
        for part, values in enumerate((np.cos(angle) * factor, -np.sin(angle) * factor)):
            row = 2 * offset + part * wide
            table[:, row : row + pieces, :, offset : offset + pieces] = values.reshape(
                devices, pieces, devices, pieces
            )
        offset += wide
    table = table.reshape(devices * per_bin, devices * per_time).astype(np.float32)
    high = table.astype(HALF_FLOAT)
    low = (table - high.astype(np.float32)).astype(HALF_FLOAT)
    return jnp.asarray(np.stack([high, low]))


def move_index(out, devices, wide):
    per_bin = 2 * sum(wide)
    base, result = 0, None
    for room in wide:
        local = out - 2 * devices * base
        one_bin = lax.div(local, jnp.full_like(local, 2 * devices))
        rest = local - one_bin * (2 * devices)
        part = jnp.where(rest >= devices, 1, 0)
        series = rest - part * devices
        value = series * per_bin + 2 * base + part * room + one_bin
        result = value if result is None else jnp.where(local >= 0, value, result)
        base += room
    return result


def moves(shape, devices, wide):
    rows = lax.broadcasted_iota(jnp.int32, shape, 0)
    columns = lax.broadcasted_iota(jnp.int32, shape, 1)
    there = jnp.where(columns == move_index(rows, devices, wide), 1.0, 0.0)
    back = jnp.where(rows == move_index(columns, devices, wide), 1.0, 0.0)
    return there.astype(HALF_FLOAT), back.astype(HALF_FLOAT)


def dot_nn(left, right):
    return jnp.dot(left, right, preferred_element_type=FLOAT)


def dot_nt(left, right):
    return lax.dot_general(left, right, (((1,), (1,)), ((), ())), preferred_element_type=FLOAT)


def spectral_body(sizes, back, refs, extra):
    devices, batches, count, pieces_list = sizes
    w1_ref, w2_ref = refs["weight0"], refs["weight1"]
    table_ref = refs["table"]
    inverse_ref, move_ref, unmove_ref = refs["tables"]
    spec_ref, signal_ref = refs["spec"], refs["signal"]
    (one, two, three, mixed, spread, bins_out, four, w1, w2) = refs["buffers"]
    (s1, r1, s2, r2, s3, r3, s4, r4, ws, wr, own) = refs["sems"]
    me = lax.axis_index("tm")
    mine = lax.axis_index("batch")
    wide = [round_up(pieces, 8) for pieces in pieces_list]
    per_time, per_bin = sum(wide), 2 * sum(wide)
    weights = ((w1_ref, w1), (w2_ref, w2))

    barrier = pltpu.get_barrier_semaphore()

    @pl.loop(1, devices)
    def _(step):
        pl.semaphore_signal(
            barrier, inc=1, device_id=(mine, lax.rem(me + step, devices)), device_id_type=MESH
        )

    for step in range(1, batches):
        pl.semaphore_signal(
            barrier, inc=1, device_id=(lax.rem(mine + step, batches), me), device_id_type=MESH
        )
    pl.semaphore_wait(barrier, devices - 1 + batches - 1 + extra.greet(barrier))

    def exchange(source, target, send_sem, recv_sem, limit_out, limit_in, rows, start):
        def remote(there, here):
            return pltpu.make_async_remote_copy(
                src_ref=source.at[pl.ds(pl.multiple_of(there * rows, rows), rows)],
                dst_ref=target.at[pl.ds(pl.multiple_of(here * rows, rows), rows)],
                send_sem=send_sem.at[there],
                recv_sem=recv_sem.at[here],
                device_id=(mine, there),
                device_id_type=MESH,
            )

        if start:

            @pl.loop(1, devices)
            def _(step):
                there = lax.rem(me + step, devices)

                @pl.when(there < limit_out)
                def _():
                    remote(there, me).start()

        else:

            @pl.loop(1, devices)
            def _(step):
                there = lax.rem(me + step, devices)

                @pl.when(there < limit_in)
                def _():
                    pltpu.make_async_remote_copy(
                        src_ref=source.at[pl.ds(0, rows)],
                        dst_ref=target.at[pl.ds(pl.multiple_of(there * rows, rows), rows)],
                        send_sem=send_sem.at[there],
                        recv_sem=recv_sem.at[there],
                        device_id=(mine, there),
                        device_id_type=MESH,
                    ).wait_recv()

    def drain(source, target, send_sem, recv_sem, limit_out, rows):
        @pl.loop(1, devices)
        def _(step):
            there = lax.rem(me + step, devices)

            @pl.when(there < limit_out)
            def _():
                pltpu.make_async_remote_copy(
                    src_ref=source.at[pl.ds(0, rows)],
                    dst_ref=target.at[pl.ds(0, rows)],
                    send_sem=send_sem.at[there],
                    recv_sem=recv_sem.at[there],
                    device_id=(mine, there),
                    device_id_type=MESH,
                ).wait_send()

    owner = me < count

    def weight_copies(index):
        source, target = weights[index]
        rows = source.shape[2]
        place = target.at[:, :, pl.ds(pl.multiple_of(mine * rows, rows), rows)]
        local = pltpu.make_async_copy(source, place, own.at[index])
        remote = []
        for step in range(1, batches):
            there = lax.rem(mine + step, batches)
            back_there = lax.rem(mine + batches - step, batches)
            other = target.at[:, :, pl.ds(pl.multiple_of(back_there * rows, rows), rows)]
            remote.append(
                [
                    pltpu.make_async_remote_copy(
                        src_ref=source,
                        dst_ref=where,
                        send_sem=ws.at[index, step],
                        recv_sem=wr.at[index, step],
                        device_id=(there, me),
                        device_id_type=MESH,
                    )
                    for where in (place, other)
                ]
            )
        return local, remote

    for index in range(2):
        local, remote = weight_copies(index)
        local.start()
        for copy, _unused in remote:
            copy.start()

    extra.open()
    inverse_ref[0], inverse_ref[1] = table_ref[0].T, table_ref[1].T
    move_ref[...], unmove_ref[...] = moves(move_ref.shape, devices, wide)
    x_ref = extra.prepare()
    exchange(x_ref, one, s1, r1, count, None, per_time, True)
    here = pltpu.make_async_copy(
        x_ref.at[pl.ds(pl.multiple_of(jnp.minimum(me, count - 1) * per_time, per_time), per_time)],
        one.at[pl.ds(pl.multiple_of(me * per_time, per_time), per_time)],
        own.at[2],
    )
    here.start()
    extra.start()
    if count < devices:
        two[pl.ds(count * per_bin, (devices - count) * per_bin)] = jnp.zeros(
            ((devices - count) * per_bin, two.shape[1]), two.dtype
        )
    here.wait()

    @pl.when(owner)
    def _():
        exchange(x_ref, one, s1, r1, None, devices, per_time, False)
        data = one[...]
        total = dot_nn(table_ref[0], data) + dot_nn(table_ref[1], data)
        bins_out[...] = total.astype(HALF_FLOAT)
        exchange(bins_out, two, s2, r2, devices, None, per_bin, True)
        place = pl.ds(pl.multiple_of(me * per_bin, per_bin), per_bin)
        two[place] = bins_out[place]

    extra.after_bins()
    exchange(bins_out, two, s2, r2, None, count, per_bin, False)
    spec_ref[...] = dot_nn(move_ref[...], two[...]).astype(HALF_FLOAT)
    extra.after_spec()
    base = 0
    for index in range(2):
        local, remote = weight_copies(index)
        local.wait()
        for copy, arrived in remote:
            copy.wait_send()
            arrived.wait_recv()
        target = weights[index][1]

        @pl.loop(0, pieces_list[index])
        def _(one_bin, base=base, target=target):
            place = pl.ds(
                pl.multiple_of(base + one_bin * 2 * devices, 2 * devices), 2 * devices
            )
            rows = spec_ref[place]
            if back:
                real = dot_nt(rows, target[one_bin, 0])
                imag = dot_nt(rows, target[one_bin, 1])
                out = jnp.concatenate(
                    [real[:devices] + imag[devices:], real[devices:] - imag[:devices]]
                )
            else:
                real = dot_nn(rows, target[one_bin, 0])
                imag = dot_nn(rows, target[one_bin, 1])
                out = jnp.concatenate(
                    [real[:devices] - imag[devices:], imag[:devices] + real[devices:]]
                )
            mixed[place] = out.astype(HALF_FLOAT)

        spare = wide[index] - pieces_list[index]
        if spare:
            mixed[
                pl.ds(base + pieces_list[index] * 2 * devices, spare * 2 * devices)
            ] = jnp.zeros((spare * 2 * devices, mixed.shape[1]), mixed.dtype)
        base += wide[index] * 2 * devices

    spread[...] = dot_nn(unmove_ref[...], mixed[...]).astype(HALF_FLOAT)
    exchange(spread, three, s3, r3, count, None, per_bin, True)
    extra.after_mixed()

    @pl.when(owner)
    def _():
        place = pl.ds(pl.multiple_of(me * per_bin, per_bin), per_bin)
        three[place] = spread[place]
        exchange(spread, three, s3, r3, None, devices, per_bin, False)
        data = three[...]
        total = dot_nn(inverse_ref[0], data) + dot_nn(inverse_ref[1], data)
        four[...] = total.astype(HALF_FLOAT)
        exchange(four, signal_ref, s4, r4, devices, None, per_time, True)
        place = pl.ds(pl.multiple_of(me * per_time, per_time), per_time)
        signal_ref[place] = four[place]

    extra.after_signal()
    exchange(four, signal_ref, s4, r4, None, count, per_time, False)
    drain(x_ref, one, s1, r1, count, per_time)
    drain(spread, three, s3, r3, count, per_bin)

    @pl.when(owner)
    def _():
        drain(bins_out, two, s2, r2, devices, per_bin)
        drain(four, signal_ref, s4, r4, devices, per_time)

    extra.finish()


class Place:
    def __init__(self, groups, members, batches):
        self.groups, self.members, self.batches = groups, members, batches
        self.me = lax.axis_index("tm")
        self.core = lax.axis_index("batch")
        self.group = lax.div(self.me, members)
        self.member = lax.rem(self.me, members)

    def device(self, group, member, core):
        return (core, group * self.members + member)

    def member_at(self, step):
        return lax.rem(self.member + step + self.members, self.members)

    def group_at(self, step):
        return lax.rem(self.group + step + self.groups, self.groups)

    def core_at(self, step):
        return lax.rem(self.core + step + self.batches, self.batches)

    def greet(self, barrier):
        greeted = 0
        for step in range(self.members):
            for turn in range(self.batches):
                if step or turn:
                    there = self.device(self.group, self.member_at(step), self.core_at(turn))
                    pl.semaphore_signal(barrier, inc=1, device_id=there, device_id_type=MESH)
                    greeted += 1
        for step in range(1, self.groups):
            for turn in range(self.batches):
                there = self.device(self.group_at(step), self.member, self.core_at(turn))
                pl.semaphore_signal(barrier, inc=1, device_id=there, device_id_type=MESH)
                greeted += 1
        return greeted


class VectorSum:
    @staticmethod
    def scratch(place_sizes, value):
        dma = pltpu.SemaphoreType.DMA
        groups, members, batches = place_sizes
        parts = [pltpu.VMEM(value.shape, value.dtype)]
        for size in (batches, members, groups):
            parts += [pltpu.VMEM((size,) + value.shape, value.dtype), dma((size,)), dma((size,))]
        return parts + [pltpu.VMEM(value.shape, value.dtype) for _ in range(2)]

    def __init__(self, place, source, out, scratch):
        self.place, self.source, self.out = place, source, out
        self.stages = [scratch[1 + 3 * k : 4 + 3 * k] for k in range(3)]
        self.values = [source, scratch[10], scratch[11]]

    def copy(self, stage, step, back):
        place = self.place
        held, send, recv = self.stages[stage]
        picks = [place.core_at, place.member_at, place.group_at]
        to = [place.core, place.member, place.group]
        to[stage] = picks[stage](step)
        return send_copy(
            self.values[stage],
            held.at[picks[stage](-step) if back else picks[stage](0)],
            send.at[step],
            recv.at[step],
            place.device(to[2], to[1], to[0]),
        )

    def start(self, stage):
        for step in range(1, self.stages[stage][0].shape[0]):
            self.copy(stage, step, False).start()

    def add(self, stage):
        held = self.stages[stage][0]
        value = self.values[stage][...]
        picks = [self.place.core_at, self.place.member_at, self.place.group_at]
        held[picks[stage](0)] = value
        for step in range(1, held.shape[0]):
            self.copy(stage, step, True).wait_recv()
        total = held[0]
        for index in range(1, held.shape[0]):
            total = total + held[index]
        target = self.out if stage == 2 else self.values[stage + 1]
        target[...] = total
        if stage < 2:
            self.start(stage + 1)

    def drain(self):
        for stage in range(3):
            for step in range(1, self.stages[stage][0].shape[0]):
                self.copy(stage, step, False).wait_send()


def send_copy(source, target, send_sem, recv_sem, there):
    return pltpu.make_async_remote_copy(
        src_ref=source,
        dst_ref=target,
        send_sem=send_sem,
        recv_sem=recv_sem,
        device_id=there,
        device_id_type=MESH,
    )


def slab(ref, dim, index, size):
    picks = [slice(None)] * len(ref.shape)
    picks[dim] = pl.ds(pl.multiple_of(index * size, size), size)
    return ref.at[tuple(picks)]


class WideExchange:
    @staticmethod
    def scratch(place_sizes, wide):
        groups, members, batches = place_sizes
        mates = members * batches
        dma = pltpu.SemaphoreType.DMA
        return [dma((mates,)), dma((mates,)), dma((wide.shape[1] // members,))]

    @staticmethod
    def shape(place_sizes, wide):
        groups, members, batches = place_sizes
        pieces, steps, series, channels = wide.shape
        return (steps // members, members * batches, pieces, series, channels // batches)

    def __init__(self, place, source, target, sems):
        self.place, self.source, self.target = place, source, target
        self.send_sem, self.recv_sem, self.local_sem = sems

    def hops(self):
        for step in range(self.place.members):
            for turn in range(self.place.batches):
                if step or turn:
                    yield step, turn

    def mate(self, step, turn):
        return self.place.core_at(turn) * self.place.members + self.place.member_at(step)

    def piece(self, one, step, turn):
        place = self.place
        steps, half = self.target.shape[0], self.target.shape[4]
        return slab(
            self.source.at[:, place.member_at(step) * steps + one], 2, place.core_at(turn), half
        )

    def own(self, one):
        return pltpu.make_async_copy(
            self.piece(one, 0, 0), self.target.at[one, self.mate(0, 0)], self.local_sem.at[one]
        )

    def whole(self, step, turn, pick):
        slot = turn * self.place.members + step
        block = self.target.at[:, pick]
        return send_copy(
            block,
            block,
            self.send_sem.at[slot],
            self.recv_sem.at[slot],
            self.place.device(
                self.place.group, self.place.member_at(step), self.place.core_at(turn)
            ),
        )

    def units(self):
        return [functools.partial(self.start, one) for one in range(self.target.shape[0])]

    def start(self, one):
        place = self.place
        self.own(one).start()
        for step, turn in self.hops():
            slot = turn * place.members + step
            send_copy(
                self.piece(one, step, turn),
                self.target.at[one, self.mate(0, 0)],
                self.send_sem.at[slot],
                self.recv_sem.at[slot],
                place.device(place.group, place.member_at(step), place.core_at(turn)),
            ).start()

    def wait(self):
        for one in range(self.target.shape[0]):
            self.own(one).wait()
        for step, turn in self.hops():
            self.whole(step, turn, self.mate(-step, -turn)).wait_recv()

    def drain(self):
        for step, turn in self.hops():
            self.whole(step, turn, self.mate(0, 0)).wait_send()


class NarrowGather:
    sems = 5

    @staticmethod
    def scratch(place_sizes, narrow):
        groups, members, batches = place_sizes
        dma = pltpu.SemaphoreType.DMA
        size = members * batches
        return [dma((members,)), dma((members,)), dma((size,)), dma((size,)), dma((1,))]

    def __init__(self, place, source, target, sems):
        self.place, self.source, self.target = place, source, target
        (self.link_send, self.link_recv, self.chip_send, self.chip_recv, self.local_sem) = sems

    def own(self):
        place = self.place
        pick = place.core * place.members + place.member
        return pltpu.make_async_copy(self.source, self.target.at[pick], self.local_sem.at[0])

    def link(self, step, pick_step):
        place = self.place
        pick = place.core * place.members + place.member_at(pick_step)
        return send_copy(
            self.source,
            self.target.at[pick],
            self.link_send.at[step],
            self.link_recv.at[step],
            place.device(place.group, place.member_at(step), place.core),
        )

    def chip(self, step, turn, source_core, target_core):
        place = self.place
        member = place.member_at(-step)
        slot = turn * place.members + step
        source = self.target.at[source_core * place.members + member] if step else self.source
        return send_copy(
            source,
            self.target.at[target_core * place.members + member],
            self.chip_send.at[slot],
            self.chip_recv.at[slot],
            place.device(place.group, place.member, place.core_at(turn)),
        )

    def start(self):
        place = self.place
        self.own().start()
        for step in range(1, place.members):
            self.link(step, 0).start()
        for turn in range(1, place.batches):
            self.chip(0, turn, place.core, place.core).start()

    def forward(self):
        place = self.place
        for step in range(1, place.members):
            self.link(step, -step).wait_recv()
            for turn in range(1, place.batches):
                self.chip(step, turn, place.core, place.core).start()

    def wait(self):
        place = self.place
        self.own().wait()
        for turn in range(1, place.batches):
            other = place.core_at(-turn)
            for step in range(place.members):
                self.chip(step, turn, place.core, other).wait_recv()

    def drain(self):
        place = self.place
        for step in range(1, place.members):
            self.link(step, 0).wait_send()
        for turn in range(1, place.batches):
            for step in range(place.members):
                self.chip(step, turn, place.core, place.core).wait_send()


class KernelProduct:
    sems = 6

    @staticmethod
    def scratch(place_sizes, kind, wide, narrow):
        groups, members, batches = place_sizes
        pieces, kernel, series, channels = wide.shape
        steps, rows = kernel // members, pieces * series
        half = channels // batches
        piece = (128, half) if kind == "down" else (half, 128)
        dma = pltpu.SemaphoreType.DMA
        return [
            pltpu.VMEM((channels, members * batches * rows), HALF_FLOAT),
            pltpu.VMEM((steps, channels, half), HALF_FLOAT),
            pltpu.VMEM((groups, steps) + piece, HALF_FLOAT),
            pltpu.VMEM((steps, 128, half), HALF_FLOAT),
            pltpu.VMEM((kernel, channels // (groups * members), half), HALF_FLOAT),
            dma((groups * batches,)),
            dma((groups * batches,)),
            dma((members,)),
            dma((members,)),
            dma((2,)),
        ]

    def __init__(self, place, kind, wide_in, narrow_in, out, scratch):
        self.place, self.kind, self.wide_in, self.narrow_in, self.out = (
            place,
            kind,
            wide_in,
            narrow_in,
            out,
        )
        (self.narrow_t, self.send, self.recv, self.total, self.gathered) = scratch[:5]
        (self.sz, self.rz, self.sf, self.rf, self.local) = scratch[5:]
        self.cores_per_group = place.groups // place.batches

    def multiply(self):
        mates, rows = self.narrow_in.shape[0], self.narrow_in.shape[1]
        self.narrow_t[...] = self.narrow_in[...].reshape(mates * rows, -1).T

        @pl.loop(0, self.wide_in.shape[0])
        def _(one):
            data = self.wide_in[one].reshape(mates * rows, -1)
            self.send[one] = dot_nn(self.narrow_t[...], data).astype(HALF_FLOAT)

    def chunk(self, group, core):
        if self.kind == "down":
            return slab(self.send, 1, group, 128)
        half = self.send.shape[1] // self.place.batches
        return slab(
            slab(self.send, 1, core, half), 2, lax.rem(group, self.cores_per_group), 128
        )

    def hops(self):
        place = self.place
        for step in range(place.groups):
            for turn in range(place.batches if self.kind == "up" else 1):
                yield step, turn

    def partial(self, step, turn, action):
        place = self.place
        group, core = place.group_at(step), place.core_at(turn)
        slot = step * place.batches + turn
        if step == 0 and turn == 0:
            copy = pltpu.make_async_copy(
                self.chunk(group, core), self.recv.at[place.group], self.local.at[0]
            )
            act = lambda: action(copy, True)
        else:
            copy = send_copy(
                self.chunk(group, core),
                self.recv.at[place.group],
                self.sz.at[slot],
                self.rz.at[slot],
                place.device(group, place.member, core),
            )
            act = lambda: action(copy, False)
        if self.kind == "down":
            act()
        else:
            pl.when(lax.div(group, self.cores_per_group) == place.core)(act)

    def start_partials(self):
        for step, turn in self.hops():
            self.partial(step, turn, lambda copy, local: copy.start())

    def sum_partials(self):
        place = self.place
        for step, turn in self.hops():
            group, core = place.group_at(-step), place.core_at(-turn)
            slot = step * place.batches + turn

            def act(step=step, turn=turn, group=group, slot=slot):
                if step == 0 and turn == 0:
                    pltpu.make_async_copy(
                        self.chunk(place.group, place.core),
                        self.recv.at[place.group],
                        self.local.at[0],
                    ).wait()
                else:
                    send_copy(
                        self.chunk(place.group, place.core),
                        self.recv.at[group],
                        self.sz.at[slot],
                        self.rz.at[slot],
                        place.device(place.group, place.member, place.core),
                    ).wait_recv()

            if self.kind == "down":
                act()
            else:
                pl.when(lax.div(place.group, self.cores_per_group) == core)(act)

        @pl.loop(0, self.total.shape[0])
        def _(one):
            value = self.recv[0, one].astype(FLOAT)
            for other in range(1, place.groups):
                value = value + self.recv[other, one].astype(FLOAT)
            value = value if self.kind == "down" else value.T
            self.total[one] = value.astype(HALF_FLOAT)

    def final(self, step, pick_step):
        place = self.place
        steps, width = self.total.shape[0], self.gathered.shape[1]
        source = slab(self.total, 1, place.member_at(step), width)
        target = slab(self.gathered, 0, place.member_at(pick_step), steps)
        if step == 0:
            return pltpu.make_async_copy(source, target, self.local.at[1])
        return send_copy(
            source,
            target,
            self.sf.at[step],
            self.rf.at[step],
            place.device(place.group, place.member_at(step), place.core),
        )

    def start_final(self):
        for step in range(self.place.members):
            self.final(step, 0).start()

    def finish(self):
        place = self.place
        self.final(0, 0).wait()
        for step in range(1, place.members):
            self.final(step, -step).wait_recv()
        self.out[...] = self.gathered[...].astype(FLOAT)
        for step in range(1, place.members):
            self.final(step, 0).wait_send()
        for step, turn in self.hops():
            if step or turn:
                self.partial(step, turn, lambda copy, local: copy.wait_send())


class MatrixSum:
    sems = 7

    @staticmethod
    def half_shape(place_sizes, kind, value):
        batches = place_sizes[2]
        shape = list(value.shape)
        if kind == "rows":
            shape[0] //= batches
        elif kind == "lanes":
            shape[-1] //= batches
        return tuple(shape)

    @staticmethod
    def piece_shape(place_sizes, kind, value):
        groups, members, batches = place_sizes
        shape = list(MatrixSum.half_shape(place_sizes, kind, value))
        dim = {"rows": 1, "lanes": len(shape) - 2, "whole": 0}[kind]
        shape[dim] //= groups * members
        return tuple(shape)

    @staticmethod
    def scratch(place_sizes, kind, value):
        groups, members, batches = place_sizes
        half = MatrixSum.half_shape(place_sizes, kind, value)
        piece = MatrixSum.piece_shape(place_sizes, kind, value)
        dma = pltpu.SemaphoreType.DMA
        return [
            pltpu.VMEM(half, value.dtype),
            pltpu.VMEM((batches,) + half, value.dtype),
            pltpu.VMEM((members, groups) + piece, value.dtype),
            pltpu.VMEM((groups,) + piece, value.dtype),
            pltpu.VMEM((groups,) + piece, value.dtype),
            dma((batches,)),
            dma((batches,)),
            dma((members * groups,)),
            dma((members * groups,)),
            dma((groups,)),
            dma((groups,)),
            dma((1 + groups,)),
        ]

    def __init__(self, place, kind, source, out, scratch):
        self.place, self.kind, self.source, self.out = place, kind, source, out
        (self.own, self.others, self.by_member, self.sums, self.by_group) = scratch[:5]
        (self.sb, self.rb, self.sm, self.rm, self.sg, self.rg, self.local) = scratch[5:]
        self.piece_dim = {"rows": 1, "lanes": len(self.own.shape) - 2, "whole": 0}[kind]

    def half(self, core):
        if self.kind == "rows":
            return slab(self.source, 0, core, self.own.shape[0])
        if self.kind == "lanes":
            return slab(self.source, len(self.own.shape) - 1, core, self.own.shape[-1])
        return self.source

    def cores(self, step, pick):
        place = self.place
        core = place.core_at(step)
        return send_copy(
            self.half(core),
            self.others.at[pick],
            self.sb.at[step],
            self.rb.at[step],
            place.device(place.group, place.member, core),
        )

    def load(self):
        return pltpu.make_async_copy(self.half(self.place.core), self.own, self.local.at[0])

    def start(self):
        self.load().start()
        for step in range(1, self.place.batches):
            self.cores(step, self.place.core).start()

    def piece(self, group, member):
        size = self.by_member.shape[2 + self.piece_dim]
        return slab(self.own, self.piece_dim, group * self.place.members + member, size)

    def members(self, step, pick_step, group):
        place = self.place
        member = place.member_at(step)
        slot = step * place.groups + group
        target = self.by_member.at[place.member_at(pick_step), group]
        if step == 0:
            return pltpu.make_async_copy(
                self.piece(group, member), target, self.local.at[1 + group]
            )
        return send_copy(
            self.piece(group, member),
            target,
            self.sm.at[slot],
            self.rm.at[slot],
            place.device(place.group, member, place.core),
        )

    def add_cores(self):
        place = self.place
        self.load().wait()
        for step in range(1, place.batches):
            self.cores(step, place.core_at(-step)).wait_recv()
        rows = self.own.shape[0]
        block = max(size for size in (1, 2, 4, 8, 16, 32, 64) if rows % size == 0)

        @pl.loop(0, rows // block)
        def _(index):
            pick = pl.ds(pl.multiple_of(index * block, block), block)
            value = self.own[pick].astype(FLOAT)
            for step in range(1, place.batches):
                value = value + self.others[place.core_at(step), pick].astype(FLOAT)
            self.own[pick] = value.astype(self.own.dtype)

        for step in range(place.members):
            for group in range(place.groups):
                self.members(step, 0, group).start()

    def groups(self, step, pick_step):
        place = self.place
        group = place.group_at(step)
        return send_copy(
            self.sums.at[group],
            self.by_group.at[place.group_at(pick_step)],
            self.sg.at[step],
            self.rg.at[step],
            place.device(group, place.member, place.core),
        )

    def add_members(self):
        place = self.place
        for step in range(place.members):
            for group in range(place.groups):
                if step == 0:
                    self.members(step, 0, group).wait()
                else:
                    self.members(step, -step, group).wait_recv()

        @pl.loop(0, place.groups)
        def _(group):
            value = self.by_member[0, group].astype(FLOAT)
            for other in range(1, place.members):
                value = value + self.by_member[other, group].astype(FLOAT)
            self.sums[group] = value.astype(self.sums.dtype)

        for step in range(1, place.groups):
            self.groups(step, 0).start()
        self.by_group[place.group] = self.sums[place.group]

    def finish(self):
        place = self.place
        for step in range(1, place.groups):
            self.groups(step, -step).wait_recv()
        value = self.by_group[0].astype(FLOAT)
        for other in range(1, place.groups):
            value = value + self.by_group[other].astype(FLOAT)
        self.out[...] = value
        for step in range(1, place.groups):
            self.groups(step, 0).wait_send()
        for step in range(1, place.members):
            for group in range(place.groups):
                self.members(step, 0, group).wait_send()
        for step in range(1, place.batches):
            self.cores(step, place.core).wait_send()


def remote_call(body, inputs, outputs, scratch, collective_id, flops, nbytes, name):
    def kernel(*refs):
        left = list(refs)
        named = {key: left.pop(0) for key in inputs}
        named.update({key: left.pop(0) for key in outputs})
        for key, shapes in scratch.items():
            named[key] = [left.pop(0) for _ in shapes]
        body(named)

    results = pl.pallas_call(
        kernel,
        out_shape=tuple(shape for shape, _ in outputs.values()),
        in_specs=[spec for _, spec in inputs.values()],
        out_specs=tuple(spec for _, spec in outputs.values()),
        scratch_shapes=[shape for shapes in scratch.values() for shape in shapes],
        compiler_params=pltpu.CompilerParams(
            collective_id=collective_id,
            has_side_effects=True,
            vmem_limit_bytes=63 * 1024 * 1024,
        ),
        cost_estimate=pl.CostEstimate(flops=flops, bytes_accessed=nbytes, transcendentals=0),
        name=name,
    )(*[value for value, _ in inputs.values()])
    return dict(zip(outputs, results))


def plane_sizes(channels):
    devices, batches = lax.axis_size("tm"), lax.axis_size("batch")
    groups = channels // 128
    if batches == 2 and channels % 256 == 0 and devices % groups == 0:
        return groups, devices // groups, batches
    return None


VMEM_SPEC = pl.BlockSpec(memory_space=pltpu.VMEM)
HBM_SPEC = pl.BlockSpec(memory_space=pl.ANY)


class SeriesGradient:
    @staticmethod
    def scratch(weights, outers, rim):
        steps, series, channels = outers[0].shape
        lead = 2 * rim + 8
        dma = pltpu.SemaphoreType.DMA
        rims = (rim, series, channels)
        return (
            [pltpu.VMEM(weight.shape, HALF_FLOAT) for weight in weights]
            + [pltpu.VMEM((steps + 2 * lead, series, channels), FLOAT) for _ in outers]
            + [pltpu.VMEM((channels // 128, steps * series, 128), FLOAT)]
            + [pltpu.VMEM(rims, FLOAT) for _ in range(4)]
            + [dma((4,)), dma((2,)), dma((2,))]
        )

    def __init__(self, weights, outers, out, scratch, halves, rim):
        self.weights, self.outers, self.out = weights, outers, out
        self.halves, self.rim = halves, rim
        count = len(weights)
        self.held, self.grads = scratch[:count], scratch[count : 2 * count]
        (self.result, self.low, self.high, self.before, self.after) = scratch[
            2 * count : 2 * count + 5
        ]
        (self.local, self.send, self.recv) = scratch[2 * count + 5 :]
        self.steps = outers[0].shape[0]
        self.series = outers[0].shape[1]
        self.lead = 2 * rim + 8
        self.me, self.core = lax.axis_index("tm"), lax.axis_index("batch")
        self.last = lax.axis_size("tm") - 1

    def greet(self, barrier):
        @pl.when(self.me > 0)
        def _():
            pl.semaphore_signal(
                barrier, inc=1, device_id=(self.core, self.me - 1), device_id_type=MESH
            )

        @pl.when(self.me < self.last)
        def _():
            pl.semaphore_signal(
                barrier, inc=1, device_id=(self.core, self.me + 1), device_id_type=MESH
            )

        return jnp.where(self.me > 0, 1, 0) + jnp.where(self.me < self.last, 1, 0)

    def loads(self, index):
        return (
            pltpu.make_async_copy(
                self.weights[index], self.held[index], self.local.at[2 * index]
            ),
            pltpu.make_async_copy(
                self.outers[index],
                self.grads[index].at[pl.ds(self.lead, self.steps)],
                self.local.at[2 * index + 1],
            ),
        )

    def start(self):
        for index in range(len(self.held)):
            for copy in self.loads(index):
                copy.start()
            grads = self.grads[index]
            zero = jnp.zeros((self.lead,) + grads.shape[1:], FLOAT)
            grads[: self.lead] = zero
            grads[self.lead + self.steps :] = zero

    def through_down(self, index, grad):
        for copy in self.loads(index):
            copy.wait()
        kernel = self.held[index].shape[0]
        pieces = self.steps // kernel
        grads = self.grads[index]

        @pl.loop(0, kernel)
        def _(one):
            value = dot_nt(grad, self.held[index][one])
            for piece in range(pieces):
                row = self.lead + piece * kernel + one
                grads[row] = (
                    grads[row] + value[piece * self.series : (piece + 1) * self.series]
                )

    def store(self, place, value, add=False):
        for lane in range(self.result.shape[0]):
            part = value[:, lane * 128 : lane * 128 + 128]
            self.result[lane, place] = self.result[lane, place] - part if add else part

    def adjoint(self):
        def means(index, sums):
            out, total = [], 0.0
            for grads, half, value in zip(self.grads, self.halves, sums):
                high = grads[index + (self.lead - self.rim + half)]
                low = grads[index + (self.lead - self.rim - half - 1)]
                value = value + high - low
                out.append(value)
                total = total + value * (1.0 / (2 * half + 1))
            return tuple(out), total

        def low_step(index, sums):
            sums, total = means(index, sums)
            self.low[index] = total
            return sums

        def step(index, sums):
            sums, total = means(index + self.rim, sums)
            value = self.grads[0][self.lead + index] + self.grads[1][self.lead + index]
            place = pl.ds(pl.multiple_of(index * self.series, self.series), self.series)
            self.store(place, value - total)
            return sums

        def high_step(index, sums):
            sums, total = means(index + (self.rim + self.steps), sums)
            self.high[index] = total
            return sums

        zero = jnp.zeros(self.low.shape[1:], FLOAT)
        sums = lax.fori_loop(0, self.rim, low_step, (zero, zero))
        sums = lax.fori_loop(0, self.steps, step, sums)
        lax.fori_loop(0, self.rim, high_step, sums)

    def edge(self, up):
        source, target = (self.high, self.before) if up else (self.low, self.after)
        index = 0 if up else 1
        return send_copy(
            source,
            target,
            self.send.at[index],
            self.recv.at[index],
            (self.core, self.me + 1 if up else self.me - 1),
        )

    def send_edges(self):
        pl.when(self.me < self.last)(lambda: self.edge(True).start())
        pl.when(self.me > 0)(lambda: self.edge(False).start())

    def finish(self):
        series = self.series
        rows, end = self.rim * series, self.steps * series

        @pl.when(self.me > 0)
        def _():
            self.edge(True).wait_recv()
            self.store(pl.ds(0, rows), self.before[...].reshape(rows, -1), True)

        @pl.when(self.me == 0)
        def _():
            total = self.low[0]
            for index in range(1, self.rim):
                total = total + self.low[index]
            self.store(pl.ds(0, series), total, True)

        @pl.when(self.me < self.last)
        def _():
            self.edge(False).wait_recv()
            self.store(pl.ds(end - rows, rows), self.after[...].reshape(rows, -1), True)

        @pl.when(self.me == self.last)
        def _():
            total = self.high[0]
            for index in range(1, self.rim):
                total = total + self.high[index]
            self.store(pl.ds(end - series, series), total, True)

        for one in range(self.out.shape[0]):
            for lane in range(self.result.shape[0]):
                value = self.result[lane, pl.ds(one, self.steps, stride=series), :]
                self.out[one, :, lane * 128 : lane * 128 + 128] = value.astype(HALF_FLOAT)
        pl.when(self.me < self.last)(lambda: self.edge(True).wait_send())
        pl.when(self.me > 0)(lambda: self.edge(False).wait_send())


def down_gradients(sizes, wides, narrows, vectors, weights, outers, halves, rim, count, matrices):
    groups, members, batches = sizes
    half = wides[0].shape[4]
    channels = half * batches
    inputs, outputs, scratch = {}, {}, {}
    for index, (wide, narrow) in enumerate(zip(wides, narrows)):
        steps = wide.shape[0] * members
        shape = jax.ShapeDtypeStruct(
            (wide.shape[2], steps, wide.shape[3], channels), HALF_FLOAT
        )
        inputs[f"wide{index}"] = (wide, VMEM_SPEC)
        inputs[f"narrow{index}"] = (narrow, HBM_SPEC)
        outputs[f"out{index}"] = (
            jax.ShapeDtypeStruct((steps, channels // (groups * members), half), FLOAT),
            VMEM_SPEC,
        )
        scratch[f"rows{index}"] = [
            pltpu.VMEM((members * batches,) + narrow.shape, HALF_FLOAT)
        ]
        scratch[f"gather{index}"] = NarrowGather.scratch(sizes, narrow)
        scratch[f"product{index}"] = KernelProduct.scratch(sizes, "down", shape, narrow)
    for index in range(len(wides)):
        inputs[f"weight{index}"] = (weights[index], HBM_SPEC)
        inputs[f"outer{index}"] = (outers[index], HBM_SPEC)
    scratch["series"] = SeriesGradient.scratch(weights, outers, rim)
    outputs["grad_series"] = (
        jax.ShapeDtypeStruct((count, outers[0].shape[0], channels), HALF_FLOAT),
        VMEM_SPEC,
    )
    for index, (kind, value) in enumerate(matrices):
        inputs[f"matrix{index}"] = (value, HBM_SPEC)
        outputs[f"matrix_sum{index}"] = (
            jax.ShapeDtypeStruct(MatrixSum.piece_shape(sizes, kind, value), FLOAT),
            VMEM_SPEC,
        )
        scratch[f"parts{index}"] = MatrixSum.scratch(sizes, kind, value)
    inputs["vectors"] = (vectors, VMEM_SPEC)
    outputs["vector_sum"] = (jax.ShapeDtypeStruct(vectors.shape, FLOAT), VMEM_SPEC)
    scratch["vector"] = VectorSum.scratch(sizes, vectors)

    def body(refs):
        place = Place(*sizes)
        back = SeriesGradient(
            [refs[f"weight{index}"] for index in range(len(wides))],
            [refs[f"outer{index}"] for index in range(len(wides))],
            refs["grad_series"],
            refs["series"],
            halves,
            rim,
        )
        barrier = pltpu.get_barrier_semaphore()
        pl.semaphore_wait(barrier, place.greet(barrier) + back.greet(barrier))
        gathers, products = [], []
        for index in range(len(wides)):
            gathers.append(
                NarrowGather(
                    place,
                    refs[f"narrow{index}"],
                    refs[f"rows{index}"][0],
                    refs[f"gather{index}"],
                )
            )
            products.append(
                KernelProduct(
                    place,
                    "down",
                    refs[f"wide{index}"],
                    refs[f"rows{index}"][0],
                    refs[f"out{index}"],
                    refs[f"product{index}"],
                )
            )
        total = VectorSum(place, refs["vectors"], refs["vector_sum"], refs["vector"])
        sums = [
            MatrixSum(
                place, kind, refs[f"matrix{i}"], refs[f"matrix_sum{i}"], refs[f"parts{i}"]
            )
            for i, (kind, _) in enumerate(matrices)
        ]
        order = list(range(len(wides)))[::-1]
        for index in order:
            gathers[index].start()
        for item in sums:
            item.start()
        total.start(0)
        back.start()
        for index in order:
            gathers[index].forward()
            gathers[index].wait()
            products[index].multiply()
            products[index].start_partials()
        for item in sums:
            item.add_cores()
        total.add(0)
        mine = place.core * members + place.member
        for index in range(len(wides)):
            back.through_down(index, refs[f"rows{index}"][0][mine])
        back.adjoint()
        back.send_edges()
        total.add(1)
        for item in sums:
            item.add_members()
        for index in order:
            products[index].sum_partials()
            products[index].start_final()
        total.add(2)
        back.finish()
        for item in sums:
            item.finish()
        for product in products:
            product.finish()
        for gather in gathers:
            gather.drain()
        total.drain()

    flops = sum(2 * wide.size * channels for wide in wides)
    results = remote_call(
        body, inputs, outputs, scratch, 2, flops, 8 * flops // channels, "down_gradients"
    )
    return (
        [results["out0"], results["out1"]],
        results["vector_sum"],
        results["grad_series"],
        [results[f"matrix_sum{index}"] for index in range(len(matrices))],
    )


def iso_gradient_kernel(lane_ref, spec_ref, specs_ref, grad_ref, grads_ref, out_ref):
    bins, _, half, channels = out_ref.shape
    rows = spec_ref.shape[0] // bins
    devices = rows // 2
    for one in range(bins):
        place = slice(one * rows, (one + 1) * rows)
        spec = [spec_ref[place]] + [specs_ref[i, place] for i in range(specs_ref.shape[0])]
        grad = [grad_ref[place]] + [grads_ref[i, place] for i in range(grads_ref.shape[0])]
        turned = [jnp.concatenate([value[devices:], -value[:devices]]) for value in grad]
        both = jnp.concatenate([jnp.concatenate(grad), jnp.concatenate(turned)], axis=1)
        value = lax.dot_general(
            jnp.concatenate(spec), both, (((0,), (0,)), ((), ())), preferred_element_type=FLOAT
        )
        out_ref[one, 0] = value[:, :channels]
        out_ref[one, 1] = value[:, channels:]


def iso_gradients(spec, specs, grad, grads, first, bins):
    rows, channels = 2 * lax.axis_size("tm"), grad.shape[1]
    half = channels // lax.axis_size("batch")
    others = specs.shape[0]
    block = 2 if bins % 2 == 0 and first % 2 == 0 else 1
    rows, first = rows * block, first // block
    core = lax.axis_index("batch")
    if half % 128:
        spec = lax.dynamic_slice_in_dim(spec, core * half, half, axis=1)
        specs = lax.dynamic_slice_in_dim(specs, core * half, half, axis=2)
        core = 0
    return pl.pallas_call(
        iso_gradient_kernel,
        out_shape=jax.ShapeDtypeStruct((bins, 2, half, channels), FLOAT),
        grid_spec=pltpu.PrefetchScalarGridSpec(
            num_scalar_prefetch=1,
            grid=(bins // block,),
            in_specs=[
                pl.BlockSpec((rows, half), lambda i, lane: (first + i, lane[0])),
                pl.BlockSpec((others, rows, half), lambda i, lane: (0, first + i, lane[0])),
                pl.BlockSpec((rows, channels), lambda i, lane: (first + i, 0)),
                pl.BlockSpec((others, rows, channels), lambda i, lane: (0, first + i, 0)),
            ],
            out_specs=pl.BlockSpec((block, 2, half, channels), lambda i, lane: (i, 0, 0, 0)),
        ),
        cost_estimate=pl.CostEstimate(
            flops=4 * (bins // block) * rows * (1 + others) * half * channels,
            bytes_accessed=8 * bins * half * channels,
            transcendentals=0,
        ),
        name="iso_gradients",
    )(jnp.full((1,), core, jnp.int32), spec, specs, grad, grads)


class RowProducts:
    @staticmethod
    def scratch(jobs):
        rows, channels = jobs[0][0].shape
        most = max(sum(right.shape[1] for right in rights) for _, rights in jobs)
        return [
            pltpu.VMEM((rows, channels), HALF_FLOAT),
            pltpu.VMEM((channels, rows), HALF_FLOAT),
            pltpu.VMEM((rows, most), HALF_FLOAT),
            pltpu.SemaphoreType.DMA((1 + max(len(rights) for _, rights in jobs),)),
        ]

    def __init__(self, jobs, scratch):
        self.jobs = jobs
        self.left, self.turned, self.right, self.sem = scratch
        self.next = 0

    def copies(self, index):
        left, rights, _ = self.jobs[index]
        copies = [pltpu.make_async_copy(left, self.left, self.sem.at[0])]
        for k, right in enumerate(rights):
            width = right.shape[1]
            target = self.right.at[:, pl.ds(k * width, width)]
            copies.append(pltpu.make_async_copy(right, target, self.sem.at[1 + k]))
        return copies

    def load(self):
        if self.next < len(self.jobs):
            for copy in self.copies(self.next):
                copy.start()

    def run(self):
        index, self.next = self.next, self.next + 1
        for copy in self.copies(index):
            copy.wait()
        self.turned[...] = self.left[...].T
        out = self.jobs[index][2]
        channels = self.left.shape[1]
        width = sum(right.shape[1] for right in self.jobs[index][1])
        for k in range(width // channels):
            chunk = pl.ds(k * channels, channels)
            value = dot_nn(self.turned[...], self.right[:, chunk]).astype(HALF_FLOAT)
            if len(out.shape) == 3:
                out[k] = value
            else:
                out[:, chunk] = value
        self.load()


class Extra:
    def __init__(self, sizes):
        self.sizes = sizes
        self.inputs, self.outputs, self.scratch = {}, {}, {}

    def bind(self, refs):
        self.refs = refs
        self.place = Place(*self.sizes) if self.sizes else None

    def greet(self, barrier):
        return self.place.greet(barrier) if self.sizes else 0

    def open(self):
        pass

    def prepare(self):
        return self.refs["x"]

    def start(self):
        pass

    def after_bins(self):
        pass

    def after_spec(self):
        pass

    def after_mixed(self):
        pass

    def after_signal(self):
        pass

    def finish(self):
        pass

    def run(self, share):
        count = max(1, round(share * self.unit_count))
        for _ in range(min(count, len(self.units))):
            self.units.pop(0)()


class Turn:
    block = 64

    @staticmethod
    def scratch(weight):
        channels, kernel, outs = weight.shape
        dma = pltpu.SemaphoreType.DMA
        return [
            pltpu.VMEM((2, Turn.block, kernel, outs), HALF_FLOAT),
            pltpu.VMEM((2, kernel, Turn.block, outs), HALF_FLOAT),
            dma((2,)),
            dma((2,)),
        ]

    def __init__(self, source, target, scratch):
        self.source, self.target = source, target
        self.read, self.turned, self.in_sem, self.out_sem = scratch
        self.total = source.shape[0] // self.block
        self.done = 0

    def load(self, index, slot):
        place = pl.ds(pl.multiple_of(index * self.block, self.block), self.block)
        return pltpu.make_async_copy(
            self.source.at[place], self.read.at[slot], self.in_sem.at[slot]
        )

    def store(self, index, slot):
        place = pl.ds(pl.multiple_of(index * self.block, self.block), self.block)
        return pltpu.make_async_copy(
            self.turned.at[slot], self.target.at[:, place], self.out_sem.at[slot]
        )

    def start(self):
        self.load(0, 0).start()

    def run(self, share):
        first, self.done = self.done, min(self.total, self.done + math.ceil(share * self.total))

        @pl.loop(first, self.done)
        def _(index):
            slot = lax.rem(index, 2)
            self.load(index, slot).wait()

            @pl.when(index + 1 < self.total)
            def _():
                self.load(index + 1, 1 - slot).start()

            @pl.when(index >= 2)
            def _():
                self.store(index - 2, slot).wait()

            self.turned[slot] = pltpu.einshape("mhd->hmd", self.read[slot])
            self.store(index, slot).start()

    def finish(self):
        self.run(1.0)
        for index in range(max(0, self.total - 2), self.total):
            self.store(index, index % 2).wait()


def by_piece(signal, rows, count):
    per_time = signal.shape[0] // count
    width = rows.shape[1] // per_time
    for lane in range(rows.shape[0]):
        value = signal[:, lane * 128 : lane * 128 + 128]
        rows[lane, : signal.shape[0], :] = value.astype(FLOAT)
        if width > count:
            rows[lane, signal.shape[0] :, :] = jnp.zeros(
                (rows.shape[1] - signal.shape[0], 128), FLOAT
            )

    def piece(index):
        return jnp.concatenate(
            [rows[lane, pl.ds(index, width, stride=per_time), :] for lane in range(rows.shape[0])],
            axis=1,
        )

    return lambda first, size: jnp.concatenate([piece(first + i) for i in range(size)])


class Front:
    halo = 16

    @staticmethod
    def scratch(series, weights, per_time, rim):
        count, steps, channels = series.shape
        wide, lanes = round_up(count, 16), channels // 128
        rows = max(steps // weight.shape[0] for weight in weights) * wide
        dma = pltpu.SemaphoreType.DMA
        return (
            [pltpu.VMEM(weight.shape, HALF_FLOAT) for weight in weights]
            + [
                pltpu.VMEM(series.shape, HALF_FLOAT),
                pltpu.VMEM((count, Front.halo, channels), HALF_FLOAT),
                pltpu.VMEM((count, Front.halo, channels), HALF_FLOAT),
                pltpu.VMEM((lanes, (steps + 2 * rim + 1) * wide, 128), FLOAT),
                pltpu.VMEM((lanes, per_time * wide, 128), FLOAT),
                pltpu.VMEM((rows, channels), FLOAT),
                pltpu.VMEM((count * per_time, channels), HALF_FLOAT),
            ]
            + [dma((1 + len(weights),)), dma((2,)), dma((2,))]
        )

    def __init__(self, source, weights, bias, seasonals, acts, scratch, halves, rim):
        self.source, self.weights, self.bias = source, weights, bias
        self.seasonals, self.acts, self.halves, self.rim = seasonals, acts, halves, rim
        self.held = scratch[: len(weights)]
        (self.series, self.before, self.after, self.wide, self.rows, self.total, self.x) = (
            scratch[len(weights) : len(weights) + 7]
        )
        (self.local, self.send, self.recv) = scratch[len(weights) + 7 :]
        self.count, self.steps, _ = source.shape
        self.width = seasonals[0].shape[2]
        self.me, self.core = lax.axis_index("tm"), lax.axis_index("batch")
        self.last = lax.axis_size("tm") - 1

    def loads(self):
        return [pltpu.make_async_copy(self.source, self.series, self.local.at[0])] + [
            pltpu.make_async_copy(weight, held, self.local.at[1 + index])
            for index, (weight, held) in enumerate(zip(self.weights, self.held))
        ]

    def edge(self, up):
        first = self.steps - self.halo if up else 0
        index = 0 if up else 1
        return send_copy(
            self.source.at[:, pl.ds(first, self.halo)],
            self.before if up else self.after,
            self.send.at[index],
            self.recv.at[index],
            (self.core, self.me + 1 if up else self.me - 1),
        )

    def start(self):
        pl.when(self.me < self.last)(lambda: self.edge(True).start())
        pl.when(self.me > 0)(lambda: self.edge(False).start())
        for copy in self.loads():
            copy.start()

    def spread(self, values, first, count):
        for lane in range(self.wide.shape[0]):
            self.wide[lane, pl.ds(first, count, stride=self.width), :] = values[
                :, lane * 128 : lane * 128 + 128
            ]

    def step(self, index):
        place = pl.ds(pl.multiple_of(index * self.width, self.width), self.width)
        return jnp.concatenate(
            [self.wide[lane, place, :] for lane in range(self.wide.shape[0])], axis=1
        )

    def repeat(self, index, first):
        value = self.step(index)
        for row in range(self.rim):
            place = pl.ds((first + row) * self.width, self.width)
            for lane in range(self.wide.shape[0]):
                self.wide[lane, place, :] = value[:, lane * 128 : lane * 128 + 128]

    def layers(self, ready):
        rim, steps, width = self.rim, self.steps, self.width
        self.wide[...] = jnp.zeros_like(self.wide)
        copies = self.loads()
        copies[0].wait()
        for one in range(self.count):
            self.spread(self.series[one].astype(FLOAT), rim * width + one, steps)

        @pl.when(self.me > 0)
        def _():
            self.edge(True).wait_recv()
            for one in range(self.count):
                self.spread(self.before[one].astype(FLOAT)[self.halo - rim :], one, rim)

        @pl.when(self.me < self.last)
        def _():
            self.edge(False).wait_recv()
            for one in range(self.count):
                first = (rim + steps) * width + one
                self.spread(self.after[one].astype(FLOAT)[:rim], first, rim)

        pl.when(self.me == 0)(lambda: self.repeat(rim, 0))
        pl.when(self.me == self.last)(lambda: self.repeat(rim + steps - 1, rim + steps))
        sums = []
        for half in self.halves:
            value = self.step(rim - half)
            for index in range(rim - half + 1, rim + half + 1):
                value = value + self.step(index)
            sums.append(value)

        def move(index, sums):
            here, later = self.step(index + rim), []
            for seasonal, half, value in zip(self.seasonals, self.halves, sums):
                kernel = seasonal.shape[1]
                part = here - value * (1.0 / (2 * half + 1))
                seasonal[lax.div(index, kernel), lax.rem(index, kernel)] = part.astype(
                    HALF_FLOAT
                )
                later.append(
                    value + self.step(index + rim + half + 1) - self.step(index + rim - half)
                )
            return tuple(later)

        lax.fori_loop(0, steps, move, tuple(sums))
        ready()
        self.rows[...] = jnp.zeros_like(self.rows)
        base = 0
        for index, (seasonal, held, act) in enumerate(zip(self.seasonals, self.held, self.acts)):
            copies[1 + index].wait()
            count = act.shape[0]
            total = self.total.at[pl.ds(0, count)]
            total[...] = jnp.broadcast_to(self.bias[index : index + 1], total.shape)

            @pl.loop(0, seasonal.shape[1])
            def _(one, total=total, seasonal=seasonal, held=held):
                total[...] += dot_nn(seasonal[:, one].reshape(total.shape), held[one])

            value = jnp.tanh(total[...])
            act[...] = value
            value = value.astype(HALF_FLOAT).astype(FLOAT)
            for lane in range(self.rows.shape[0]):
                self.rows[lane, pl.ds(base * width, count), :] = value[
                    :, lane * 128 : lane * 128 + 128
                ]
            base += round_up(count // width, 8)
        per_time = self.x.shape[0] // self.count
        for one in range(self.count):
            for lane in range(self.rows.shape[0]):
                value = self.rows[lane, pl.ds(one, per_time, stride=width), :]
                self.x[
                    one * per_time : (one + 1) * per_time, lane * 128 : lane * 128 + 128
                ] = value.astype(HALF_FLOAT)

    def finish(self):
        pl.when(self.me < self.last)(lambda: self.edge(True).wait_send())
        pl.when(self.me > 0)(lambda: self.edge(False).wait_send())

    def turn(self, source):
        return pltpu.make_async_copy(source, self.series, self.local.at[0])

    def turned(self, source, target):
        self.turn(source).wait()
        for one in range(self.count):
            self.spread(self.series[one].astype(FLOAT), self.rim * self.width + one, self.steps)

        @pl.loop(0, self.steps)
        def _(index):
            target[index] = self.step(index + self.rim).astype(HALF_FLOAT)


class ForwardExtra(Extra):
    def __init__(self, sizes, wides, weights, front):
        super().__init__(sizes)
        self.front = front
        if front:
            series, cotangent, down_weights, bias, per_time, halves, rim = front
            count, steps, channels = series.shape
            series_rows = round_up(count, 16)
            self.inputs["series"] = (series, HBM_SPEC)
            self.inputs["down_bias"] = (bias, VMEM_SPEC)
            for index, weight in enumerate(down_weights):
                kernel = weight.shape[0]
                self.inputs[f"down{index}"] = (weight, HBM_SPEC)
                self.outputs[f"seasonal{index}"] = (
                    jax.ShapeDtypeStruct(
                        (steps // kernel, kernel, series_rows, channels), HALF_FLOAT
                    ),
                    VMEM_SPEC,
                )
                self.outputs[f"down_act{index}"] = (
                    jax.ShapeDtypeStruct((steps // kernel * series_rows, channels), FLOAT),
                    VMEM_SPEC,
                )
                rows = self.outputs[f"down_act{index}"][0].shape
                self.outputs[f"iso_act{index}"] = (
                    jax.ShapeDtypeStruct(rows, FLOAT),
                    VMEM_SPEC,
                )
                self.outputs[f"inner{index}"] = (
                    jax.ShapeDtypeStruct(rows, HALF_FLOAT),
                    VMEM_SPEC,
                )
            self.inputs["cotangent"] = (cotangent, HBM_SPEC)
            self.outputs["cotangent_steps"] = (
                jax.ShapeDtypeStruct((steps, series_rows, channels), HALF_FLOAT),
                VMEM_SPEC,
            )
            self.scratch["front"] = Front.scratch(series, down_weights, per_time, rim)
            wides = [self.outputs[f"seasonal{index}"][0] for index in range(len(down_weights))]
        self.turn_count = len(weights)
        for index, weight in enumerate(weights):
            channels, kernel, outs = weight.shape
            self.inputs[f"turn{index}"] = (weight, HBM_SPEC)
            self.outputs[f"turned{index}"] = (
                jax.ShapeDtypeStruct((kernel, channels, outs), HALF_FLOAT),
                HBM_SPEC,
            )
            self.scratch[f"turning{index}"] = Turn.scratch(weight)
        self.count = len(wides) if sizes else 0
        for index in range(self.count):
            if not front:
                self.inputs[f"wide{index}"] = (wides[index], HBM_SPEC)
            self.outputs[f"gathered{index}"] = (
                jax.ShapeDtypeStruct(WideExchange.shape(sizes, wides[index]), HALF_FLOAT),
                HBM_SPEC,
            )
            self.scratch[f"exchange{index}"] = WideExchange.scratch(sizes, wides[index])

    def bind(self, refs):
        super().bind(refs)
        self.exchanges = [
            WideExchange(
                self.place,
                refs[f"seasonal{i}" if self.front else f"wide{i}"],
                refs[f"gathered{i}"],
                refs[f"exchange{i}"],
            )
            for i in range(self.count)
        ]
        self.units = [unit for item in self.exchanges for unit in item.units()]
        self.unit_count = len(self.units)
        self.turns = [
            Turn(refs[f"turn{i}"], refs[f"turned{i}"], refs[f"turning{i}"])
            for i in range(self.turn_count)
        ]

    def inner(self):
        refs, base = self.refs, 0
        count = self.front[0].shape[0]
        rows = by_piece(refs["signal"], self.layers.rows, count)
        table = refs["down_bias"]
        for index in range(self.count):
            act_ref = refs[f"iso_act{index}"]
            pieces = act_ref.shape[0] // self.layers.width
            act = jnp.tanh(rows(base, pieces) + table[2 + index : 3 + index])
            down = refs[f"down_act{index}"][...].astype(HALF_FLOAT).astype(FLOAT)
            hat, _ = normed(act + down)
            act_ref[...] = act
            out = hat * table[8:9] + table[11:12]
            refs[f"inner{index}"][...] = out.astype(HALF_FLOAT)
            base += round_up(pieces, 8)

    def open(self):
        for item in self.turns:
            item.start()
        if not self.front:
            return
        refs, count = self.refs, self.count
        halves, rim = self.front[5:]
        self.layers = Front(
            refs["series"],
            [refs[f"down{i}"] for i in range(count)],
            refs["down_bias"],
            [refs[f"seasonal{i}"] for i in range(count)],
            [refs[f"down_act{i}"] for i in range(count)],
            refs["front"],
            halves,
            rim,
        )
        self.layers.start()

    def prepare(self):
        if not self.front:
            return super().prepare()
        self.layers.layers(functools.partial(self.run, 0.45))
        return self.layers.x

    def start(self):
        self.run(0.15)
        if self.front:
            self.layers.turn(self.refs["cotangent"]).start()
        for item in self.turns:
            item.run(0.25)

    def after_bins(self):
        self.run(0.55)
        if self.front:
            self.layers.turned(self.refs["cotangent"], self.refs["cotangent_steps"])
        for item in self.turns:
            item.run(0.25)

    def after_mixed(self):
        self.run(1.0)
        for item in self.turns:
            item.run(0.375)

    def after_signal(self):
        for item in self.turns:
            item.run(0.125)

    def finish(self):
        if self.front:
            self.inner()
            self.layers.finish()
        for item in self.turns:
            item.finish()
        for item in self.exchanges:
            item.wait()
            item.drain()


class BackwardExtra(Extra):
    def __init__(self, sizes, spec, wides, narrows, jobs, inners, acts, counts):
        super().__init__(sizes)
        self.counts = counts
        if sizes:
            for i, (inner, act) in enumerate(zip(inners, acts)):
                self.inputs[f"inner_grad{i}"] = (inner, VMEM_SPEC)
                self.inputs[f"act{i}"] = (act, VMEM_SPEC)
                self.outputs[f"down_grad{i}"] = (
                    jax.ShapeDtypeStruct(act.shape, HALF_FLOAT),
                    VMEM_SPEC,
                )
            channels = spec.shape[1]
            self.outputs["down_sums"] = (jax.ShapeDtypeStruct((8, channels), FLOAT), VMEM_SPEC)
            per_time, width = counts[1:]
            self.scratch["piece_rows"] = [
                pltpu.VMEM((channels // 128, per_time * width, 128), FLOAT)
            ]
        self.batches = lax.axis_size("batch")
        others = jax.ShapeDtypeStruct((self.batches - 1,) + spec.shape, HALF_FLOAT)
        self.inputs["spec_forward"] = (spec, HBM_SPEC)
        self.outputs["specs"] = (others, HBM_SPEC)
        self.outputs["grads"] = (others, HBM_SPEC)
        dma = pltpu.SemaphoreType.DMA
        self.scratch["other_sems"] = [dma((self.batches,))] * 4
        self.count = len(wides) if sizes else 0
        self.job_sizes = [len(rights) for _, rights, _ in jobs] if sizes else []
        if sizes:
            for i, (left, rights, shape) in enumerate(jobs):
                self.inputs[f"left{i}"] = (left, HBM_SPEC)
                for k, right in enumerate(rights):
                    self.inputs[f"right{i}_{k}"] = (right, HBM_SPEC)
                self.outputs[f"matrix{i}"] = (
                    jax.ShapeDtypeStruct(shape, HALF_FLOAT),
                    VMEM_SPEC,
                )
            self.scratch["row_products"] = RowProducts.scratch(
                [(left, rights) for left, rights, _ in jobs]
            )
        for i in range(self.count):
            wide, narrow = wides[i], narrows[i]
            groups, members, batches = sizes
            channels = narrow.shape[1]
            self.inputs[f"wide{i}"] = (wide, HBM_SPEC)
            self.inputs[f"narrow{i}"] = (narrow, HBM_SPEC)
            self.outputs[f"up{i}"] = (
                jax.ShapeDtypeStruct(
                    (wide.shape[1], channels // (groups * members), channels // batches), FLOAT
                ),
                VMEM_SPEC,
            )
            self.scratch[f"wide_in{i}"] = [
                pltpu.VMEM(WideExchange.shape(sizes, wide), HALF_FLOAT)
            ]
            self.scratch[f"rows{i}"] = [
                pltpu.VMEM((members * batches,) + narrow.shape, HALF_FLOAT)
            ]
            self.scratch[f"exchange{i}"] = WideExchange.scratch(sizes, wide)
            self.scratch[f"gather{i}"] = NarrowGather.scratch(sizes, narrow)
            self.scratch[f"product{i}"] = KernelProduct.scratch(sizes, "up", wide, narrow)

    def bind(self, refs):
        super().bind(refs)
        self.exchanges, self.gathers, self.products = [], [], []
        for i in range(self.count):
            wide_in, rows = refs[f"wide_in{i}"][0], refs[f"rows{i}"][0]
            self.exchanges.append(
                WideExchange(self.place, refs[f"wide{i}"], wide_in, refs[f"exchange{i}"])
            )
            self.gathers.append(
                NarrowGather(self.place, refs[f"narrow{i}"], rows, refs[f"gather{i}"])
            )
            self.products.append(
                KernelProduct(self.place, "up", wide_in, rows, refs[f"up{i}"], refs[f"product{i}"])
            )
        jobs = [
            (
                refs[f"left{i}"],
                [refs[f"right{i}_{k}"] for k in range(size)],
                refs[f"matrix{i}"],
            )
            for i, size in enumerate(self.job_sizes)
        ]
        self.row_products = RowProducts(jobs, refs["row_products"]) if jobs else None

    def other(self, index, turn):
        source, target = (
            (self.refs["spec_forward"], self.refs["specs"]),
            (self.refs["spec"], self.refs["grads"]),
        )[index]
        sems = self.refs["other_sems"]
        core = lax.rem(lax.axis_index("batch") + turn, self.batches)
        return send_copy(
            source,
            target.at[turn - 1],
            sems[2 * index].at[turn],
            sems[2 * index + 1].at[turn],
            (core, lax.axis_index("tm")),
        )

    def start(self):
        self.units = [unit for item in self.exchanges[::-1] for unit in item.units()]
        self.unit_count = len(self.units)
        for turn in range(1, self.batches):
            self.other(0, turn).start()
        for item in self.gathers:
            item.start()
        if self.row_products:
            self.row_products.load()

    def after_bins(self):
        self.run(0.6)
        for item in self.gathers:
            item.forward()
        if self.row_products:
            self.row_products.run()

    def after_mixed(self):
        self.run(1.0)

    def after_spec(self):
        for turn in range(1, self.batches):
            self.other(1, turn).start()

    def multiply(self, index):
        self.exchanges[index].wait()
        self.gathers[index].wait()
        self.products[index].multiply()
        self.products[index].start_partials()

    def after_signal(self):
        for index in range(self.count)[::-1]:
            self.multiply(index)

    def down_grads(self):
        refs, base = self.refs, 0
        count, _, width = self.counts
        rows = by_piece(refs["signal"], refs["piece_rows"][0], count)
        refs["down_sums"][...] = jnp.zeros_like(refs["down_sums"])
        for index in range(self.count):
            act = refs[f"act{index}"][...]
            pieces = act.shape[0] // width
            grad = rows(base, pieces) + refs[f"inner_grad{index}"][...]
            grad = (grad * (1.0 - act * act)).astype(HALF_FLOAT)
            refs[f"down_grad{index}"][...] = grad
            refs["down_sums"][index : index + 1] = jnp.sum(
                grad.astype(FLOAT), axis=0, keepdims=True
            )
            base += round_up(pieces, 8)

    def finish(self):
        if self.count:
            self.down_grads()
            for _ in range(1, len(self.job_sizes)):
                self.row_products.run()
        for item in self.products[::-1]:
            item.sum_partials()
            item.start_final()
        for item in self.products:
            item.finish()
        for item in self.exchanges + self.gathers:
            item.drain()
        for index in range(2):
            for turn in range(1, self.batches):
                self.other(index, turn).wait()


def spectral(values, shapes, weights, back, extra):
    devices, batches = lax.axis_size("tm"), lax.axis_size("batch")
    pieces_list = tuple(shape[1] for shape in shapes)
    count, _, channels = shapes[0]
    wide = [round_up(pieces, 8) for pieces in pieces_list]
    per_time, per_bin = sum(wide), 2 * sum(wide)
    assert count <= devices and per_time % 16 == 0
    inputs = {}
    if values:
        packed = jnp.concatenate(
            [
                jnp.pad(value, ((0, 0), (0, room - value.shape[1]), (0, 0)))
                for value, room in zip(values, wide)
            ],
            axis=1,
        ).reshape(count * per_time, channels)
        inputs["x"] = (packed, HBM_SPEC)
    table = spectral_constants(devices, pieces_list)
    rows_time, rows_bin = devices * per_time, devices * per_bin
    dma = pltpu.SemaphoreType.DMA
    for index, weight in enumerate(weights):
        inputs[f"weight{index}"] = (weight, HBM_SPEC)
    inputs["table"] = (table, VMEM_SPEC)
    outputs = {
        "spec": (jax.ShapeDtypeStruct((rows_bin, channels), HALF_FLOAT), VMEM_SPEC),
        "signal": (jax.ShapeDtypeStruct((count * per_time, channels), HALF_FLOAT), VMEM_SPEC),
    }
    scratch = {
        "buffers": [pltpu.VMEM((rows_time, channels), HALF_FLOAT)]
        + [pltpu.VMEM((rows_bin, channels), HALF_FLOAT)] * 5
        + [pltpu.VMEM((rows_time, channels), HALF_FLOAT)]
        + [
            pltpu.VMEM((weight.shape[0], 2, weight.shape[2] * batches, channels), HALF_FLOAT)
            for weight in weights
        ],
        "tables": [
            pltpu.VMEM((2, rows_time, rows_bin), HALF_FLOAT),
            pltpu.VMEM((rows_bin, rows_bin), HALF_FLOAT),
            pltpu.VMEM((rows_bin, rows_bin), HALF_FLOAT),
        ],
        "sems": [dma((devices,))] * 8 + [dma((2, batches)), dma((2, batches)), dma((3,))],
    }
    inputs.update(extra.inputs)
    outputs.update(extra.outputs)
    scratch.update(extra.scratch)
    sizes = (devices, batches, count, pieces_list)

    def body(refs):
        extra.bind(refs)
        spectral_body(sizes, back, refs, extra)

    results = remote_call(
        body,
        inputs,
        outputs,
        scratch,
        1 if back else 0,
        2 * rows_bin * channels * channels * 4,
        4 * channels * channels * sum(pieces_list),
        "spectral_back" if back else "spectral_forward",
    )
    signal = results["signal"].reshape(count, per_time, channels)
    signals, offset = [], 0
    for pieces, room in zip(pieces_list, wide):
        signals.append(signal[:, offset : offset + pieces])
        offset += room
    return results, signals


def gelu_pair(value):
    slope = math.sqrt(2.0 / math.pi)
    square = value * value
    bent = jnp.tanh(slope * value * (1.0 + 0.044715 * square))
    rise = 0.5 * (1.0 + bent)
    turn = 0.5 * slope * value * (1.0 - bent * bent) * (1.0 + 3.0 * 0.044715 * square)
    return (value * rise).astype(HALF_FLOAT), (rise + turn).astype(HALF_FLOAT)


def by_time(values):
    turned = jnp.swapaxes(values, 0, 1)
    extra = -turned.shape[1] % 16
    return jnp.pad(turned, ((0, 0), (0, extra)) + ((0, 0),) * (turned.ndim - 2))


def by_series(values, count):
    return jnp.swapaxes(values[:, :count], 0, 1)


def neighbours(low_side, high_side):
    count = lax.axis_size("tm")
    onward = [(i, i + 1) for i in range(count - 1)]
    return (
        lax.ppermute(high_side, "tm", onward),
        lax.ppermute(low_side, "tm", [(j, i) for i, j in onward]),
    )


def window_sum(values, first, width, count):
    total, level, size = None, values, 1
    while width:
        if width & 1:
            part = level[first : first + count]
            total = part if total is None else total + part
            first += size
        width >>= 1
        if width:
            level = level[:-size] + level[size:]
            size *= 2
    return total


def seasonal_parts(series, halves, rim):
    steps = series.shape[0]
    before, after = neighbours(series[:rim], series[steps - rim :])
    position = lax.axis_index("tm")
    before = jnp.where(position == 0, jnp.broadcast_to(series[:1], before.shape), before)
    is_final = position == lax.axis_size("tm") - 1
    after = jnp.where(is_final, jnp.broadcast_to(series[-1:], after.shape), after)
    wide = jnp.concatenate([before, series, after]).astype(FLOAT)
    parts = []
    for half in halves:
        mean = window_sum(wide, rim - half, 2 * half + 1, steps) / (2 * half + 1)
        parts.append((series.astype(FLOAT) - mean).astype(HALF_FLOAT))
    return parts


def series_gradient(grads, halves, rim):
    steps = grads[0].shape[0]
    wide = 0.0
    for grad, half in zip(grads, halves):
        padded = jnp.pad(grad, ((2 * rim, 2 * rim), (0, 0), (0, 0)))
        wide = wide + window_sum(padded, rim - half, 2 * half + 1, steps + 2 * rim) / (
            2 * half + 1
        )
    low_rim, high_rim = wide[:rim], wide[rim + steps :]
    before, after = neighbours(low_rim, high_rim)
    position = lax.axis_index("tm")
    is_final = position == lax.axis_size("tm") - 1
    low_sum = jnp.pad(jnp.sum(low_rim, axis=0, keepdims=True), ((0, rim - 1), (0, 0), (0, 0)))
    high_sum = jnp.pad(jnp.sum(high_rim, axis=0, keepdims=True), ((rim - 1, 0), (0, 0), (0, 0)))
    before = jnp.where(position == 0, low_sum, before)
    after = jnp.where(is_final, high_sum, after)
    middle = jnp.zeros((steps - 2 * rim,) + before.shape[1:], FLOAT)
    edges = jnp.concatenate([before, middle, after])
    return (sum(grads) - wide[rim : rim + steps] - edges).astype(HALF_FLOAT)


def step_block(kernel, sizes=(4, 3, 2, 1)):
    return next(size for size in sizes if kernel % size == 0)


def row_spec(block):
    return pl.BlockSpec(block, lambda i: (0,) * len(block))


def steps_spec(values, block):
    pieces, _, series, channels = values.shape
    return pl.BlockSpec((pieces, block, series, channels), lambda i: (0, i, 0, 0))


def weight_spec(weight, block):
    return pl.BlockSpec((block,) + weight.shape[1:], lambda i: (i, 0, 0))


def local_call(kernel, grid, inputs, outputs, flops, nbytes, name):
    return pl.pallas_call(
        kernel,
        out_shape=tuple(shape for shape, _ in outputs),
        grid=(grid,),
        in_specs=[spec for _, spec in inputs],
        out_specs=tuple(spec for _, spec in outputs),
        compiler_params=pltpu.CompilerParams(vmem_limit_bytes=48 * 1024 * 1024),
        cost_estimate=pl.CostEstimate(
            flops=flops, bytes_accessed=nbytes, transcendentals=0
        ),
        name=name,
    )(*[value for value, _ in inputs])


def down_kernel(x_ref, w_ref, b_ref, out_ref):
    step = pl.program_id(0)

    @pl.when(step == 0)
    def _():
        out_ref[...] = jnp.broadcast_to(b_ref[...], out_ref.shape)

    total = out_ref[...]
    for one in range(w_ref.shape[0]):
        total = total + dot_nn(x_ref[:, one].reshape(total.shape), w_ref[one])
    out_ref[...] = total

    @pl.when(step == pl.num_programs(0) - 1)
    def _():
        out_ref[...] = jnp.tanh(out_ref[...])


def down_layer(seasonal, weight, bias_row):
    pieces, kernel, series, channels = seasonal.shape
    block = step_block(kernel)
    rows = pieces * series
    (down_act,) = local_call(
        down_kernel,
        kernel // block,
        [
            (seasonal, steps_spec(seasonal, block)),
            (weight, weight_spec(weight, block)),
            (bias_row[None], row_spec((1, channels))),
        ],
        [(jax.ShapeDtypeStruct((rows, channels), FLOAT), row_spec((rows, channels)))],
        2 * seasonal.size * channels,
        2 * (seasonal.size + weight.size),
        "down_layer",
    )
    return down_act


def normed(values):
    center = values - jnp.mean(values, axis=-1, keepdims=True)
    spread = jnp.mean(center * center, axis=-1, keepdims=True)
    scale = lax.rsqrt(spread + EPSILON)
    return center * scale, scale


def normed_back(grad, hat, scale):
    return (
        grad
        - jnp.mean(grad, axis=-1, keepdims=True)
        - hat * jnp.mean(grad * hat, axis=-1, keepdims=True)
    ) * scale


def up_kernel(picks, inner_ref, x_ref, w_ref, rows_ref, act_ref, out_ref):
    bias_row, gain_row, shift_row = (rows_ref[i : i + 1] for i in picks)
    inner = inner_ref[...]
    for one in range(w_ref.shape[0]):
        act = jnp.tanh(dot_nn(inner, w_ref[one]) + bias_row)
        hat, _ = normed(act + x_ref[:, one].reshape(act.shape).astype(FLOAT))
        act_ref[:, one] = act.reshape(act_ref.shape[0], act_ref.shape[2], act_ref.shape[3])
        out = (hat * gain_row + shift_row).astype(HALF_FLOAT)
        out_ref[:, one] = out.reshape(out_ref.shape[0], out_ref.shape[2], out_ref.shape[3])


def up_layer(inner, seasonal, weight, rows, picks):
    pieces, kernel, series, channels = seasonal.shape
    block = step_block(kernel, (8, 6, 4, 3, 2, 1))
    return local_call(
        functools.partial(up_kernel, picks),
        kernel // block,
        [
            (inner, row_spec(inner.shape)),
            (seasonal, steps_spec(seasonal, block)),
            (weight, weight_spec(weight, block)),
            (rows, row_spec(rows.shape)),
        ],
        [
            (jax.ShapeDtypeStruct(seasonal.shape, FLOAT), steps_spec(seasonal, block)),
            (jax.ShapeDtypeStruct(seasonal.shape, HALF_FLOAT), steps_spec(seasonal, block)),
        ],
        2 * seasonal.size * channels,
        8 * seasonal.size + 2 * weight.size,
        "up_layer",
    )


def up_back_kernel(
    grad_ref, merge_ref, act_ref, x_ref, w_ref, gain_ref, outer_ref, up_ref, inner_ref, sums_ref
):
    @pl.when(pl.program_id(0) == 0)
    def _():
        inner_ref[...] = jnp.zeros_like(inner_ref)
        sums_ref[...] = jnp.zeros_like(sums_ref)

    shape = inner_ref.shape
    block = (x_ref.shape[0], x_ref.shape[2], x_ref.shape[3])
    gain_row = gain_ref[8:9]
    total = inner_ref[...]
    sums = [sums_ref[i : i + 1] for i in range(3)]
    for one in range(w_ref.shape[0]):
        grad = dot_nt(grad_ref[:, one].reshape(shape), merge_ref[0])
        act = act_ref[:, one].reshape(shape)
        hat, scale = normed(act + x_ref[:, one].reshape(shape).astype(FLOAT))
        outer = normed_back(grad * gain_row, hat, scale)
        up = (outer * (1.0 - act * act)).astype(HALF_FLOAT)
        total = total + dot_nt(up, w_ref[one])
        outer_ref[:, one] = outer.reshape(block)
        up_ref[:, one] = up.reshape(block)
        for i, value in enumerate((up.astype(FLOAT), grad * hat, grad)):
            sums[i] = sums[i] + jnp.sum(value, axis=0, keepdims=True)
    inner_ref[...] = total
    for i in range(3):
        sums_ref[i : i + 1] = sums[i]


def up_layer_back(grad, merge, index, act, seasonal, weight, table):
    pieces, kernel, series, channels = seasonal.shape
    block = step_block(kernel)
    rows = pieces * series
    spec = steps_spec(seasonal, block)
    return local_call(
        up_back_kernel,
        kernel // block,
        [
            (grad, spec),
            (merge, pl.BlockSpec((1,) + merge.shape[1:], lambda i: (index, 0, 0))),
            (act, spec),
            (seasonal, spec),
            (weight, weight_spec(weight, block)),
            (table, row_spec(table.shape)),
        ],
        [
            (jax.ShapeDtypeStruct(seasonal.shape, FLOAT), spec),
            (jax.ShapeDtypeStruct(seasonal.shape, HALF_FLOAT), spec),
            (jax.ShapeDtypeStruct((rows, channels), FLOAT), row_spec((rows, channels))),
            (jax.ShapeDtypeStruct((8, channels), FLOAT), row_spec((8, channels))),
        ],
        4 * seasonal.size * channels,
        14 * seasonal.size + 2 * weight.size,
        "up_layer_back",
    )


def head_kernel(
    one_ref,
    two_ref,
    cot_ref,
    mask_ref,
    table_ref,
    bias_ref,
    merge_ref,
    hidden_w_ref,
    output_w_ref,
    result_ref,
    first_ref,
    hidden_ref,
    grad_hidden_ref,
    feed_ref,
    merged_ref,
    sums_ref,
    hidden_sums_ref,
    slope_ref,
    rows_ref,
):
    @pl.when(pl.program_id(0) == 0)
    def _():
        sums_ref[...] = jnp.zeros_like(sums_ref)
        hidden_sums_ref[...] = jnp.zeros_like(hidden_sums_ref)

    channels = one_ref.shape[1]
    chunks = [pl.ds(k * channels, channels) for k in range(hidden_ref.shape[1] // channels)]
    gain_first, gain_final = table_ref[9:10], table_ref[10:11]
    merged = dot_nn(one_ref[...], merge_ref[0]) + dot_nn(two_ref[...], merge_ref[1])
    merged = merged + table_ref[6:7]
    hat_first, scale_first = normed(merged)
    first = (hat_first * gain_first + table_ref[12:13]).astype(HALF_FLOAT)
    first_ref[...] = first
    final = merged + table_ref[7:8]
    for chunk in chunks:
        value = dot_nn(first, hidden_w_ref[:, chunk]) + bias_ref[:, chunk]
        hidden, slope = gelu_pair(value)
        hidden_ref[:, chunk] = hidden
        slope_ref[:, chunk] = slope
        final = final + dot_nn(hidden, output_w_ref[chunk])
    hat_final, scale_final = normed(final)
    mask = mask_ref[...]
    result = (hat_final * gain_final + table_ref[13:14]) * mask
    for lane in range(rows_ref.shape[0]):
        rows_ref[lane] = result[:, lane * 128 : lane * 128 + 128]
    count, steps = result_ref.shape[0], result_ref.shape[1]
    series = rows_ref.shape[1] // steps
    for one in range(count):
        for lane in range(rows_ref.shape[0]):
            value = rows_ref[lane, pl.ds(one, steps, stride=series), :]
            result_ref[one, :, lane * 128 : lane * 128 + 128] = value.astype(HALF_FLOAT)
    grad = cot_ref[...].astype(FLOAT) * mask
    grad_final = normed_back(grad * gain_final, hat_final, scale_final)
    feed = grad_final.astype(HALF_FLOAT)
    feed_ref[...] = feed
    grad_first = jnp.zeros_like(merged)
    for chunk in chunks:
        value = dot_nt(feed, output_w_ref[chunk]) * slope_ref[:, chunk].astype(FLOAT)
        value = value.astype(HALF_FLOAT)
        grad_hidden_ref[:, chunk] = value
        hidden_sums_ref[0:1, chunk] += jnp.sum(value.astype(FLOAT), axis=0, keepdims=True)
        grad_first = grad_first + dot_nt(value, hidden_w_ref[:, chunk])
    grad_merged = grad_final + normed_back(grad_first * gain_first, hat_first, scale_first)
    low = grad_merged.astype(HALF_FLOAT)
    merged_ref[...] = low
    parts = (
        grad_first * hat_first,
        grad * hat_final,
        grad_first,
        grad,
        low.astype(FLOAT),
        feed.astype(FLOAT),
    )
    for row, value in enumerate(parts):
        sums_ref[row : row + 1] += jnp.sum(value, axis=0, keepdims=True)


def head(outs, cotangent, mask_rows, table, bias, merge, hidden_w, output_w, count):
    total, channels = outs[0].shape
    steps = cotangent.shape[0]
    series = total // steps
    block_steps = 32 if steps % 32 == 0 else 16
    rows, hidden = block_steps * series, hidden_w.shape[1]
    block, wide = (
        pl.BlockSpec((rows, channels), lambda i: (i, 0)),
        pl.BlockSpec((rows, hidden), lambda i: (i, 0)),
    )
    low, low_wide = (
        jax.ShapeDtypeStruct((total, channels), HALF_FLOAT),
        jax.ShapeDtypeStruct((total, hidden), HALF_FLOAT),
    )

    def held(value):
        return pl.BlockSpec(value.shape, lambda i: (0,) * value.ndim)

    return pl.pallas_call(
        head_kernel,
        out_shape=(
            jax.ShapeDtypeStruct((count, steps, channels), HALF_FLOAT),
            low,
            low_wide,
            low_wide,
            low,
            low,
            jax.ShapeDtypeStruct((8, channels), FLOAT),
            jax.ShapeDtypeStruct((8, hidden), FLOAT),
        ),
        grid=(steps // block_steps,),
        in_specs=[
            block,
            block,
            block,
            pl.BlockSpec((rows, 1), lambda i: (i, 0)),
            held(table),
            held(bias),
            held(merge),
            held(hidden_w),
            held(output_w),
        ],
        out_specs=(
            pl.BlockSpec((count, block_steps, channels), lambda i: (0, i, 0)),
            block,
            wide,
            wide,
            block,
            block,
            pl.BlockSpec((8, channels), lambda i: (0, 0)),
            pl.BlockSpec((8, hidden), lambda i: (0, 0)),
        ),
        scratch_shapes=[
            pltpu.VMEM((rows, hidden), HALF_FLOAT),
            pltpu.VMEM((channels // 128, rows, 128), FLOAT),
        ],
        compiler_params=pltpu.CompilerParams(vmem_limit_bytes=56 * 1024 * 1024),
        cost_estimate=pl.CostEstimate(
            flops=2 * total * channels * (4 * channels + 4 * hidden),
            bytes_accessed=total * (14 * channels + 4 * hidden),
            transcendentals=total * hidden,
        ),
        name="head",
    )(
        outs[0],
        outs[1],
        cotangent.reshape(total, channels),
        mask_rows,
        table,
        bias,
        merge,
        hidden_w,
        output_w,
    )


def down_back_kernel(grad_ref, w_ref, outer_ref, out_ref):
    grad = grad_ref[...]
    block = (out_ref.shape[0], out_ref.shape[2], out_ref.shape[3])
    for one in range(w_ref.shape[0]):
        out_ref[:, one] = dot_nt(grad, w_ref[one]).reshape(block) + outer_ref[:, one]


def down_layer_back(grad, weight, outer):
    pieces, kernel, series, channels = outer.shape
    block = step_block(kernel)
    spec = steps_spec(outer, block)
    (seasonal_grad,) = local_call(
        down_back_kernel,
        kernel // block,
        [(grad, row_spec(grad.shape)), (weight, weight_spec(weight, block)), (outer, spec)],
        [(jax.ShapeDtypeStruct(outer.shape, FLOAT), spec)],
        2 * outer.size * channels,
        8 * outer.size + 2 * weight.size,
        "down_layer_back",
    )
    return seasonal_grad


class Branch:
    def __init__(self, index, shape, down_weight, table):
        self.index, self.table = index, table
        self.count, steps, channels = shape
        self.kernel = down_weight.shape[0]
        self.pieces = steps // self.kernel
        self.series = round_up(self.count, 16)
        self.down_weight = down_weight
        self.gain_row, self.shift_row = table[8], table[11]

    def down(self, seasonal, down_act=None):
        self.seasonal = seasonal.reshape(self.pieces, self.kernel, self.series, -1)
        if down_act is None:
            down_act = down_layer(self.seasonal, self.down_weight, self.table[self.index])
        self.down_act = down_act
        self.down_low = down_act.astype(HALF_FLOAT)

    def to_series(self, rows):
        return by_series(rows.reshape(self.pieces, self.series, -1), self.count)

    def from_series(self, values):
        return by_time(values).reshape(self.pieces * self.series, -1)

    def inner(self, iso_out):
        act = jnp.tanh(self.from_series(iso_out).astype(FLOAT) + self.table[2 + self.index])
        inner_in = act + self.down_low.astype(FLOAT)
        return act, layer_norm(inner_in, self.gain_row, self.shift_row).astype(HALF_FLOAT)

    def up(self, iso_act, inner_low, up_weight):
        self.up_weight, self.iso_act, self.inner_low = up_weight, iso_act, inner_low
        self.act, out = up_layer(
            inner_low, self.seasonal, up_weight, self.table, (4 + self.index, 8, 11)
        )
        return out.reshape(-1, out.shape[3])

    def up_back(self, grad_merged, merge):
        self.outer, self.grad_up, grad_inner, sums = up_layer_back(
            grad_merged.reshape(self.seasonal.shape),
            merge,
            self.index,
            self.act,
            self.seasonal,
            self.up_weight,
            self.table,
        )
        inner_in = self.iso_act + self.down_low.astype(FLOAT)
        _, inner_pull = jax.vjp(layer_norm, inner_in, self.gain_row, self.shift_row)
        self.grad_inner_in, gain_inner, shift_inner = inner_pull(grad_inner)
        grad_iso = self.grad_inner_in * (1.0 - self.iso_act * self.iso_act)
        self.iso_sum, self.up_sum = jnp.sum(grad_iso, axis=0), sums[0]
        self.gain_sum, self.shift_sum = sums[1] + gain_inner, sums[2] + shift_inner
        return grad_iso.astype(HALF_FLOAT)

    def down_back(self, grad_signal):
        grad_down = self.from_series(grad_signal).astype(FLOAT) + self.grad_inner_in
        self.grad_down = (grad_down * (1.0 - self.down_act * self.down_act)).astype(HALF_FLOAT)
        return jnp.sum(self.grad_down.astype(FLOAT), axis=0)

    def seasonal_back(self):
        grad = down_layer_back(self.grad_down, self.down_weight, self.outer)
        return grad.reshape(-1, self.series, grad.shape[3])


def batch_split(values, split, join):
    return lax.all_to_all(values, "batch", split_axis=split, concat_axis=join, tiled=True)


def time_sum(values, dim):
    return lax.psum_scatter(
        values.astype(HALF_FLOAT), "tm", scatter_dimension=dim, tiled=True
    ).astype(FLOAT)


def plain_gradients(wides, narrows, downs):
    results = []
    for wide, narrow, down in zip(wides, narrows, downs):
        wide = jnp.swapaxes(wide, 0, 1).reshape(wide.shape[1], -1, wide.shape[3])
        if down:
            wide, narrow = batch_split(wide, 2, 1), lax.all_gather(narrow, "batch", tiled=True)
            value = jnp.einsum("knc,nd->kcd", wide, narrow, preferred_element_type=FLOAT)
        else:
            wide = lax.all_gather(wide, "batch", axis=1, tiled=True)
            narrow = batch_split(narrow, 1, 0)
            value = jnp.einsum("nd,knc->dkc", narrow, wide, preferred_element_type=FLOAT)
        results.append(time_sum(value, 2))
    return results


def plain_sums(matrices):
    results = []
    for kind, value in matrices:
        batch_dim, time_dim = (0, 1) if kind == "rows" else (value.ndim - 1, value.ndim - 2)
        value = lax.psum_scatter(
            value.astype(FLOAT), "batch", scatter_dimension=batch_dim, tiled=True
        )
        results.append(time_sum(value, time_dim))
    return results


def per_device(
    series_in,
    out_cotangent,
    out_mask,
    down_twelve,
    down_sixteen,
    iso_twelve,
    iso_sixteen,
    up_twelve,
    up_sixteen,
    branch_bias,
    merge_weight,
    hidden_weight,
    hidden_bias,
    output_weight,
    head_bias,
    norm_gain,
    norm_shift,
):
    series_dev, step_count, channels = series_in.shape
    halves = (down_twelve.shape[0] // 2, down_sixteen.shape[0] // 2)
    rim = max(halves)
    hidden_rows = hidden_bias.reshape(-1, channels)
    table = jnp.concatenate([branch_bias, head_bias, norm_gain, norm_shift, hidden_rows])
    table = jnp.pad(table, ((0, -table.shape[0] % 8), (0, 0))).astype(FLOAT)
    down_weights = (down_twelve, down_sixteen)
    branches = [
        Branch(k, series_in.shape, down_weights[k], table) for k in range(2)
    ]
    iso_weights = (iso_twelve, iso_sixteen)
    sizes = plane_sizes(channels)
    up_weights = [up_twelve, up_sixteen]
    turns = [weight for weight in up_weights if weight.shape[1] % 8 == 0]
    shapes = [(series_dev, branch.pieces, channels) for branch in branches]
    if sizes:
        per_time = sum(round_up(branch.pieces, 8) for branch in branches)
        values, wides = None, []
        front = (series_in, out_cotangent, down_weights, table, per_time, halves, rim)
    else:
        for branch, seasonal in zip(branches, seasonal_parts(by_time(series_in), halves, rim)):
            branch.down(seasonal)
        values = [branch.to_series(branch.down_low) for branch in branches]
        wides = [branch.seasonal for branch in branches]
        front = None
    forward, iso_outs = spectral(
        values, shapes, iso_weights, False, ForwardExtra(sizes, wides, turns, front)
    )
    if sizes:
        for k in range(2):
            branches[k].down(forward[f"seasonal{k}"], forward[f"down_act{k}"])
        inners = [(forward[f"iso_act{k}"], forward[f"inner{k}"]) for k in range(2)]
        cotangent = forward["cotangent_steps"]
    else:
        inners = [branches[k].inner(iso_outs[k]) for k in range(2)]
        cotangent = by_time(out_cotangent)
    turned = [forward[f"turned{i}"] for i in range(len(turns))]
    up_weights = [
        jnp.swapaxes(weight, 0, 1) if weight.shape[1] % 8 else turned.pop(0)
        for weight in up_weights
    ]
    outs = [
        branch.up(*inner, weight)
        for branch, inner, weight in zip(branches, inners, up_weights)
    ]
    row_count = outs[0].shape[0]
    mask_rows = by_time(out_mask.astype(FLOAT)).reshape(row_count, 1)
    hidden_row = table[14 : 14 + hidden_rows.shape[0]].reshape(1, -1)
    result, first_low, hidden_low, grad_hidden_pre, grad_feed, grad_merged, sums, hidden_sums = head(
        outs,
        cotangent,
        mask_rows,
        table,
        hidden_row,
        merge_weight,
        hidden_weight,
        output_weight,
        series_dev,
    )
    gain_first, gain_final, shift_first, shift_final = (sums[k] for k in range(4))
    grad_merge_bias, grad_output_bias, grad_hidden_bias = sums[4], sums[5], hidden_sums[0]
    hidden_size = hidden_low.shape[1]
    jobs = (
        (first_low, [grad_hidden_pre], (channels, hidden_size)),
        (grad_feed, [hidden_low], (channels, hidden_size)),
        (grad_merged, outs, (2, channels, channels)),
    )
    job_kinds = ("rows", "lanes", "lanes")
    grad_isos = [branches[k].up_back(grad_merged, merge_weight) for k in range(2)]
    up_wides = [branch.grad_up for branch in branches]
    up_narrows = [branch.inner_low for branch in branches]
    backward, grad_signals = spectral(
        [branch.to_series(grad) for branch, grad in zip(branches, grad_isos)],
        shapes,
        iso_weights,
        True,
        BackwardExtra(
            sizes,
            forward["spec"],
            up_wides,
            up_narrows,
            jobs,
            [branch.grad_inner_in for branch in branches],
            [branch.down_act for branch in branches],
            (
                series_dev,
                sum(round_up(branch.pieces, 8) for branch in branches),
                branches[0].series,
            ),
        ),
    )
    iso_parts, first = [], 0
    for bins in (branches[0].pieces, branches[1].pieces):
        iso_parts.append(
            iso_gradients(
                forward["spec"],
                backward["specs"],
                backward["spec"],
                backward["grads"],
                first,
                bins,
            )
        )
        first += round_up(bins, 8)
    if sizes:
        matrices = [(kind, backward[f"matrix{i}"]) for i, kind in enumerate(job_kinds)]
        down_sums = backward["down_sums"][:2]
        down_narrows = [backward["down_grad0"], backward["down_grad1"]]
    else:
        matrices = []
        for kind, (left, rights, shape) in zip(job_kinds, jobs):
            values = [
                jnp.einsum("nd,nf->df", left, right, preferred_element_type=FLOAT)
                for right in rights
            ]
            matrices.append((kind, jnp.stack(values).astype(HALF_FLOAT).reshape(shape)))
        down_sums = jnp.stack([branches[k].down_back(grad_signals[k]) for k in range(2)])
        down_narrows = [branch.grad_down for branch in branches]
    one, two = branches
    singles = (one.iso_sum, two.iso_sum, one.up_sum, two.up_sum)
    singles += (one.gain_sum + two.gain_sum, gain_first, gain_final)
    singles += (one.shift_sum + two.shift_sum, shift_first, shift_final)
    singles += (grad_merge_bias, grad_output_bias)
    vectors = jnp.concatenate(
        [down_sums] + [row[None] for row in singles] + [grad_hidden_bias.reshape(-1, channels)]
    )
    vectors = jnp.pad(vectors, ((0, -vectors.shape[0] % 8), (0, 0)))
    if sizes:
        downs, vectors, grad_series, sums = down_gradients(
            sizes,
            (forward["gathered0"], forward["gathered1"]),
            down_narrows,
            vectors,
            (down_twelve, down_sixteen),
            [branch.outer.reshape(step_count, -1, channels) for branch in branches],
            halves,
            rim,
            series_dev,
            matrices,
        )
        downs = [jnp.transpose(value, (0, 2, 1)) for value in downs]
        ups = [jnp.transpose(backward[key], (2, 0, 1)) for key in ("up0", "up1")]
    else:
        vectors = lax.psum(vectors, ("tm", "batch"))
        grad_seasonals = [branch.seasonal_back() for branch in branches]
        grad_series = by_series(series_gradient(grad_seasonals, halves, rim), series_dev)
        downs = plain_gradients(wides, down_narrows, (True, True))
        ups = plain_gradients(up_wides, up_narrows, (False, False))
        sums = plain_sums(matrices)
    me, devices = lax.axis_index("tm"), lax.axis_size("tm")
    width = channels // devices
    rows = lax.dynamic_slice_in_dim(vectors[:14], me * width, width, axis=1)
    hidden_width = hidden_bias.shape[0] // devices
    hidden_sum = vectors[14 : 14 + hidden_rows.shape[0]].reshape(-1)
    vector_parts = (
        rows[:6],
        lax.dynamic_slice_in_dim(hidden_sum, me * hidden_width, hidden_width),
        rows[12:14],
        rows[6:9],
        rows[9:12],
    )
    return (
        result,
        grad_series,
        downs[0],
        downs[1],
        iso_parts[0],
        iso_parts[1],
        ups[0],
        ups[1],
        vector_parts[0],
        jnp.swapaxes(sums[2], 1, 2),
        sums[0],
        vector_parts[1],
        sums[1].T,
        vector_parts[2],
        vector_parts[3],
        vector_parts[4],
    )


def solution(mesh):
    placed = (
        P("batch", "tm", None),
        P("batch", "tm", None),
        P("batch", "tm"),
        P(),
        P(),
        P("tm", None, "batch", None),
        P("tm", None, "batch", None),
        P(),
        P(),
        P(),
        P(),
        P(),
        P(),
        P(),
        P(),
        P(),
        P(),
    )
    return jax.shard_map(
        per_device,
        mesh=mesh,
        in_specs=placed,
        out_specs=(
            P("batch", "tm", None),
            P("batch", "tm", None),
            P(None, "batch", "tm"),
            P(None, "batch", "tm"),
            P("tm", None, "batch", None),
            P("tm", None, "batch", None),
            P("batch", None, "tm"),
            P("batch", None, "tm"),
            P(None, "tm"),
            P(None, "batch", "tm"),
            P("batch", "tm"),
            P("tm"),
            P("batch", "tm"),
            P(None, "tm"),
            P(None, "tm"),
            P(None, "tm"),
        ),
        check_vma=False,
    )
```

```python
import functools
import math

import jax
import jax.numpy as jnp
import numpy as np
from jax import lax
from jax.experimental import pallas as pl
from jax.experimental.pallas import tpu as pltpu
from jax.sharding import PartitionSpec as P

FLOAT = jnp.float32
HALF_FLOAT = jnp.bfloat16
HIGHEST = lax.Precision.HIGHEST
EPSILON = 1e-05
MESH = pl.DeviceIdType.MESH


def layer_norm(values, gain_row, bias_row):
    center = values - jnp.mean(values, axis=-1, keepdims=True)
    spread = jnp.mean(center * center, axis=-1, keepdims=True)
    return center * lax.rsqrt(spread + EPSILON) * gain_row + bias_row


def round_up(value, multiple):
    return -(-value // multiple) * multiple


def spectral_constants(devices, pieces_list):
    padded = [round_up(pieces, 8) for pieces in pieces_list]
    per_time, per_bin = sum(padded), 2 * sum(padded)
    table = np.zeros((devices, per_bin, devices, per_time), np.float64)
    offset = 0
    for pieces, wide in zip(pieces_list, padded):
        length = devices * pieces
        index = np.arange(length)
        angle = (2.0 * math.pi / length) * (np.outer(index, index) % length)
        factor = 1.0 / math.sqrt(length)
        for part, values in enumerate((np.cos(angle) * factor, -np.sin(angle) * factor)):
            row = 2 * offset + part * wide
            table[:, row : row + pieces, :, offset : offset + pieces] = values.reshape(
                devices, pieces, devices, pieces
            )
        offset += wide
    table = table.reshape(devices * per_bin, devices * per_time).astype(np.float32)
    high = table.astype(HALF_FLOAT)
    low = (table - high.astype(np.float32)).astype(HALF_FLOAT)
    return jnp.asarray(np.stack([high, low]))


def move_index(out, devices, wide):
    per_bin = 2 * sum(wide)
    base, result = 0, None
    for room in wide:
        local = out - 2 * devices * base
        one_bin = lax.div(local, jnp.full_like(local, 2 * devices))
        rest = local - one_bin * (2 * devices)
        part = jnp.where(rest >= devices, 1, 0)
        series = rest - part * devices
        value = series * per_bin + 2 * base + part * room + one_bin
        result = value if result is None else jnp.where(local >= 0, value, result)
        base += room
    return result


def moves(shape, devices, wide):
    rows = lax.broadcasted_iota(jnp.int32, shape, 0)
    columns = lax.broadcasted_iota(jnp.int32, shape, 1)
    there = jnp.where(columns == move_index(rows, devices, wide), 1.0, 0.0)
    back = jnp.where(rows == move_index(columns, devices, wide), 1.0, 0.0)
    return there.astype(HALF_FLOAT), back.astype(HALF_FLOAT)


def dot_nn(left, right):
    return jnp.dot(left, right, preferred_element_type=FLOAT)


def dot_nt(left, right):
    return lax.dot_general(left, right, (((1,), (1,)), ((), ())), preferred_element_type=FLOAT)


def spectral_body(sizes, back, refs, extra):
    devices, batches, count, pieces_list = sizes
    w1_ref, w2_ref = refs["weight0"], refs["weight1"]
    table_ref = refs["table"]
    inverse_ref, move_ref, unmove_ref = refs["tables"]
    spec_ref, signal_ref = refs["spec"], refs["signal"]
    (one, two, three, mixed, spread, bins_out, four, w1, w2) = refs["buffers"]
    (s1, r1, s2, r2, s3, r3, s4, r4, ws, wr, own) = refs["sems"]
    me = lax.axis_index("tm")
    mine = lax.axis_index("batch")
    wide = [round_up(pieces, 8) for pieces in pieces_list]
    per_time, per_bin = sum(wide), 2 * sum(wide)
    weights = ((w1_ref, w1), (w2_ref, w2))

    barrier = pltpu.get_barrier_semaphore()

    @pl.loop(1, devices)
    def _(step):
        pl.semaphore_signal(
            barrier, inc=1, device_id=(mine, lax.rem(me + step, devices)), device_id_type=MESH
        )

    for step in range(1, batches):
        pl.semaphore_signal(
            barrier, inc=1, device_id=(lax.rem(mine + step, batches), me), device_id_type=MESH
        )
    pl.semaphore_wait(barrier, devices - 1 + batches - 1 + extra.greet(barrier))

    def exchange(source, target, send_sem, recv_sem, limit_out, limit_in, rows, start):
        def remote(there, here):
            return pltpu.make_async_remote_copy(
                src_ref=source.at[pl.ds(pl.multiple_of(there * rows, rows), rows)],
                dst_ref=target.at[pl.ds(pl.multiple_of(here * rows, rows), rows)],
                send_sem=send_sem.at[there],
                recv_sem=recv_sem.at[here],
                device_id=(mine, there),
                device_id_type=MESH,
            )

        if start:

            @pl.loop(1, devices)
            def _(step):
                there = lax.rem(me + step, devices)

                @pl.when(there < limit_out)
                def _():
                    remote(there, me).start()

        else:

            @pl.loop(1, devices)
            def _(step):
                there = lax.rem(me + step, devices)

                @pl.when(there < limit_in)
                def _():
                    pltpu.make_async_remote_copy(
                        src_ref=source.at[pl.ds(0, rows)],
                        dst_ref=target.at[pl.ds(pl.multiple_of(there * rows, rows), rows)],
                        send_sem=send_sem.at[there],
                        recv_sem=recv_sem.at[there],
                        device_id=(mine, there),
                        device_id_type=MESH,
                    ).wait_recv()

    def drain(source, target, send_sem, recv_sem, limit_out, rows):
        @pl.loop(1, devices)
        def _(step):
            there = lax.rem(me + step, devices)

            @pl.when(there < limit_out)
            def _():
                pltpu.make_async_remote_copy(
                    src_ref=source.at[pl.ds(0, rows)],
                    dst_ref=target.at[pl.ds(0, rows)],
                    send_sem=send_sem.at[there],
                    recv_sem=recv_sem.at[there],
                    device_id=(mine, there),
                    device_id_type=MESH,
                ).wait_send()

    owner = me < count

    def weight_copies(index):
        source, target = weights[index]
        rows = source.shape[2]
        place = target.at[:, :, pl.ds(pl.multiple_of(mine * rows, rows), rows)]
        local = pltpu.make_async_copy(source, place, own.at[index])
        remote = []
        for step in range(1, batches):
            there = lax.rem(mine + step, batches)
            back_there = lax.rem(mine + batches - step, batches)
            other = target.at[:, :, pl.ds(pl.multiple_of(back_there * rows, rows), rows)]
            remote.append(
                [
                    pltpu.make_async_remote_copy(
                        src_ref=source,
                        dst_ref=where,
                        send_sem=ws.at[index, step],
                        recv_sem=wr.at[index, step],
                        device_id=(there, me),
                        device_id_type=MESH,
                    )
                    for where in (place, other)
                ]
            )
        return local, remote

    for index in range(2):
        local, remote = weight_copies(index)
        local.start()
        for copy, _unused in remote:
            copy.start()

    extra.open()
    inverse_ref[0], inverse_ref[1] = table_ref[0].T, table_ref[1].T
    move_ref[...], unmove_ref[...] = moves(move_ref.shape, devices, wide)
    x_ref = extra.prepare()
    exchange(x_ref, one, s1, r1, count, None, per_time, True)
    here = pltpu.make_async_copy(
        x_ref.at[pl.ds(pl.multiple_of(jnp.minimum(me, count - 1) * per_time, per_time), per_time)],
        one.at[pl.ds(pl.multiple_of(me * per_time, per_time), per_time)],
        own.at[2],
    )
    here.start()
    extra.start()
    if count < devices:
        two[pl.ds(count * per_bin, (devices - count) * per_bin)] = jnp.zeros(
            ((devices - count) * per_bin, two.shape[1]), two.dtype
        )
    here.wait()

    @pl.when(owner)
    def _():
        exchange(x_ref, one, s1, r1, None, devices, per_time, False)
        data = one[...]
        total = dot_nn(table_ref[0], data) + dot_nn(table_ref[1], data)
        bins_out[...] = total.astype(HALF_FLOAT)
        exchange(bins_out, two, s2, r2, devices, None, per_bin, True)
        place = pl.ds(pl.multiple_of(me * per_bin, per_bin), per_bin)
        two[place] = bins_out[place]

    extra.after_bins()
    exchange(bins_out, two, s2, r2, None, count, per_bin, False)
    spec_ref[...] = dot_nn(move_ref[...], two[...]).astype(HALF_FLOAT)
    extra.after_spec()
    base = 0
    for index in range(2):
        local, remote = weight_copies(index)
        local.wait()
        for copy, arrived in remote:
            copy.wait_send()
            arrived.wait_recv()
        target = weights[index][1]

        @pl.loop(0, pieces_list[index])
        def _(one_bin, base=base, target=target):
            place = pl.ds(
                pl.multiple_of(base + one_bin * 2 * devices, 2 * devices), 2 * devices
            )
            rows = spec_ref[place]
            if back:
                real = dot_nt(rows, target[one_bin, 0])
                imag = dot_nt(rows, target[one_bin, 1])
                out = jnp.concatenate(
                    [real[:devices] + imag[devices:], real[devices:] - imag[:devices]]
                )
            else:
                real = dot_nn(rows, target[one_bin, 0])
                imag = dot_nn(rows, target[one_bin, 1])
                out = jnp.concatenate(
                    [real[:devices] - imag[devices:], imag[:devices] + real[devices:]]
                )
            mixed[place] = out.astype(HALF_FLOAT)

        spare = wide[index] - pieces_list[index]
        if spare:
            mixed[
                pl.ds(base + pieces_list[index] * 2 * devices, spare * 2 * devices)
            ] = jnp.zeros((spare * 2 * devices, mixed.shape[1]), mixed.dtype)
        base += wide[index] * 2 * devices

    spread[...] = dot_nn(unmove_ref[...], mixed[...]).astype(HALF_FLOAT)
    exchange(spread, three, s3, r3, count, None, per_bin, True)
    extra.after_mixed()

    @pl.when(owner)
    def _():
        place = pl.ds(pl.multiple_of(me * per_bin, per_bin), per_bin)
        three[place] = spread[place]
        exchange(spread, three, s3, r3, None, devices, per_bin, False)
        data = three[...]
        total = dot_nn(inverse_ref[0], data) + dot_nn(inverse_ref[1], data)
        four[...] = total.astype(HALF_FLOAT)
        exchange(four, signal_ref, s4, r4, devices, None, per_time, True)
        place = pl.ds(pl.multiple_of(me * per_time, per_time), per_time)
        signal_ref[place] = four[place]

    extra.after_signal()
    exchange(four, signal_ref, s4, r4, None, count, per_time, False)
    drain(x_ref, one, s1, r1, count, per_time)
    drain(spread, three, s3, r3, count, per_bin)

    @pl.when(owner)
    def _():
        drain(bins_out, two, s2, r2, devices, per_bin)
        drain(four, signal_ref, s4, r4, devices, per_time)

    extra.finish()


class Place:
    def __init__(self, groups, members, batches):
        self.groups, self.members, self.batches = groups, members, batches
        self.me = lax.axis_index("tm")
        self.core = lax.axis_index("batch")
        self.group = lax.div(self.me, members)
        self.member = lax.rem(self.me, members)

    def device(self, group, member, core):
        return (core, group * self.members + member)

    def member_at(self, step):
        return lax.rem(self.member + step + self.members, self.members)

    def group_at(self, step):
        return lax.rem(self.group + step + self.groups, self.groups)

    def core_at(self, step):
        return lax.rem(self.core + step + self.batches, self.batches)

    def greet(self, barrier):
        greeted = 0
        for step in range(self.members):
            for turn in range(self.batches):
                if step or turn:
                    there = self.device(self.group, self.member_at(step), self.core_at(turn))
                    pl.semaphore_signal(barrier, inc=1, device_id=there, device_id_type=MESH)
                    greeted += 1
        for step in range(1, self.groups):
            for turn in range(self.batches):
                there = self.device(self.group_at(step), self.member, self.core_at(turn))
                pl.semaphore_signal(barrier, inc=1, device_id=there, device_id_type=MESH)
                greeted += 1
        return greeted


class VectorSum:
    @staticmethod
    def scratch(place_sizes, value):
        dma = pltpu.SemaphoreType.DMA
        groups, members, batches = place_sizes
        parts = [pltpu.VMEM(value.shape, value.dtype)]
        for size in (batches, members, groups):
            parts += [pltpu.VMEM((size,) + value.shape, value.dtype), dma((size,)), dma((size,))]
        return parts + [pltpu.VMEM(value.shape, value.dtype) for _ in range(2)]

    def __init__(self, place, source, out, scratch):
        self.place, self.source, self.out = place, source, out
        self.stages = [scratch[1 + 3 * k : 4 + 3 * k] for k in range(3)]
        self.values = [source, scratch[10], scratch[11]]

    def copy(self, stage, step, back):
        place = self.place
        held, send, recv = self.stages[stage]
        picks = [place.core_at, place.member_at, place.group_at]
        to = [place.core, place.member, place.group]
        to[stage] = picks[stage](step)
        return send_copy(
            self.values[stage],
            held.at[picks[stage](-step) if back else picks[stage](0)],
            send.at[step],
            recv.at[step],
            place.device(to[2], to[1], to[0]),
        )

    def start(self, stage):
        for step in range(1, self.stages[stage][0].shape[0]):
            self.copy(stage, step, False).start()

    def add(self, stage):
        held = self.stages[stage][0]
        value = self.values[stage][...]
        picks = [self.place.core_at, self.place.member_at, self.place.group_at]
        held[picks[stage](0)] = value
        for step in range(1, held.shape[0]):
            self.copy(stage, step, True).wait_recv()
        total = held[0]
        for index in range(1, held.shape[0]):
            total = total + held[index]
        target = self.out if stage == 2 else self.values[stage + 1]
        target[...] = total
        if stage < 2:
            self.start(stage + 1)

    def drain(self):
        for stage in range(3):
            for step in range(1, self.stages[stage][0].shape[0]):
                self.copy(stage, step, False).wait_send()


def send_copy(source, target, send_sem, recv_sem, there):
    return pltpu.make_async_remote_copy(
        src_ref=source,
        dst_ref=target,
        send_sem=send_sem,
        recv_sem=recv_sem,
        device_id=there,
        device_id_type=MESH,
    )


def slab(ref, dim, index, size):
    picks = [slice(None)] * len(ref.shape)
    picks[dim] = pl.ds(pl.multiple_of(index * size, size), size)
    return ref.at[tuple(picks)]


class WideExchange:
    @staticmethod
    def scratch(place_sizes, wide):
        groups, members, batches = place_sizes
        mates = members * batches
        dma = pltpu.SemaphoreType.DMA
        return [dma((mates,)), dma((mates,)), dma((wide.shape[1] // members,))]

    @staticmethod
    def shape(place_sizes, wide):
        groups, members, batches = place_sizes
        pieces, steps, series, channels = wide.shape
        return (steps // members, members * batches, pieces, series, channels // batches)

    def __init__(self, place, source, target, sems):
        self.place, self.source, self.target = place, source, target
        self.send_sem, self.recv_sem, self.local_sem = sems

    def hops(self):
        for step in range(self.place.members):
            for turn in range(self.place.batches):
                if step or turn:
                    yield step, turn

    def mate(self, step, turn):
        return self.place.core_at(turn) * self.place.members + self.place.member_at(step)

    def piece(self, one, step, turn):
        place = self.place
        steps, half = self.target.shape[0], self.target.shape[4]
        return slab(
            self.source.at[:, place.member_at(step) * steps + one], 2, place.core_at(turn), half
        )

    def own(self, one):
        return pltpu.make_async_copy(
            self.piece(one, 0, 0), self.target.at[one, self.mate(0, 0)], self.local_sem.at[one]
        )

    def whole(self, step, turn, pick):
        slot = turn * self.place.members + step
        block = self.target.at[:, pick]
        return send_copy(
            block,
            block,
            self.send_sem.at[slot],
            self.recv_sem.at[slot],
            self.place.device(
                self.place.group, self.place.member_at(step), self.place.core_at(turn)
            ),
        )

    def units(self):
        return [functools.partial(self.start, one) for one in range(self.target.shape[0])]

    def start(self, one):
        place = self.place
        self.own(one).start()
        for step, turn in self.hops():
            slot = turn * place.members + step
            send_copy(
                self.piece(one, step, turn),
                self.target.at[one, self.mate(0, 0)],
                self.send_sem.at[slot],
                self.recv_sem.at[slot],
                place.device(place.group, place.member_at(step), place.core_at(turn)),
            ).start()

    def wait(self):
        for one in range(self.target.shape[0]):
            self.own(one).wait()
        for step, turn in self.hops():
            self.whole(step, turn, self.mate(-step, -turn)).wait_recv()

    def drain(self):
        for step, turn in self.hops():
            self.whole(step, turn, self.mate(0, 0)).wait_send()


class NarrowGather:
    sems = 5

    @staticmethod
    def scratch(place_sizes, narrow):
        groups, members, batches = place_sizes
        dma = pltpu.SemaphoreType.DMA
        size = members * batches
        return [dma((members,)), dma((members,)), dma((size,)), dma((size,)), dma((1,))]

    def __init__(self, place, source, target, sems):
        self.place, self.source, self.target = place, source, target
        (self.link_send, self.link_recv, self.chip_send, self.chip_recv, self.local_sem) = sems

    def own(self):
        place = self.place
        pick = place.core * place.members + place.member
        return pltpu.make_async_copy(self.source, self.target.at[pick], self.local_sem.at[0])

    def link(self, step, pick_step):
        place = self.place
        pick = place.core * place.members + place.member_at(pick_step)
        return send_copy(
            self.source,
            self.target.at[pick],
            self.link_send.at[step],
            self.link_recv.at[step],
            place.device(place.group, place.member_at(step), place.core),
        )

    def chip(self, step, turn, source_core, target_core):
        place = self.place
        member = place.member_at(-step)
        slot = turn * place.members + step
        source = self.target.at[source_core * place.members + member] if step else self.source
        return send_copy(
            source,
            self.target.at[target_core * place.members + member],
            self.chip_send.at[slot],
            self.chip_recv.at[slot],
            place.device(place.group, place.member, place.core_at(turn)),
        )

    def start(self):
        place = self.place
        self.own().start()
        for step in range(1, place.members):
            self.link(step, 0).start()
        for turn in range(1, place.batches):
            self.chip(0, turn, place.core, place.core).start()

    def forward(self):
        place = self.place
        for step in range(1, place.members):
            self.link(step, -step).wait_recv()
            for turn in range(1, place.batches):
                self.chip(step, turn, place.core, place.core).start()

    def wait(self):
        place = self.place
        self.own().wait()
        for turn in range(1, place.batches):
            other = place.core_at(-turn)
            for step in range(place.members):
                self.chip(step, turn, place.core, other).wait_recv()

    def drain(self):
        place = self.place
        for step in range(1, place.members):
            self.link(step, 0).wait_send()
        for turn in range(1, place.batches):
            for step in range(place.members):
                self.chip(step, turn, place.core, place.core).wait_send()


class KernelProduct:
    sems = 6

    @staticmethod
    def scratch(place_sizes, kind, wide, narrow):
        groups, members, batches = place_sizes
        pieces, kernel, series, channels = wide.shape
        steps, rows = kernel // members, pieces * series
        half = channels // batches
        piece = (128, half) if kind == "down" else (half, 128)
        dma = pltpu.SemaphoreType.DMA
        return [
            pltpu.VMEM((channels, members * batches * rows), HALF_FLOAT),
            pltpu.VMEM((steps, channels, half), HALF_FLOAT),
            pltpu.VMEM((groups, steps) + piece, HALF_FLOAT),
            pltpu.VMEM((steps, 128, half), HALF_FLOAT),
            pltpu.VMEM((kernel, channels // (groups * members), half), HALF_FLOAT),
            dma((groups * batches,)),
            dma((groups * batches,)),
            dma((members,)),
            dma((members,)),
            dma((2,)),
        ]

    def __init__(self, place, kind, wide_in, narrow_in, out, scratch):
        self.place, self.kind, self.wide_in, self.narrow_in, self.out = (
            place,
            kind,
            wide_in,
            narrow_in,
            out,
        )
        (self.narrow_t, self.send, self.recv, self.total, self.gathered) = scratch[:5]
        (self.sz, self.rz, self.sf, self.rf, self.local) = scratch[5:]
        self.cores_per_group = place.groups // place.batches

    def multiply(self):
        mates, rows = self.narrow_in.shape[0], self.narrow_in.shape[1]
        self.narrow_t[...] = self.narrow_in[...].reshape(mates * rows, -1).T

        @pl.loop(0, self.wide_in.shape[0])
        def _(one):
            data = self.wide_in[one].reshape(mates * rows, -1)
            self.send[one] = dot_nn(self.narrow_t[...], data).astype(HALF_FLOAT)

    def chunk(self, group, core):
        if self.kind == "down":
            return slab(self.send, 1, group, 128)
        half = self.send.shape[1] // self.place.batches
        return slab(
            slab(self.send, 1, core, half), 2, lax.rem(group, self.cores_per_group), 128
        )

    def hops(self):
        place = self.place
        for step in range(place.groups):
            for turn in range(place.batches if self.kind == "up" else 1):
                yield step, turn

    def partial(self, step, turn, action):
        place = self.place
        group, core = place.group_at(step), place.core_at(turn)
        slot = step * place.batches + turn
        if step == 0 and turn == 0:
            copy = pltpu.make_async_copy(
                self.chunk(group, core), self.recv.at[place.group], self.local.at[0]
            )
            act = lambda: action(copy, True)
        else:
            copy = send_copy(
                self.chunk(group, core),
                self.recv.at[place.group],
                self.sz.at[slot],
                self.rz.at[slot],
                place.device(group, place.member, core),
            )
            act = lambda: action(copy, False)
        if self.kind == "down":
            act()
        else:
            pl.when(lax.div(group, self.cores_per_group) == place.core)(act)

    def start_partials(self):
        for step, turn in self.hops():
            self.partial(step, turn, lambda copy, local: copy.start())

    def sum_partials(self):
        place = self.place
        for step, turn in self.hops():
            group, core = place.group_at(-step), place.core_at(-turn)
            slot = step * place.batches + turn

            def act(step=step, turn=turn, group=group, slot=slot):
                if step == 0 and turn == 0:
                    pltpu.make_async_copy(
                        self.chunk(place.group, place.core),
                        self.recv.at[place.group],
                        self.local.at[0],
                    ).wait()
                else:
                    send_copy(
                        self.chunk(place.group, place.core),
                        self.recv.at[group],
                        self.sz.at[slot],
                        self.rz.at[slot],
                        place.device(place.group, place.member, place.core),
                    ).wait_recv()

            if self.kind == "down":
                act()
            else:
                pl.when(lax.div(place.group, self.cores_per_group) == core)(act)

        @pl.loop(0, self.total.shape[0])
        def _(one):
            value = self.recv[0, one].astype(FLOAT)
            for other in range(1, place.groups):
                value = value + self.recv[other, one].astype(FLOAT)
            value = value if self.kind == "down" else value.T
            self.total[one] = value.astype(HALF_FLOAT)

    def final(self, step, pick_step):
        place = self.place
        steps, width = self.total.shape[0], self.gathered.shape[1]
        source = slab(self.total, 1, place.member_at(step), width)
        target = slab(self.gathered, 0, place.member_at(pick_step), steps)
        if step == 0:
            return pltpu.make_async_copy(source, target, self.local.at[1])
        return send_copy(
            source,
            target,
            self.sf.at[step],
            self.rf.at[step],
            place.device(place.group, place.member_at(step), place.core),
        )

    def start_final(self):
        for step in range(self.place.members):
            self.final(step, 0).start()

    def finish(self):
        place = self.place
        self.final(0, 0).wait()
        for step in range(1, place.members):
            self.final(step, -step).wait_recv()
        self.out[...] = self.gathered[...].astype(FLOAT)
        for step in range(1, place.members):
            self.final(step, 0).wait_send()
        for step, turn in self.hops():
            if step or turn:
                self.partial(step, turn, lambda copy, local: copy.wait_send())


class MatrixSum:
    sems = 7

    @staticmethod
    def half_shape(place_sizes, kind, value):
        batches = place_sizes[2]
        shape = list(value.shape)
        if kind == "rows":
            shape[0] //= batches
        elif kind == "lanes":
            shape[-1] //= batches
        return tuple(shape)

    @staticmethod
    def piece_shape(place_sizes, kind, value):
        groups, members, batches = place_sizes
        shape = list(MatrixSum.half_shape(place_sizes, kind, value))
        dim = {"rows": 1, "lanes": len(shape) - 2, "whole": 0}[kind]
        shape[dim] //= groups * members
        return tuple(shape)

    @staticmethod
    def scratch(place_sizes, kind, value):
        groups, members, batches = place_sizes
        half = MatrixSum.half_shape(place_sizes, kind, value)
        piece = MatrixSum.piece_shape(place_sizes, kind, value)
        dma = pltpu.SemaphoreType.DMA
        return [
            pltpu.VMEM(half, value.dtype),
            pltpu.VMEM((batches,) + half, value.dtype),
            pltpu.VMEM((members, groups) + piece, value.dtype),
            pltpu.VMEM((groups,) + piece, value.dtype),
            pltpu.VMEM((groups,) + piece, value.dtype),
            dma((batches,)),
            dma((batches,)),
            dma((members * groups,)),
            dma((members * groups,)),
            dma((groups,)),
            dma((groups,)),
            dma((1 + groups,)),
        ]

    def __init__(self, place, kind, source, out, scratch):
        self.place, self.kind, self.source, self.out = place, kind, source, out
        (self.own, self.others, self.by_member, self.sums, self.by_group) = scratch[:5]
        (self.sb, self.rb, self.sm, self.rm, self.sg, self.rg, self.local) = scratch[5:]
        self.piece_dim = {"rows": 1, "lanes": len(self.own.shape) - 2, "whole": 0}[kind]

    def half(self, core):
        if self.kind == "rows":
            return slab(self.source, 0, core, self.own.shape[0])
        if self.kind == "lanes":
            return slab(self.source, len(self.own.shape) - 1, core, self.own.shape[-1])
        return self.source

    def cores(self, step, pick):
        place = self.place
        core = place.core_at(step)
        return send_copy(
            self.half(core),
            self.others.at[pick],
            self.sb.at[step],
            self.rb.at[step],
            place.device(place.group, place.member, core),
        )

    def load(self):
        return pltpu.make_async_copy(self.half(self.place.core), self.own, self.local.at[0])

    def start(self):
        self.load().start()
        for step in range(1, self.place.batches):
            self.cores(step, self.place.core).start()

    def piece(self, group, member):
        size = self.by_member.shape[2 + self.piece_dim]
        return slab(self.own, self.piece_dim, group * self.place.members + member, size)

    def members(self, step, pick_step, group):
        place = self.place
        member = place.member_at(step)
        slot = step * place.groups + group
        target = self.by_member.at[place.member_at(pick_step), group]
        if step == 0:
            return pltpu.make_async_copy(
                self.piece(group, member), target, self.local.at[1 + group]
            )
        return send_copy(
            self.piece(group, member),
            target,
            self.sm.at[slot],
            self.rm.at[slot],
            place.device(place.group, member, place.core),
        )

    def add_cores(self):
        place = self.place
        self.load().wait()
        for step in range(1, place.batches):
            self.cores(step, place.core_at(-step)).wait_recv()
        rows = self.own.shape[0]
        block = max(size for size in (1, 2, 4, 8, 16, 32, 64) if rows % size == 0)

        @pl.loop(0, rows // block)
        def _(index):
            pick = pl.ds(pl.multiple_of(index * block, block), block)
            value = self.own[pick].astype(FLOAT)
            for step in range(1, place.batches):
                value = value + self.others[place.core_at(step), pick].astype(FLOAT)
            self.own[pick] = value.astype(self.own.dtype)

        for step in range(place.members):
            for group in range(place.groups):
                self.members(step, 0, group).start()

    def groups(self, step, pick_step):
        place = self.place
        group = place.group_at(step)
        return send_copy(
            self.sums.at[group],
            self.by_group.at[place.group_at(pick_step)],
            self.sg.at[step],
            self.rg.at[step],
            place.device(group, place.member, place.core),
        )

    def add_members(self):
        place = self.place
        for step in range(place.members):
            for group in range(place.groups):
                if step == 0:
                    self.members(step, 0, group).wait()
                else:
                    self.members(step, -step, group).wait_recv()

        @pl.loop(0, place.groups)
        def _(group):
            value = self.by_member[0, group].astype(FLOAT)
            for other in range(1, place.members):
                value = value + self.by_member[other, group].astype(FLOAT)
            self.sums[group] = value.astype(self.sums.dtype)

        for step in range(1, place.groups):
            self.groups(step, 0).start()
        self.by_group[place.group] = self.sums[place.group]

    def finish(self):
        place = self.place
        for step in range(1, place.groups):
            self.groups(step, -step).wait_recv()
        value = self.by_group[0].astype(FLOAT)
        for other in range(1, place.groups):
            value = value + self.by_group[other].astype(FLOAT)
        self.out[...] = value
        for step in range(1, place.groups):
            self.groups(step, 0).wait_send()
        for step in range(1, place.members):
            for group in range(place.groups):
                self.members(step, 0, group).wait_send()
        for step in range(1, place.batches):
            self.cores(step, place.core).wait_send()


def remote_call(body, inputs, outputs, scratch, collective_id, flops, nbytes, name):
    def kernel(*refs):
        left = list(refs)
        named = {key: left.pop(0) for key in inputs}
        named.update({key: left.pop(0) for key in outputs})
        for key, shapes in scratch.items():
            named[key] = [left.pop(0) for _ in shapes]
        body(named)

    results = pl.pallas_call(
        kernel,
        out_shape=tuple(shape for shape, _ in outputs.values()),
        in_specs=[spec for _, spec in inputs.values()],
        out_specs=tuple(spec for _, spec in outputs.values()),
        scratch_shapes=[shape for shapes in scratch.values() for shape in shapes],
        compiler_params=pltpu.CompilerParams(
            collective_id=collective_id,
            has_side_effects=True,
            vmem_limit_bytes=63 * 1024 * 1024,
        ),
        cost_estimate=pl.CostEstimate(flops=flops, bytes_accessed=nbytes, transcendentals=0),
        name=name,
    )(*[value for value, _ in inputs.values()])
    return dict(zip(outputs, results))


def plane_sizes(channels):
    devices, batches = lax.axis_size("tm"), lax.axis_size("batch")
    groups = channels // 128
    if batches == 2 and channels % 256 == 0 and devices % groups == 0:
        return groups, devices // groups, batches
    return None


VMEM_SPEC = pl.BlockSpec(memory_space=pltpu.VMEM)
HBM_SPEC = pl.BlockSpec(memory_space=pl.ANY)


class SeriesGradient:
    @staticmethod
    def scratch(weights, outers, rim):
        steps, series, channels = outers[0].shape
        lead = 2 * rim + 8
        dma = pltpu.SemaphoreType.DMA
        rims = (rim, series, channels)
        return (
            [pltpu.VMEM(weight.shape, HALF_FLOAT) for weight in weights]
            + [pltpu.VMEM((steps + 2 * lead, series, channels), FLOAT) for _ in outers]
            + [pltpu.VMEM((channels // 128, steps * series, 128), FLOAT)]
            + [pltpu.VMEM(rims, FLOAT) for _ in range(4)]
            + [dma((4,)), dma((2,)), dma((2,))]
        )

    def __init__(self, weights, outers, out, scratch, halves, rim):
        self.weights, self.outers, self.out = weights, outers, out
        self.halves, self.rim = halves, rim
        count = len(weights)
        self.held, self.grads = scratch[:count], scratch[count : 2 * count]
        (self.result, self.low, self.high, self.before, self.after) = scratch[
            2 * count : 2 * count + 5
        ]
        (self.local, self.send, self.recv) = scratch[2 * count + 5 :]
        self.steps = outers[0].shape[0]
        self.series = outers[0].shape[1]
        self.lead = 2 * rim + 8
        self.me, self.core = lax.axis_index("tm"), lax.axis_index("batch")
        self.last = lax.axis_size("tm") - 1

    def greet(self, barrier):
        @pl.when(self.me > 0)
        def _():
            pl.semaphore_signal(
                barrier, inc=1, device_id=(self.core, self.me - 1), device_id_type=MESH
            )

        @pl.when(self.me < self.last)
        def _():
            pl.semaphore_signal(
                barrier, inc=1, device_id=(self.core, self.me + 1), device_id_type=MESH
            )

        return jnp.where(self.me > 0, 1, 0) + jnp.where(self.me < self.last, 1, 0)

    def loads(self, index):
        return (
            pltpu.make_async_copy(
                self.weights[index], self.held[index], self.local.at[2 * index]
            ),
            pltpu.make_async_copy(
                self.outers[index],
                self.grads[index].at[pl.ds(self.lead, self.steps)],
                self.local.at[2 * index + 1],
            ),
        )

    def start(self):
        for index in range(len(self.held)):
            for copy in self.loads(index):
                copy.start()
            grads = self.grads[index]
            zero = jnp.zeros((self.lead,) + grads.shape[1:], FLOAT)
            grads[: self.lead] = zero
            grads[self.lead + self.steps :] = zero

    def through_down(self, index, grad):
        for copy in self.loads(index):
            copy.wait()
        kernel = self.held[index].shape[0]
        pieces = self.steps // kernel
        grads = self.grads[index]

        @pl.loop(0, kernel)
        def _(one):
            value = dot_nt(grad, self.held[index][one])
            for piece in range(pieces):
                row = self.lead + piece * kernel + one
                grads[row] = (
                    grads[row] + value[piece * self.series : (piece + 1) * self.series]
                )

    def store(self, place, value, add=False):
        for lane in range(self.result.shape[0]):
            part = value[:, lane * 128 : lane * 128 + 128]
            self.result[lane, place] = self.result[lane, place] - part if add else part

    def adjoint(self):
        def means(index, sums):
            out, total = [], 0.0
            for grads, half, value in zip(self.grads, self.halves, sums):
                high = grads[index + (self.lead - self.rim + half)]
                low = grads[index + (self.lead - self.rim - half - 1)]
                value = value + high - low
                out.append(value)
                total = total + value * (1.0 / (2 * half + 1))
            return tuple(out), total

        def low_step(index, sums):
            sums, total = means(index, sums)
            self.low[index] = total
            return sums

        def step(index, sums):
            sums, total = means(index + self.rim, sums)
            value = self.grads[0][self.lead + index] + self.grads[1][self.lead + index]
            place = pl.ds(pl.multiple_of(index * self.series, self.series), self.series)
            self.store(place, value - total)
            return sums

        def high_step(index, sums):
            sums, total = means(index + (self.rim + self.steps), sums)
            self.high[index] = total
            return sums

        zero = jnp.zeros(self.low.shape[1:], FLOAT)
        sums = lax.fori_loop(0, self.rim, low_step, (zero, zero))
        sums = lax.fori_loop(0, self.steps, step, sums)
        lax.fori_loop(0, self.rim, high_step, sums)

    def edge(self, up):
        source, target = (self.high, self.before) if up else (self.low, self.after)
        index = 0 if up else 1
        return send_copy(
            source,
            target,
            self.send.at[index],
            self.recv.at[index],
            (self.core, self.me + 1 if up else self.me - 1),
        )

    def send_edges(self):
        pl.when(self.me < self.last)(lambda: self.edge(True).start())
        pl.when(self.me > 0)(lambda: self.edge(False).start())

    def finish(self):
        series = self.series
        rows, end = self.rim * series, self.steps * series

        @pl.when(self.me > 0)
        def _():
            self.edge(True).wait_recv()
            self.store(pl.ds(0, rows), self.before[...].reshape(rows, -1), True)

        @pl.when(self.me == 0)
        def _():
            total = self.low[0]
            for index in range(1, self.rim):
                total = total + self.low[index]
            self.store(pl.ds(0, series), total, True)

        @pl.when(self.me < self.last)
        def _():
            self.edge(False).wait_recv()
            self.store(pl.ds(end - rows, rows), self.after[...].reshape(rows, -1), True)

        @pl.when(self.me == self.last)
        def _():
            total = self.high[0]
            for index in range(1, self.rim):
                total = total + self.high[index]
            self.store(pl.ds(end - series, series), total, True)

        for one in range(self.out.shape[0]):
            for lane in range(self.result.shape[0]):
                value = self.result[lane, pl.ds(one, self.steps, stride=series), :]
                self.out[one, :, lane * 128 : lane * 128 + 128] = value.astype(HALF_FLOAT)
        pl.when(self.me < self.last)(lambda: self.edge(True).wait_send())
        pl.when(self.me > 0)(lambda: self.edge(False).wait_send())


def down_gradients(sizes, wides, narrows, vectors, weights, outers, halves, rim, count, matrices):
    groups, members, batches = sizes
    half = wides[0].shape[4]
    channels = half * batches
    inputs, outputs, scratch = {}, {}, {}
    for index, (wide, narrow) in enumerate(zip(wides, narrows)):
        steps = wide.shape[0] * members
        shape = jax.ShapeDtypeStruct(
            (wide.shape[2], steps, wide.shape[3], channels), HALF_FLOAT
        )
        inputs[f"wide{index}"] = (wide, VMEM_SPEC)
        inputs[f"narrow{index}"] = (narrow, HBM_SPEC)
        outputs[f"out{index}"] = (
            jax.ShapeDtypeStruct((steps, channels // (groups * members), half), FLOAT),
            VMEM_SPEC,
        )
        scratch[f"rows{index}"] = [
            pltpu.VMEM((members * batches,) + narrow.shape, HALF_FLOAT)
        ]
        scratch[f"gather{index}"] = NarrowGather.scratch(sizes, narrow)
        scratch[f"product{index}"] = KernelProduct.scratch(sizes, "down", shape, narrow)
    for index in range(len(wides)):
        inputs[f"weight{index}"] = (weights[index], HBM_SPEC)
        inputs[f"outer{index}"] = (outers[index], HBM_SPEC)
    scratch["series"] = SeriesGradient.scratch(weights, outers, rim)
    outputs["grad_series"] = (
        jax.ShapeDtypeStruct((count, outers[0].shape[0], channels), HALF_FLOAT),
        VMEM_SPEC,
    )
    for index, (kind, value) in enumerate(matrices):
        inputs[f"matrix{index}"] = (value, HBM_SPEC)
        outputs[f"matrix_sum{index}"] = (
            jax.ShapeDtypeStruct(MatrixSum.piece_shape(sizes, kind, value), FLOAT),
            VMEM_SPEC,
        )
        scratch[f"parts{index}"] = MatrixSum.scratch(sizes, kind, value)
    inputs["vectors"] = (vectors, VMEM_SPEC)
    outputs["vector_sum"] = (jax.ShapeDtypeStruct(vectors.shape, FLOAT), VMEM_SPEC)
    scratch["vector"] = VectorSum.scratch(sizes, vectors)

    def body(refs):
        place = Place(*sizes)
        back = SeriesGradient(
            [refs[f"weight{index}"] for index in range(len(wides))],
            [refs[f"outer{index}"] for index in range(len(wides))],
            refs["grad_series"],
            refs["series"],
            halves,
            rim,
        )
        barrier = pltpu.get_barrier_semaphore()
        pl.semaphore_wait(barrier, place.greet(barrier) + back.greet(barrier))
        gathers, products = [], []
        for index in range(len(wides)):
            gathers.append(
                NarrowGather(
                    place,
                    refs[f"narrow{index}"],
                    refs[f"rows{index}"][0],
                    refs[f"gather{index}"],
                )
            )
            products.append(
                KernelProduct(
                    place,
                    "down",
                    refs[f"wide{index}"],
                    refs[f"rows{index}"][0],
                    refs[f"out{index}"],
                    refs[f"product{index}"],
                )
            )
        total = VectorSum(place, refs["vectors"], refs["vector_sum"], refs["vector"])
        sums = [
            MatrixSum(
                place, kind, refs[f"matrix{i}"], refs[f"matrix_sum{i}"], refs[f"parts{i}"]
            )
            for i, (kind, _) in enumerate(matrices)
        ]
        order = list(range(len(wides)))[::-1]
        for index in order:
            gathers[index].start()
        for item in sums:
            item.start()
        total.start(0)
        back.start()
        for index in order:
            gathers[index].forward()
            gathers[index].wait()
            products[index].multiply()
            products[index].start_partials()
        for item in sums:
            item.add_cores()
        total.add(0)
        mine = place.core * members + place.member
        for index in range(len(wides)):
            back.through_down(index, refs[f"rows{index}"][0][mine])
        back.adjoint()
        back.send_edges()
        total.add(1)
        for item in sums:
            item.add_members()
        for index in order:
            products[index].sum_partials()
            products[index].start_final()
        total.add(2)
        back.finish()
        for item in sums:
            item.finish()
        for product in products:
            product.finish()
        for gather in gathers:
            gather.drain()
        total.drain()

    flops = sum(2 * wide.size * channels for wide in wides)
    results = remote_call(
        body, inputs, outputs, scratch, 2, flops, 8 * flops // channels, "down_gradients"
    )
    return (
        [results["out0"], results["out1"]],
        results["vector_sum"],
        results["grad_series"],
        [results[f"matrix_sum{index}"] for index in range(len(matrices))],
    )


def iso_gradient_kernel(lane_ref, spec_ref, specs_ref, grad_ref, grads_ref, out_ref):
    bins, _, half, channels = out_ref.shape
    rows = spec_ref.shape[0] // bins
    devices = rows // 2
    for one in range(bins):
        place = slice(one * rows, (one + 1) * rows)
        spec = [spec_ref[place]] + [specs_ref[i, place] for i in range(specs_ref.shape[0])]
        grad = [grad_ref[place]] + [grads_ref[i, place] for i in range(grads_ref.shape[0])]
        turned = [jnp.concatenate([value[devices:], -value[:devices]]) for value in grad]
        both = jnp.concatenate([jnp.concatenate(grad), jnp.concatenate(turned)], axis=1)
        value = lax.dot_general(
            jnp.concatenate(spec), both, (((0,), (0,)), ((), ())), preferred_element_type=FLOAT
        )
        out_ref[one, 0] = value[:, :channels]
        out_ref[one, 1] = value[:, channels:]


def iso_gradients(spec, specs, grad, grads, first, bins):
    rows, channels = 2 * lax.axis_size("tm"), grad.shape[1]
    half = channels // lax.axis_size("batch")
    others = specs.shape[0]
    block = 2 if bins % 2 == 0 and first % 2 == 0 else 1
    rows, first = rows * block, first // block
    core = lax.axis_index("batch")
    if half % 128:
        spec = lax.dynamic_slice_in_dim(spec, core * half, half, axis=1)
        specs = lax.dynamic_slice_in_dim(specs, core * half, half, axis=2)
        core = 0
    return pl.pallas_call(
        iso_gradient_kernel,
        out_shape=jax.ShapeDtypeStruct((bins, 2, half, channels), FLOAT),
        grid_spec=pltpu.PrefetchScalarGridSpec(
            num_scalar_prefetch=1,
            grid=(bins // block,),
            in_specs=[
                pl.BlockSpec((rows, half), lambda i, lane: (first + i, lane[0])),
                pl.BlockSpec((others, rows, half), lambda i, lane: (0, first + i, lane[0])),
                pl.BlockSpec((rows, channels), lambda i, lane: (first + i, 0)),
                pl.BlockSpec((others, rows, channels), lambda i, lane: (0, first + i, 0)),
            ],
            out_specs=pl.BlockSpec((block, 2, half, channels), lambda i, lane: (i, 0, 0, 0)),
        ),
        cost_estimate=pl.CostEstimate(
            flops=4 * (bins // block) * rows * (1 + others) * half * channels,
            bytes_accessed=8 * bins * half * channels,
            transcendentals=0,
        ),
        name="iso_gradients",
    )(jnp.full((1,), core, jnp.int32), spec, specs, grad, grads)


class RowProducts:
    @staticmethod
    def scratch(jobs):
        rows, channels = jobs[0][0].shape
        most = max(sum(right.shape[1] for right in rights) for _, rights in jobs)
        return [
            pltpu.VMEM((rows, channels), HALF_FLOAT),
            pltpu.VMEM((channels, rows), HALF_FLOAT),
            pltpu.VMEM((rows, most), HALF_FLOAT),
            pltpu.SemaphoreType.DMA((1 + max(len(rights) for _, rights in jobs),)),
        ]

    def __init__(self, jobs, scratch):
        self.jobs = jobs
        self.left, self.turned, self.right, self.sem = scratch
        self.next = 0

    def copies(self, index):
        left, rights, _ = self.jobs[index]
        copies = [pltpu.make_async_copy(left, self.left, self.sem.at[0])]
        for k, right in enumerate(rights):
            width = right.shape[1]
            target = self.right.at[:, pl.ds(k * width, width)]
            copies.append(pltpu.make_async_copy(right, target, self.sem.at[1 + k]))
        return copies

    def load(self):
        if self.next < len(self.jobs):
            for copy in self.copies(self.next):
                copy.start()

    def run(self):
        index, self.next = self.next, self.next + 1
        for copy in self.copies(index):
            copy.wait()
        self.turned[...] = self.left[...].T
        out = self.jobs[index][2]
        channels = self.left.shape[1]
        width = sum(right.shape[1] for right in self.jobs[index][1])
        for k in range(width // channels):
            chunk = pl.ds(k * channels, channels)
            value = dot_nn(self.turned[...], self.right[:, chunk]).astype(HALF_FLOAT)
            if len(out.shape) == 3:
                out[k] = value
            else:
                out[:, chunk] = value
        self.load()


class Extra:
    def __init__(self, sizes):
        self.sizes = sizes
        self.inputs, self.outputs, self.scratch = {}, {}, {}

    def bind(self, refs):
        self.refs = refs
        self.place = Place(*self.sizes) if self.sizes else None

    def greet(self, barrier):
        return self.place.greet(barrier) if self.sizes else 0

    def open(self):
        pass

    def prepare(self):
        return self.refs["x"]

    def start(self):
        pass

    def after_bins(self):
        pass

    def after_spec(self):
        pass

    def after_mixed(self):
        pass

    def after_signal(self):
        pass

    def finish(self):
        pass

    def run(self, share):
        count = max(1, round(share * self.unit_count))
        for _ in range(min(count, len(self.units))):
            self.units.pop(0)()


class Turn:
    block = 64

    @staticmethod
    def scratch(weight):
        channels, kernel, outs = weight.shape
        dma = pltpu.SemaphoreType.DMA
        return [
            pltpu.VMEM((2, Turn.block, kernel, outs), HALF_FLOAT),
            pltpu.VMEM((2, kernel, Turn.block, outs), HALF_FLOAT),
            dma((2,)),
            dma((2,)),
        ]

    def __init__(self, source, target, scratch):
        self.source, self.target = source, target
        self.read, self.turned, self.in_sem, self.out_sem = scratch
        self.total = source.shape[0] // self.block
        self.done = 0

    def load(self, index, slot):
        place = pl.ds(pl.multiple_of(index * self.block, self.block), self.block)
        return pltpu.make_async_copy(
            self.source.at[place], self.read.at[slot], self.in_sem.at[slot]
        )

    def store(self, index, slot):
        place = pl.ds(pl.multiple_of(index * self.block, self.block), self.block)
        return pltpu.make_async_copy(
            self.turned.at[slot], self.target.at[:, place], self.out_sem.at[slot]
        )

    def start(self):
        self.load(0, 0).start()

    def run(self, share):
        first, self.done = self.done, min(self.total, self.done + math.ceil(share * self.total))

        @pl.loop(first, self.done)
        def _(index):
            slot = lax.rem(index, 2)
            self.load(index, slot).wait()

            @pl.when(index + 1 < self.total)
            def _():
                self.load(index + 1, 1 - slot).start()

            @pl.when(index >= 2)
            def _():
                self.store(index - 2, slot).wait()

            self.turned[slot] = pltpu.einshape("mhd->hmd", self.read[slot])
            self.store(index, slot).start()

    def finish(self):
        self.run(1.0)
        for index in range(max(0, self.total - 2), self.total):
            self.store(index, index % 2).wait()


def by_piece(signal, rows, count):
    per_time = signal.shape[0] // count
    width = rows.shape[1] // per_time
    for lane in range(rows.shape[0]):
        value = signal[:, lane * 128 : lane * 128 + 128]
        rows[lane, : signal.shape[0], :] = value.astype(FLOAT)
        if width > count:
            rows[lane, signal.shape[0] :, :] = jnp.zeros(
                (rows.shape[1] - signal.shape[0], 128), FLOAT
            )

    def piece(index):
        return jnp.concatenate(
            [rows[lane, pl.ds(index, width, stride=per_time), :] for lane in range(rows.shape[0])],
            axis=1,
        )

    return lambda first, size: jnp.concatenate([piece(first + i) for i in range(size)])


class Front:
    halo = 16

    @staticmethod
    def scratch(series, weights, per_time, rim):
        count, steps, channels = series.shape
        wide, lanes = round_up(count, 16), channels // 128
        rows = max(steps // weight.shape[0] for weight in weights) * wide
        dma = pltpu.SemaphoreType.DMA
        return (
            [pltpu.VMEM(weight.shape, HALF_FLOAT) for weight in weights]
            + [
                pltpu.VMEM(series.shape, HALF_FLOAT),
                pltpu.VMEM((count, Front.halo, channels), HALF_FLOAT),
                pltpu.VMEM((count, Front.halo, channels), HALF_FLOAT),
                pltpu.VMEM((lanes, (steps + 2 * rim + 1) * wide, 128), FLOAT),
                pltpu.VMEM((lanes, per_time * wide, 128), FLOAT),
                pltpu.VMEM((rows, channels), FLOAT),
                pltpu.VMEM((count * per_time, channels), HALF_FLOAT),
            ]
            + [dma((1 + len(weights),)), dma((2,)), dma((2,))]
        )

    def __init__(self, source, weights, bias, seasonals, acts, scratch, halves, rim):
        self.source, self.weights, self.bias = source, weights, bias
        self.seasonals, self.acts, self.halves, self.rim = seasonals, acts, halves, rim
        self.held = scratch[: len(weights)]
        (self.series, self.before, self.after, self.wide, self.rows, self.total, self.x) = (
            scratch[len(weights) : len(weights) + 7]
        )
        (self.local, self.send, self.recv) = scratch[len(weights) + 7 :]
        self.count, self.steps, _ = source.shape
        self.width = seasonals[0].shape[2]
        self.me, self.core = lax.axis_index("tm"), lax.axis_index("batch")
        self.last = lax.axis_size("tm") - 1

    def loads(self):
        return [pltpu.make_async_copy(self.source, self.series, self.local.at[0])] + [
            pltpu.make_async_copy(weight, held, self.local.at[1 + index])
            for index, (weight, held) in enumerate(zip(self.weights, self.held))
        ]

    def edge(self, up):
        first = self.steps - self.halo if up else 0
        index = 0 if up else 1
        return send_copy(
            self.source.at[:, pl.ds(first, self.halo)],
            self.before if up else self.after,
            self.send.at[index],
            self.recv.at[index],
            (self.core, self.me + 1 if up else self.me - 1),
        )

    def start(self):
        pl.when(self.me < self.last)(lambda: self.edge(True).start())
        pl.when(self.me > 0)(lambda: self.edge(False).start())
        for copy in self.loads():
            copy.start()

    def spread(self, values, first, count):
        for lane in range(self.wide.shape[0]):
            self.wide[lane, pl.ds(first, count, stride=self.width), :] = values[
                :, lane * 128 : lane * 128 + 128
            ]

    def step(self, index):
        place = pl.ds(pl.multiple_of(index * self.width, self.width), self.width)
        return jnp.concatenate(
            [self.wide[lane, place, :] for lane in range(self.wide.shape[0])], axis=1
        )

    def repeat(self, index, first):
        value = self.step(index)
        for row in range(self.rim):
            place = pl.ds((first + row) * self.width, self.width)
            for lane in range(self.wide.shape[0]):
                self.wide[lane, place, :] = value[:, lane * 128 : lane * 128 + 128]

    def layers(self, ready):
        rim, steps, width = self.rim, self.steps, self.width
        self.wide[...] = jnp.zeros_like(self.wide)
        copies = self.loads()
        copies[0].wait()
        for one in range(self.count):
            self.spread(self.series[one].astype(FLOAT), rim * width + one, steps)

        @pl.when(self.me > 0)
        def _():
            self.edge(True).wait_recv()
            for one in range(self.count):
                self.spread(self.before[one].astype(FLOAT)[self.halo - rim :], one, rim)

        @pl.when(self.me < self.last)
        def _():
            self.edge(False).wait_recv()
            for one in range(self.count):
                first = (rim + steps) * width + one
                self.spread(self.after[one].astype(FLOAT)[:rim], first, rim)

        pl.when(self.me == 0)(lambda: self.repeat(rim, 0))
        pl.when(self.me == self.last)(lambda: self.repeat(rim + steps - 1, rim + steps))
        sums = []
        for half in self.halves:
            value = self.step(rim - half)
            for index in range(rim - half + 1, rim + half + 1):
                value = value + self.step(index)
            sums.append(value)

        def move(index, sums):
            here, later = self.step(index + rim), []
            for seasonal, half, value in zip(self.seasonals, self.halves, sums):
                kernel = seasonal.shape[1]
                part = here - value * (1.0 / (2 * half + 1))
                seasonal[lax.div(index, kernel), lax.rem(index, kernel)] = part.astype(
                    HALF_FLOAT
                )
                later.append(
                    value + self.step(index + rim + half + 1) - self.step(index + rim - half)
                )
            return tuple(later)

        lax.fori_loop(0, steps, move, tuple(sums))
        ready()
        self.rows[...] = jnp.zeros_like(self.rows)
        base = 0
        for index, (seasonal, held, act) in enumerate(zip(self.seasonals, self.held, self.acts)):
            copies[1 + index].wait()
            count = act.shape[0]
            total = self.total.at[pl.ds(0, count)]
            total[...] = jnp.broadcast_to(self.bias[index : index + 1], total.shape)

            @pl.loop(0, seasonal.shape[1])
            def _(one, total=total, seasonal=seasonal, held=held):
                total[...] += dot_nn(seasonal[:, one].reshape(total.shape), held[one])

            value = jnp.tanh(total[...])
            act[...] = value
            value = value.astype(HALF_FLOAT).astype(FLOAT)
            for lane in range(self.rows.shape[0]):
                self.rows[lane, pl.ds(base * width, count), :] = value[
                    :, lane * 128 : lane * 128 + 128
                ]
            base += round_up(count // width, 8)
        per_time = self.x.shape[0] // self.count
        for one in range(self.count):
            for lane in range(self.rows.shape[0]):
                value = self.rows[lane, pl.ds(one, per_time, stride=width), :]
                self.x[
                    one * per_time : (one + 1) * per_time, lane * 128 : lane * 128 + 128
                ] = value.astype(HALF_FLOAT)

    def finish(self):
        pl.when(self.me < self.last)(lambda: self.edge(True).wait_send())
        pl.when(self.me > 0)(lambda: self.edge(False).wait_send())

    def turn(self, source):
        return pltpu.make_async_copy(source, self.series, self.local.at[0])

    def turned(self, source, target):
        self.turn(source).wait()
        for one in range(self.count):
            self.spread(self.series[one].astype(FLOAT), self.rim * self.width + one, self.steps)

        @pl.loop(0, self.steps)
        def _(index):
            target[index] = self.step(index + self.rim).astype(HALF_FLOAT)


class ForwardExtra(Extra):
    def __init__(self, sizes, wides, weights, front):
        super().__init__(sizes)
        self.front = front
        if front:
            series, cotangent, down_weights, bias, per_time, halves, rim = front
            count, steps, channels = series.shape
            series_rows = round_up(count, 16)
            self.inputs["series"] = (series, HBM_SPEC)
            self.inputs["down_bias"] = (bias, VMEM_SPEC)
            for index, weight in enumerate(down_weights):
                kernel = weight.shape[0]
                self.inputs[f"down{index}"] = (weight, HBM_SPEC)
                self.outputs[f"seasonal{index}"] = (
                    jax.ShapeDtypeStruct(
                        (steps // kernel, kernel, series_rows, channels), HALF_FLOAT
                    ),
                    VMEM_SPEC,
                )
                self.outputs[f"down_act{index}"] = (
                    jax.ShapeDtypeStruct((steps // kernel * series_rows, channels), FLOAT),
                    VMEM_SPEC,
                )
                rows = self.outputs[f"down_act{index}"][0].shape
                self.outputs[f"iso_act{index}"] = (
                    jax.ShapeDtypeStruct(rows, FLOAT),
                    VMEM_SPEC,
                )
                self.outputs[f"inner{index}"] = (
                    jax.ShapeDtypeStruct(rows, HALF_FLOAT),
                    VMEM_SPEC,
                )
            self.inputs["cotangent"] = (cotangent, HBM_SPEC)
            self.outputs["cotangent_steps"] = (
                jax.ShapeDtypeStruct((steps, series_rows, channels), HALF_FLOAT),
                VMEM_SPEC,
            )
            self.scratch["front"] = Front.scratch(series, down_weights, per_time, rim)
            wides = [self.outputs[f"seasonal{index}"][0] for index in range(len(down_weights))]
        self.turn_count = len(weights)
        for index, weight in enumerate(weights):
            channels, kernel, outs = weight.shape
            self.inputs[f"turn{index}"] = (weight, HBM_SPEC)
            self.outputs[f"turned{index}"] = (
                jax.ShapeDtypeStruct((kernel, channels, outs), HALF_FLOAT),
                HBM_SPEC,
            )
            self.scratch[f"turning{index}"] = Turn.scratch(weight)
        self.count = len(wides) if sizes else 0
        for index in range(self.count):
            if not front:
                self.inputs[f"wide{index}"] = (wides[index], HBM_SPEC)
            self.outputs[f"gathered{index}"] = (
                jax.ShapeDtypeStruct(WideExchange.shape(sizes, wides[index]), HALF_FLOAT),
                HBM_SPEC,
            )
            self.scratch[f"exchange{index}"] = WideExchange.scratch(sizes, wides[index])

    def bind(self, refs):
        super().bind(refs)
        self.exchanges = [
            WideExchange(
                self.place,
                refs[f"seasonal{i}" if self.front else f"wide{i}"],
                refs[f"gathered{i}"],
                refs[f"exchange{i}"],
            )
            for i in range(self.count)
        ]
        self.units = [unit for item in self.exchanges for unit in item.units()]
        self.unit_count = len(self.units)
        self.turns = [
            Turn(refs[f"turn{i}"], refs[f"turned{i}"], refs[f"turning{i}"])
            for i in range(self.turn_count)
        ]

    def inner(self):
        refs, base = self.refs, 0
        count = self.front[0].shape[0]
        rows = by_piece(refs["signal"], self.layers.rows, count)
        table = refs["down_bias"]
        for index in range(self.count):
            act_ref = refs[f"iso_act{index}"]
            pieces = act_ref.shape[0] // self.layers.width
            act = jnp.tanh(rows(base, pieces) + table[2 + index : 3 + index])
            down = refs[f"down_act{index}"][...].astype(HALF_FLOAT).astype(FLOAT)
            hat, _ = normed(act + down)
            act_ref[...] = act
            out = hat * table[8:9] + table[11:12]
            refs[f"inner{index}"][...] = out.astype(HALF_FLOAT)
            base += round_up(pieces, 8)

    def open(self):
        for item in self.turns:
            item.start()
        if not self.front:
            return
        refs, count = self.refs, self.count
        halves, rim = self.front[5:]
        self.layers = Front(
            refs["series"],
            [refs[f"down{i}"] for i in range(count)],
            refs["down_bias"],
            [refs[f"seasonal{i}"] for i in range(count)],
            [refs[f"down_act{i}"] for i in range(count)],
            refs["front"],
            halves,
            rim,
        )
        self.layers.start()

    def prepare(self):
        if not self.front:
            return super().prepare()
        self.layers.layers(functools.partial(self.run, 0.45))
        return self.layers.x

    def start(self):
        self.run(0.15)
        if self.front:
            self.layers.turn(self.refs["cotangent"]).start()
        for item in self.turns:
            item.run(0.25)

    def after_bins(self):
        self.run(0.55)
        if self.front:
            self.layers.turned(self.refs["cotangent"], self.refs["cotangent_steps"])
        for item in self.turns:
            item.run(0.25)

    def after_mixed(self):
        self.run(1.0)
        for item in self.turns:
            item.run(0.375)

    def after_signal(self):
        for item in self.turns:
            item.run(0.125)

    def finish(self):
        if self.front:
            self.inner()
            self.layers.finish()
        for item in self.turns:
            item.finish()
        for item in self.exchanges:
            item.wait()
            item.drain()


class BackwardExtra(Extra):
    def __init__(self, sizes, spec, wides, narrows, jobs, inners, acts, counts):
        super().__init__(sizes)
        self.counts = counts
        if sizes:
            for i, (inner, act) in enumerate(zip(inners, acts)):
                self.inputs[f"inner_grad{i}"] = (inner, VMEM_SPEC)
                self.inputs[f"act{i}"] = (act, VMEM_SPEC)
                self.outputs[f"down_grad{i}"] = (
                    jax.ShapeDtypeStruct(act.shape, HALF_FLOAT),
                    VMEM_SPEC,
                )
            channels = spec.shape[1]
            self.outputs["down_sums"] = (jax.ShapeDtypeStruct((8, channels), FLOAT), VMEM_SPEC)
            per_time, width = counts[1:]
            self.scratch["piece_rows"] = [
                pltpu.VMEM((channels // 128, per_time * width, 128), FLOAT)
            ]
        self.batches = lax.axis_size("batch")
        others = jax.ShapeDtypeStruct((self.batches - 1,) + spec.shape, HALF_FLOAT)
        self.inputs["spec_forward"] = (spec, HBM_SPEC)
        self.outputs["specs"] = (others, HBM_SPEC)
        self.outputs["grads"] = (others, HBM_SPEC)
        dma = pltpu.SemaphoreType.DMA
        self.scratch["other_sems"] = [dma((self.batches,))] * 4
        self.count = len(wides) if sizes else 0
        self.job_sizes = [len(rights) for _, rights, _ in jobs] if sizes else []
        if sizes:
            for i, (left, rights, shape) in enumerate(jobs):
                self.inputs[f"left{i}"] = (left, HBM_SPEC)
                for k, right in enumerate(rights):
                    self.inputs[f"right{i}_{k}"] = (right, HBM_SPEC)
                self.outputs[f"matrix{i}"] = (
                    jax.ShapeDtypeStruct(shape, HALF_FLOAT),
                    VMEM_SPEC,
                )
            self.scratch["row_products"] = RowProducts.scratch(
                [(left, rights) for left, rights, _ in jobs]
            )
        for i in range(self.count):
            wide, narrow = wides[i], narrows[i]
            groups, members, batches = sizes
            channels = narrow.shape[1]
            self.inputs[f"wide{i}"] = (wide, HBM_SPEC)
            self.inputs[f"narrow{i}"] = (narrow, HBM_SPEC)
            self.outputs[f"up{i}"] = (
                jax.ShapeDtypeStruct(
                    (wide.shape[1], channels // (groups * members), channels // batches), FLOAT
                ),
                VMEM_SPEC,
            )
            self.scratch[f"wide_in{i}"] = [
                pltpu.VMEM(WideExchange.shape(sizes, wide), HALF_FLOAT)
            ]
            self.scratch[f"rows{i}"] = [
                pltpu.VMEM((members * batches,) + narrow.shape, HALF_FLOAT)
            ]
            self.scratch[f"exchange{i}"] = WideExchange.scratch(sizes, wide)
            self.scratch[f"gather{i}"] = NarrowGather.scratch(sizes, narrow)
            self.scratch[f"product{i}"] = KernelProduct.scratch(sizes, "up", wide, narrow)

    def bind(self, refs):
        super().bind(refs)
        self.exchanges, self.gathers, self.products = [], [], []
        for i in range(self.count):
            wide_in, rows = refs[f"wide_in{i}"][0], refs[f"rows{i}"][0]
            self.exchanges.append(
                WideExchange(self.place, refs[f"wide{i}"], wide_in, refs[f"exchange{i}"])
            )
            self.gathers.append(
                NarrowGather(self.place, refs[f"narrow{i}"], rows, refs[f"gather{i}"])
            )
            self.products.append(
                KernelProduct(self.place, "up", wide_in, rows, refs[f"up{i}"], refs[f"product{i}"])
            )
        jobs = [
            (
                refs[f"left{i}"],
                [refs[f"right{i}_{k}"] for k in range(size)],
                refs[f"matrix{i}"],
            )
            for i, size in enumerate(self.job_sizes)
        ]
        self.row_products = RowProducts(jobs, refs["row_products"]) if jobs else None

    def other(self, index, turn):
        source, target = (
            (self.refs["spec_forward"], self.refs["specs"]),
            (self.refs["spec"], self.refs["grads"]),
        )[index]
        sems = self.refs["other_sems"]
        core = lax.rem(lax.axis_index("batch") + turn, self.batches)
        return send_copy(
            source,
            target.at[turn - 1],
            sems[2 * index].at[turn],
            sems[2 * index + 1].at[turn],
            (core, lax.axis_index("tm")),
        )

    def start(self):
        self.units = [unit for item in self.exchanges[::-1] for unit in item.units()]
        self.unit_count = len(self.units)
        for turn in range(1, self.batches):
            self.other(0, turn).start()
        for item in self.gathers:
            item.start()
        if self.row_products:
            self.row_products.load()

    def after_bins(self):
        self.run(0.6)
        for item in self.gathers:
            item.forward()
        if self.row_products:
            self.row_products.run()

    def after_mixed(self):
        self.run(1.0)

    def after_spec(self):
        for turn in range(1, self.batches):
            self.other(1, turn).start()

    def multiply(self, index):
        self.exchanges[index].wait()
        self.gathers[index].wait()
        self.products[index].multiply()
        self.products[index].start_partials()

    def after_signal(self):
        for index in range(self.count)[::-1]:
            self.multiply(index)

    def down_grads(self):
        refs, base = self.refs, 0
        count, _, width = self.counts
        rows = by_piece(refs["signal"], refs["piece_rows"][0], count)
        refs["down_sums"][...] = jnp.zeros_like(refs["down_sums"])
        for index in range(self.count):
            act = refs[f"act{index}"][...]
            pieces = act.shape[0] // width
            grad = rows(base, pieces) + refs[f"inner_grad{index}"][...]
            grad = (grad * (1.0 - act * act)).astype(HALF_FLOAT)
            refs[f"down_grad{index}"][...] = grad
            refs["down_sums"][index : index + 1] = jnp.sum(
                grad.astype(FLOAT), axis=0, keepdims=True
            )
            base += round_up(pieces, 8)

    def finish(self):
        if self.count:
            self.down_grads()
            for _ in range(1, len(self.job_sizes)):
                self.row_products.run()
        for item in self.products[::-1]:
            item.sum_partials()
            item.start_final()
        for item in self.products:
            item.finish()
        for item in self.exchanges + self.gathers:
            item.drain()
        for index in range(2):
            for turn in range(1, self.batches):
                self.other(index, turn).wait()


def spectral(values, shapes, weights, back, extra):
    devices, batches = lax.axis_size("tm"), lax.axis_size("batch")
    pieces_list = tuple(shape[1] for shape in shapes)
    count, _, channels = shapes[0]
    wide = [round_up(pieces, 8) for pieces in pieces_list]
    per_time, per_bin = sum(wide), 2 * sum(wide)
    assert count <= devices and per_time % 16 == 0
    inputs = {}
    if values:
        packed = jnp.concatenate(
            [
                jnp.pad(value, ((0, 0), (0, room - value.shape[1]), (0, 0)))
                for value, room in zip(values, wide)
            ],
            axis=1,
        ).reshape(count * per_time, channels)
        inputs["x"] = (packed, HBM_SPEC)
    table = spectral_constants(devices, pieces_list)
    rows_time, rows_bin = devices * per_time, devices * per_bin
    dma = pltpu.SemaphoreType.DMA
    for index, weight in enumerate(weights):
        inputs[f"weight{index}"] = (weight, HBM_SPEC)
    inputs["table"] = (table, VMEM_SPEC)
    outputs = {
        "spec": (jax.ShapeDtypeStruct((rows_bin, channels), HALF_FLOAT), VMEM_SPEC),
        "signal": (jax.ShapeDtypeStruct((count * per_time, channels), HALF_FLOAT), VMEM_SPEC),
    }
    scratch = {
        "buffers": [pltpu.VMEM((rows_time, channels), HALF_FLOAT)]
        + [pltpu.VMEM((rows_bin, channels), HALF_FLOAT)] * 5
        + [pltpu.VMEM((rows_time, channels), HALF_FLOAT)]
        + [
            pltpu.VMEM((weight.shape[0], 2, weight.shape[2] * batches, channels), HALF_FLOAT)
            for weight in weights
        ],
        "tables": [
            pltpu.VMEM((2, rows_time, rows_bin), HALF_FLOAT),
            pltpu.VMEM((rows_bin, rows_bin), HALF_FLOAT),
            pltpu.VMEM((rows_bin, rows_bin), HALF_FLOAT),
        ],
        "sems": [dma((devices,))] * 8 + [dma((2, batches)), dma((2, batches)), dma((3,))],
    }
    inputs.update(extra.inputs)
    outputs.update(extra.outputs)
    scratch.update(extra.scratch)
    sizes = (devices, batches, count, pieces_list)

    def body(refs):
        extra.bind(refs)
        spectral_body(sizes, back, refs, extra)

    results = remote_call(
        body,
        inputs,
        outputs,
        scratch,
        1 if back else 0,
        2 * rows_bin * channels * channels * 4,
        4 * channels * channels * sum(pieces_list),
        "spectral_back" if back else "spectral_forward",
    )
    signal = results["signal"].reshape(count, per_time, channels)
    signals, offset = [], 0
    for pieces, room in zip(pieces_list, wide):
        signals.append(signal[:, offset : offset + pieces])
        offset += room
    return results, signals


def gelu_pair(value):
    slope = math.sqrt(2.0 / math.pi)
    square = value * value
    bent = jnp.tanh(slope * value * (1.0 + 0.044715 * square))
    rise = 0.5 * (1.0 + bent)
    turn = 0.5 * slope * value * (1.0 - bent * bent) * (1.0 + 3.0 * 0.044715 * square)
    return (value * rise).astype(HALF_FLOAT), (rise + turn).astype(HALF_FLOAT)


def by_time(values):
    turned = jnp.swapaxes(values, 0, 1)
    extra = -turned.shape[1] % 16
    return jnp.pad(turned, ((0, 0), (0, extra)) + ((0, 0),) * (turned.ndim - 2))


def by_series(values, count):
    return jnp.swapaxes(values[:, :count], 0, 1)


def neighbours(low_side, high_side):
    count = lax.axis_size("tm")
    onward = [(i, i + 1) for i in range(count - 1)]
    return (
        lax.ppermute(high_side, "tm", onward),
        lax.ppermute(low_side, "tm", [(j, i) for i, j in onward]),
    )


def window_sum(values, first, width, count):
    total, level, size = None, values, 1
    while width:
        if width & 1:
            part = level[first : first + count]
            total = part if total is None else total + part
            first += size
        width >>= 1
        if width:
            level = level[:-size] + level[size:]
            size *= 2
    return total


def seasonal_parts(series, halves, rim):
    steps = series.shape[0]
    before, after = neighbours(series[:rim], series[steps - rim :])
    position = lax.axis_index("tm")
    before = jnp.where(position == 0, jnp.broadcast_to(series[:1], before.shape), before)
    is_final = position == lax.axis_size("tm") - 1
    after = jnp.where(is_final, jnp.broadcast_to(series[-1:], after.shape), after)
    wide = jnp.concatenate([before, series, after]).astype(FLOAT)
    parts = []
    for half in halves:
        mean = window_sum(wide, rim - half, 2 * half + 1, steps) / (2 * half + 1)
        parts.append((series.astype(FLOAT) - mean).astype(HALF_FLOAT))
    return parts


def series_gradient(grads, halves, rim):
    steps = grads[0].shape[0]
    wide = 0.0
    for grad, half in zip(grads, halves):
        padded = jnp.pad(grad, ((2 * rim, 2 * rim), (0, 0), (0, 0)))
        wide = wide + window_sum(padded, rim - half, 2 * half + 1, steps + 2 * rim) / (
            2 * half + 1
        )
    low_rim, high_rim = wide[:rim], wide[rim + steps :]
    before, after = neighbours(low_rim, high_rim)
    position = lax.axis_index("tm")
    is_final = position == lax.axis_size("tm") - 1
    low_sum = jnp.pad(jnp.sum(low_rim, axis=0, keepdims=True), ((0, rim - 1), (0, 0), (0, 0)))
    high_sum = jnp.pad(jnp.sum(high_rim, axis=0, keepdims=True), ((rim - 1, 0), (0, 0), (0, 0)))
    before = jnp.where(position == 0, low_sum, before)
    after = jnp.where(is_final, high_sum, after)
    middle = jnp.zeros((steps - 2 * rim,) + before.shape[1:], FLOAT)
    edges = jnp.concatenate([before, middle, after])
    return (sum(grads) - wide[rim : rim + steps] - edges).astype(HALF_FLOAT)


def step_block(kernel, sizes=(4, 3, 2, 1)):
    return next(size for size in sizes if kernel % size == 0)


def row_spec(block):
    return pl.BlockSpec(block, lambda i: (0,) * len(block))


def steps_spec(values, block):
    pieces, _, series, channels = values.shape
    return pl.BlockSpec((pieces, block, series, channels), lambda i: (0, i, 0, 0))


def weight_spec(weight, block):
    return pl.BlockSpec((block,) + weight.shape[1:], lambda i: (i, 0, 0))


def local_call(kernel, grid, inputs, outputs, flops, nbytes, name):
    return pl.pallas_call(
        kernel,
        out_shape=tuple(shape for shape, _ in outputs),
        grid=(grid,),
        in_specs=[spec for _, spec in inputs],
        out_specs=tuple(spec for _, spec in outputs),
        compiler_params=pltpu.CompilerParams(vmem_limit_bytes=48 * 1024 * 1024),
        cost_estimate=pl.CostEstimate(
            flops=flops, bytes_accessed=nbytes, transcendentals=0
        ),
        name=name,
    )(*[value for value, _ in inputs])


def down_kernel(x_ref, w_ref, b_ref, out_ref):
    step = pl.program_id(0)

    @pl.when(step == 0)
    def _():
        out_ref[...] = jnp.broadcast_to(b_ref[...], out_ref.shape)

    total = out_ref[...]
    for one in range(w_ref.shape[0]):
        total = total + dot_nn(x_ref[:, one].reshape(total.shape), w_ref[one])
    out_ref[...] = total

    @pl.when(step == pl.num_programs(0) - 1)
    def _():
        out_ref[...] = jnp.tanh(out_ref[...])


def down_layer(seasonal, weight, bias_row):
    pieces, kernel, series, channels = seasonal.shape
    block = step_block(kernel)
    rows = pieces * series
    (down_act,) = local_call(
        down_kernel,
        kernel // block,
        [
            (seasonal, steps_spec(seasonal, block)),
            (weight, weight_spec(weight, block)),
            (bias_row[None], row_spec((1, channels))),
        ],
        [(jax.ShapeDtypeStruct((rows, channels), FLOAT), row_spec((rows, channels)))],
        2 * seasonal.size * channels,
        2 * (seasonal.size + weight.size),
        "down_layer",
    )
    return down_act


def normed(values):
    center = values - jnp.mean(values, axis=-1, keepdims=True)
    spread = jnp.mean(center * center, axis=-1, keepdims=True)
    scale = lax.rsqrt(spread + EPSILON)
    return center * scale, scale


def normed_back(grad, hat, scale):
    return (
        grad
        - jnp.mean(grad, axis=-1, keepdims=True)
        - hat * jnp.mean(grad * hat, axis=-1, keepdims=True)
    ) * scale


def up_kernel(picks, inner_ref, x_ref, w_ref, rows_ref, act_ref, out_ref):
    bias_row, gain_row, shift_row = (rows_ref[i : i + 1] for i in picks)
    inner = inner_ref[...]
    for one in range(w_ref.shape[0]):
        act = jnp.tanh(dot_nn(inner, w_ref[one]) + bias_row)
        hat, _ = normed(act + x_ref[:, one].reshape(act.shape).astype(FLOAT))
        act_ref[:, one] = act.reshape(act_ref.shape[0], act_ref.shape[2], act_ref.shape[3])
        out = (hat * gain_row + shift_row).astype(HALF_FLOAT)
        out_ref[:, one] = out.reshape(out_ref.shape[0], out_ref.shape[2], out_ref.shape[3])


def up_layer(inner, seasonal, weight, rows, picks):
    pieces, kernel, series, channels = seasonal.shape
    block = step_block(kernel, (8, 6, 4, 3, 2, 1))
    return local_call(
        functools.partial(up_kernel, picks),
        kernel // block,
        [
            (inner, row_spec(inner.shape)),
            (seasonal, steps_spec(seasonal, block)),
            (weight, weight_spec(weight, block)),
            (rows, row_spec(rows.shape)),
        ],
        [
            (jax.ShapeDtypeStruct(seasonal.shape, FLOAT), steps_spec(seasonal, block)),
            (jax.ShapeDtypeStruct(seasonal.shape, HALF_FLOAT), steps_spec(seasonal, block)),
        ],
        2 * seasonal.size * channels,
        8 * seasonal.size + 2 * weight.size,
        "up_layer",
    )


def up_back_kernel(
    grad_ref, merge_ref, act_ref, x_ref, w_ref, gain_ref, outer_ref, up_ref, inner_ref, sums_ref
):
    @pl.when(pl.program_id(0) == 0)
    def _():
        inner_ref[...] = jnp.zeros_like(inner_ref)
        sums_ref[...] = jnp.zeros_like(sums_ref)

    shape = inner_ref.shape
    block = (x_ref.shape[0], x_ref.shape[2], x_ref.shape[3])
    gain_row = gain_ref[8:9]
    total = inner_ref[...]
    sums = [sums_ref[i : i + 1] for i in range(3)]
    for one in range(w_ref.shape[0]):
        grad = dot_nt(grad_ref[:, one].reshape(shape), merge_ref[0])
        act = act_ref[:, one].reshape(shape)
        hat, scale = normed(act + x_ref[:, one].reshape(shape).astype(FLOAT))
        outer = normed_back(grad * gain_row, hat, scale)
        up = (outer * (1.0 - act * act)).astype(HALF_FLOAT)
        total = total + dot_nt(up, w_ref[one])
        outer_ref[:, one] = outer.reshape(block)
        up_ref[:, one] = up.reshape(block)
        for i, value in enumerate((up.astype(FLOAT), grad * hat, grad)):
            sums[i] = sums[i] + jnp.sum(value, axis=0, keepdims=True)
    inner_ref[...] = total
    for i in range(3):
        sums_ref[i : i + 1] = sums[i]


def up_layer_back(grad, merge, index, act, seasonal, weight, table):
    pieces, kernel, series, channels = seasonal.shape
    block = step_block(kernel)
    rows = pieces * series
    spec = steps_spec(seasonal, block)
    return local_call(
        up_back_kernel,
        kernel // block,
        [
            (grad, spec),
            (merge, pl.BlockSpec((1,) + merge.shape[1:], lambda i: (index, 0, 0))),
            (act, spec),
            (seasonal, spec),
            (weight, weight_spec(weight, block)),
            (table, row_spec(table.shape)),
        ],
        [
            (jax.ShapeDtypeStruct(seasonal.shape, FLOAT), spec),
            (jax.ShapeDtypeStruct(seasonal.shape, HALF_FLOAT), spec),
            (jax.ShapeDtypeStruct((rows, channels), FLOAT), row_spec((rows, channels))),
            (jax.ShapeDtypeStruct((8, channels), FLOAT), row_spec((8, channels))),
        ],
        4 * seasonal.size * channels,
        14 * seasonal.size + 2 * weight.size,
        "up_layer_back",
    )


def head_kernel(
    one_ref,
    two_ref,
    cot_ref,
    mask_ref,
    table_ref,
    bias_ref,
    merge_ref,
    hidden_w_ref,
    output_w_ref,
    result_ref,
    first_ref,
    hidden_ref,
    grad_hidden_ref,
    feed_ref,
    merged_ref,
    sums_ref,
    hidden_sums_ref,
    slope_ref,
    rows_ref,
):
    @pl.when(pl.program_id(0) == 0)
    def _():
        sums_ref[...] = jnp.zeros_like(sums_ref)
        hidden_sums_ref[...] = jnp.zeros_like(hidden_sums_ref)

    channels = one_ref.shape[1]
    chunks = [pl.ds(k * channels, channels) for k in range(hidden_ref.shape[1] // channels)]
    gain_first, gain_final = table_ref[9:10], table_ref[10:11]
    merged = dot_nn(one_ref[...], merge_ref[0]) + dot_nn(two_ref[...], merge_ref[1])
    merged = merged + table_ref[6:7]
    hat_first, scale_first = normed(merged)
    first = (hat_first * gain_first + table_ref[12:13]).astype(HALF_FLOAT)
    first_ref[...] = first
    final = merged + table_ref[7:8]
    for chunk in chunks:
        value = dot_nn(first, hidden_w_ref[:, chunk]) + bias_ref[:, chunk]
        hidden, slope = gelu_pair(value)
        hidden_ref[:, chunk] = hidden
        slope_ref[:, chunk] = slope
        final = final + dot_nn(hidden, output_w_ref[chunk])
    hat_final, scale_final = normed(final)
    mask = mask_ref[...]
    result = (hat_final * gain_final + table_ref[13:14]) * mask
    for lane in range(rows_ref.shape[0]):
        rows_ref[lane] = result[:, lane * 128 : lane * 128 + 128]
    count, steps = result_ref.shape[0], result_ref.shape[1]
    series = rows_ref.shape[1] // steps
    for one in range(count):
        for lane in range(rows_ref.shape[0]):
            value = rows_ref[lane, pl.ds(one, steps, stride=series), :]
            result_ref[one, :, lane * 128 : lane * 128 + 128] = value.astype(HALF_FLOAT)
    grad = cot_ref[...].astype(FLOAT) * mask
    grad_final = normed_back(grad * gain_final, hat_final, scale_final)
    feed = grad_final.astype(HALF_FLOAT)
    feed_ref[...] = feed
    grad_first = jnp.zeros_like(merged)
    for chunk in chunks:
        value = dot_nt(feed, output_w_ref[chunk]) * slope_ref[:, chunk].astype(FLOAT)
        value = value.astype(HALF_FLOAT)
        grad_hidden_ref[:, chunk] = value
        hidden_sums_ref[0:1, chunk] += jnp.sum(value.astype(FLOAT), axis=0, keepdims=True)
        grad_first = grad_first + dot_nt(value, hidden_w_ref[:, chunk])
    grad_merged = grad_final + normed_back(grad_first * gain_first, hat_first, scale_first)
    low = grad_merged.astype(HALF_FLOAT)
    merged_ref[...] = low
    parts = (
        grad_first * hat_first,
        grad * hat_final,
        grad_first,
        grad,
        low.astype(FLOAT),
        feed.astype(FLOAT),
    )
    for row, value in enumerate(parts):
        sums_ref[row : row + 1] += jnp.sum(value, axis=0, keepdims=True)


def head(outs, cotangent, mask_rows, table, bias, merge, hidden_w, output_w, count):
    total, channels = outs[0].shape
    steps = cotangent.shape[0]
    series = total // steps
    block_steps = 48 if steps % 48 == 0 else 16
    rows, hidden = block_steps * series, hidden_w.shape[1]
    block, wide = (
        pl.BlockSpec((rows, channels), lambda i: (i, 0)),
        pl.BlockSpec((rows, hidden), lambda i: (i, 0)),
    )
    low, low_wide = (
        jax.ShapeDtypeStruct((total, channels), HALF_FLOAT),
        jax.ShapeDtypeStruct((total, hidden), HALF_FLOAT),
    )

    def held(value):
        return pl.BlockSpec(value.shape, lambda i: (0,) * value.ndim)

    return pl.pallas_call(
        head_kernel,
        out_shape=(
            jax.ShapeDtypeStruct((count, steps, channels), HALF_FLOAT),
            low,
            low_wide,
            low_wide,
            low,
            low,
            jax.ShapeDtypeStruct((8, channels), FLOAT),
            jax.ShapeDtypeStruct((8, hidden), FLOAT),
        ),
        grid=(steps // block_steps,),
        in_specs=[
            block,
            block,
            block,
            pl.BlockSpec((rows, 1), lambda i: (i, 0)),
            held(table),
            held(bias),
            held(merge),
            held(hidden_w),
            held(output_w),
        ],
        out_specs=(
            pl.BlockSpec((count, block_steps, channels), lambda i: (0, i, 0)),
            block,
            wide,
            wide,
            block,
            block,
            pl.BlockSpec((8, channels), lambda i: (0, 0)),
            pl.BlockSpec((8, hidden), lambda i: (0, 0)),
        ),
        scratch_shapes=[
            pltpu.VMEM((rows, hidden), HALF_FLOAT),
            pltpu.VMEM((channels // 128, rows, 128), FLOAT),
        ],
        compiler_params=pltpu.CompilerParams(vmem_limit_bytes=56 * 1024 * 1024),
        cost_estimate=pl.CostEstimate(
            flops=2 * total * channels * (4 * channels + 4 * hidden),
            bytes_accessed=total * (14 * channels + 4 * hidden),
            transcendentals=total * hidden,
        ),
        name="head",
    )(
        outs[0],
        outs[1],
        cotangent.reshape(total, channels),
        mask_rows,
        table,
        bias,
        merge,
        hidden_w,
        output_w,
    )


def down_back_kernel(grad_ref, w_ref, outer_ref, out_ref):
    grad = grad_ref[...]
    block = (out_ref.shape[0], out_ref.shape[2], out_ref.shape[3])
    for one in range(w_ref.shape[0]):
        out_ref[:, one] = dot_nt(grad, w_ref[one]).reshape(block) + outer_ref[:, one]


def down_layer_back(grad, weight, outer):
    pieces, kernel, series, channels = outer.shape
    block = step_block(kernel)
    spec = steps_spec(outer, block)
    (seasonal_grad,) = local_call(
        down_back_kernel,
        kernel // block,
        [(grad, row_spec(grad.shape)), (weight, weight_spec(weight, block)), (outer, spec)],
        [(jax.ShapeDtypeStruct(outer.shape, FLOAT), spec)],
        2 * outer.size * channels,
        8 * outer.size + 2 * weight.size,
        "down_layer_back",
    )
    return seasonal_grad


class Branch:
    def __init__(self, index, shape, down_weight, table):
        self.index, self.table = index, table
        self.count, steps, channels = shape
        self.kernel = down_weight.shape[0]
        self.pieces = steps // self.kernel
        self.series = round_up(self.count, 16)
        self.down_weight = down_weight
        self.gain_row, self.shift_row = table[8], table[11]

    def down(self, seasonal, down_act=None):
        self.seasonal = seasonal.reshape(self.pieces, self.kernel, self.series, -1)
        if down_act is None:
            down_act = down_layer(self.seasonal, self.down_weight, self.table[self.index])
        self.down_act = down_act
        self.down_low = down_act.astype(HALF_FLOAT)

    def to_series(self, rows):
        return by_series(rows.reshape(self.pieces, self.series, -1), self.count)

    def from_series(self, values):
        return by_time(values).reshape(self.pieces * self.series, -1)

    def inner(self, iso_out):
        act = jnp.tanh(self.from_series(iso_out).astype(FLOAT) + self.table[2 + self.index])
        inner_in = act + self.down_low.astype(FLOAT)
        return act, layer_norm(inner_in, self.gain_row, self.shift_row).astype(HALF_FLOAT)

    def up(self, iso_act, inner_low, up_weight):
        self.up_weight, self.iso_act, self.inner_low = up_weight, iso_act, inner_low
        self.act, out = up_layer(
            inner_low, self.seasonal, up_weight, self.table, (4 + self.index, 8, 11)
        )
        return out.reshape(-1, out.shape[3])

    def up_back(self, grad_merged, merge):
        self.outer, self.grad_up, grad_inner, sums = up_layer_back(
            grad_merged.reshape(self.seasonal.shape),
            merge,
            self.index,
            self.act,
            self.seasonal,
            self.up_weight,
            self.table,
        )
        inner_in = self.iso_act + self.down_low.astype(FLOAT)
        _, inner_pull = jax.vjp(layer_norm, inner_in, self.gain_row, self.shift_row)
        self.grad_inner_in, gain_inner, shift_inner = inner_pull(grad_inner)
        grad_iso = self.grad_inner_in * (1.0 - self.iso_act * self.iso_act)
        self.iso_sum, self.up_sum = jnp.sum(grad_iso, axis=0), sums[0]
        self.gain_sum, self.shift_sum = sums[1] + gain_inner, sums[2] + shift_inner
        return grad_iso.astype(HALF_FLOAT)

    def down_back(self, grad_signal):
        grad_down = self.from_series(grad_signal).astype(FLOAT) + self.grad_inner_in
        self.grad_down = (grad_down * (1.0 - self.down_act * self.down_act)).astype(HALF_FLOAT)
        return jnp.sum(self.grad_down.astype(FLOAT), axis=0)

    def seasonal_back(self):
        grad = down_layer_back(self.grad_down, self.down_weight, self.outer)
        return grad.reshape(-1, self.series, grad.shape[3])


def batch_split(values, split, join):
    return lax.all_to_all(values, "batch", split_axis=split, concat_axis=join, tiled=True)


def time_sum(values, dim):
    return lax.psum_scatter(
        values.astype(HALF_FLOAT), "tm", scatter_dimension=dim, tiled=True
    ).astype(FLOAT)


def plain_gradients(wides, narrows, downs):
    results = []
    for wide, narrow, down in zip(wides, narrows, downs):
        wide = jnp.swapaxes(wide, 0, 1).reshape(wide.shape[1], -1, wide.shape[3])
        if down:
            wide, narrow = batch_split(wide, 2, 1), lax.all_gather(narrow, "batch", tiled=True)
            value = jnp.einsum("knc,nd->kcd", wide, narrow, preferred_element_type=FLOAT)
        else:
            wide = lax.all_gather(wide, "batch", axis=1, tiled=True)
            narrow = batch_split(narrow, 1, 0)
            value = jnp.einsum("nd,knc->dkc", narrow, wide, preferred_element_type=FLOAT)
        results.append(time_sum(value, 2))
    return results


def plain_sums(matrices):
    results = []
    for kind, value in matrices:
        batch_dim, time_dim = (0, 1) if kind == "rows" else (value.ndim - 1, value.ndim - 2)
        value = lax.psum_scatter(
            value.astype(FLOAT), "batch", scatter_dimension=batch_dim, tiled=True
        )
        results.append(time_sum(value, time_dim))
    return results


def per_device(
    series_in,
    out_cotangent,
    out_mask,
    down_twelve,
    down_sixteen,
    iso_twelve,
    iso_sixteen,
    up_twelve,
    up_sixteen,
    branch_bias,
    merge_weight,
    hidden_weight,
    hidden_bias,
    output_weight,
    head_bias,
    norm_gain,
    norm_shift,
):
    series_dev, step_count, channels = series_in.shape
    halves = (down_twelve.shape[0] // 2, down_sixteen.shape[0] // 2)
    rim = max(halves)
    hidden_rows = hidden_bias.reshape(-1, channels)
    table = jnp.concatenate([branch_bias, head_bias, norm_gain, norm_shift, hidden_rows])
    table = jnp.pad(table, ((0, -table.shape[0] % 8), (0, 0))).astype(FLOAT)
    down_weights = (down_twelve, down_sixteen)
    branches = [
        Branch(k, series_in.shape, down_weights[k], table) for k in range(2)
    ]
    iso_weights = (iso_twelve, iso_sixteen)
    sizes = plane_sizes(channels)
    up_weights = [up_twelve, up_sixteen]
    turns = [weight for weight in up_weights if weight.shape[1] % 8 == 0]
    shapes = [(series_dev, branch.pieces, channels) for branch in branches]
    if sizes:
        per_time = sum(round_up(branch.pieces, 8) for branch in branches)
        values, wides = None, []
        front = (series_in, out_cotangent, down_weights, table, per_time, halves, rim)
    else:
        for branch, seasonal in zip(branches, seasonal_parts(by_time(series_in), halves, rim)):
            branch.down(seasonal)
        values = [branch.to_series(branch.down_low) for branch in branches]
        wides = [branch.seasonal for branch in branches]
        front = None
    forward, iso_outs = spectral(
        values, shapes, iso_weights, False, ForwardExtra(sizes, wides, turns, front)
    )
    if sizes:
        for k in range(2):
            branches[k].down(forward[f"seasonal{k}"], forward[f"down_act{k}"])
        inners = [(forward[f"iso_act{k}"], forward[f"inner{k}"]) for k in range(2)]
        cotangent = forward["cotangent_steps"]
    else:
        inners = [branches[k].inner(iso_outs[k]) for k in range(2)]
        cotangent = by_time(out_cotangent)
    turned = [forward[f"turned{i}"] for i in range(len(turns))]
    up_weights = [
        jnp.swapaxes(weight, 0, 1) if weight.shape[1] % 8 else turned.pop(0)
        for weight in up_weights
    ]
    outs = [
        branch.up(*inner, weight)
        for branch, inner, weight in zip(branches, inners, up_weights)
    ]
    row_count = outs[0].shape[0]
    mask_rows = by_time(out_mask.astype(FLOAT)).reshape(row_count, 1)
    hidden_row = table[14 : 14 + hidden_rows.shape[0]].reshape(1, -1)
    result, first_low, hidden_low, grad_hidden_pre, grad_feed, grad_merged, sums, hidden_sums = head(
        outs,
        cotangent,
        mask_rows,
        table,
        hidden_row,
        merge_weight,
        hidden_weight,
        output_weight,
        series_dev,
    )
    gain_first, gain_final, shift_first, shift_final = (sums[k] for k in range(4))
    grad_merge_bias, grad_output_bias, grad_hidden_bias = sums[4], sums[5], hidden_sums[0]
    hidden_size = hidden_low.shape[1]
    jobs = (
        (first_low, [grad_hidden_pre], (channels, hidden_size)),
        (grad_feed, [hidden_low], (channels, hidden_size)),
        (grad_merged, outs, (2, channels, channels)),
    )
    job_kinds = ("rows", "lanes", "lanes")
    grad_isos = [branches[k].up_back(grad_merged, merge_weight) for k in range(2)]
    up_wides = [branch.grad_up for branch in branches]
    up_narrows = [branch.inner_low for branch in branches]
    backward, grad_signals = spectral(
        [branch.to_series(grad) for branch, grad in zip(branches, grad_isos)],
        shapes,
        iso_weights,
        True,
        BackwardExtra(
            sizes,
            forward["spec"],
            up_wides,
            up_narrows,
            jobs,
            [branch.grad_inner_in for branch in branches],
            [branch.down_act for branch in branches],
            (
                series_dev,
                sum(round_up(branch.pieces, 8) for branch in branches),
                branches[0].series,
            ),
        ),
    )
    iso_parts, first = [], 0
    for bins in (branches[0].pieces, branches[1].pieces):
        iso_parts.append(
            iso_gradients(
                forward["spec"],
                backward["specs"],
                backward["spec"],
                backward["grads"],
                first,
                bins,
            )
        )
        first += round_up(bins, 8)
    if sizes:
        matrices = [(kind, backward[f"matrix{i}"]) for i, kind in enumerate(job_kinds)]
        down_sums = backward["down_sums"][:2]
        down_narrows = [backward["down_grad0"], backward["down_grad1"]]
    else:
        matrices = []
        for kind, (left, rights, shape) in zip(job_kinds, jobs):
            values = [
                jnp.einsum("nd,nf->df", left, right, preferred_element_type=FLOAT)
                for right in rights
            ]
            matrices.append((kind, jnp.stack(values).astype(HALF_FLOAT).reshape(shape)))
        down_sums = jnp.stack([branches[k].down_back(grad_signals[k]) for k in range(2)])
        down_narrows = [branch.grad_down for branch in branches]
    one, two = branches
    singles = (one.iso_sum, two.iso_sum, one.up_sum, two.up_sum)
    singles += (one.gain_sum + two.gain_sum, gain_first, gain_final)
    singles += (one.shift_sum + two.shift_sum, shift_first, shift_final)
    singles += (grad_merge_bias, grad_output_bias)
    vectors = jnp.concatenate(
        [down_sums] + [row[None] for row in singles] + [grad_hidden_bias.reshape(-1, channels)]
    )
    vectors = jnp.pad(vectors, ((0, -vectors.shape[0] % 8), (0, 0)))
    if sizes:
        downs, vectors, grad_series, sums = down_gradients(
            sizes,
            (forward["gathered0"], forward["gathered1"]),
            down_narrows,
            vectors,
            (down_twelve, down_sixteen),
            [branch.outer.reshape(step_count, -1, channels) for branch in branches],
            halves,
            rim,
            series_dev,
            matrices,
        )
        downs = [jnp.transpose(value, (0, 2, 1)) for value in downs]
        ups = [jnp.transpose(backward[key], (2, 0, 1)) for key in ("up0", "up1")]
    else:
        vectors = lax.psum(vectors, ("tm", "batch"))
        grad_seasonals = [branch.seasonal_back() for branch in branches]
        grad_series = by_series(series_gradient(grad_seasonals, halves, rim), series_dev)
        downs = plain_gradients(wides, down_narrows, (True, True))
        ups = plain_gradients(up_wides, up_narrows, (False, False))
        sums = plain_sums(matrices)
    me, devices = lax.axis_index("tm"), lax.axis_size("tm")
    width = channels // devices
    rows = lax.dynamic_slice_in_dim(vectors[:14], me * width, width, axis=1)
    hidden_width = hidden_bias.shape[0] // devices
    hidden_sum = vectors[14 : 14 + hidden_rows.shape[0]].reshape(-1)
    vector_parts = (
        rows[:6],
        lax.dynamic_slice_in_dim(hidden_sum, me * hidden_width, hidden_width),
        rows[12:14],
        rows[6:9],
        rows[9:12],
    )
    return (
        result,
        grad_series,
        downs[0],
        downs[1],
        iso_parts[0],
        iso_parts[1],
        ups[0],
        ups[1],
        vector_parts[0],
        jnp.swapaxes(sums[2], 1, 2),
        sums[0],
        vector_parts[1],
        sums[1].T,
        vector_parts[2],
        vector_parts[3],
        vector_parts[4],
    )


def solution(mesh):
    placed = (
        P("batch", "tm", None),
        P("batch", "tm", None),
        P("batch", "tm"),
        P(),
        P(),
        P("tm", None, "batch", None),
        P("tm", None, "batch", None),
        P(),
        P(),
        P(),
        P(),
        P(),
        P(),
        P(),
        P(),
        P(),
        P(),
    )
    return jax.shard_map(
        per_device,
        mesh=mesh,
        in_specs=placed,
        out_specs=(
            P("batch", "tm", None),
            P("batch", "tm", None),
            P(None, "batch", "tm"),
            P(None, "batch", "tm"),
            P("tm", None, "batch", None),
            P("tm", None, "batch", None),
            P("batch", None, "tm"),
            P("batch", None, "tm"),
            P(None, "tm"),
            P(None, "batch", "tm"),
            P("batch", "tm"),
            P("tm"),
            P("batch", "tm"),
            P(None, "tm"),
            P(None, "tm"),
            P(None, "tm"),
        ),
        check_vma=False,
    )
```
